32 devices in a mesh: dp: 4 (over x, core), ctx: 4 (over z), tensor: 2 (over y).
Axes of the slice: x: 2, y: 2, z: 4, core: 2. Of those that a mesh axis runs over, the one named last changes fastest.
Arguments:
- hidden_in: bfloat16 [8192, 1536], P(('dp', 'ctx')), may hold values from -6 to 6
- attn_gain: float32 [1536], replicated, may hold values from 0.5 to 1.5
- q_weight: bfloat16 [1536, 1536], P(None, 'tensor'), may hold values from -0.21875 to 0.21875
- key_matrix: bfloat16 [1536, 512], P(None, 'tensor'), may hold values from -0.15625 to 0.15625
- value_matrix: bfloat16 [1536, 512], P(None, 'tensor'), may hold values from -0.15625 to 0.15625
- o_weight: bfloat16 [1536, 1536], P(None, 'tensor'), may hold values from -1.75 to 1.75
- moe_gain: float32 [1536], replicated, may hold values from 0.5 to 1.5
- router_weight: bfloat16 [1536, 24], replicated, may hold values from -0.078125 to 0.078125
- gate_weight: bfloat16 [24, 1536, 512], P(None, None, 'tensor'), may hold values from -0.15625 to 0.15625
- up_weight: bfloat16 [24, 1536, 512], P(None, None, 'tensor'), may hold values from -0.15625 to 0.15625
- down_weight: bfloat16 [24, 1536, 512], P(None, None, 'tensor'), may hold values from -1 to 1
- segments: int32 [8192], P('dp'), may hold values from 0 to 1, as said below
- expert_picks: int32 [8192, 8], P(('dp', 'ctx')), may hold values from 0 to 23, all different within a row; in each aligned block of 512 rows (0 to 511, 512 to 1023, ...) at most 341 rows name the same one
- output_grad: bfloat16 [8192, 1536], P(('dp', 'ctx')), may hold values from -6 to 6
Outputs:
- output: bfloat16 [8192, 1536], P(('dp', 'ctx'))
- input_grad: float32 [8192, 1536], P(('dp', 'ctx'))
- grad_attn_gain: float32 [1536], P(('dp', 'ctx'))
- grad_q: float32 [1536, 1536], P(('dp', 'ctx'), 'tensor')
- grad_k: float32 [1536, 512], P(('dp', 'ctx'), 'tensor')
- grad_v: float32 [1536, 512], P(('dp', 'ctx'), 'tensor')
- grad_o: float32 [1536, 1536], P(('dp', 'ctx'), 'tensor')
- grad_moe_gain: float32 [1536], P(('dp', 'ctx'))
- grad_router: float32 [1536, 24], P(('dp', 'ctx'))
- grad_gate: float32 [24, 1536, 512], P(None, ('dp', 'ctx'), 'tensor')
- grad_up: float32 [24, 1536, 512], P(None, ('dp', 'ctx'), 'tensor')
- grad_down: float32 [24, 1536, 512], P(None, ('dp', 'ctx'), 'tensor')
The draws below stay inside these ranges and needn't reach their ends.
Inputs may be any that keep to these rules, and one draw needn't show every extreme that they name: `segments`: within each sequence of 2048 tokens documents are runs of one number, 1, 2, 3 and so on from its start; each sequence holds exactly 1 documents of 200 to 2000 tokens each; tokens after the last document hold 0. `expert_picks`: the 8 experts of a row are different. In each aligned block of 512 rows (the rows of one device) no expert is named by more than 341 rows.
All inputs are finite; a program needn't handle non-finite values.
Results may differ from the reference program's by a relative error of at most 0.03.
Values may be sent and summed in bfloat16 or wider, within the bound.
A program may use at most 384 MiB of HBM per device.

```python
import math
import jax
import jax.numpy as jnp
import numpy as np
from jax import lax

MODEL_WIDTH = 1536
QUERY_HEADS = 24
KEY_VALUE_HEADS = 8
HEAD_SIZE = 64
FF = 512
TOPK = 8
NEXP = 24
DOC_MIN = 200
DOC_MAX = 2000
TOK_DEV = 512
CAP = 341
SEQUENCE_TOKENS = 2048
TOKENS = 8192


def draw_segments(key, part):
    seq_count = TOKENS // SEQUENCE_TOKENS
    doc_count = SEQUENCE_TOKENS // DOC_MAX

    def one_sequence(seq_key):
        lengths = jax.random.randint(seq_key, (doc_count,), DOC_MIN, DOC_MAX + 1, dtype=jnp.int32)
        doc_ends = jnp.cumsum(lengths, dtype=jnp.int32)
        token_positions = jnp.arange(SEQUENCE_TOKENS, dtype=jnp.int32)
        doc_index = jnp.sum((token_positions[:, None] >= doc_ends[None, :]).astype(jnp.int32), axis=1, dtype=jnp.int32)
        return jnp.where(doc_index < doc_count, doc_index + 1, 0).astype(jnp.int32)
    return jax.vmap(one_sequence)(jax.random.split(jax.random.fold_in(key, 17), seq_count)).reshape(-1)


def block_levels(rng, extent, shards, low, high):
    def one(position, blocks):
        steps = jax.random.uniform(jax.random.fold_in(jax.random.fold_in(rng, 6), position), (blocks,), jnp.float32, low / len(shards), high / len(shards))
        return jnp.repeat(jnp.exp(steps), extent[position] // blocks).reshape((-1,) + (1,) * (len(extent) - position - 1))

    loudness = one(*shards[0])
    for cut in shards[1:]:
        loudness = loudness * one(*cut)
    return loudness


def assign_block(key, own, number, rows, amount, top, limit, slope):
    ranking = jax.random.permutation(key, amount)
    crowded, usual = load_shares(amount, rows * top, limit, slope, True), load_shares(amount, rows * top, limit, slope, False)
    places = jnp.arange(amount)

    def named(tallies, rotation):
        used = int((tallies > 0).sum())
        fixed = max(1, used // 4)
        moved = fixed + (places - fixed + rotation * (used - fixed)) % max(1, amount - fixed)
        return jnp.zeros((amount,), jnp.int32).at[ranking[jnp.where(places < fixed, places, moved)]].set(jnp.asarray(tallies, jnp.int32))

    tallies = jnp.where(number % 4 == 0, named(crowded, number // 4), named(usual, number - number // 4 - 1))
    mixed = jax.random.permutation(jax.random.fold_in(own, 3), amount)
    donor, taker = mixed[0:amount // 2 * 2:2], mixed[1:amount // 2 * 2:2]
    margin = jnp.minimum(tallies[donor] - 1, limit - tallies[taker]) // 2
    margin = jnp.where((donor == ranking[0]) | (taker == ranking[0]) | (tallies[taker] == 0), 0, jnp.maximum(margin, 0))
    moved = jax.random.randint(jax.random.fold_in(own, 4), (amount // 2,), 0, 1 << 20) % (margin + 1)
    tallies = tallies.at[donor].add(-moved).at[taker].add(moved)
    items = jnp.searchsorted(jnp.cumsum(tallies), jnp.arange(rows * top), side="right").astype(jnp.int32)
    grid = items.reshape(top, rows).T
    grid = grid[jax.random.permutation(jax.random.fold_in(own, 1), rows)]
    rotation = jax.random.randint(jax.random.fold_in(own, 2), (rows, 1), 0, top)
    return jnp.take_along_axis(grid, (jnp.arange(top)[None, :] + rotation) % top, axis=1)


def load_shares(number_of, total, reach, slope, full):
    weights = [(1 << 20) // math.isqrt(standing ** slope) + 1 for standing in range(1, number_of + 1)]
    largest = reach if full else min(reach, max(-(-total // number_of), total * weights[0] // sum(weights)))
    least = 1 if total - largest >= number_of - 1 else 0
    holding, spare = [largest] + [least] * (number_of - 1), total - largest - least * (number_of - 1)
    while spare > 0:
        candidates = [i for i in range(1, number_of) if holding[i] < largest] or [i for i in range(1, number_of) if holding[i] < reach]
        pool, remaining = sum([weights[i] for i in candidates]), spare
        for i in candidates:
            more = min(reach - holding[i], max(1, remaining * weights[i] // pool), spare)
            holding[i] = holding[i] + more
            spare = spare - more
    return np.array(holding)


def bell_draw(key, dims, deviation, most, cuts=(), kind=jnp.bfloat16):
    level = block_levels(key, dims, cuts, -0.22, 0.18) if cuts else 1.0
    array = jax.random.normal(key, dims, jnp.float32) * deviation * level
    return jnp.minimum(jnp.maximum(array, -most), most).astype(kind)


def setup_inputs(seed: int = 0) -> dict:
    streams_of = jax.random.split(jax.random.key(seed), 15)
    hidden_in = bell_draw(streams_of[0], (TOKENS, MODEL_WIDTH), 1.0, 6.0, ((0, 16),))
    attn_gain = jnp.clip(1.0 + 0.1 * jax.random.normal(streams_of[1], (MODEL_WIDTH,), jnp.float32), 0.5, 1.5)
    q_weight = bell_draw(streams_of[2], (MODEL_WIDTH, QUERY_HEADS * HEAD_SIZE), (MODEL_WIDTH // 2) ** -0.5, 0.21875, ((1, 2),))
    key_matrix = bell_draw(streams_of[3], (MODEL_WIDTH, KEY_VALUE_HEADS * HEAD_SIZE), MODEL_WIDTH ** -0.5, 0.15625, ((1, 2),))
    value_matrix = bell_draw(streams_of[4], (MODEL_WIDTH, KEY_VALUE_HEADS * HEAD_SIZE), MODEL_WIDTH ** -0.5, 0.15625, ((1, 2),))
    o_weight = bell_draw(streams_of[5], (MODEL_WIDTH, QUERY_HEADS * HEAD_SIZE), (max(QUERY_HEADS * HEAD_SIZE // 128, 1)) ** -0.5, 1.75, ((1, 2),))
    moe_gain = jnp.clip(1.0 + 0.1 * jax.random.normal(streams_of[6], (MODEL_WIDTH,), jnp.float32), 0.5, 1.5)
    router_weight = bell_draw(streams_of[7], (MODEL_WIDTH, NEXP), (4 * MODEL_WIDTH) ** -0.5, 0.078125)
    gate_weight = bell_draw(streams_of[8], (NEXP, MODEL_WIDTH, FF), MODEL_WIDTH ** -0.5, 0.15625, ((2, 2),))
    up_weight = bell_draw(streams_of[9], (NEXP, MODEL_WIDTH, FF), MODEL_WIDTH ** -0.5, 0.15625, ((2, 2),))
    down_weight = bell_draw(streams_of[10], (NEXP, MODEL_WIDTH, FF), (max(FF // 16, 1)) ** -0.5, 1.0, ((2, 2),))
    segments = draw_segments(jax.random.fold_in(streams_of[14], 71), 0)
    expert_picks_keys = jax.random.split(jax.random.fold_in(streams_of[12], 1), TOKENS // TOK_DEV)
    expert_picks_turns = jax.random.permutation(jax.random.fold_in(streams_of[12], 3), TOKENS // TOK_DEV)
    expert_picks = jax.vmap(lambda own, number: assign_block(jax.random.fold_in(streams_of[12], 2), own, number, TOK_DEV, NEXP, TOPK, CAP, 1))(expert_picks_keys, expert_picks_turns).reshape((TOKENS, TOPK))
    output_grad = bell_draw(streams_of[13], (TOKENS, MODEL_WIDTH), 1.0, 6.0, ((0, 16),))
    return dict(hidden_in=hidden_in, attn_gain=attn_gain, q_weight=q_weight, key_matrix=key_matrix, value_matrix=value_matrix, o_weight=o_weight, moe_gain=moe_gain, router_weight=router_weight, gate_weight=gate_weight, up_weight=up_weight, down_weight=down_weight, segments=segments, expert_picks=expert_picks, output_grad=output_grad)


EPSILON = 1e-06
ROPE_BASE = 10000.0
NEGATIVE = -1e+30
HIGHEST = lax.Precision.HIGHEST

@jax.custom_vjp
def lower_precision(v):
    return lax.optimization_barrier(v.astype(jnp.bfloat16)).astype(jnp.float32)

@jax.custom_vjp
def lower_precision_backward(v):
    return v

def low_keep(v):
    return (lower_precision(v), None)

def low_pass(kept, grad):
    return (grad,)

def back_keep(v):
    return (v, None)

def back_low(kept, grad):
    return (lower_precision(grad),)
lower_precision.defvjp(low_keep, low_pass)
lower_precision_backward.defvjp(back_keep, back_low)

def product_highest(left, right):
    return jnp.dot(left, right, precision=HIGHEST)

def normalize(rows, gain):
    scale_inv = lax.rsqrt(lax.optimization_barrier(jnp.mean(rows * rows, axis=-1, keepdims=True)) + EPSILON)
    return rows * scale_inv * gain

def apply_rotary(value_rows, token_positions):
    half_dim = value_rows.shape[-1] // 2
    frequency = ROPE_BASE ** (-jnp.arange(half_dim, dtype=jnp.float32) / half_dim)
    angles = token_positions.astype(jnp.float32)[:, None] * frequency[None, :]
    cosine = jnp.cos(angles)[:, None, :]
    sine_part = jnp.sin(angles)[:, None, :]
    first_half = value_rows[..., :half_dim]
    second = value_rows[..., half_dim:]
    return jnp.concatenate([first_half * cosine - second * sine_part, second * cosine + first_half * sine_part], axis=-1)

def dispatch(expert_picks, experts, capacity):
    flat_ids = expert_picks.reshape(-1).astype(jnp.int32)
    sort_order = jnp.argsort(flat_ids, stable=True).astype(jnp.int32)
    sorted_ids = flat_ids[sort_order]
    onehot = sorted_ids[:, None] == jnp.arange(experts, dtype=jnp.int32)[None, :]
    counts = lax.optimization_barrier(jnp.sum(onehot.astype(jnp.int32), axis=0, dtype=jnp.int32))
    starts = (jnp.cumsum(counts, dtype=jnp.int32) - counts).astype(jnp.int32)
    start_of = lax.optimization_barrier(jnp.sum(jnp.where(onehot, starts[None, :], 0), axis=1, dtype=jnp.int32))
    rank_in = jnp.arange(flat_ids.shape[0], dtype=jnp.int32) - start_of
    slot_sorted = (sorted_ids * capacity + rank_in).astype(jnp.int32)
    slot_of_pair = jnp.zeros_like(flat_ids).at[sort_order].set(slot_sorted)
    pair_of_slot = jnp.full((experts * capacity,), flat_ids.shape[0], jnp.int32).at[slot_sorted].set(sort_order)
    return (slot_of_pair, pair_of_slot)

def attend(normed_sequence, seq_segments, q_weight, key_matrix, value_matrix, o_weight):
    token_positions = jnp.arange(SEQUENCE_TOKENS, dtype=jnp.int32)
    query_rows = lower_precision_backward(product_highest(normed_sequence, q_weight)).reshape(SEQUENCE_TOKENS, QUERY_HEADS, HEAD_SIZE)
    key_projected = lower_precision_backward(product_highest(normed_sequence, key_matrix)).reshape(SEQUENCE_TOKENS, KEY_VALUE_HEADS, HEAD_SIZE)
    value_rows = lower_precision(lower_precision_backward(product_highest(normed_sequence, value_matrix))).reshape(SEQUENCE_TOKENS, KEY_VALUE_HEADS, HEAD_SIZE)
    query_rotated = lower_precision(apply_rotary(query_rows, token_positions)).reshape(SEQUENCE_TOKENS, KEY_VALUE_HEADS, QUERY_HEADS // KEY_VALUE_HEADS, HEAD_SIZE)
    key_rot = lower_precision(apply_rotary(key_projected, token_positions))
    block_rows = math.gcd(SEQUENCE_TOKENS, 512)
    score_scale = 1.0 / math.sqrt(HEAD_SIZE)

    def one_block(block_index):
        offset = block_index * block_rows
        query_block = lax.dynamic_slice_in_dim(query_rotated, offset, block_rows, 0)
        query_pos = offset + jnp.arange(block_rows, dtype=jnp.int32)
        query_seg = lax.dynamic_slice_in_dim(seq_segments, offset, block_rows, 0)
        scores = lower_precision_backward(jnp.einsum('tkgd,nkd->kgtn', query_block, key_rot, precision=HIGHEST) * score_scale)
        allowed = (query_seg[:, None] == seq_segments[None, :]) & (token_positions[None, :] <= query_pos[:, None])
        scores = jnp.where(allowed, scores, NEGATIVE)
        probability = lower_precision(jax.nn.softmax(scores, axis=-1))
        attended = jnp.einsum('kgtn,nkd->tkgd', probability, value_rows, precision=HIGHEST)
        return attended.reshape(block_rows, QUERY_HEADS * HEAD_SIZE)
    attended = lax.map(jax.checkpoint(one_block), jnp.arange(SEQUENCE_TOKENS // block_rows, dtype=jnp.int32))
    attended = lower_precision(lower_precision_backward(attended.reshape(SEQUENCE_TOKENS, QUERY_HEADS * HEAD_SIZE)))
    return jnp.dot(attended, o_weight.T, precision=HIGHEST)

def moe_block(normed_block, picks_block, router_weight, gate_weight, up_weight, down_weight):
    logits = lower_precision_backward(product_highest(normed_block, router_weight))
    onehot = picks_block[:, :, None] == jnp.arange(NEXP, dtype=jnp.int32)[None, None, :]
    picked = lax.optimization_barrier(jnp.sum(jnp.where(onehot, logits[:, None, :], 0.0), axis=2))
    gate_probs = jax.nn.softmax(picked, axis=-1)
    slot_of_pair, pair_of_slot = dispatch(picks_block, NEXP, CAP)
    token_ids = pair_of_slot // TOPK
    normed_pad = jnp.concatenate([normed_block, jnp.zeros((1, MODEL_WIDTH), jnp.float32)], axis=0)
    slot_rows = normed_pad[token_ids].reshape(NEXP, CAP, MODEL_WIDTH)
    gate_act = lower_precision_backward(jnp.einsum('ecd,edf->ecf', slot_rows, gate_weight, precision=HIGHEST))
    up_act = lower_precision_backward(jnp.einsum('ecd,edf->ecf', slot_rows, up_weight, precision=HIGHEST))
    hidden = lower_precision(jax.nn.silu(gate_act) * up_act)
    expert_out = lower_precision_backward(jnp.einsum('ecf,edf->ecd', hidden, down_weight, precision=HIGHEST))
    pair_out = expert_out.reshape(NEXP * CAP, MODEL_WIDTH)[slot_of_pair].reshape(TOK_DEV, TOPK, MODEL_WIDTH)
    return lax.optimization_barrier(jnp.sum(gate_probs[:, :, None] * pair_out, axis=1))

def forward(hidden_in, attn_gain, q_weight, key_matrix, value_matrix, o_weight, moe_gain, router_weight, gate_weight, up_weight, down_weight, segments, expert_picks):
    normed_one = lower_precision(normalize(hidden_in, attn_gain))
    seq_count = TOKENS // SEQUENCE_TOKENS
    seq_inputs = (normed_one.reshape(seq_count, SEQUENCE_TOKENS, MODEL_WIDTH), segments.reshape(seq_count, SEQUENCE_TOKENS))
    mixed_attn = lax.map(lambda seq_pair: attend(seq_pair[0], seq_pair[1], q_weight, key_matrix, value_matrix, o_weight), seq_inputs)
    resid = hidden_in + lower_precision_backward(mixed_attn.reshape(TOKENS, MODEL_WIDTH))
    normed_two = lower_precision(normalize(resid, moe_gain))
    block_count = TOKENS // TOK_DEV
    block_inputs = (normed_two.reshape(block_count, TOK_DEV, MODEL_WIDTH), expert_picks.reshape(block_count, TOK_DEV, TOPK))
    mixed_moe = lax.map(jax.checkpoint(lambda block_pair: moe_block(block_pair[0], block_pair[1], router_weight, gate_weight, up_weight, down_weight)), block_inputs)
    return resid + mixed_moe.reshape(TOKENS, MODEL_WIDTH)

def reference(hidden_in, attn_gain, q_weight, key_matrix, value_matrix, o_weight, moe_gain, router_weight, gate_weight, up_weight, down_weight, segments, expert_picks, output_grad):
    floats = [hidden_in, attn_gain, q_weight, key_matrix, value_matrix, o_weight, moe_gain, router_weight, gate_weight, up_weight, down_weight]
    floats = [array_part.astype(jnp.float32) for array_part in floats]

    def forward_fn(*params):
        return forward(*params, segments, expert_picks)
    result, pullback = jax.vjp(forward_fn, *floats)
    gradients = pullback(output_grad.astype(jnp.float32))
    return (result.astype(jnp.bfloat16), gradients[0], gradients[1], gradients[2], gradients[3], gradients[4], gradients[5], gradients[6], gradients[7], gradients[8], gradients[9], gradients[10])
```

```python
import math

import jax
import jax.numpy as jnp
from jax import lax
from jax.experimental import pallas as pl
from jax.experimental.pallas import tpu as pltpu
from jax.sharding import PartitionSpec as P

HEAD_SIZE = 64
NEXP = 24
CAP = 341


EPSILON = 1e-06
ROPE_BASE = 10000.0
NEGATIVE = -1e30
HIGHEST = lax.Precision.HIGHEST


def normalize(rows, gain):
    scale_inv = lax.rsqrt(jnp.mean(rows * rows, axis=-1, keepdims=True) + EPSILON)
    return (rows * scale_inv * gain, scale_inv)


def norm_backward(rows, scale_inv, gain, grad_normed):
    weighted = gain * grad_normed
    grad_gain = jnp.sum(grad_normed * rows * scale_inv, axis=0)
    inner_mean = jnp.mean(weighted * rows, axis=-1, keepdims=True)
    grad_rows = scale_inv * weighted - rows * scale_inv * scale_inv * scale_inv * inner_mean
    return (grad_rows, grad_gain)


def apply_rotary(value_rows, token_positions, direction):
    half_dim = value_rows.shape[-1] // 2
    frequency = ROPE_BASE ** (-jnp.arange(half_dim, dtype=jnp.float32) / half_dim)
    angles = token_positions.astype(jnp.float32)[:, None] * frequency[None, :]
    cosine = jnp.cos(angles)[:, None, :]
    sine_part = direction * jnp.sin(angles)[:, None, :]
    first_half = value_rows[..., :half_dim]
    second = value_rows[..., half_dim:]
    return jnp.concatenate(
        [first_half * cosine - second * sine_part, second * cosine + first_half * sine_part],
        axis=-1,
    )


def contract_rows(left, right):
    return lax.dot_general(
        left, right, (((0,), (0,)), ((), ())), preferred_element_type=jnp.float32
    )


def contract_rows_exact(left, right):
    return lax.dot_general(
        left, right, (((0,), (0,)), ((), ())), precision=HIGHEST, preferred_element_type=jnp.float32
    )


def contract_cols(left, right):
    return lax.dot_general(
        left, right, (((1,), (1,)), ((), ())), preferred_element_type=jnp.float32
    )


def _expert_body(
    n2_ref, n2t_ref, dy_ref, dyt_ref, gcol_ref, grow_ref, wg_ref, wu_ref, wd_ref,
    acc_ref, dgate_ref, gg_ref, gu_ref, gd_ref, dn2_ref,
):
    f32 = jnp.float32
    bf16 = jnp.bfloat16
    nt = (((1,), (1,)), ((), ()))

    @pl.when(pl.program_id(0) == 0)
    def _():
        acc_ref[...] = jnp.zeros_like(acc_ref)
        dn2_ref[...] = jnp.zeros_like(dn2_ref)

    n2 = n2_ref[...]
    wg = wg_ref[0]
    wu = wu_ref[0]
    wd = wd_ref[0]
    gate_act = jnp.dot(n2, wg, preferred_element_type=f32)
    up_act = jnp.dot(n2, wu, preferred_element_type=f32)
    sig = 1.0 / (1.0 + jnp.exp(-gate_act))
    silu = gate_act * sig
    hidden = (silu * up_act).astype(bf16)
    expert_out = lax.dot_general(hidden, wd, nt, preferred_element_type=f32)
    gc = gcol_ref[0]
    acc_ref[...] += gc * expert_out
    dy = dy_ref[...].astype(f32)
    dgate_ref[0] = jnp.sum(expert_out * dy, axis=1, keepdims=True)
    deo = (gc * dy).astype(bf16)
    grad_hidden = jnp.dot(deo, wd, preferred_element_type=f32)
    deo_t = (grow_ref[0] * dyt_ref[...].astype(f32)).astype(bf16)
    gd_ref[0] = jnp.dot(deo_t, hidden, preferred_element_type=f32)
    grad_gate_act = (grad_hidden * up_act * sig * (1.0 + gate_act * (1.0 - sig))).astype(bf16)
    grad_up_act = (grad_hidden * silu).astype(bf16)
    n2t = n2t_ref[...]
    gg_ref[0] = jnp.dot(n2t, grad_gate_act, preferred_element_type=f32)
    gu_ref[0] = jnp.dot(n2t, grad_up_act, preferred_element_type=f32)
    dn2_ref[...] += lax.dot_general(
        grad_gate_act, wg, nt, preferred_element_type=f32
    ) + lax.dot_general(grad_up_act, wu, nt, preferred_element_type=f32)


def expert_kernel(n2, n2t, dy, dyt, gcol, grow, wg, wu, wd):
    tokens, width = n2.shape
    experts, _, hidden = wg.shape
    f32 = jnp.float32
    whole = lambda shape: pl.BlockSpec(shape, lambda e: (0,) * len(shape))
    per_expert = lambda shape: pl.BlockSpec((1,) + shape, lambda e: (e,) + (0,) * len(shape))
    flops = experts * tokens * width * hidden * 2 * 9
    return pl.pallas_call(
        _expert_body,
        grid=(experts,),
        in_specs=[
            whole((tokens, width)),
            whole((width, tokens)),
            whole((tokens, width)),
            whole((width, tokens)),
            per_expert((tokens, 1)),
            per_expert((1, tokens)),
            per_expert((width, hidden)),
            per_expert((width, hidden)),
            per_expert((width, hidden)),
        ],
        out_specs=[
            whole((tokens, width)),
            per_expert((tokens, 1)),
            per_expert((width, hidden)),
            per_expert((width, hidden)),
            per_expert((width, hidden)),
            whole((tokens, width)),
        ],
        out_shape=[
            jax.ShapeDtypeStruct((tokens, width), f32),
            jax.ShapeDtypeStruct((experts, tokens, 1), f32),
            jax.ShapeDtypeStruct((experts, width, hidden), f32),
            jax.ShapeDtypeStruct((experts, width, hidden), f32),
            jax.ShapeDtypeStruct((experts, width, hidden), f32),
            jax.ShapeDtypeStruct((tokens, width), f32),
        ],
        compiler_params=pltpu.CompilerParams(
            dimension_semantics=("arbitrary",), vmem_limit_bytes=64 * 1024 * 1024
        ),
        cost_estimate=pl.CostEstimate(
            flops=flops,
            transcendentals=experts * tokens * hidden,
            bytes_accessed=experts * width * hidden * (3 * 2 + 3 * 4) + tokens * width * 16,
        ),
    )(n2, n2t, dy, dyt, gcol, grow, wg, wu, wd)


def per_device(
    hidden_in,
    attn_gain,
    q_weight,
    key_matrix,
    value_matrix,
    o_weight,
    moe_gain,
    router_weight,
    gate_weight,
    up_weight,
    down_weight,
    segments,
    expert_picks,
    output_grad,
):
    bf16 = jnp.bfloat16
    f32 = jnp.float32
    token_count = hidden_in.shape[0]
    ctx_index = lax.axis_index("ctx")
    heads_local = q_weight.shape[1] // HEAD_SIZE
    kv_local = key_matrix.shape[1] // HEAD_SIZE
    group_size = heads_local // kv_local
    score_scale = 1.0 / math.sqrt(HEAD_SIZE)
    token_positions = ctx_index * token_count + jnp.arange(token_count, dtype=jnp.int32)
    segment_here = lax.dynamic_slice_in_dim(segments, ctx_index * token_count, token_count)
    inputs_f32 = hidden_in.astype(f32)
    normed_f32, scale_one = normalize(inputs_f32, attn_gain)
    normed_one = normed_f32.astype(bf16)
    query_rows = jnp.dot(normed_one, q_weight, preferred_element_type=f32).reshape(
        token_count, heads_local, HEAD_SIZE
    )
    keys_raw = jnp.dot(normed_one, key_matrix, preferred_element_type=f32).reshape(
        token_count, kv_local, HEAD_SIZE
    )
    values_raw = jnp.dot(normed_one, value_matrix, preferred_element_type=f32)
    query_grouped = (
        apply_rotary(query_rows, token_positions, 1.0)
        .astype(bf16)
        .reshape(token_count, kv_local, group_size, HEAD_SIZE)
    )
    key_flat = (
        apply_rotary(keys_raw, token_positions, 1.0)
        .astype(bf16)
        .reshape(token_count, kv_local * HEAD_SIZE)
    )
    value_flat = values_raw.astype(bf16)

    def piece_mask(piece_rows):
        key_pos = jnp.arange(piece_rows, dtype=jnp.int32)
        return (segment_here[:, None] == segments[None, :]) & (
            key_pos[None, :] <= token_positions[:, None]
        )

    pieces = (
        lax.all_gather(key_flat, "ctx", axis=0, tiled=True),
        lax.all_gather(value_flat, "ctx", axis=0, tiled=True),
    )
    run_max = jnp.full((kv_local, group_size, token_count), NEGATIVE, f32)
    piece_rows = pieces[0].shape[0]
    key_piece = pieces[0].reshape(piece_rows, kv_local, HEAD_SIZE)
    value_piece = pieces[1].reshape(piece_rows, kv_local, HEAD_SIZE)
    allowed = piece_mask(piece_rows)
    scores = (
        jnp.einsum("tkgd,nkd->kgtn", query_grouped, key_piece, preferred_element_type=f32)
        * score_scale
    )
    scores = jnp.where(allowed, scores, NEGATIVE)
    new_max = jnp.maximum(run_max, jnp.max(scores, axis=-1))
    weights = jnp.where(allowed, jnp.exp(scores - new_max[..., None]), 0.0)
    run_sum = jnp.sum(weights, axis=-1)
    accumulated = jnp.einsum(
        "kgtn,nkd->kgtd", weights.astype(bf16), value_piece, preferred_element_type=f32
    )
    fold_state = (new_max, run_sum, accumulated)
    run_max, run_sum, accumulated = fold_state
    attn_grouped = accumulated / run_sum[..., None]
    log_sum = run_max + jnp.log(run_sum)
    attn_bf = (
        jnp.transpose(attn_grouped, (2, 0, 1, 3))
        .reshape(token_count, heads_local * HEAD_SIZE)
        .astype(bf16)
    )
    attn_partial = contract_cols(attn_bf, o_weight)
    mixed_attn = lax.psum(attn_partial.astype(jnp.bfloat16), "tensor").astype(jnp.float32)
    resid = inputs_f32 + mixed_attn
    normed_two_f32, scale_two = normalize(resid, moe_gain)
    normed_two = normed_two_f32.astype(bf16)
    logits = jnp.dot(normed_two, router_weight, preferred_element_type=f32)
    expert_range = jnp.arange(NEXP, dtype=jnp.int32)
    picked_onehot = expert_picks[:, :, None] == expert_range[None, None, :]
    picked = jnp.sum(jnp.where(picked_onehot, logits[:, None, :], 0.0), axis=2)
    gate_probs = jax.nn.softmax(picked, axis=-1)
    gates_dense = jnp.sum(jnp.where(picked_onehot, gate_probs[:, :, None], 0.0), axis=1)
    gates_by_expert = jnp.transpose(gates_dense)
    cot_bf = output_grad
    moe_acc, gate_parts, grad_gate, grad_up, grad_down, moe_grad_rows = expert_kernel(
        normed_two,
        jnp.transpose(normed_two),
        cot_bf,
        jnp.transpose(cot_bf),
        gates_by_expert[:, :, None],
        gates_by_expert[:, None, :],
        gate_weight,
        up_weight,
        down_weight,
    )
    cot_f32 = output_grad.astype(f32)
    moe_total = lax.psum(moe_acc.astype(jnp.bfloat16), "tensor").astype(jnp.float32)
    output = (resid + moe_total).astype(bf16)
    grad_rows_all = moe_grad_rows
    gate_parts = gate_parts[:, :, 0]
    grad_gate_out, grad_up_out, grad_down_out = (
        lax.psum_scatter(
            grad_gate.astype(jnp.bfloat16), ("dp", "ctx"), scatter_dimension=1, tiled=True
        ).astype(jnp.float32),
        lax.psum_scatter(
            grad_up.astype(jnp.bfloat16), ("dp", "ctx"), scatter_dimension=1, tiled=True
        ).astype(jnp.float32),
        lax.psum_scatter(
            grad_down.astype(jnp.bfloat16), ("dp", "ctx"), scatter_dimension=1, tiled=True
        ).astype(jnp.float32),
    )
    gate_pair = jnp.sum(
        jnp.where(picked_onehot, jnp.transpose(gate_parts)[:, None, :], 0.0), axis=2
    )
    moe_summed, gate_summed = (
        lax.psum(grad_rows_all.astype(jnp.bfloat16), "tensor").astype(jnp.float32),
        lax.psum(gate_pair.astype(jnp.bfloat16), "tensor").astype(jnp.float32),
    )
    grad_picked = gate_probs * (
        gate_summed - jnp.sum(gate_probs * gate_summed, axis=1, keepdims=True)
    )
    grad_logits = jnp.sum(jnp.where(picked_onehot, grad_picked[:, :, None], 0.0), axis=1).astype(
        bf16
    )
    grad_router = contract_rows(normed_two, grad_logits)
    grad_normed_two = moe_summed + contract_cols(grad_logits, router_weight)
    grad_two_rows, grad_moe_gain = norm_backward(resid, scale_two, moe_gain, grad_normed_two)
    grad_resid = cot_f32 + grad_two_rows
    grad_mix = grad_resid.astype(bf16)
    grad_o = contract_rows(grad_mix, attn_bf)
    grad_attn = jnp.dot(grad_mix, o_weight, preferred_element_type=f32).astype(bf16)
    grad_attn_grouped = jnp.transpose(
        grad_attn.reshape(token_count, kv_local, group_size, HEAD_SIZE), (1, 2, 0, 3)
    )
    row_delta = jnp.sum(grad_attn_grouped.astype(f32) * attn_grouped, axis=-1)
    pieces = (
        lax.all_gather(key_flat, "ctx", axis=0, tiled=True),
        lax.all_gather(value_flat, "ctx", axis=0, tiled=True),
    )
    piece_rows = pieces[0].shape[0]
    key_piece = pieces[0].reshape(piece_rows, kv_local, HEAD_SIZE)
    value_piece = pieces[1].reshape(piece_rows, kv_local, HEAD_SIZE)
    allowed = piece_mask(piece_rows)
    scores = (
        jnp.einsum("tkgd,nkd->kgtn", query_grouped, key_piece, preferred_element_type=f32)
        * score_scale
    )
    probability = jnp.where(allowed, jnp.exp(scores - log_sum[..., None]), 0.0)
    grad_probs = jnp.einsum(
        "kgtd,nkd->kgtn", grad_attn_grouped, value_piece, preferred_element_type=f32
    )
    grad_scores = (probability * (grad_probs - row_delta[..., None])).astype(bf16)
    grad_query = score_scale * jnp.einsum(
        "kgtn,nkd->kgtd", grad_scores, key_piece, preferred_element_type=f32
    )
    key_part = score_scale * jnp.einsum(
        "kgtn,tkgd->nkd", grad_scores, query_grouped, preferred_element_type=f32
    )
    value_part = jnp.einsum(
        "kgtn,kgtd->nkd", probability.astype(bf16), grad_attn_grouped, preferred_element_type=f32
    )
    grad_keys_all = key_part.reshape(piece_rows, kv_local * HEAD_SIZE)
    grad_values_all = value_part.reshape(piece_rows, kv_local * HEAD_SIZE)
    back_state = (grad_query, grad_keys_all, grad_values_all)
    grad_query, grad_keys_all, grad_values_all = back_state
    grad_keys_here, grad_values_here = (
        lax.psum_scatter(
            grad_keys_all.astype(jnp.bfloat16), "ctx", scatter_dimension=0, tiled=True
        ).astype(jnp.float32),
        lax.psum_scatter(
            grad_values_all.astype(jnp.bfloat16), "ctx", scatter_dimension=0, tiled=True
        ).astype(jnp.float32),
    )
    grad_query_rows = jnp.transpose(grad_query, (2, 0, 1, 3)).reshape(
        token_count, heads_local, HEAD_SIZE
    )
    grad_query_bf = (
        apply_rotary(grad_query_rows, token_positions, -1.0)
        .reshape(token_count, heads_local * HEAD_SIZE)
        .astype(bf16)
    )
    grad_key_bf = (
        apply_rotary(
            grad_keys_here.reshape(token_count, kv_local, HEAD_SIZE), token_positions, -1.0
        )
        .reshape(token_count, kv_local * HEAD_SIZE)
        .astype(bf16)
    )
    grad_value_bf = grad_values_here.astype(bf16)
    grad_q = contract_rows(normed_one, grad_query_bf)
    grad_k = contract_rows(normed_one, grad_key_bf)
    grad_v = contract_rows(normed_one, grad_value_bf)
    partial_one = (
        contract_cols(grad_query_bf, q_weight)
        + contract_cols(grad_key_bf, key_matrix)
        + contract_cols(grad_value_bf, value_matrix)
    )
    grad_normed_one = lax.psum(partial_one.astype(jnp.bfloat16), "tensor").astype(jnp.float32)
    grad_one_rows, grad_attn_gain = norm_backward(inputs_f32, scale_one, attn_gain, grad_normed_one)
    input_grad = grad_resid + grad_one_rows
    dense_out = (
        lax.psum_scatter(
            grad_attn_gain.astype(jnp.bfloat16), ("dp", "ctx"), scatter_dimension=0, tiled=True
        ).astype(jnp.float32),
        lax.psum_scatter(
            grad_q.astype(jnp.bfloat16), ("dp", "ctx"), scatter_dimension=0, tiled=True
        ).astype(jnp.float32),
        lax.psum_scatter(
            grad_k.astype(jnp.bfloat16), ("dp", "ctx"), scatter_dimension=0, tiled=True
        ).astype(jnp.float32),
        lax.psum_scatter(
            grad_v.astype(jnp.bfloat16), ("dp", "ctx"), scatter_dimension=0, tiled=True
        ).astype(jnp.float32),
        lax.psum_scatter(
            grad_o.astype(jnp.bfloat16), ("dp", "ctx"), scatter_dimension=0, tiled=True
        ).astype(jnp.float32),
        lax.psum_scatter(
            grad_moe_gain.astype(jnp.bfloat16), ("dp", "ctx"), scatter_dimension=0, tiled=True
        ).astype(jnp.float32),
        lax.psum_scatter(
            grad_router.astype(jnp.bfloat16), ("dp", "ctx"), scatter_dimension=0, tiled=True
        ).astype(jnp.float32),
    )
    return (
        output,
        input_grad,
        dense_out[0],
        dense_out[1],
        dense_out[2],
        dense_out[3],
        dense_out[4],
        dense_out[5],
        dense_out[6],
        grad_gate_out,
        grad_up_out,
        grad_down_out,
    )


def solution(mesh):
    return jax.shard_map(
        per_device,
        mesh=mesh,
        in_specs=(
            P(("dp", "ctx"), None),
            P(),
            P(None, "tensor"),
            P(None, "tensor"),
            P(None, "tensor"),
            P(None, "tensor"),
            P(),
            P(),
            P(None, None, "tensor"),
            P(None, None, "tensor"),
            P(None, None, "tensor"),
            P("dp"),
            P(("dp", "ctx"), None),
            P(("dp", "ctx"), None),
        ),
        out_specs=(
            P(("dp", "ctx"), None),
            P(("dp", "ctx"), None),
            P(("dp", "ctx")),
            P(("dp", "ctx"), "tensor"),
            P(("dp", "ctx"), "tensor"),
            P(("dp", "ctx"), "tensor"),
            P(("dp", "ctx"), "tensor"),
            P(("dp", "ctx")),
            P(("dp", "ctx"), None),
            P(None, ("dp", "ctx"), "tensor"),
            P(None, ("dp", "ctx"), "tensor"),
            P(None, ("dp", "ctx"), "tensor"),
        ),
        check_vma=False,
    )
```

```python
import functools
import math

import jax
import jax.numpy as jnp
from jax import lax
from jax.experimental import pallas as pl
from jax.experimental.pallas import tpu as pltpu
from jax.sharding import PartitionSpec as P

HEAD_SIZE = 64
NEXP = 24
CAP = 341


EPSILON = 1e-06
ROPE_BASE = 10000.0
NEGATIVE = -1e30
HIGHEST = lax.Precision.HIGHEST


def normalize(rows, gain):
    scale_inv = lax.rsqrt(jnp.mean(rows * rows, axis=-1, keepdims=True) + EPSILON)
    return (rows * scale_inv * gain, scale_inv)


def norm_backward(rows, scale_inv, gain, grad_normed):
    weighted = gain * grad_normed
    grad_gain = jnp.sum(grad_normed * rows * scale_inv, axis=0)
    inner_mean = jnp.mean(weighted * rows, axis=-1, keepdims=True)
    grad_rows = scale_inv * weighted - rows * scale_inv * scale_inv * scale_inv * inner_mean
    return (grad_rows, grad_gain)


def apply_rotary(value_rows, token_positions, direction):
    half_dim = value_rows.shape[-1] // 2
    frequency = ROPE_BASE ** (-jnp.arange(half_dim, dtype=jnp.float32) / half_dim)
    angles = token_positions.astype(jnp.float32)[:, None] * frequency[None, :]
    cosine = jnp.cos(angles)[:, None, :]
    sine_part = direction * jnp.sin(angles)[:, None, :]
    first_half = value_rows[..., :half_dim]
    second = value_rows[..., half_dim:]
    return jnp.concatenate(
        [first_half * cosine - second * sine_part, second * cosine + first_half * sine_part],
        axis=-1,
    )


def contract_rows(left, right):
    return lax.dot_general(
        left, right, (((0,), (0,)), ((), ())), preferred_element_type=jnp.float32
    )


def contract_rows_exact(left, right):
    return lax.dot_general(
        left, right, (((0,), (0,)), ((), ())), precision=HIGHEST, preferred_element_type=jnp.float32
    )


def contract_cols(left, right):
    return lax.dot_general(
        left, right, (((1,), (1,)), ((), ())), preferred_element_type=jnp.float32
    )


def _expert_body(
    n2_ref, n2t_ref, dy_ref, dyt_ref, gcol_ref, grow_ref, wg_ref, wu_ref, wd_ref,
    acc_ref, dgate_ref, gg_ref, gu_ref, gd_ref, dn2_ref,
):
    f32 = jnp.float32
    bf16 = jnp.bfloat16
    nt = (((1,), (1,)), ((), ()))

    @pl.when(pl.program_id(0) == 0)
    def _():
        acc_ref[...] = jnp.zeros_like(acc_ref)
        dn2_ref[...] = jnp.zeros_like(dn2_ref)

    n2 = n2_ref[...]
    wg = wg_ref[0]
    wu = wu_ref[0]
    wd = wd_ref[0]
    gate_act = jnp.dot(n2, wg, preferred_element_type=f32)
    up_act = jnp.dot(n2, wu, preferred_element_type=f32)
    sig = 1.0 / (1.0 + jnp.exp(-gate_act))
    silu = gate_act * sig
    hidden = (silu * up_act).astype(bf16)
    expert_out = lax.dot_general(hidden, wd, nt, preferred_element_type=f32)
    gc = gcol_ref[0]
    acc_ref[...] += gc * expert_out
    dy = dy_ref[...].astype(f32)
    dgate_ref[0] = jnp.sum(expert_out * dy, axis=1, keepdims=True)
    deo = (gc * dy).astype(bf16)
    grad_hidden = jnp.dot(deo, wd, preferred_element_type=f32)
    deo_t = (grow_ref[0] * dyt_ref[...].astype(f32)).astype(bf16)
    gd_ref[0] = jnp.dot(deo_t, hidden, preferred_element_type=f32).astype(bf16)
    grad_gate_act = (grad_hidden * up_act * sig * (1.0 + gate_act * (1.0 - sig))).astype(bf16)
    grad_up_act = (grad_hidden * silu).astype(bf16)
    n2t = n2t_ref[...]
    gg_ref[0] = jnp.dot(n2t, grad_gate_act, preferred_element_type=f32).astype(bf16)
    gu_ref[0] = jnp.dot(n2t, grad_up_act, preferred_element_type=f32).astype(bf16)
    dn2_ref[...] += lax.dot_general(
        grad_gate_act, wg, nt, preferred_element_type=f32
    ) + lax.dot_general(grad_up_act, wu, nt, preferred_element_type=f32)


def expert_kernel(n2, n2t, dy, dyt, gcol, grow, wg, wu, wd):
    tokens, width = n2.shape
    experts, _, hidden = wg.shape
    f32 = jnp.float32
    whole = lambda shape: pl.BlockSpec(shape, lambda e: (0,) * len(shape))
    per_expert = lambda shape: pl.BlockSpec((1,) + shape, lambda e: (e,) + (0,) * len(shape))
    flops = experts * tokens * width * hidden * 2 * 9
    return pl.pallas_call(
        _expert_body,
        grid=(experts,),
        in_specs=[
            whole((tokens, width)),
            whole((width, tokens)),
            whole((tokens, width)),
            whole((width, tokens)),
            per_expert((tokens, 1)),
            per_expert((1, tokens)),
            per_expert((width, hidden)),
            per_expert((width, hidden)),
            per_expert((width, hidden)),
        ],
        out_specs=[
            whole((tokens, width)),
            per_expert((tokens, 1)),
            per_expert((width, hidden)),
            per_expert((width, hidden)),
            per_expert((width, hidden)),
            whole((tokens, width)),
        ],
        out_shape=[
            jax.ShapeDtypeStruct((tokens, width), f32),
            jax.ShapeDtypeStruct((experts, tokens, 1), f32),
            jax.ShapeDtypeStruct((experts, width, hidden), jnp.bfloat16),
            jax.ShapeDtypeStruct((experts, width, hidden), jnp.bfloat16),
            jax.ShapeDtypeStruct((experts, width, hidden), jnp.bfloat16),
            jax.ShapeDtypeStruct((tokens, width), f32),
        ],
        compiler_params=pltpu.CompilerParams(
            dimension_semantics=("arbitrary",), vmem_limit_bytes=64 * 1024 * 1024
        ),
        cost_estimate=pl.CostEstimate(
            flops=flops,
            transcendentals=experts * tokens * hidden,
            bytes_accessed=experts * width * hidden * (3 * 2 + 3 * 2) + tokens * width * 16,
        ),
    )(n2, n2t, dy, dyt, gcol, grow, wg, wu, wd)


MESH = pl.DeviceIdType.MESH


def _exchange_body(axis, n, per_peer, src_ref, out_ref, send_sems, recv_sems):
    me = lax.axis_index(axis)
    barrier = pltpu.get_barrier_semaphore()
    for k in range(1, n):
        peer = lax.rem(me + k, n)
        pl.semaphore_signal(barrier, 1, device_id={axis: peer}, device_id_type=MESH)
    pl.semaphore_wait(barrier, n - 1)
    sends = []
    for k in range(1, n):
        peer = lax.rem(me + k, n)
        copy = pltpu.make_async_remote_copy(
            src_ref=src_ref.at[peer] if per_peer else src_ref,
            dst_ref=out_ref.at[me],
            send_sem=send_sems.at[k - 1],
            recv_sem=recv_sems.at[k - 1],
            device_id={axis: peer},
            device_id_type=MESH,
        )
        copy.start()
        sends.append(copy)
    for k in range(1, n):
        source = lax.rem(me + n - k, n)
        pltpu.make_async_remote_copy(
            src_ref=src_ref.at[source] if per_peer else src_ref,
            dst_ref=out_ref.at[source],
            send_sem=send_sems.at[k - 1],
            recv_sem=recv_sems.at[k - 1],
            device_id={axis: source},
            device_id_type=MESH,
        ).wait_recv()
    for copy in sends:
        copy.wait_send()


def exchange(x, axis, n, per_peer, collective_id):
    block = x.shape[1:] if per_peer else x.shape
    nbytes = math.prod(block) * x.dtype.itemsize
    return pl.pallas_call(
        functools.partial(_exchange_body, axis, n, per_peer),
        out_shape=jax.ShapeDtypeStruct((n,) + tuple(block), x.dtype),
        in_specs=[pl.BlockSpec(memory_space=pl.ANY)],
        out_specs=pl.BlockSpec(memory_space=pl.ANY),
        scratch_shapes=[pltpu.SemaphoreType.DMA((n - 1,)), pltpu.SemaphoreType.DMA((n - 1,))],
        compiler_params=pltpu.CompilerParams(collective_id=collective_id, has_side_effects=True),
        cost_estimate=pl.CostEstimate(flops=0, transcendentals=0, bytes_accessed=2 * (n - 1) * nbytes),
    )(x)


def gather_axis(x, axis, n, collective_id):
    got = exchange(x, axis, n, False, collective_id)
    return lax.dynamic_update_slice_in_dim(got, x[None], lax.axis_index(axis), 0)


def sum_axis(x, axis, collective_id):
    got = exchange(x, axis, 2, False, collective_id)
    me = lax.axis_index(axis)
    other = lax.dynamic_index_in_dim(got, 1 - me, 0, keepdims=False)
    return x.astype(jnp.float32) + other.astype(jnp.float32)


def scatter_sum_axis(x, axis, n, collective_id):
    got = exchange(x, axis, n, True, collective_id)
    me = lax.axis_index(axis)
    own = lax.dynamic_index_in_dim(x, me, 0, keepdims=True)
    full = lax.dynamic_update_slice_in_dim(got, own, me, 0)
    return jnp.sum(full.astype(jnp.float32), axis=0)


def per_device(
    hidden_in,
    attn_gain,
    q_weight,
    key_matrix,
    value_matrix,
    o_weight,
    moe_gain,
    router_weight,
    gate_weight,
    up_weight,
    down_weight,
    segments,
    expert_picks,
    output_grad,
):
    bf16 = jnp.bfloat16
    f32 = jnp.float32
    token_count = hidden_in.shape[0]
    ctx_index = lax.axis_index("ctx")
    heads_local = q_weight.shape[1] // HEAD_SIZE
    kv_local = key_matrix.shape[1] // HEAD_SIZE
    group_size = heads_local // kv_local
    score_scale = 1.0 / math.sqrt(HEAD_SIZE)
    token_positions = ctx_index * token_count + jnp.arange(token_count, dtype=jnp.int32)
    segment_here = lax.dynamic_slice_in_dim(segments, ctx_index * token_count, token_count)
    inputs_f32 = hidden_in.astype(f32)
    normed_f32, scale_one = normalize(inputs_f32, attn_gain)
    normed_one = normed_f32.astype(bf16)
    query_rows = jnp.dot(normed_one, q_weight, preferred_element_type=f32).reshape(
        token_count, heads_local, HEAD_SIZE
    )
    keys_raw = jnp.dot(normed_one, key_matrix, preferred_element_type=f32).reshape(
        token_count, kv_local, HEAD_SIZE
    )
    values_raw = jnp.dot(normed_one, value_matrix, preferred_element_type=f32)
    query_grouped = (
        apply_rotary(query_rows, token_positions, 1.0)
        .astype(bf16)
        .reshape(token_count, kv_local, group_size, HEAD_SIZE)
    )
    key_flat = (
        apply_rotary(keys_raw, token_positions, 1.0)
        .astype(bf16)
        .reshape(token_count, kv_local * HEAD_SIZE)
    )
    value_flat = values_raw.astype(bf16)

    def piece_mask(piece_rows):
        key_pos = jnp.arange(piece_rows, dtype=jnp.int32)
        return (segment_here[:, None] == segments[None, :]) & (
            key_pos[None, :] <= token_positions[:, None]
        )

    ctx_count = segments.shape[0] // token_count
    kv_both = gather_axis(jnp.concatenate([key_flat, value_flat], axis=1), "ctx", ctx_count, 1)
    run_max = jnp.full((kv_local, group_size, token_count), NEGATIVE, f32)
    piece_rows = ctx_count * token_count
    kv_width = kv_local * HEAD_SIZE
    key_piece = kv_both[:, :, :kv_width].reshape(piece_rows, kv_local, HEAD_SIZE)
    value_piece = kv_both[:, :, kv_width:].reshape(piece_rows, kv_local, HEAD_SIZE)
    allowed = piece_mask(piece_rows)
    scores = (
        jnp.einsum("tkgd,nkd->kgtn", query_grouped, key_piece, preferred_element_type=f32)
        * score_scale
    )
    scores = jnp.where(allowed, scores, NEGATIVE)
    new_max = jnp.maximum(run_max, jnp.max(scores, axis=-1))
    weights = jnp.where(allowed, jnp.exp(scores - new_max[..., None]), 0.0)
    run_sum = jnp.sum(weights, axis=-1)
    accumulated = jnp.einsum(
        "kgtn,nkd->kgtd", weights.astype(bf16), value_piece, preferred_element_type=f32
    )
    fold_state = (new_max, run_sum, accumulated)
    run_max, run_sum, accumulated = fold_state
    attn_grouped = accumulated / run_sum[..., None]
    log_sum = run_max + jnp.log(run_sum)
    attn_bf = (
        jnp.transpose(attn_grouped, (2, 0, 1, 3))
        .reshape(token_count, heads_local * HEAD_SIZE)
        .astype(bf16)
    )
    attn_partial = contract_cols(attn_bf, o_weight)
    mixed_attn = sum_axis(attn_partial.astype(bf16), "tensor", 2)
    resid = inputs_f32 + mixed_attn
    normed_two_f32, scale_two = normalize(resid, moe_gain)
    normed_two = normed_two_f32.astype(bf16)
    logits = jnp.dot(normed_two, router_weight, preferred_element_type=f32)
    expert_range = jnp.arange(NEXP, dtype=jnp.int32)
    picked_onehot = expert_picks[:, :, None] == expert_range[None, None, :]
    picked = jnp.sum(jnp.where(picked_onehot, logits[:, None, :], 0.0), axis=2)
    gate_probs = jax.nn.softmax(picked, axis=-1)
    gates_dense = jnp.sum(jnp.where(picked_onehot, gate_probs[:, :, None], 0.0), axis=1)
    gates_by_expert = jnp.transpose(gates_dense)
    cot_bf = output_grad
    moe_acc, gate_parts, grad_gate, grad_up, grad_down, moe_grad_rows = expert_kernel(
        normed_two,
        jnp.transpose(normed_two),
        cot_bf,
        jnp.transpose(cot_bf),
        gates_by_expert[:, :, None],
        gates_by_expert[:, None, :],
        gate_weight,
        up_weight,
        down_weight,
    )
    cot_f32 = output_grad.astype(f32)
    moe_total = sum_axis(moe_acc.astype(bf16), "tensor", 3)
    output = (resid + moe_total).astype(bf16)
    grad_rows_all = moe_grad_rows
    gate_parts = gate_parts[:, :, 0]
    grad_gate_out, grad_up_out, grad_down_out = (
        lax.psum_scatter(grad_gate, ("dp", "ctx"), scatter_dimension=1, tiled=True).astype(
            jnp.float32
        ),
        lax.psum_scatter(grad_up, ("dp", "ctx"), scatter_dimension=1, tiled=True).astype(
            jnp.float32
        ),
        lax.psum_scatter(grad_down, ("dp", "ctx"), scatter_dimension=1, tiled=True).astype(
            jnp.float32
        ),
    )
    gate_pair = jnp.sum(
        jnp.where(picked_onehot, jnp.transpose(gate_parts)[:, None, :], 0.0), axis=2
    )
    moe_summed = sum_axis(grad_rows_all.astype(bf16), "tensor", 4)
    gate_summed = sum_axis(gate_pair.astype(bf16), "tensor", 5)
    grad_picked = gate_probs * (
        gate_summed - jnp.sum(gate_probs * gate_summed, axis=1, keepdims=True)
    )
    grad_logits = jnp.sum(jnp.where(picked_onehot, grad_picked[:, :, None], 0.0), axis=1).astype(
        bf16
    )
    grad_router = contract_rows(normed_two, grad_logits)
    grad_normed_two = moe_summed + contract_cols(grad_logits, router_weight)
    grad_two_rows, grad_moe_gain = norm_backward(resid, scale_two, moe_gain, grad_normed_two)
    grad_resid = cot_f32 + grad_two_rows
    grad_mix = grad_resid.astype(bf16)
    grad_o = contract_rows(grad_mix, attn_bf)
    grad_attn = jnp.dot(grad_mix, o_weight, preferred_element_type=f32).astype(bf16)
    grad_attn_grouped = jnp.transpose(
        grad_attn.reshape(token_count, kv_local, group_size, HEAD_SIZE), (1, 2, 0, 3)
    )
    row_delta = jnp.sum(grad_attn_grouped.astype(f32) * attn_grouped, axis=-1)
    allowed = piece_mask(piece_rows)
    scores = (
        jnp.einsum("tkgd,nkd->kgtn", query_grouped, key_piece, preferred_element_type=f32)
        * score_scale
    )
    probability = jnp.where(allowed, jnp.exp(scores - log_sum[..., None]), 0.0)
    grad_probs = jnp.einsum(
        "kgtd,nkd->kgtn", grad_attn_grouped, value_piece, preferred_element_type=f32
    )
    grad_scores = (probability * (grad_probs - row_delta[..., None])).astype(bf16)
    grad_query = score_scale * jnp.einsum(
        "kgtn,nkd->kgtd", grad_scores, key_piece, preferred_element_type=f32
    )
    key_part = score_scale * jnp.einsum(
        "kgtn,tkgd->nkd", grad_scores, query_grouped, preferred_element_type=f32
    )
    value_part = jnp.einsum(
        "kgtn,kgtd->nkd", probability.astype(bf16), grad_attn_grouped, preferred_element_type=f32
    )
    grad_keys_all = key_part.reshape(piece_rows, kv_local * HEAD_SIZE)
    grad_values_all = value_part.reshape(piece_rows, kv_local * HEAD_SIZE)
    back_state = (grad_query, grad_keys_all, grad_values_all)
    grad_query, grad_keys_all, grad_values_all = back_state
    grad_kv_here = scatter_sum_axis(
        jnp.concatenate([grad_keys_all, grad_values_all], axis=1)
        .astype(bf16)
        .reshape(ctx_count, token_count, 2 * kv_width),
        "ctx",
        ctx_count,
        6,
    )
    grad_keys_here = grad_kv_here[:, :kv_width]
    grad_values_here = grad_kv_here[:, kv_width:]
    grad_query_rows = jnp.transpose(grad_query, (2, 0, 1, 3)).reshape(
        token_count, heads_local, HEAD_SIZE
    )
    grad_query_bf = (
        apply_rotary(grad_query_rows, token_positions, -1.0)
        .reshape(token_count, heads_local * HEAD_SIZE)
        .astype(bf16)
    )
    grad_key_bf = (
        apply_rotary(
            grad_keys_here.reshape(token_count, kv_local, HEAD_SIZE), token_positions, -1.0
        )
        .reshape(token_count, kv_local * HEAD_SIZE)
        .astype(bf16)
    )
    grad_value_bf = grad_values_here.astype(bf16)
    grad_q = contract_rows(normed_one, grad_query_bf)
    grad_k = contract_rows(normed_one, grad_key_bf)
    grad_v = contract_rows(normed_one, grad_value_bf)
    partial_one = (
        contract_cols(grad_query_bf, q_weight)
        + contract_cols(grad_key_bf, key_matrix)
        + contract_cols(grad_value_bf, value_matrix)
    )
    grad_normed_one = sum_axis(partial_one.astype(bf16), "tensor", 7)
    grad_one_rows, grad_attn_gain = norm_backward(inputs_f32, scale_one, attn_gain, grad_normed_one)
    input_grad = grad_resid + grad_one_rows
    q_cols, o_cols, k_cols = grad_q.shape[1], grad_o.shape[1], grad_k.shape[1]
    dense_all = jnp.concatenate(
        [
            grad_q.astype(bf16),
            grad_o.astype(bf16),
            grad_k.astype(bf16),
            grad_v.astype(bf16),
            grad_router.astype(bf16),
            grad_attn_gain[:, None].astype(bf16),
            grad_moe_gain[:, None].astype(bf16),
        ],
        axis=1,
    )
    dense_here = lax.psum_scatter(dense_all, ("dp", "ctx"), scatter_dimension=0, tiled=True).astype(
        f32
    )
    spans = [q_cols, o_cols, k_cols, k_cols, router_weight.shape[1], 1, 1]
    cuts = [sum(spans[:i]) for i in range(len(spans) + 1)]
    pieces_out = [dense_here[:, cuts[i] : cuts[i + 1]] for i in range(len(spans))]
    dense_out = (
        pieces_out[5][:, 0],
        pieces_out[0],
        pieces_out[2],
        pieces_out[3],
        pieces_out[1],
        pieces_out[6][:, 0],
        pieces_out[4],
    )
    return (
        output,
        input_grad,
        dense_out[0],
        dense_out[1],
        dense_out[2],
        dense_out[3],
        dense_out[4],
        dense_out[5],
        dense_out[6],
        grad_gate_out,
        grad_up_out,
        grad_down_out,
    )


def solution(mesh):
    return jax.shard_map(
        per_device,
        mesh=mesh,
        in_specs=(
            P(("dp", "ctx"), None),
            P(),
            P(None, "tensor"),
            P(None, "tensor"),
            P(None, "tensor"),
            P(None, "tensor"),
            P(),
            P(),
            P(None, None, "tensor"),
            P(None, None, "tensor"),
            P(None, None, "tensor"),
            P("dp"),
            P(("dp", "ctx"), None),
            P(("dp", "ctx"), None),
        ),
        out_specs=(
            P(("dp", "ctx"), None),
            P(("dp", "ctx"), None),
            P(("dp", "ctx")),
            P(("dp", "ctx"), "tensor"),
            P(("dp", "ctx"), "tensor"),
            P(("dp", "ctx"), "tensor"),
            P(("dp", "ctx"), "tensor"),
            P(("dp", "ctx")),
            P(("dp", "ctx"), None),
            P(None, ("dp", "ctx"), "tensor"),
            P(None, ("dp", "ctx"), "tensor"),
            P(None, ("dp", "ctx"), "tensor"),
        ),
        check_vma=False,
    )
```

```python
import functools
import math

import jax
import jax.numpy as jnp
from jax import lax
from jax.experimental import pallas as pl
from jax.experimental.pallas import tpu as pltpu
from jax.sharding import PartitionSpec as P

HEAD_SIZE = 64
NEXP = 24
CAP = 341


EPSILON = 1e-06
ROPE_BASE = 10000.0
NEGATIVE = -1e30
HIGHEST = lax.Precision.HIGHEST


def normalize(rows, gain):
    scale_inv = lax.rsqrt(jnp.mean(rows * rows, axis=-1, keepdims=True) + EPSILON)
    return (rows * scale_inv * gain, scale_inv)


def norm_backward(rows, scale_inv, gain, grad_normed):
    weighted = gain * grad_normed
    grad_gain = jnp.sum(grad_normed * rows * scale_inv, axis=0)
    inner_mean = jnp.mean(weighted * rows, axis=-1, keepdims=True)
    grad_rows = scale_inv * weighted - rows * scale_inv * scale_inv * scale_inv * inner_mean
    return (grad_rows, grad_gain)


def apply_rotary(value_rows, token_positions, direction):
    half_dim = value_rows.shape[-1] // 2
    frequency = ROPE_BASE ** (-jnp.arange(half_dim, dtype=jnp.float32) / half_dim)
    angles = token_positions.astype(jnp.float32)[:, None] * frequency[None, :]
    cosine = jnp.cos(angles)[:, None, :]
    sine_part = direction * jnp.sin(angles)[:, None, :]
    first_half = value_rows[..., :half_dim]
    second = value_rows[..., half_dim:]
    return jnp.concatenate(
        [first_half * cosine - second * sine_part, second * cosine + first_half * sine_part],
        axis=-1,
    )


def contract_rows(left, right):
    return lax.dot_general(
        left, right, (((0,), (0,)), ((), ())), preferred_element_type=jnp.float32
    )


def contract_rows_exact(left, right):
    return lax.dot_general(
        left, right, (((0,), (0,)), ((), ())), precision=HIGHEST, preferred_element_type=jnp.float32
    )


def contract_cols(left, right):
    return lax.dot_general(
        left, right, (((1,), (1,)), ((), ())), preferred_element_type=jnp.float32
    )


def _expert_body(
    n2_ref, n2t_ref, dy_ref, dyt_ref, gcol_ref, grow_ref, wg_ref, wu_ref, wd_ref,
    acc_ref, dgate_ref, gg_ref, gu_ref, gd_ref, dn2_ref,
):
    f32 = jnp.float32
    bf16 = jnp.bfloat16
    nt = (((1,), (1,)), ((), ()))

    @pl.when(pl.program_id(0) == 0)
    def _():
        acc_ref[...] = jnp.zeros_like(acc_ref)
        dn2_ref[...] = jnp.zeros_like(dn2_ref)

    n2 = n2_ref[...]
    wg = wg_ref[0]
    wu = wu_ref[0]
    wd = wd_ref[0]
    gate_act = jnp.dot(n2, wg, preferred_element_type=f32)
    up_act = jnp.dot(n2, wu, preferred_element_type=f32)
    sig = 1.0 / (1.0 + jnp.exp(-gate_act))
    silu = gate_act * sig
    hidden = (silu * up_act).astype(bf16)
    expert_out = lax.dot_general(hidden, wd, nt, preferred_element_type=f32)
    gc = gcol_ref[0]
    acc_ref[...] += gc * expert_out
    dy = dy_ref[...].astype(f32)
    dgate_ref[0] = jnp.sum(expert_out * dy, axis=1, keepdims=True)
    deo = (gc * dy).astype(bf16)
    grad_hidden = jnp.dot(deo, wd, preferred_element_type=f32)
    deo_t = (grow_ref[0] * dyt_ref[...].astype(f32)).astype(bf16)
    gd_ref[0] = jnp.dot(deo_t, hidden, preferred_element_type=f32).astype(bf16)
    grad_gate_act = (grad_hidden * up_act * sig * (1.0 + gate_act * (1.0 - sig))).astype(bf16)
    grad_up_act = (grad_hidden * silu).astype(bf16)
    n2t = n2t_ref[...]
    gg_ref[0] = jnp.dot(n2t, grad_gate_act, preferred_element_type=f32).astype(bf16)
    gu_ref[0] = jnp.dot(n2t, grad_up_act, preferred_element_type=f32).astype(bf16)
    dn2_ref[...] += lax.dot_general(
        grad_gate_act, wg, nt, preferred_element_type=f32
    ) + lax.dot_general(grad_up_act, wu, nt, preferred_element_type=f32)


def expert_kernel(n2, n2t, dy, dyt, gcol, grow, wg, wu, wd):
    tokens, width = n2.shape
    experts, _, hidden = wg.shape
    f32 = jnp.float32
    whole = lambda shape: pl.BlockSpec(shape, lambda e: (0,) * len(shape))
    per_expert = lambda shape: pl.BlockSpec((1,) + shape, lambda e: (e,) + (0,) * len(shape))
    flops = experts * tokens * width * hidden * 2 * 9
    return pl.pallas_call(
        _expert_body,
        grid=(experts,),
        in_specs=[
            whole((tokens, width)),
            whole((width, tokens)),
            whole((tokens, width)),
            whole((width, tokens)),
            per_expert((tokens, 1)),
            per_expert((1, tokens)),
            per_expert((width, hidden)),
            per_expert((width, hidden)),
            per_expert((width, hidden)),
        ],
        out_specs=[
            whole((tokens, width)),
            per_expert((tokens, 1)),
            per_expert((width, hidden)),
            per_expert((width, hidden)),
            per_expert((width, hidden)),
            whole((tokens, width)),
        ],
        out_shape=[
            jax.ShapeDtypeStruct((tokens, width), f32),
            jax.ShapeDtypeStruct((experts, tokens, 1), f32),
            jax.ShapeDtypeStruct((experts, width, hidden), jnp.bfloat16),
            jax.ShapeDtypeStruct((experts, width, hidden), jnp.bfloat16),
            jax.ShapeDtypeStruct((experts, width, hidden), jnp.bfloat16),
            jax.ShapeDtypeStruct((tokens, width), f32),
        ],
        compiler_params=pltpu.CompilerParams(
            dimension_semantics=("arbitrary",), vmem_limit_bytes=64 * 1024 * 1024
        ),
        cost_estimate=pl.CostEstimate(
            flops=flops,
            transcendentals=experts * tokens * hidden,
            bytes_accessed=experts * width * hidden * (3 * 2 + 3 * 2) + tokens * width * 16,
        ),
    )(n2, n2t, dy, dyt, gcol, grow, wg, wu, wd)


MESH = pl.DeviceIdType.MESH


def _exchange_body(axis, n, per_peer, src_ref, out_ref, send_sems, recv_sems):
    me = lax.axis_index(axis)
    barrier = pltpu.get_barrier_semaphore()
    for k in range(1, n):
        peer = lax.rem(me + k, n)
        pl.semaphore_signal(barrier, 1, device_id={axis: peer}, device_id_type=MESH)
    pl.semaphore_wait(barrier, n - 1)
    sends = []
    for k in range(1, n):
        peer = lax.rem(me + k, n)
        copy = pltpu.make_async_remote_copy(
            src_ref=src_ref.at[peer] if per_peer else src_ref,
            dst_ref=out_ref.at[me],
            send_sem=send_sems.at[k - 1],
            recv_sem=recv_sems.at[k - 1],
            device_id={axis: peer},
            device_id_type=MESH,
        )
        copy.start()
        sends.append(copy)
    for k in range(1, n):
        source = lax.rem(me + n - k, n)
        pltpu.make_async_remote_copy(
            src_ref=src_ref.at[source] if per_peer else src_ref,
            dst_ref=out_ref.at[source],
            send_sem=send_sems.at[k - 1],
            recv_sem=recv_sems.at[k - 1],
            device_id={axis: source},
            device_id_type=MESH,
        ).wait_recv()
    for copy in sends:
        copy.wait_send()


def exchange(x, axis, n, per_peer, collective_id):
    block = x.shape[1:] if per_peer else x.shape
    nbytes = math.prod(block) * x.dtype.itemsize
    return pl.pallas_call(
        functools.partial(_exchange_body, axis, n, per_peer),
        out_shape=jax.ShapeDtypeStruct((n,) + tuple(block), x.dtype),
        in_specs=[pl.BlockSpec(memory_space=pl.ANY)],
        out_specs=pl.BlockSpec(memory_space=pl.ANY),
        scratch_shapes=[pltpu.SemaphoreType.DMA((n - 1,)), pltpu.SemaphoreType.DMA((n - 1,))],
        compiler_params=pltpu.CompilerParams(collective_id=collective_id, has_side_effects=True),
        cost_estimate=pl.CostEstimate(flops=0, transcendentals=0, bytes_accessed=2 * (n - 1) * nbytes),
    )(x)


def gather_axis(x, axis, n, collective_id):
    got = exchange(x, axis, n, False, collective_id)
    return lax.dynamic_update_slice_in_dim(got, x[None], lax.axis_index(axis), 0)


def sum_axis(x, axis, collective_id):
    got = exchange(x, axis, 2, False, collective_id)
    me = lax.axis_index(axis)
    other = lax.dynamic_index_in_dim(got, 1 - me, 0, keepdims=False)
    return x.astype(jnp.float32) + other.astype(jnp.float32)


def scatter_sum_axis(x, axis, n, collective_id):
    got = exchange(x, axis, n, True, collective_id)
    me = lax.axis_index(axis)
    own = lax.dynamic_index_in_dim(x, me, 0, keepdims=True)
    full = lax.dynamic_update_slice_in_dim(got, own, me, 0)
    return jnp.sum(full.astype(jnp.float32), axis=0)


def per_device(
    hidden_in,
    attn_gain,
    q_weight,
    key_matrix,
    value_matrix,
    o_weight,
    moe_gain,
    router_weight,
    gate_weight,
    up_weight,
    down_weight,
    segments,
    expert_picks,
    output_grad,
):
    bf16 = jnp.bfloat16
    f32 = jnp.float32
    token_count = hidden_in.shape[0]
    ctx_index = lax.axis_index("ctx")
    heads_local = q_weight.shape[1] // HEAD_SIZE
    kv_local = key_matrix.shape[1] // HEAD_SIZE
    group_size = heads_local // kv_local
    score_scale = 1.0 / math.sqrt(HEAD_SIZE)
    token_positions = ctx_index * token_count + jnp.arange(token_count, dtype=jnp.int32)
    segment_here = lax.dynamic_slice_in_dim(segments, ctx_index * token_count, token_count)
    inputs_f32 = hidden_in.astype(f32)
    normed_f32, scale_one = normalize(inputs_f32, attn_gain)
    normed_one = normed_f32.astype(bf16)
    query_rows = jnp.dot(normed_one, q_weight, preferred_element_type=f32).reshape(
        token_count, heads_local, HEAD_SIZE
    )
    keys_raw = jnp.dot(normed_one, key_matrix, preferred_element_type=f32).reshape(
        token_count, kv_local, HEAD_SIZE
    )
    values_raw = jnp.dot(normed_one, value_matrix, preferred_element_type=f32)
    query_grouped = (
        apply_rotary(query_rows, token_positions, 1.0)
        .astype(bf16)
        .reshape(token_count, kv_local, group_size, HEAD_SIZE)
    )
    key_flat = (
        apply_rotary(keys_raw, token_positions, 1.0)
        .astype(bf16)
        .reshape(token_count, kv_local * HEAD_SIZE)
    )
    value_flat = values_raw.astype(bf16)

    def piece_mask(piece_rows):
        key_pos = jnp.arange(piece_rows, dtype=jnp.int32)
        return (segment_here[:, None] == segments[None, :]) & (
            key_pos[None, :] <= token_positions[:, None]
        )

    ctx_count = segments.shape[0] // token_count
    kv_both = gather_axis(jnp.concatenate([key_flat, value_flat], axis=1), "ctx", ctx_count, 1)
    run_max = jnp.full((kv_local, group_size, token_count), NEGATIVE, f32)
    piece_rows = ctx_count * token_count
    kv_width = kv_local * HEAD_SIZE
    key_piece = kv_both[:, :, :kv_width].reshape(piece_rows, kv_local, HEAD_SIZE)
    value_piece = kv_both[:, :, kv_width:].reshape(piece_rows, kv_local, HEAD_SIZE)
    allowed = piece_mask(piece_rows)
    scores = (
        jnp.einsum("tkgd,nkd->kgtn", query_grouped, key_piece, preferred_element_type=f32)
        * score_scale
    )
    scores = jnp.where(allowed, scores, NEGATIVE)
    new_max = jnp.maximum(run_max, jnp.max(scores, axis=-1))
    weights = jnp.where(allowed, jnp.exp(scores - new_max[..., None]), 0.0)
    run_sum = jnp.sum(weights, axis=-1)
    accumulated = jnp.einsum(
        "kgtn,nkd->kgtd", weights.astype(bf16), value_piece, preferred_element_type=f32
    )
    fold_state = (new_max, run_sum, accumulated)
    run_max, run_sum, accumulated = fold_state
    attn_grouped = accumulated / run_sum[..., None]
    log_sum = run_max + jnp.log(run_sum)
    attn_bf = (
        jnp.transpose(attn_grouped, (2, 0, 1, 3))
        .reshape(token_count, heads_local * HEAD_SIZE)
        .astype(bf16)
    )
    attn_partial = contract_cols(attn_bf, o_weight)
    mixed_attn = sum_axis(attn_partial.astype(bf16), "tensor", 2)
    resid = inputs_f32 + mixed_attn
    normed_two_f32, scale_two = normalize(resid, moe_gain)
    normed_two = normed_two_f32.astype(bf16)
    logits = jnp.dot(normed_two, router_weight, preferred_element_type=f32)
    expert_range = jnp.arange(NEXP, dtype=jnp.int32)
    picked_onehot = expert_picks[:, :, None] == expert_range[None, None, :]
    picked = jnp.sum(jnp.where(picked_onehot, logits[:, None, :], 0.0), axis=2)
    gate_probs = jax.nn.softmax(picked, axis=-1)
    gates_dense = jnp.sum(jnp.where(picked_onehot, gate_probs[:, :, None], 0.0), axis=1)
    gates_by_expert = jnp.transpose(gates_dense)
    cot_bf = output_grad
    moe_acc, gate_parts, grad_gate, grad_up, grad_down, moe_grad_rows = expert_kernel(
        normed_two,
        jnp.transpose(normed_two),
        cot_bf,
        jnp.transpose(cot_bf),
        gates_by_expert[:, :, None],
        gates_by_expert[:, None, :],
        gate_weight,
        up_weight,
        down_weight,
    )
    cot_f32 = output_grad.astype(f32)
    moe_total = sum_axis(moe_acc.astype(bf16), "tensor", 3)
    output = (resid + moe_total).astype(bf16)
    grad_rows_all = moe_grad_rows
    gate_parts = gate_parts[:, :, 0]
    grad_gate_out, grad_up_out, grad_down_out = (
        lax.psum_scatter(grad_gate, ("dp", "ctx"), scatter_dimension=1, tiled=True).astype(
            jnp.float32
        ),
        lax.psum_scatter(grad_up, ("dp", "ctx"), scatter_dimension=1, tiled=True).astype(
            jnp.float32
        ),
        lax.psum_scatter(grad_down, ("dp", "ctx"), scatter_dimension=1, tiled=True).astype(
            jnp.float32
        ),
    )
    gate_pair = jnp.sum(
        jnp.where(picked_onehot, jnp.transpose(gate_parts)[:, None, :], 0.0), axis=2
    )
    moe_summed = sum_axis(grad_rows_all.astype(bf16), "tensor", 4)
    gate_summed = sum_axis(gate_pair.astype(bf16), "tensor", 5)
    grad_picked = gate_probs * (
        gate_summed - jnp.sum(gate_probs * gate_summed, axis=1, keepdims=True)
    )
    grad_logits = jnp.sum(jnp.where(picked_onehot, grad_picked[:, :, None], 0.0), axis=1).astype(
        bf16
    )
    grad_router = contract_rows(normed_two, grad_logits)
    grad_normed_two = moe_summed + contract_cols(grad_logits, router_weight)
    grad_two_rows, grad_moe_gain = norm_backward(resid, scale_two, moe_gain, grad_normed_two)
    grad_resid = cot_f32 + grad_two_rows
    grad_mix = grad_resid.astype(bf16)
    grad_o = contract_rows(grad_mix, attn_bf)
    grad_attn = jnp.dot(grad_mix, o_weight, preferred_element_type=f32).astype(bf16)
    grad_attn_grouped = jnp.transpose(
        grad_attn.reshape(token_count, kv_local, group_size, HEAD_SIZE), (1, 2, 0, 3)
    )
    row_delta = jnp.sum(grad_attn_grouped.astype(f32) * attn_grouped, axis=-1)
    allowed = piece_mask(piece_rows)
    scores = (
        jnp.einsum("tkgd,nkd->kgtn", query_grouped, key_piece, preferred_element_type=f32)
        * score_scale
    )
    probability = jnp.where(allowed, jnp.exp(scores - log_sum[..., None]), 0.0)
    grad_probs = jnp.einsum(
        "kgtd,nkd->kgtn", grad_attn_grouped, value_piece, preferred_element_type=f32
    )
    grad_scores = (probability * (grad_probs - row_delta[..., None])).astype(bf16)
    grad_query = score_scale * jnp.einsum(
        "kgtn,nkd->kgtd", grad_scores, key_piece, preferred_element_type=f32
    )
    key_part = score_scale * jnp.einsum(
        "kgtn,tkgd->nkd", grad_scores, query_grouped, preferred_element_type=f32
    )
    value_part = jnp.einsum(
        "kgtn,kgtd->nkd", probability.astype(bf16), grad_attn_grouped, preferred_element_type=f32
    )
    grad_keys_all = key_part.reshape(piece_rows, kv_local * HEAD_SIZE)
    grad_values_all = value_part.reshape(piece_rows, kv_local * HEAD_SIZE)
    back_state = (grad_query, grad_keys_all, grad_values_all)
    grad_query, grad_keys_all, grad_values_all = back_state
    grad_kv_here = scatter_sum_axis(
        jnp.concatenate([grad_keys_all, grad_values_all], axis=1)
        .astype(bf16)
        .reshape(ctx_count, token_count, 2 * kv_width),
        "ctx",
        ctx_count,
        6,
    )
    grad_keys_here = grad_kv_here[:, :kv_width]
    grad_values_here = grad_kv_here[:, kv_width:]
    grad_query_rows = jnp.transpose(grad_query, (2, 0, 1, 3)).reshape(
        token_count, heads_local, HEAD_SIZE
    )
    grad_query_bf = (
        apply_rotary(grad_query_rows, token_positions, -1.0)
        .reshape(token_count, heads_local * HEAD_SIZE)
        .astype(bf16)
    )
    grad_key_bf = (
        apply_rotary(
            grad_keys_here.reshape(token_count, kv_local, HEAD_SIZE), token_positions, -1.0
        )
        .reshape(token_count, kv_local * HEAD_SIZE)
        .astype(bf16)
    )
    grad_value_bf = grad_values_here.astype(bf16)
    grad_q = contract_rows(normed_one, grad_query_bf)
    grad_k = contract_rows(normed_one, grad_key_bf)
    grad_v = contract_rows(normed_one, grad_value_bf)
    partial_one = (
        contract_cols(grad_query_bf, q_weight)
        + contract_cols(grad_key_bf, key_matrix)
        + contract_cols(grad_value_bf, value_matrix)
    )
    grad_normed_one = sum_axis(partial_one.astype(bf16), "tensor", 7)
    grad_one_rows, grad_attn_gain = norm_backward(inputs_f32, scale_one, attn_gain, grad_normed_one)
    input_grad = grad_resid + grad_one_rows
    q_cols, o_cols, k_cols = grad_q.shape[1], grad_o.shape[1], grad_k.shape[1]
    dense_all = jnp.concatenate(
        [
            grad_q.astype(bf16),
            grad_o.astype(bf16),
            grad_k.astype(bf16),
            grad_v.astype(bf16),
            grad_router.astype(bf16),
            grad_attn_gain[:, None].astype(bf16),
            grad_moe_gain[:, None].astype(bf16),
        ],
        axis=1,
    )
    dense_all, grad_gate_out, grad_up_out, grad_down_out = lax.optimization_barrier(
        (dense_all, grad_gate_out, grad_up_out, grad_down_out)
    )
    dense_here = lax.psum_scatter(dense_all, ("dp", "ctx"), scatter_dimension=0, tiled=True).astype(
        f32
    )
    spans = [q_cols, o_cols, k_cols, k_cols, router_weight.shape[1], 1, 1]
    cuts = [sum(spans[:i]) for i in range(len(spans) + 1)]
    pieces_out = [dense_here[:, cuts[i] : cuts[i + 1]] for i in range(len(spans))]
    dense_out = (
        pieces_out[5][:, 0],
        pieces_out[0],
        pieces_out[2],
        pieces_out[3],
        pieces_out[1],
        pieces_out[6][:, 0],
        pieces_out[4],
    )
    return (
        output,
        input_grad,
        dense_out[0],
        dense_out[1],
        dense_out[2],
        dense_out[3],
        dense_out[4],
        dense_out[5],
        dense_out[6],
        grad_gate_out,
        grad_up_out,
        grad_down_out,
    )


def solution(mesh):
    return jax.shard_map(
        per_device,
        mesh=mesh,
        in_specs=(
            P(("dp", "ctx"), None),
            P(),
            P(None, "tensor"),
            P(None, "tensor"),
            P(None, "tensor"),
            P(None, "tensor"),
            P(),
            P(),
            P(None, None, "tensor"),
            P(None, None, "tensor"),
            P(None, None, "tensor"),
            P("dp"),
            P(("dp", "ctx"), None),
            P(("dp", "ctx"), None),
        ),
        out_specs=(
            P(("dp", "ctx"), None),
            P(("dp", "ctx"), None),
            P(("dp", "ctx")),
            P(("dp", "ctx"), "tensor"),
            P(("dp", "ctx"), "tensor"),
            P(("dp", "ctx"), "tensor"),
            P(("dp", "ctx"), "tensor"),
            P(("dp", "ctx")),
            P(("dp", "ctx"), None),
            P(None, ("dp", "ctx"), "tensor"),
            P(None, ("dp", "ctx"), "tensor"),
            P(None, ("dp", "ctx"), "tensor"),
        ),
        check_vma=False,
    )
```

```python
import functools
import math

import jax
import jax.numpy as jnp
from jax import lax
from jax.experimental import pallas as pl
from jax.experimental.pallas import tpu as pltpu
from jax.sharding import PartitionSpec as P

HEAD_SIZE = 64
NEXP = 24
CAP = 341


EPSILON = 1e-06
ROPE_BASE = 10000.0
NEGATIVE = -1e30
HIGHEST = lax.Precision.HIGHEST


def normalize(rows, gain):
    scale_inv = lax.rsqrt(jnp.mean(rows * rows, axis=-1, keepdims=True) + EPSILON)
    return (rows * scale_inv * gain, scale_inv)


def norm_backward(rows, scale_inv, gain, grad_normed):
    weighted = gain * grad_normed
    grad_gain = jnp.sum(grad_normed * rows * scale_inv, axis=0)
    inner_mean = jnp.mean(weighted * rows, axis=-1, keepdims=True)
    grad_rows = scale_inv * weighted - rows * scale_inv * scale_inv * scale_inv * inner_mean
    return (grad_rows, grad_gain)


def apply_rotary(value_rows, token_positions, direction):
    half_dim = value_rows.shape[-1] // 2
    frequency = ROPE_BASE ** (-jnp.arange(half_dim, dtype=jnp.float32) / half_dim)
    angles = token_positions.astype(jnp.float32)[:, None] * frequency[None, :]
    cosine = jnp.cos(angles)[:, None, :]
    sine_part = direction * jnp.sin(angles)[:, None, :]
    first_half = value_rows[..., :half_dim]
    second = value_rows[..., half_dim:]
    return jnp.concatenate(
        [first_half * cosine - second * sine_part, second * cosine + first_half * sine_part],
        axis=-1,
    )


def contract_rows(left, right):
    return lax.dot_general(
        left, right, (((0,), (0,)), ((), ())), preferred_element_type=jnp.float32
    )


def contract_rows_exact(left, right):
    return lax.dot_general(
        left, right, (((0,), (0,)), ((), ())), precision=HIGHEST, preferred_element_type=jnp.float32
    )


def contract_cols(left, right):
    return lax.dot_general(
        left, right, (((1,), (1,)), ((), ())), preferred_element_type=jnp.float32
    )


def _store_split(out_ref, value):
    cores, _, groups, rows, _ = out_ref.shape
    for x in range(groups):
        for c in range(cores):
            start = (x * cores + c) * rows
            out_ref[c, 0, x] = value[start : start + rows].astype(out_ref.dtype)


def _expert_body(
    n2_ref, n2t_ref, dy_ref, dyt_ref, gcol_ref, grow_ref, wg_ref, wu_ref, wd_ref,
    acc_ref, dgate_ref, gg_ref, gu_ref, gd_ref, dn2_ref,
):
    f32 = jnp.float32
    bf16 = jnp.bfloat16
    nt = (((1,), (1,)), ((), ()))

    @pl.when(pl.program_id(0) == 0)
    def _():
        acc_ref[...] = jnp.zeros_like(acc_ref)
        dn2_ref[...] = jnp.zeros_like(dn2_ref)

    n2 = n2_ref[...]
    wg = wg_ref[0]
    wu = wu_ref[0]
    wd = wd_ref[0]
    gate_act = jnp.dot(n2, wg, preferred_element_type=f32)
    up_act = jnp.dot(n2, wu, preferred_element_type=f32)
    sig = 1.0 / (1.0 + jnp.exp(-gate_act))
    silu = gate_act * sig
    hidden = (silu * up_act).astype(bf16)
    expert_out = lax.dot_general(hidden, wd, nt, preferred_element_type=f32)
    gc = gcol_ref[0]
    acc_ref[...] += gc * expert_out
    dy = dy_ref[...].astype(f32)
    dgate_ref[0] = jnp.sum(expert_out * dy, axis=1, keepdims=True)
    deo = (gc * dy).astype(bf16)
    grad_hidden = jnp.dot(deo, wd, preferred_element_type=f32)
    deo_t = (grow_ref[0] * dyt_ref[...].astype(f32)).astype(bf16)
    _store_split(gd_ref, jnp.dot(deo_t, hidden, preferred_element_type=f32))
    grad_gate_act = (grad_hidden * up_act * sig * (1.0 + gate_act * (1.0 - sig))).astype(bf16)
    grad_up_act = (grad_hidden * silu).astype(bf16)
    n2t = n2t_ref[...]
    _store_split(gg_ref, jnp.dot(n2t, grad_gate_act, preferred_element_type=f32))
    _store_split(gu_ref, jnp.dot(n2t, grad_up_act, preferred_element_type=f32))
    dn2_ref[...] += lax.dot_general(
        grad_gate_act, wg, nt, preferred_element_type=f32
    ) + lax.dot_general(grad_up_act, wu, nt, preferred_element_type=f32)


def expert_kernel(n2, n2t, dy, dyt, gcol, grow, wg, wu, wd, groups):
    tokens, width = n2.shape
    experts, _, hidden = wg.shape
    f32 = jnp.float32
    whole = lambda shape: pl.BlockSpec(shape, lambda e: (0,) * len(shape))
    per_expert = lambda shape: pl.BlockSpec((1,) + shape, lambda e: (e,) + (0,) * len(shape))
    flops = experts * tokens * width * hidden * 2 * 9
    split_rows = width // (groups * 2)
    split = pl.BlockSpec((2, 1, groups, split_rows, hidden), lambda e: (0, e, 0, 0, 0))
    return pl.pallas_call(
        _expert_body,
        grid=(experts,),
        in_specs=[
            whole((tokens, width)),
            whole((width, tokens)),
            whole((tokens, width)),
            whole((width, tokens)),
            per_expert((tokens, 1)),
            per_expert((1, tokens)),
            per_expert((width, hidden)),
            per_expert((width, hidden)),
            per_expert((width, hidden)),
        ],
        out_specs=[
            whole((tokens, width)),
            per_expert((tokens, 1)),
            split,
            split,
            split,
            whole((tokens, width)),
        ],
        out_shape=[
            jax.ShapeDtypeStruct((tokens, width), f32),
            jax.ShapeDtypeStruct((experts, tokens, 1), f32),
            jax.ShapeDtypeStruct((2, experts, groups, split_rows, hidden), jnp.bfloat16),
            jax.ShapeDtypeStruct((2, experts, groups, split_rows, hidden), jnp.bfloat16),
            jax.ShapeDtypeStruct((2, experts, groups, split_rows, hidden), jnp.bfloat16),
            jax.ShapeDtypeStruct((tokens, width), f32),
        ],
        compiler_params=pltpu.CompilerParams(
            dimension_semantics=("arbitrary",), vmem_limit_bytes=64 * 1024 * 1024
        ),
        cost_estimate=pl.CostEstimate(
            flops=flops,
            transcendentals=experts * tokens * hidden,
            bytes_accessed=experts * width * hidden * (3 * 2 + 3 * 2) + tokens * width * 16,
        ),
    )(n2, n2t, dy, dyt, gcol, grow, wg, wu, wd)


MESH = pl.DeviceIdType.MESH


def _exchange_body(axis, n, per_peer, src_ref, out_ref, send_sems, recv_sems):
    me = lax.axis_index(axis)
    barrier = pltpu.get_barrier_semaphore()
    for k in range(1, n):
        peer = lax.rem(me + k, n)
        pl.semaphore_signal(barrier, 1, device_id={axis: peer}, device_id_type=MESH)
    pl.semaphore_wait(barrier, n - 1)
    sends = []
    for k in range(1, n):
        peer = lax.rem(me + k, n)
        copy = pltpu.make_async_remote_copy(
            src_ref=src_ref.at[peer] if per_peer else src_ref,
            dst_ref=out_ref.at[me],
            send_sem=send_sems.at[k - 1],
            recv_sem=recv_sems.at[k - 1],
            device_id={axis: peer},
            device_id_type=MESH,
        )
        copy.start()
        sends.append(copy)
    for k in range(1, n):
        source = lax.rem(me + n - k, n)
        pltpu.make_async_remote_copy(
            src_ref=src_ref.at[source] if per_peer else src_ref,
            dst_ref=out_ref.at[source],
            send_sem=send_sems.at[k - 1],
            recv_sem=recv_sems.at[k - 1],
            device_id={axis: source},
            device_id_type=MESH,
        ).wait_recv()
    for copy in sends:
        copy.wait_send()


def exchange(x, axis, n, per_peer, collective_id):
    block = x.shape[1:] if per_peer else x.shape
    nbytes = math.prod(block) * x.dtype.itemsize
    return pl.pallas_call(
        functools.partial(_exchange_body, axis, n, per_peer),
        out_shape=jax.ShapeDtypeStruct((n,) + tuple(block), x.dtype),
        in_specs=[pl.BlockSpec(memory_space=pl.ANY)],
        out_specs=pl.BlockSpec(memory_space=pl.ANY),
        scratch_shapes=[pltpu.SemaphoreType.DMA((n - 1,)), pltpu.SemaphoreType.DMA((n - 1,))],
        compiler_params=pltpu.CompilerParams(collective_id=collective_id, has_side_effects=True),
        cost_estimate=pl.CostEstimate(flops=0, transcendentals=0, bytes_accessed=2 * (n - 1) * nbytes),
    )(x)


def gather_axis(x, axis, n, collective_id):
    got = exchange(x, axis, n, False, collective_id)
    return lax.dynamic_update_slice_in_dim(got, x[None], lax.axis_index(axis), 0)


def sum_axis(x, axis, collective_id):
    got = exchange(x, axis, 2, False, collective_id)
    me = lax.axis_index(axis)
    other = lax.dynamic_index_in_dim(got, 1 - me, 0, keepdims=False)
    return x.astype(jnp.float32) + other.astype(jnp.float32)


def core_reduce(x, collective_id):
    got = exchange(x, "core", 2, True, collective_id)
    me = lax.axis_index("core")
    own = lax.dynamic_index_in_dim(x, me, 0, keepdims=False)
    other = lax.dynamic_index_in_dim(got, 1 - me, 0, keepdims=False)
    return (own.astype(jnp.float32) + other.astype(jnp.float32)).astype(jnp.bfloat16)


def scatter_sum_axis(x, axis, n, collective_id):
    got = exchange(x, axis, n, True, collective_id)
    me = lax.axis_index(axis)
    own = lax.dynamic_index_in_dim(x, me, 0, keepdims=True)
    full = lax.dynamic_update_slice_in_dim(got, own, me, 0)
    return jnp.sum(full.astype(jnp.float32), axis=0)


def per_device(
    dpx_count,
    hidden_in,
    attn_gain,
    q_weight,
    key_matrix,
    value_matrix,
    o_weight,
    moe_gain,
    router_weight,
    gate_weight,
    up_weight,
    down_weight,
    segments,
    expert_picks,
    output_grad,
):
    bf16 = jnp.bfloat16
    f32 = jnp.float32
    token_count = hidden_in.shape[0]
    ctx_index = lax.axis_index("ctx")
    heads_local = q_weight.shape[1] // HEAD_SIZE
    kv_local = key_matrix.shape[1] // HEAD_SIZE
    group_size = heads_local // kv_local
    score_scale = 1.0 / math.sqrt(HEAD_SIZE)
    token_positions = ctx_index * token_count + jnp.arange(token_count, dtype=jnp.int32)
    segment_here = lax.dynamic_slice_in_dim(segments, ctx_index * token_count, token_count)
    inputs_f32 = hidden_in.astype(f32)
    normed_f32, scale_one = normalize(inputs_f32, attn_gain)
    normed_one = normed_f32.astype(bf16)
    query_rows = jnp.dot(normed_one, q_weight, preferred_element_type=f32).reshape(
        token_count, heads_local, HEAD_SIZE
    )
    keys_raw = jnp.dot(normed_one, key_matrix, preferred_element_type=f32).reshape(
        token_count, kv_local, HEAD_SIZE
    )
    values_raw = jnp.dot(normed_one, value_matrix, preferred_element_type=f32)
    query_grouped = (
        apply_rotary(query_rows, token_positions, 1.0)
        .astype(bf16)
        .reshape(token_count, kv_local, group_size, HEAD_SIZE)
    )
    key_flat = (
        apply_rotary(keys_raw, token_positions, 1.0)
        .astype(bf16)
        .reshape(token_count, kv_local * HEAD_SIZE)
    )
    value_flat = values_raw.astype(bf16)

    def piece_mask(piece_rows):
        key_pos = jnp.arange(piece_rows, dtype=jnp.int32)
        return (segment_here[:, None] == segments[None, :]) & (
            key_pos[None, :] <= token_positions[:, None]
        )

    ctx_count = segments.shape[0] // token_count
    kv_both = gather_axis(jnp.concatenate([key_flat, value_flat], axis=1), "ctx", ctx_count, 1)
    run_max = jnp.full((kv_local, group_size, token_count), NEGATIVE, f32)
    piece_rows = ctx_count * token_count
    kv_width = kv_local * HEAD_SIZE
    key_piece = kv_both[:, :, :kv_width].reshape(piece_rows, kv_local, HEAD_SIZE)
    value_piece = kv_both[:, :, kv_width:].reshape(piece_rows, kv_local, HEAD_SIZE)
    allowed = piece_mask(piece_rows)
    scores = (
        jnp.einsum("tkgd,nkd->kgtn", query_grouped, key_piece, preferred_element_type=f32)
        * score_scale
    )
    scores = jnp.where(allowed, scores, NEGATIVE)
    new_max = jnp.maximum(run_max, jnp.max(scores, axis=-1))
    weights = jnp.where(allowed, jnp.exp(scores - new_max[..., None]), 0.0)
    run_sum = jnp.sum(weights, axis=-1)
    accumulated = jnp.einsum(
        "kgtn,nkd->kgtd", weights.astype(bf16), value_piece, preferred_element_type=f32
    )
    fold_state = (new_max, run_sum, accumulated)
    run_max, run_sum, accumulated = fold_state
    attn_grouped = accumulated / run_sum[..., None]
    log_sum = run_max + jnp.log(run_sum)
    attn_bf = (
        jnp.transpose(attn_grouped, (2, 0, 1, 3))
        .reshape(token_count, heads_local * HEAD_SIZE)
        .astype(bf16)
    )
    attn_partial = contract_cols(attn_bf, o_weight)
    mixed_attn = sum_axis(attn_partial.astype(bf16), "tensor", 2)
    resid = inputs_f32 + mixed_attn
    normed_two_f32, scale_two = normalize(resid, moe_gain)
    normed_two = normed_two_f32.astype(bf16)
    logits = jnp.dot(normed_two, router_weight, preferred_element_type=f32)
    expert_range = jnp.arange(NEXP, dtype=jnp.int32)
    picked_onehot = expert_picks[:, :, None] == expert_range[None, None, :]
    picked = jnp.sum(jnp.where(picked_onehot, logits[:, None, :], 0.0), axis=2)
    gate_probs = jax.nn.softmax(picked, axis=-1)
    gates_dense = jnp.sum(jnp.where(picked_onehot, gate_probs[:, :, None], 0.0), axis=1)
    gates_by_expert = jnp.transpose(gates_dense)
    cot_bf = output_grad
    moe_acc, gate_parts, grad_gate, grad_up, grad_down, moe_grad_rows = expert_kernel(
        normed_two,
        jnp.transpose(normed_two),
        cot_bf,
        jnp.transpose(cot_bf),
        gates_by_expert[:, :, None],
        gates_by_expert[:, None, :],
        gate_weight,
        up_weight,
        down_weight,
        dpx_count,
    )
    cot_f32 = output_grad.astype(f32)
    moe_total = sum_axis(moe_acc.astype(bf16), "tensor", 3)
    output = (resid + moe_total).astype(bf16)
    grad_rows_all = moe_grad_rows
    gate_parts = gate_parts[:, :, 0]
    grad_gate_out, grad_up_out, grad_down_out = [
        lax.psum_scatter(
            core_reduce(g, cid).reshape(g.shape[1], -1, g.shape[4]),
            ("dpx", "ctx"),
            scatter_dimension=1,
            tiled=True,
        ).astype(jnp.float32)
        for g, cid in ((grad_gate, 8), (grad_up, 9), (grad_down, 10))
    ]
    gate_pair = jnp.sum(
        jnp.where(picked_onehot, jnp.transpose(gate_parts)[:, None, :], 0.0), axis=2
    )
    moe_summed = sum_axis(grad_rows_all.astype(bf16), "tensor", 4)
    gate_summed = sum_axis(gate_pair.astype(bf16), "tensor", 5)
    grad_picked = gate_probs * (
        gate_summed - jnp.sum(gate_probs * gate_summed, axis=1, keepdims=True)
    )
    grad_logits = jnp.sum(jnp.where(picked_onehot, grad_picked[:, :, None], 0.0), axis=1).astype(
        bf16
    )
    grad_router = contract_rows(normed_two, grad_logits)
    grad_normed_two = moe_summed + contract_cols(grad_logits, router_weight)
    grad_two_rows, grad_moe_gain = norm_backward(resid, scale_two, moe_gain, grad_normed_two)
    grad_resid = cot_f32 + grad_two_rows
    grad_mix = grad_resid.astype(bf16)
    grad_o = contract_rows(grad_mix, attn_bf)
    grad_attn = jnp.dot(grad_mix, o_weight, preferred_element_type=f32).astype(bf16)
    grad_attn_grouped = jnp.transpose(
        grad_attn.reshape(token_count, kv_local, group_size, HEAD_SIZE), (1, 2, 0, 3)
    )
    row_delta = jnp.sum(grad_attn_grouped.astype(f32) * attn_grouped, axis=-1)
    allowed = piece_mask(piece_rows)
    scores = (
        jnp.einsum("tkgd,nkd->kgtn", query_grouped, key_piece, preferred_element_type=f32)
        * score_scale
    )
    probability = jnp.where(allowed, jnp.exp(scores - log_sum[..., None]), 0.0)
    grad_probs = jnp.einsum(
        "kgtd,nkd->kgtn", grad_attn_grouped, value_piece, preferred_element_type=f32
    )
    grad_scores = (probability * (grad_probs - row_delta[..., None])).astype(bf16)
    grad_query = score_scale * jnp.einsum(
        "kgtn,nkd->kgtd", grad_scores, key_piece, preferred_element_type=f32
    )
    key_part = score_scale * jnp.einsum(
        "kgtn,tkgd->nkd", grad_scores, query_grouped, preferred_element_type=f32
    )
    value_part = jnp.einsum(
        "kgtn,kgtd->nkd", probability.astype(bf16), grad_attn_grouped, preferred_element_type=f32
    )
    grad_keys_all = key_part.reshape(piece_rows, kv_local * HEAD_SIZE)
    grad_values_all = value_part.reshape(piece_rows, kv_local * HEAD_SIZE)
    back_state = (grad_query, grad_keys_all, grad_values_all)
    grad_query, grad_keys_all, grad_values_all = back_state
    grad_kv_here = scatter_sum_axis(
        jnp.concatenate([grad_keys_all, grad_values_all], axis=1)
        .astype(bf16)
        .reshape(ctx_count, token_count, 2 * kv_width),
        "ctx",
        ctx_count,
        6,
    )
    grad_keys_here = grad_kv_here[:, :kv_width]
    grad_values_here = grad_kv_here[:, kv_width:]
    grad_query_rows = jnp.transpose(grad_query, (2, 0, 1, 3)).reshape(
        token_count, heads_local, HEAD_SIZE
    )
    grad_query_bf = (
        apply_rotary(grad_query_rows, token_positions, -1.0)
        .reshape(token_count, heads_local * HEAD_SIZE)
        .astype(bf16)
    )
    grad_key_bf = (
        apply_rotary(
            grad_keys_here.reshape(token_count, kv_local, HEAD_SIZE), token_positions, -1.0
        )
        .reshape(token_count, kv_local * HEAD_SIZE)
        .astype(bf16)
    )
    grad_value_bf = grad_values_here.astype(bf16)
    grad_q = contract_rows(normed_one, grad_query_bf)
    grad_k = contract_rows(normed_one, grad_key_bf)
    grad_v = contract_rows(normed_one, grad_value_bf)
    partial_one = (
        contract_cols(grad_query_bf, q_weight)
        + contract_cols(grad_key_bf, key_matrix)
        + contract_cols(grad_value_bf, value_matrix)
    )
    grad_normed_one = sum_axis(partial_one.astype(bf16), "tensor", 7)
    grad_one_rows, grad_attn_gain = norm_backward(inputs_f32, scale_one, attn_gain, grad_normed_one)
    input_grad = grad_resid + grad_one_rows
    q_cols, o_cols, k_cols = grad_q.shape[1], grad_o.shape[1], grad_k.shape[1]
    small = jnp.concatenate(
        [
            grad_router,
            grad_attn_gain[:, None],
            grad_moe_gain[:, None],
            jnp.zeros((grad_router.shape[0], 128 - grad_router.shape[1] - 2), f32),
        ],
        axis=1,
    )
    dense_all = jnp.concatenate(
        [grad_q, grad_o, grad_k, grad_v, small], axis=1
    ).astype(bf16)
    width = dense_all.shape[0]
    dense_all = jnp.transpose(
        dense_all.reshape(dpx_count, 2, width // (2 * dpx_count), dense_all.shape[1]), (1, 0, 2, 3)
    )
    dense_all, grad_gate_out, grad_up_out, grad_down_out = lax.optimization_barrier(
        (dense_all, grad_gate_out, grad_up_out, grad_down_out)
    )
    dense_half = core_reduce(dense_all, 11)
    dense_here = lax.psum_scatter(
        dense_half.reshape(-1, dense_half.shape[-1]), ("dpx", "ctx"), scatter_dimension=0, tiled=True
    ).astype(f32)
    spans = [q_cols, o_cols, k_cols, k_cols, router_weight.shape[1], 1, 1]
    cuts = [sum(spans[:i]) for i in range(len(spans) + 1)]
    pieces_out = [dense_here[:, cuts[i] : cuts[i + 1]] for i in range(len(spans))]
    dense_out = (
        pieces_out[5][:, 0],
        pieces_out[0],
        pieces_out[2],
        pieces_out[3],
        pieces_out[1],
        pieces_out[6][:, 0],
        pieces_out[4],
    )
    return (
        output,
        input_grad,
        dense_out[0],
        dense_out[1],
        dense_out[2],
        dense_out[3],
        dense_out[4],
        dense_out[5],
        dense_out[6],
        grad_gate_out,
        grad_up_out,
        grad_down_out,
    )


def solution(mesh):
    dp_count, ctx_count, tensor_count = (mesh.shape[a] for a in ("dp", "ctx", "tensor"))
    split_mesh = jax.sharding.Mesh(
        mesh.devices.reshape(dp_count // 2, 2, ctx_count, tensor_count), ("dpx", "core", "ctx", "tensor")
    )
    return jax.shard_map(
        functools.partial(per_device, dp_count // 2),
        mesh=split_mesh,
        in_specs=(
            P(("dpx", "core", "ctx"), None),
            P(),
            P(None, "tensor"),
            P(None, "tensor"),
            P(None, "tensor"),
            P(None, "tensor"),
            P(),
            P(),
            P(None, None, "tensor"),
            P(None, None, "tensor"),
            P(None, None, "tensor"),
            P(("dpx", "core")),
            P(("dpx", "core", "ctx"), None),
            P(("dpx", "core", "ctx"), None),
        ),
        out_specs=(
            P(("dpx", "core", "ctx"), None),
            P(("dpx", "core", "ctx"), None),
            P(("dpx", "core", "ctx")),
            P(("dpx", "core", "ctx"), "tensor"),
            P(("dpx", "core", "ctx"), "tensor"),
            P(("dpx", "core", "ctx"), "tensor"),
            P(("dpx", "core", "ctx"), "tensor"),
            P(("dpx", "core", "ctx")),
            P(("dpx", "core", "ctx"), None),
            P(None, ("dpx", "core", "ctx"), "tensor"),
            P(None, ("dpx", "core", "ctx"), "tensor"),
            P(None, ("dpx", "core", "ctx"), "tensor"),
        ),
        check_vma=False,
    )
```

```python
import functools
import math

import jax
import jax.numpy as jnp
from jax import lax
from jax.experimental import pallas as pl
from jax.experimental.pallas import tpu as pltpu
from jax.sharding import PartitionSpec as P

HEAD_SIZE = 64
NEXP = 24
CAP = 341


EPSILON = 1e-06
ROPE_BASE = 10000.0
NEGATIVE = -1e30
HIGHEST = lax.Precision.HIGHEST


def normalize(rows, gain):
    scale_inv = lax.rsqrt(jnp.mean(rows * rows, axis=-1, keepdims=True) + EPSILON)
    return (rows * scale_inv * gain, scale_inv)


def norm_backward(rows, scale_inv, gain, grad_normed):
    weighted = gain * grad_normed
    grad_gain = jnp.sum(grad_normed * rows * scale_inv, axis=0)
    inner_mean = jnp.mean(weighted * rows, axis=-1, keepdims=True)
    grad_rows = scale_inv * weighted - rows * scale_inv * scale_inv * scale_inv * inner_mean
    return (grad_rows, grad_gain)


def apply_rotary(value_rows, token_positions, direction):
    half_dim = value_rows.shape[-1] // 2
    frequency = ROPE_BASE ** (-jnp.arange(half_dim, dtype=jnp.float32) / half_dim)
    angles = token_positions.astype(jnp.float32)[:, None] * frequency[None, :]
    cosine = jnp.cos(angles)[:, None, :]
    sine_part = direction * jnp.sin(angles)[:, None, :]
    first_half = value_rows[..., :half_dim]
    second = value_rows[..., half_dim:]
    return jnp.concatenate(
        [first_half * cosine - second * sine_part, second * cosine + first_half * sine_part],
        axis=-1,
    )


def contract_rows(left, right):
    return lax.dot_general(
        left, right, (((0,), (0,)), ((), ())), preferred_element_type=jnp.float32
    )


def contract_rows_exact(left, right):
    return lax.dot_general(
        left, right, (((0,), (0,)), ((), ())), precision=HIGHEST, preferred_element_type=jnp.float32
    )


def contract_cols(left, right):
    return lax.dot_general(
        left, right, (((1,), (1,)), ((), ())), preferred_element_type=jnp.float32
    )


def _store_split(out_ref, value):
    cores, _, groups, rows, _ = out_ref.shape
    for x in range(groups):
        for c in range(cores):
            start = (x * cores + c) * rows
            out_ref[c, 0, x] = value[start : start + rows].astype(out_ref.dtype)


def _expert_body(
    n2_ref, n2t_ref, dy_ref, dyt_ref, gcol_ref, grow_ref, wg_ref, wu_ref, wd_ref,
    acc_ref, dgate_ref, gg_ref, gu_ref, gd_ref, dn2_ref,
):
    f32 = jnp.float32
    bf16 = jnp.bfloat16
    nt = (((1,), (1,)), ((), ()))

    @pl.when(pl.program_id(0) == 0)
    def _():
        acc_ref[...] = jnp.zeros_like(acc_ref)
        dn2_ref[...] = jnp.zeros_like(dn2_ref)

    n2 = n2_ref[...]
    wg = wg_ref[0]
    wu = wu_ref[0]
    wd = wd_ref[0]
    gate_act = jnp.dot(n2, wg, preferred_element_type=f32)
    up_act = jnp.dot(n2, wu, preferred_element_type=f32)
    sig = 1.0 / (1.0 + jnp.exp(-gate_act))
    silu = gate_act * sig
    hidden = (silu * up_act).astype(bf16)
    expert_out = lax.dot_general(hidden, wd, nt, preferred_element_type=f32)
    gc = gcol_ref[0]
    acc_ref[...] += gc * expert_out
    dy = dy_ref[...].astype(f32)
    dgate_ref[0] = jnp.sum(expert_out * dy, axis=1, keepdims=True)
    deo = (gc * dy).astype(bf16)
    grad_hidden = jnp.dot(deo, wd, preferred_element_type=f32)
    deo_t = (grow_ref[0] * dyt_ref[...].astype(f32)).astype(bf16)
    _store_split(gd_ref, jnp.dot(deo_t, hidden, preferred_element_type=f32))
    grad_gate_act = (grad_hidden * up_act * sig * (1.0 + gate_act * (1.0 - sig))).astype(bf16)
    grad_up_act = (grad_hidden * silu).astype(bf16)
    n2t = n2t_ref[...]
    _store_split(gg_ref, jnp.dot(n2t, grad_gate_act, preferred_element_type=f32))
    _store_split(gu_ref, jnp.dot(n2t, grad_up_act, preferred_element_type=f32))
    dn2_ref[...] += lax.dot_general(
        grad_gate_act, wg, nt, preferred_element_type=f32
    ) + lax.dot_general(grad_up_act, wu, nt, preferred_element_type=f32)


def expert_kernel(n2, n2t, dy, dyt, gcol, grow, wg, wu, wd, groups):
    tokens, width = n2.shape
    experts, _, hidden = wg.shape
    f32 = jnp.float32
    whole = lambda shape: pl.BlockSpec(shape, lambda e: (0,) * len(shape))
    per_expert = lambda shape: pl.BlockSpec((1,) + shape, lambda e: (e,) + (0,) * len(shape))
    flops = experts * tokens * width * hidden * 2 * 9
    split_rows = width // (groups * 2)
    split = pl.BlockSpec((2, 1, groups, split_rows, hidden), lambda e: (0, e, 0, 0, 0))
    return pl.pallas_call(
        _expert_body,
        grid=(experts,),
        in_specs=[
            whole((tokens, width)),
            whole((width, tokens)),
            whole((tokens, width)),
            whole((width, tokens)),
            per_expert((tokens, 1)),
            per_expert((1, tokens)),
            per_expert((width, hidden)),
            per_expert((width, hidden)),
            per_expert((width, hidden)),
        ],
        out_specs=[
            whole((tokens, width)),
            per_expert((tokens, 1)),
            split,
            split,
            split,
            whole((tokens, width)),
        ],
        out_shape=[
            jax.ShapeDtypeStruct((tokens, width), f32),
            jax.ShapeDtypeStruct((experts, tokens, 1), f32),
            jax.ShapeDtypeStruct((2, experts, groups, split_rows, hidden), jnp.bfloat16),
            jax.ShapeDtypeStruct((2, experts, groups, split_rows, hidden), jnp.bfloat16),
            jax.ShapeDtypeStruct((2, experts, groups, split_rows, hidden), jnp.bfloat16),
            jax.ShapeDtypeStruct((tokens, width), f32),
        ],
        compiler_params=pltpu.CompilerParams(
            dimension_semantics=("arbitrary",), vmem_limit_bytes=64 * 1024 * 1024
        ),
        cost_estimate=pl.CostEstimate(
            flops=flops,
            transcendentals=experts * tokens * hidden,
            bytes_accessed=experts * width * hidden * (3 * 2 + 3 * 2) + tokens * width * 16,
        ),
    )(n2, n2t, dy, dyt, gcol, grow, wg, wu, wd)


MESH = pl.DeviceIdType.MESH


def _exchange_body(axis, n, per_peer, src_ref, out_ref, send_sems, recv_sems):
    me = lax.axis_index(axis)
    barrier = pltpu.get_barrier_semaphore()
    for k in range(1, n):
        peer = lax.rem(me + k, n)
        pl.semaphore_signal(barrier, 1, device_id={axis: peer}, device_id_type=MESH)
    pl.semaphore_wait(barrier, n - 1)
    sends = []
    for k in range(1, n):
        peer = lax.rem(me + k, n)
        copy = pltpu.make_async_remote_copy(
            src_ref=src_ref.at[peer] if per_peer else src_ref,
            dst_ref=out_ref.at[me],
            send_sem=send_sems.at[k - 1],
            recv_sem=recv_sems.at[k - 1],
            device_id={axis: peer},
            device_id_type=MESH,
        )
        copy.start()
        sends.append(copy)
    for k in range(1, n):
        source = lax.rem(me + n - k, n)
        pltpu.make_async_remote_copy(
            src_ref=src_ref.at[source] if per_peer else src_ref,
            dst_ref=out_ref.at[source],
            send_sem=send_sems.at[k - 1],
            recv_sem=recv_sems.at[k - 1],
            device_id={axis: source},
            device_id_type=MESH,
        ).wait_recv()
    for copy in sends:
        copy.wait_send()


def exchange(x, axis, n, per_peer, collective_id):
    block = x.shape[1:] if per_peer else x.shape
    nbytes = math.prod(block) * x.dtype.itemsize
    return pl.pallas_call(
        functools.partial(_exchange_body, axis, n, per_peer),
        out_shape=jax.ShapeDtypeStruct((n,) + tuple(block), x.dtype),
        in_specs=[pl.BlockSpec(memory_space=pl.ANY)],
        out_specs=pl.BlockSpec(memory_space=pl.ANY),
        scratch_shapes=[pltpu.SemaphoreType.DMA((n - 1,)), pltpu.SemaphoreType.DMA((n - 1,))],
        compiler_params=pltpu.CompilerParams(collective_id=collective_id, has_side_effects=True),
        cost_estimate=pl.CostEstimate(flops=0, transcendentals=0, bytes_accessed=2 * (n - 1) * nbytes),
    )(x)


def gather_axis(x, axis, n, collective_id):
    got = exchange(x, axis, n, False, collective_id)
    return lax.dynamic_update_slice_in_dim(got, x[None], lax.axis_index(axis), 0)


def sum_axis(x, axis, collective_id):
    got = exchange(x, axis, 2, False, collective_id)
    me = lax.axis_index(axis)
    other = lax.dynamic_index_in_dim(got, 1 - me, 0, keepdims=False)
    return x.astype(jnp.float32) + other.astype(jnp.float32)


def core_reduce(x, collective_id):
    got = exchange(x, "core", 2, True, collective_id)
    me = lax.axis_index("core")
    own = lax.dynamic_index_in_dim(x, me, 0, keepdims=False)
    other = lax.dynamic_index_in_dim(got, 1 - me, 0, keepdims=False)
    return (own.astype(jnp.float32) + other.astype(jnp.float32)).astype(jnp.bfloat16)


def scatter_sum_axis(x, axis, n, collective_id):
    got = exchange(x, axis, n, True, collective_id)
    me = lax.axis_index(axis)
    own = lax.dynamic_index_in_dim(x, me, 0, keepdims=True)
    full = lax.dynamic_update_slice_in_dim(got, own, me, 0)
    return jnp.sum(full.astype(jnp.float32), axis=0)


def _flash_body(ctx_ref, q_ref, k_ref, v_ref, qseg_ref, qpos_ref, kseg_ref, o_ref, lse_ref, m_sc, l_sc, acc_sc):
    f32 = jnp.float32
    block = pl.program_id(1)

    @pl.when(block == 0)
    def _():
        m_sc[...] = jnp.full_like(m_sc, NEGATIVE)
        l_sc[...] = jnp.zeros_like(l_sc)
        acc_sc[...] = jnp.zeros_like(acc_sc)

    @pl.when(block <= ctx_ref[0])
    def _():
        keys = k_ref[0]
        width = keys.shape[0]
        scores = lax.dot_general(
            q_ref[0], keys, (((1,), (1,)), ((), ())), preferred_element_type=f32
        ) * (1.0 / math.sqrt(HEAD_SIZE))
        key_pos = block * width + lax.broadcasted_iota(jnp.int32, (1, width), 1)
        allowed = (qseg_ref[...] == kseg_ref[...]) & (key_pos <= qpos_ref[...])
        scores = jnp.where(allowed, scores, NEGATIVE)
        m_old = m_sc[...]
        m_new = jnp.maximum(m_old, jnp.max(scores, axis=1, keepdims=True))
        alpha = jnp.exp(m_old - m_new)
        weights = jnp.where(allowed, jnp.exp(scores - m_new), 0.0)
        l_sc[...] = alpha * l_sc[...] + jnp.sum(weights, axis=1, keepdims=True)
        acc_sc[...] = alpha * acc_sc[...] + jnp.dot(
            weights.astype(jnp.bfloat16), v_ref[0], preferred_element_type=f32
        )
        m_sc[...] = m_new

    @pl.when(block == pl.num_programs(1) - 1)
    def _():
        o_ref[0] = acc_sc[...] / l_sc[...]
        lse_ref[0] = m_sc[...] + jnp.log(l_sc[...])


def flash_forward(ctx_index, q, k, v, qseg, qpos, kseg, width):
    heads, rows, depth = q.shape
    blocks = k.shape[1] // width
    f32 = jnp.float32
    capped = lambda h, b, c: (h, jnp.minimum(b, c[0]), 0)
    grid_spec = pltpu.PrefetchScalarGridSpec(
        num_scalar_prefetch=1,
        grid=(heads, blocks),
        in_specs=[
            pl.BlockSpec((1, rows, depth), lambda h, b, c: (h, 0, 0)),
            pl.BlockSpec((1, width, depth), capped),
            pl.BlockSpec((1, width, depth), capped),
            pl.BlockSpec((rows, 1), lambda h, b, c: (0, 0)),
            pl.BlockSpec((rows, 1), lambda h, b, c: (0, 0)),
            pl.BlockSpec((1, width), lambda h, b, c: (0, jnp.minimum(b, c[0]))),
        ],
        out_specs=[
            pl.BlockSpec((1, rows, depth), lambda h, b, c: (h, 0, 0)),
            pl.BlockSpec((1, rows, 1), lambda h, b, c: (h, 0, 0)),
        ],
        scratch_shapes=[
            pltpu.VMEM((rows, 1), f32),
            pltpu.VMEM((rows, 1), f32),
            pltpu.VMEM((rows, depth), f32),
        ],
    )
    return pl.pallas_call(
        _flash_body,
        grid_spec=grid_spec,
        out_shape=[
            jax.ShapeDtypeStruct((heads, rows, depth), f32),
            jax.ShapeDtypeStruct((heads, rows, 1), f32),
        ],
        compiler_params=pltpu.CompilerParams(
            dimension_semantics=("arbitrary", "arbitrary"), vmem_limit_bytes=48 * 1024 * 1024
        ),
        cost_estimate=pl.CostEstimate(
            flops=heads * rows * k.shape[1] * depth * 4,
            transcendentals=heads * rows * k.shape[1],
            bytes_accessed=(q.size + k.size + v.size) * 2 + heads * rows * depth * 4,
        ),
    )(jnp.reshape(ctx_index, (1,)).astype(jnp.int32), q, k, v, qseg, qpos, kseg)


def per_device(
    dpx_count,
    hidden_in,
    attn_gain,
    q_weight,
    key_matrix,
    value_matrix,
    o_weight,
    moe_gain,
    router_weight,
    gate_weight,
    up_weight,
    down_weight,
    segments,
    expert_picks,
    output_grad,
):
    bf16 = jnp.bfloat16
    f32 = jnp.float32
    token_count = hidden_in.shape[0]
    ctx_index = lax.axis_index("ctx")
    heads_local = q_weight.shape[1] // HEAD_SIZE
    kv_local = key_matrix.shape[1] // HEAD_SIZE
    group_size = heads_local // kv_local
    score_scale = 1.0 / math.sqrt(HEAD_SIZE)
    token_positions = ctx_index * token_count + jnp.arange(token_count, dtype=jnp.int32)
    segment_here = lax.dynamic_slice_in_dim(segments, ctx_index * token_count, token_count)
    inputs_f32 = hidden_in.astype(f32)
    o_full = lax.all_gather(o_weight, "tensor", axis=1, tiled=True)
    normed_f32, scale_one = normalize(inputs_f32, attn_gain)
    normed_one = normed_f32.astype(bf16)
    query_rows = jnp.dot(normed_one, q_weight, preferred_element_type=f32).reshape(
        token_count, heads_local, HEAD_SIZE
    )
    keys_raw = jnp.dot(normed_one, key_matrix, preferred_element_type=f32).reshape(
        token_count, kv_local, HEAD_SIZE
    )
    values_raw = jnp.dot(normed_one, value_matrix, preferred_element_type=f32)
    query_grouped = (
        apply_rotary(query_rows, token_positions, 1.0)
        .astype(bf16)
        .reshape(token_count, kv_local, group_size, HEAD_SIZE)
    )
    key_flat = (
        apply_rotary(keys_raw, token_positions, 1.0)
        .astype(bf16)
        .reshape(token_count, kv_local * HEAD_SIZE)
    )
    value_flat = values_raw.astype(bf16)

    def piece_mask(piece_rows):
        key_pos = jnp.arange(piece_rows, dtype=jnp.int32)
        return (segment_here[:, None] == segments[None, :]) & (
            key_pos[None, :] <= token_positions[:, None]
        )

    ctx_count = segments.shape[0] // token_count
    kv_both = gather_axis(jnp.concatenate([key_flat, value_flat], axis=1), "ctx", ctx_count, 1)
    piece_rows = ctx_count * token_count
    kv_width = kv_local * HEAD_SIZE
    key_piece = kv_both[:, :, :kv_width].reshape(piece_rows, kv_local, HEAD_SIZE)
    value_piece = kv_both[:, :, kv_width:].reshape(piece_rows, kv_local, HEAD_SIZE)
    row_segments = jnp.tile(segment_here, group_size)[:, None]
    row_positions = jnp.tile(token_positions, group_size)[:, None]
    attn_rows, lse_rows = flash_forward(
        ctx_index,
        jnp.transpose(query_grouped, (1, 2, 0, 3)).reshape(kv_local, group_size * token_count, HEAD_SIZE),
        jnp.transpose(key_piece, (1, 0, 2)),
        jnp.transpose(value_piece, (1, 0, 2)),
        row_segments,
        row_positions,
        segments[None, :],
        token_count,
    )
    attn_grouped = attn_rows.reshape(kv_local, group_size, token_count, HEAD_SIZE)
    log_sum = lse_rows.reshape(kv_local, group_size, token_count)
    attn_bf = (
        jnp.transpose(attn_grouped, (2, 0, 1, 3))
        .reshape(token_count, heads_local * HEAD_SIZE)
        .astype(bf16)
    )
    tensor_count = o_weight.shape[0] // o_weight.shape[1]
    attn_all = gather_axis(attn_bf, "tensor", tensor_count, 2)
    attn_full = jnp.transpose(attn_all, (1, 0, 2)).reshape(token_count, tensor_count * attn_bf.shape[1])
    mixed_attn = contract_cols(attn_full, o_full)
    resid = inputs_f32 + mixed_attn
    normed_two_f32, scale_two = normalize(resid, moe_gain)
    normed_two = normed_two_f32.astype(bf16)
    logits = jnp.dot(normed_two, router_weight, preferred_element_type=f32)
    expert_range = jnp.arange(NEXP, dtype=jnp.int32)
    picked_onehot = expert_picks[:, :, None] == expert_range[None, None, :]
    picked = jnp.sum(jnp.where(picked_onehot, logits[:, None, :], 0.0), axis=2)
    gate_probs = jax.nn.softmax(picked, axis=-1)
    gates_dense = jnp.sum(jnp.where(picked_onehot, gate_probs[:, :, None], 0.0), axis=1)
    gates_by_expert = jnp.transpose(gates_dense)
    cot_bf = output_grad
    moe_acc, gate_parts, grad_gate, grad_up, grad_down, moe_grad_rows = expert_kernel(
        normed_two,
        jnp.transpose(normed_two),
        cot_bf,
        jnp.transpose(cot_bf),
        gates_by_expert[:, :, None],
        gates_by_expert[:, None, :],
        gate_weight,
        up_weight,
        down_weight,
        dpx_count,
    )
    cot_f32 = output_grad.astype(f32)
    moe_total = sum_axis(moe_acc.astype(bf16), "tensor", 3)
    output = (resid + moe_total).astype(bf16)
    grad_rows_all = moe_grad_rows
    gate_parts = gate_parts[:, :, 0]
    grad_gate_out, grad_up_out, grad_down_out = [
        lax.psum_scatter(
            core_reduce(g, cid).reshape(g.shape[1], -1, g.shape[4]),
            ("dpx", "ctx"),
            scatter_dimension=1,
            tiled=True,
        ).astype(jnp.float32)
        for g, cid in ((grad_gate, 8), (grad_up, 9), (grad_down, 10))
    ]
    gate_pair = jnp.sum(
        jnp.where(picked_onehot, jnp.transpose(gate_parts)[:, None, :], 0.0), axis=2
    )
    moe_summed = sum_axis(grad_rows_all.astype(bf16), "tensor", 4)
    gate_summed = sum_axis(gate_pair.astype(bf16), "tensor", 5)
    grad_picked = gate_probs * (
        gate_summed - jnp.sum(gate_probs * gate_summed, axis=1, keepdims=True)
    )
    grad_logits = jnp.sum(jnp.where(picked_onehot, grad_picked[:, :, None], 0.0), axis=1).astype(
        bf16
    )
    grad_router = contract_rows(normed_two, grad_logits)
    grad_normed_two = moe_summed + contract_cols(grad_logits, router_weight)
    grad_two_rows, grad_moe_gain = norm_backward(resid, scale_two, moe_gain, grad_normed_two)
    grad_resid = cot_f32 + grad_two_rows
    grad_mix = grad_resid.astype(bf16)
    grad_o = contract_rows(grad_mix, attn_bf)
    grad_attn = jnp.dot(grad_mix, o_weight, preferred_element_type=f32).astype(bf16)
    grad_attn_grouped = jnp.transpose(
        grad_attn.reshape(token_count, kv_local, group_size, HEAD_SIZE), (1, 2, 0, 3)
    )
    row_delta = jnp.sum(grad_attn_grouped.astype(f32) * attn_grouped, axis=-1)
    allowed = piece_mask(piece_rows)
    scores = (
        jnp.einsum("tkgd,nkd->kgtn", query_grouped, key_piece, preferred_element_type=f32)
        * score_scale
    )
    probability = jnp.where(allowed, jnp.exp(scores - log_sum[..., None]), 0.0)
    grad_probs = jnp.einsum(
        "kgtd,nkd->kgtn", grad_attn_grouped, value_piece, preferred_element_type=f32
    )
    grad_scores = (probability * (grad_probs - row_delta[..., None])).astype(bf16)
    grad_query = score_scale * jnp.einsum(
        "kgtn,nkd->kgtd", grad_scores, key_piece, preferred_element_type=f32
    )
    key_part = score_scale * jnp.einsum(
        "kgtn,tkgd->nkd", grad_scores, query_grouped, preferred_element_type=f32
    )
    value_part = jnp.einsum(
        "kgtn,kgtd->nkd", probability.astype(bf16), grad_attn_grouped, preferred_element_type=f32
    )
    grad_keys_all = key_part.reshape(piece_rows, kv_local * HEAD_SIZE)
    grad_values_all = value_part.reshape(piece_rows, kv_local * HEAD_SIZE)
    back_state = (grad_query, grad_keys_all, grad_values_all)
    grad_query, grad_keys_all, grad_values_all = back_state
    grad_kv_here = scatter_sum_axis(
        jnp.concatenate([grad_keys_all, grad_values_all], axis=1)
        .astype(bf16)
        .reshape(ctx_count, token_count, 2 * kv_width),
        "ctx",
        ctx_count,
        6,
    )
    grad_keys_here = grad_kv_here[:, :kv_width]
    grad_values_here = grad_kv_here[:, kv_width:]
    grad_query_rows = jnp.transpose(grad_query, (2, 0, 1, 3)).reshape(
        token_count, heads_local, HEAD_SIZE
    )
    grad_query_bf = (
        apply_rotary(grad_query_rows, token_positions, -1.0)
        .reshape(token_count, heads_local * HEAD_SIZE)
        .astype(bf16)
    )
    grad_key_bf = (
        apply_rotary(
            grad_keys_here.reshape(token_count, kv_local, HEAD_SIZE), token_positions, -1.0
        )
        .reshape(token_count, kv_local * HEAD_SIZE)
        .astype(bf16)
    )
    grad_value_bf = grad_values_here.astype(bf16)
    grad_q = contract_rows(normed_one, grad_query_bf)
    grad_k = contract_rows(normed_one, grad_key_bf)
    grad_v = contract_rows(normed_one, grad_value_bf)
    partial_one = (
        contract_cols(grad_query_bf, q_weight)
        + contract_cols(grad_key_bf, key_matrix)
        + contract_cols(grad_value_bf, value_matrix)
    )
    grad_normed_one = sum_axis(partial_one.astype(bf16), "tensor", 7)
    grad_one_rows, grad_attn_gain = norm_backward(inputs_f32, scale_one, attn_gain, grad_normed_one)
    input_grad = grad_resid + grad_one_rows
    q_cols, o_cols, k_cols = grad_q.shape[1], grad_o.shape[1], grad_k.shape[1]
    small = jnp.concatenate(
        [
            grad_router,
            grad_attn_gain[:, None],
            grad_moe_gain[:, None],
            jnp.zeros((grad_router.shape[0], 128 - grad_router.shape[1] - 2), f32),
        ],
        axis=1,
    )
    dense_all = jnp.concatenate(
        [grad_q, grad_o, grad_k, grad_v, small], axis=1
    ).astype(bf16)
    width = dense_all.shape[0]
    dense_all = jnp.transpose(
        dense_all.reshape(dpx_count, 2, width // (2 * dpx_count), dense_all.shape[1]), (1, 0, 2, 3)
    )
    dense_all, grad_gate_out, grad_up_out, grad_down_out = lax.optimization_barrier(
        (dense_all, grad_gate_out, grad_up_out, grad_down_out)
    )
    dense_half = core_reduce(dense_all, 11)
    dense_here = lax.psum_scatter(
        dense_half.reshape(-1, dense_half.shape[-1]), ("dpx", "ctx"), scatter_dimension=0, tiled=True
    ).astype(f32)
    spans = [q_cols, o_cols, k_cols, k_cols, router_weight.shape[1], 1, 1]
    cuts = [sum(spans[:i]) for i in range(len(spans) + 1)]
    pieces_out = [dense_here[:, cuts[i] : cuts[i + 1]] for i in range(len(spans))]
    dense_out = (
        pieces_out[5][:, 0],
        pieces_out[0],
        pieces_out[2],
        pieces_out[3],
        pieces_out[1],
        pieces_out[6][:, 0],
        pieces_out[4],
    )
    return (
        output,
        input_grad,
        dense_out[0],
        dense_out[1],
        dense_out[2],
        dense_out[3],
        dense_out[4],
        dense_out[5],
        dense_out[6],
        grad_gate_out,
        grad_up_out,
        grad_down_out,
    )


def solution(mesh):
    dp_count, ctx_count, tensor_count = (mesh.shape[a] for a in ("dp", "ctx", "tensor"))
    split_mesh = jax.sharding.Mesh(
        mesh.devices.reshape(dp_count // 2, 2, ctx_count, tensor_count), ("dpx", "core", "ctx", "tensor")
    )
    return jax.shard_map(
        functools.partial(per_device, dp_count // 2),
        mesh=split_mesh,
        in_specs=(
            P(("dpx", "core", "ctx"), None),
            P(),
            P(None, "tensor"),
            P(None, "tensor"),
            P(None, "tensor"),
            P(None, "tensor"),
            P(),
            P(),
            P(None, None, "tensor"),
            P(None, None, "tensor"),
            P(None, None, "tensor"),
            P(("dpx", "core")),
            P(("dpx", "core", "ctx"), None),
            P(("dpx", "core", "ctx"), None),
        ),
        out_specs=(
            P(("dpx", "core", "ctx"), None),
            P(("dpx", "core", "ctx"), None),
            P(("dpx", "core", "ctx")),
            P(("dpx", "core", "ctx"), "tensor"),
            P(("dpx", "core", "ctx"), "tensor"),
            P(("dpx", "core", "ctx"), "tensor"),
            P(("dpx", "core", "ctx"), "tensor"),
            P(("dpx", "core", "ctx")),
            P(("dpx", "core", "ctx"), None),
            P(None, ("dpx", "core", "ctx"), "tensor"),
            P(None, ("dpx", "core", "ctx"), "tensor"),
            P(None, ("dpx", "core", "ctx"), "tensor"),
        ),
        check_vma=False,
    )
```

```python
import functools
import math

import jax
import jax.numpy as jnp
from jax import lax
from jax.experimental import pallas as pl
from jax.experimental.pallas import tpu as pltpu
from jax.sharding import PartitionSpec as P

HEAD_SIZE = 64
NEXP = 24
CAP = 341


EPSILON = 1e-06
ROPE_BASE = 10000.0
NEGATIVE = -1e30
HIGHEST = lax.Precision.HIGHEST


def normalize(rows, gain):
    scale_inv = lax.rsqrt(jnp.mean(rows * rows, axis=-1, keepdims=True) + EPSILON)
    return (rows * scale_inv * gain, scale_inv)


def norm_backward(rows, scale_inv, gain, grad_normed):
    weighted = gain * grad_normed
    grad_gain = jnp.sum(grad_normed * rows * scale_inv, axis=0)
    inner_mean = jnp.mean(weighted * rows, axis=-1, keepdims=True)
    grad_rows = scale_inv * weighted - rows * scale_inv * scale_inv * scale_inv * inner_mean
    return (grad_rows, grad_gain)


def apply_rotary(value_rows, token_positions, direction):
    half_dim = value_rows.shape[-1] // 2
    frequency = ROPE_BASE ** (-jnp.arange(half_dim, dtype=jnp.float32) / half_dim)
    angles = token_positions.astype(jnp.float32)[:, None] * frequency[None, :]
    cosine = jnp.cos(angles)[:, None, :]
    sine_part = direction * jnp.sin(angles)[:, None, :]
    first_half = value_rows[..., :half_dim]
    second = value_rows[..., half_dim:]
    return jnp.concatenate(
        [first_half * cosine - second * sine_part, second * cosine + first_half * sine_part],
        axis=-1,
    )


def contract_rows(left, right):
    return lax.dot_general(
        left, right, (((0,), (0,)), ((), ())), preferred_element_type=jnp.float32
    )


def contract_rows_exact(left, right):
    return lax.dot_general(
        left, right, (((0,), (0,)), ((), ())), precision=HIGHEST, preferred_element_type=jnp.float32
    )


def contract_cols(left, right):
    return lax.dot_general(
        left, right, (((1,), (1,)), ((), ())), preferred_element_type=jnp.float32
    )


def _store_split(out_ref, value):
    cores, _, groups, rows, _ = out_ref.shape
    for x in range(groups):
        for c in range(cores):
            start = (x * cores + c) * rows
            out_ref[c, 0, x] = value[start : start + rows].astype(out_ref.dtype)


def _grad_body(
    n2_ref, n2t_ref, dy_ref, dyt_ref, gcol_ref, grow_ref, wg_ref, wu_ref, wd_ref,
    gg_ref, gu_ref, gd_ref, hid_ref, dga_ref, dua_ref,
):
    f32 = jnp.float32
    bf16 = jnp.bfloat16
    n2 = n2_ref[...]
    wd = wd_ref[0]
    gate_act = jnp.dot(n2, wg_ref[0], preferred_element_type=f32)
    up_act = jnp.dot(n2, wu_ref[0], preferred_element_type=f32)
    sig = 1.0 / (1.0 + jnp.exp(-gate_act))
    silu = gate_act * sig
    hidden = (silu * up_act).astype(bf16)
    hid_ref[0] = hidden
    deo = (gcol_ref[0] * dy_ref[...].astype(f32)).astype(bf16)
    grad_hidden = jnp.dot(deo, wd, preferred_element_type=f32)
    deo_t = (grow_ref[0] * dyt_ref[...].astype(f32)).astype(bf16)
    _store_split(gd_ref, jnp.dot(deo_t, hidden, preferred_element_type=f32))
    grad_gate_act = (grad_hidden * up_act * sig * (1.0 + gate_act * (1.0 - sig))).astype(bf16)
    grad_up_act = (grad_hidden * silu).astype(bf16)
    dga_ref[0] = grad_gate_act
    dua_ref[0] = grad_up_act
    n2t = n2t_ref[...]
    _store_split(gg_ref, jnp.dot(n2t, grad_gate_act, preferred_element_type=f32))
    _store_split(gu_ref, jnp.dot(n2t, grad_up_act, preferred_element_type=f32))


def _rows_body(hid_ref, dga_ref, dua_ref, dy_ref, gcol_ref, wg_ref, wu_ref, wd_ref, acc_ref, dgate_ref, dn2_ref):
    f32 = jnp.float32
    nt = (((1,), (1,)), ((), ()))

    @pl.when(pl.program_id(0) == 0)
    def _():
        acc_ref[...] = jnp.zeros_like(acc_ref)
        dn2_ref[...] = jnp.zeros_like(dn2_ref)

    expert_out = lax.dot_general(hid_ref[0], wd_ref[0], nt, preferred_element_type=f32)
    acc_ref[...] += gcol_ref[0] * expert_out
    dgate_ref[0] = jnp.sum(expert_out * dy_ref[...].astype(f32), axis=1, keepdims=True)
    dn2_ref[...] += lax.dot_general(
        dga_ref[0], wg_ref[0], nt, preferred_element_type=f32
    ) + lax.dot_general(dua_ref[0], wu_ref[0], nt, preferred_element_type=f32)


def expert_grad_kernel(n2, n2t, dy, dyt, gcol, grow, wg, wu, wd, groups):
    tokens, width = n2.shape
    experts, _, hidden = wg.shape
    bf16 = jnp.bfloat16
    whole = lambda shape: pl.BlockSpec(shape, lambda e: (0,) * len(shape))
    per_expert = lambda shape: pl.BlockSpec((1,) + shape, lambda e: (e,) + (0,) * len(shape))
    split_rows = width // (groups * 2)
    split = pl.BlockSpec((2, 1, groups, split_rows, hidden), lambda e: (0, e, 0, 0, 0))
    split_shape = jax.ShapeDtypeStruct((2, experts, groups, split_rows, hidden), bf16)
    act_shape = jax.ShapeDtypeStruct((experts, tokens, hidden), bf16)
    return pl.pallas_call(
        _grad_body,
        grid=(experts,),
        in_specs=[
            whole((tokens, width)),
            whole((width, tokens)),
            whole((tokens, width)),
            whole((width, tokens)),
            per_expert((tokens, 1)),
            per_expert((1, tokens)),
            per_expert((width, hidden)),
            per_expert((width, hidden)),
            per_expert((width, hidden)),
        ],
        out_specs=[split, split, split]
        + [per_expert((tokens, hidden))] * 3,
        out_shape=[split_shape] * 3 + [act_shape] * 3,
        compiler_params=pltpu.CompilerParams(
            dimension_semantics=("arbitrary",), vmem_limit_bytes=64 * 1024 * 1024
        ),
        cost_estimate=pl.CostEstimate(
            flops=experts * tokens * width * hidden * 2 * 6,
            transcendentals=experts * tokens * hidden,
            bytes_accessed=experts * width * hidden * 12 + tokens * width * 8 + experts * tokens * hidden * 6,
        ),
    )(n2, n2t, dy, dyt, gcol, grow, wg, wu, wd)


def expert_rows_kernel(hid, dga, dua, dy, gcol, wg, wu, wd):
    experts, tokens, hidden = hid.shape
    width = dy.shape[1]
    f32 = jnp.float32
    whole = lambda shape: pl.BlockSpec(shape, lambda e: (0,) * len(shape))
    per_expert = lambda shape: pl.BlockSpec((1,) + shape, lambda e: (e,) + (0,) * len(shape))
    return pl.pallas_call(
        _rows_body,
        grid=(experts,),
        in_specs=[
            per_expert((tokens, hidden)),
            per_expert((tokens, hidden)),
            per_expert((tokens, hidden)),
            whole((tokens, width)),
            per_expert((tokens, 1)),
            per_expert((width, hidden)),
            per_expert((width, hidden)),
            per_expert((width, hidden)),
        ],
        out_specs=[whole((tokens, width)), per_expert((tokens, 1)), whole((tokens, width))],
        out_shape=[
            jax.ShapeDtypeStruct((tokens, width), f32),
            jax.ShapeDtypeStruct((experts, tokens, 1), f32),
            jax.ShapeDtypeStruct((tokens, width), f32),
        ],
        compiler_params=pltpu.CompilerParams(
            dimension_semantics=("arbitrary",), vmem_limit_bytes=64 * 1024 * 1024
        ),
        cost_estimate=pl.CostEstimate(
            flops=experts * tokens * width * hidden * 2 * 3,
            transcendentals=0,
            bytes_accessed=experts * width * hidden * 6 + tokens * width * 10 + experts * tokens * hidden * 6,
        ),
    )(hid, dga, dua, dy, gcol, wg, wu, wd)

MESH = pl.DeviceIdType.MESH


def _exchange_body(axis, n, per_peer, src_ref, out_ref, send_sems, recv_sems):
    me = lax.axis_index(axis)
    barrier = pltpu.get_barrier_semaphore()
    for k in range(1, n):
        peer = lax.rem(me + k, n)
        pl.semaphore_signal(barrier, 1, device_id={axis: peer}, device_id_type=MESH)
    pl.semaphore_wait(barrier, n - 1)
    sends = []
    for k in range(1, n):
        peer = lax.rem(me + k, n)
        copy = pltpu.make_async_remote_copy(
            src_ref=src_ref.at[peer] if per_peer else src_ref,
            dst_ref=out_ref.at[me],
            send_sem=send_sems.at[k - 1],
            recv_sem=recv_sems.at[k - 1],
            device_id={axis: peer},
            device_id_type=MESH,
        )
        copy.start()
        sends.append(copy)
    for k in range(1, n):
        source = lax.rem(me + n - k, n)
        pltpu.make_async_remote_copy(
            src_ref=src_ref.at[source] if per_peer else src_ref,
            dst_ref=out_ref.at[source],
            send_sem=send_sems.at[k - 1],
            recv_sem=recv_sems.at[k - 1],
            device_id={axis: source},
            device_id_type=MESH,
        ).wait_recv()
    for copy in sends:
        copy.wait_send()


def exchange(x, axis, n, per_peer, collective_id):
    block = x.shape[1:] if per_peer else x.shape
    nbytes = math.prod(block) * x.dtype.itemsize
    return pl.pallas_call(
        functools.partial(_exchange_body, axis, n, per_peer),
        out_shape=jax.ShapeDtypeStruct((n,) + tuple(block), x.dtype),
        in_specs=[pl.BlockSpec(memory_space=pl.ANY)],
        out_specs=pl.BlockSpec(memory_space=pl.ANY),
        scratch_shapes=[pltpu.SemaphoreType.DMA((n - 1,)), pltpu.SemaphoreType.DMA((n - 1,))],
        compiler_params=pltpu.CompilerParams(collective_id=collective_id, has_side_effects=True),
        cost_estimate=pl.CostEstimate(flops=0, transcendentals=0, bytes_accessed=2 * (n - 1) * nbytes),
    )(x)


def gather_axis(x, axis, n, collective_id):
    got = exchange(x, axis, n, False, collective_id)
    return lax.dynamic_update_slice_in_dim(got, x[None], lax.axis_index(axis), 0)


def sum_axis(x, axis, collective_id):
    got = exchange(x, axis, 2, False, collective_id)
    me = lax.axis_index(axis)
    other = lax.dynamic_index_in_dim(got, 1 - me, 0, keepdims=False)
    return x.astype(jnp.float32) + other.astype(jnp.float32)


def core_reduce(x, collective_id):
    got = exchange(x, "core", 2, True, collective_id)
    me = lax.axis_index("core")
    own = lax.dynamic_index_in_dim(x, me, 0, keepdims=False)
    other = lax.dynamic_index_in_dim(got, 1 - me, 0, keepdims=False)
    return (own.astype(jnp.float32) + other.astype(jnp.float32)).astype(jnp.bfloat16)


def scatter_sum_axis(x, axis, n, collective_id):
    got = exchange(x, axis, n, True, collective_id)
    me = lax.axis_index(axis)
    own = lax.dynamic_index_in_dim(x, me, 0, keepdims=True)
    full = lax.dynamic_update_slice_in_dim(got, own, me, 0)
    return jnp.sum(full.astype(jnp.float32), axis=0)


def _flash_body(ctx_ref, q_ref, k_ref, v_ref, qseg_ref, qpos_ref, kseg_ref, o_ref, lse_ref, m_sc, l_sc, acc_sc):
    f32 = jnp.float32
    block = pl.program_id(1)

    @pl.when(block == 0)
    def _():
        m_sc[...] = jnp.full_like(m_sc, NEGATIVE)
        l_sc[...] = jnp.zeros_like(l_sc)
        acc_sc[...] = jnp.zeros_like(acc_sc)

    @pl.when(block <= ctx_ref[0])
    def _():
        keys = k_ref[0]
        width = keys.shape[0]
        scores = lax.dot_general(
            q_ref[0], keys, (((1,), (1,)), ((), ())), preferred_element_type=f32
        ) * (1.0 / math.sqrt(HEAD_SIZE))
        key_pos = block * width + lax.broadcasted_iota(jnp.int32, (1, width), 1)
        allowed = (qseg_ref[...] == kseg_ref[...]) & (key_pos <= qpos_ref[...])
        scores = jnp.where(allowed, scores, NEGATIVE)
        m_old = m_sc[...]
        m_new = jnp.maximum(m_old, jnp.max(scores, axis=1, keepdims=True))
        alpha = jnp.exp(m_old - m_new)
        weights = jnp.where(allowed, jnp.exp(scores - m_new), 0.0)
        l_sc[...] = alpha * l_sc[...] + jnp.sum(weights, axis=1, keepdims=True)
        acc_sc[...] = alpha * acc_sc[...] + jnp.dot(
            weights.astype(jnp.bfloat16), v_ref[0], preferred_element_type=f32
        )
        m_sc[...] = m_new

    @pl.when(block == pl.num_programs(1) - 1)
    def _():
        o_ref[0] = acc_sc[...] / l_sc[...]
        lse_ref[0] = m_sc[...] + jnp.log(l_sc[...])


def flash_forward(ctx_index, q, k, v, qseg, qpos, kseg, width):
    heads, rows, depth = q.shape
    blocks = k.shape[1] // width
    f32 = jnp.float32
    capped = lambda h, b, c: (h, jnp.minimum(b, c[0]), 0)
    grid_spec = pltpu.PrefetchScalarGridSpec(
        num_scalar_prefetch=1,
        grid=(heads, blocks),
        in_specs=[
            pl.BlockSpec((1, rows, depth), lambda h, b, c: (h, 0, 0)),
            pl.BlockSpec((1, width, depth), capped),
            pl.BlockSpec((1, width, depth), capped),
            pl.BlockSpec((rows, 1), lambda h, b, c: (0, 0)),
            pl.BlockSpec((rows, 1), lambda h, b, c: (0, 0)),
            pl.BlockSpec((1, width), lambda h, b, c: (0, jnp.minimum(b, c[0]))),
        ],
        out_specs=[
            pl.BlockSpec((1, rows, depth), lambda h, b, c: (h, 0, 0)),
            pl.BlockSpec((1, rows, 1), lambda h, b, c: (h, 0, 0)),
        ],
        scratch_shapes=[
            pltpu.VMEM((rows, 1), f32),
            pltpu.VMEM((rows, 1), f32),
            pltpu.VMEM((rows, depth), f32),
        ],
    )
    return pl.pallas_call(
        _flash_body,
        grid_spec=grid_spec,
        out_shape=[
            jax.ShapeDtypeStruct((heads, rows, depth), f32),
            jax.ShapeDtypeStruct((heads, rows, 1), f32),
        ],
        compiler_params=pltpu.CompilerParams(
            dimension_semantics=("arbitrary", "arbitrary"), vmem_limit_bytes=48 * 1024 * 1024
        ),
        cost_estimate=pl.CostEstimate(
            flops=heads * rows * k.shape[1] * depth * 4,
            transcendentals=heads * rows * k.shape[1],
            bytes_accessed=(q.size + k.size + v.size) * 2 + heads * rows * depth * 4,
        ),
    )(jnp.reshape(ctx_index, (1,)).astype(jnp.int32), q, k, v, qseg, qpos, kseg)


def per_device(
    dpx_count,
    hidden_in,
    attn_gain,
    q_weight,
    key_matrix,
    value_matrix,
    o_weight,
    moe_gain,
    router_weight,
    gate_weight,
    up_weight,
    down_weight,
    segments,
    expert_picks,
    output_grad,
):
    bf16 = jnp.bfloat16
    f32 = jnp.float32
    token_count = hidden_in.shape[0]
    ctx_index = lax.axis_index("ctx")
    heads_local = q_weight.shape[1] // HEAD_SIZE
    kv_local = key_matrix.shape[1] // HEAD_SIZE
    group_size = heads_local // kv_local
    score_scale = 1.0 / math.sqrt(HEAD_SIZE)
    token_positions = ctx_index * token_count + jnp.arange(token_count, dtype=jnp.int32)
    segment_here = lax.dynamic_slice_in_dim(segments, ctx_index * token_count, token_count)
    inputs_f32 = hidden_in.astype(f32)
    o_full = lax.all_gather(o_weight, "tensor", axis=1, tiled=True)
    normed_f32, scale_one = normalize(inputs_f32, attn_gain)
    normed_one = normed_f32.astype(bf16)
    query_rows = jnp.dot(normed_one, q_weight, preferred_element_type=f32).reshape(
        token_count, heads_local, HEAD_SIZE
    )
    keys_raw = jnp.dot(normed_one, key_matrix, preferred_element_type=f32).reshape(
        token_count, kv_local, HEAD_SIZE
    )
    values_raw = jnp.dot(normed_one, value_matrix, preferred_element_type=f32)
    query_grouped = (
        apply_rotary(query_rows, token_positions, 1.0)
        .astype(bf16)
        .reshape(token_count, kv_local, group_size, HEAD_SIZE)
    )
    key_flat = (
        apply_rotary(keys_raw, token_positions, 1.0)
        .astype(bf16)
        .reshape(token_count, kv_local * HEAD_SIZE)
    )
    value_flat = values_raw.astype(bf16)

    def piece_mask(piece_rows):
        key_pos = jnp.arange(piece_rows, dtype=jnp.int32)
        return (segment_here[:, None] == segments[None, :]) & (
            key_pos[None, :] <= token_positions[:, None]
        )

    ctx_count = segments.shape[0] // token_count
    kv_both = gather_axis(jnp.concatenate([key_flat, value_flat], axis=1), "ctx", ctx_count, 1)
    piece_rows = ctx_count * token_count
    kv_width = kv_local * HEAD_SIZE
    key_piece = kv_both[:, :, :kv_width].reshape(piece_rows, kv_local, HEAD_SIZE)
    value_piece = kv_both[:, :, kv_width:].reshape(piece_rows, kv_local, HEAD_SIZE)
    row_segments = jnp.tile(segment_here, group_size)[:, None]
    row_positions = jnp.tile(token_positions, group_size)[:, None]
    attn_rows, lse_rows = flash_forward(
        ctx_index,
        jnp.transpose(query_grouped, (1, 2, 0, 3)).reshape(kv_local, group_size * token_count, HEAD_SIZE),
        jnp.transpose(key_piece, (1, 0, 2)),
        jnp.transpose(value_piece, (1, 0, 2)),
        row_segments,
        row_positions,
        segments[None, :],
        token_count,
    )
    attn_grouped = attn_rows.reshape(kv_local, group_size, token_count, HEAD_SIZE)
    log_sum = lse_rows.reshape(kv_local, group_size, token_count)
    attn_bf = (
        jnp.transpose(attn_grouped, (2, 0, 1, 3))
        .reshape(token_count, heads_local * HEAD_SIZE)
        .astype(bf16)
    )
    tensor_count = o_weight.shape[0] // o_weight.shape[1]
    attn_all = gather_axis(attn_bf, "tensor", tensor_count, 2)
    attn_full = jnp.transpose(attn_all, (1, 0, 2)).reshape(token_count, tensor_count * attn_bf.shape[1])
    mixed_attn = contract_cols(attn_full, o_full)
    resid = inputs_f32 + mixed_attn
    normed_two_f32, scale_two = normalize(resid, moe_gain)
    normed_two = normed_two_f32.astype(bf16)
    logits = jnp.dot(normed_two, router_weight, preferred_element_type=f32)
    expert_range = jnp.arange(NEXP, dtype=jnp.int32)
    picked_onehot = expert_picks[:, :, None] == expert_range[None, None, :]
    picked = jnp.sum(jnp.where(picked_onehot, logits[:, None, :], 0.0), axis=2)
    gate_probs = jax.nn.softmax(picked, axis=-1)
    gates_dense = jnp.sum(jnp.where(picked_onehot, gate_probs[:, :, None], 0.0), axis=1)
    gates_by_expert = jnp.transpose(gates_dense)
    cot_bf = output_grad
    gcol = gates_by_expert[:, :, None]
    grad_gate, grad_up, grad_down, hid_all, dga_all, dua_all = expert_grad_kernel(
        normed_two,
        jnp.transpose(normed_two),
        cot_bf,
        jnp.transpose(cot_bf),
        gcol,
        gates_by_expert[:, None, :],
        gate_weight,
        up_weight,
        down_weight,
        dpx_count,
    )
    gate_half = core_reduce(grad_gate, 8)
    gate_half, hid_all, dga_all, dua_all = lax.optimization_barrier(
        (gate_half, hid_all, dga_all, dua_all)
    )
    moe_acc, gate_parts, moe_grad_rows = expert_rows_kernel(
        hid_all, dga_all, dua_all, cot_bf, gcol, gate_weight, up_weight, down_weight
    )
    cot_f32 = output_grad.astype(f32)
    moe_total = sum_axis(moe_acc.astype(bf16), "tensor", 3)
    output = (resid + moe_total).astype(bf16)
    grad_rows_all = moe_grad_rows
    gate_parts = gate_parts[:, :, 0]
    grad_gate_out, grad_up_out, grad_down_out = [
        lax.psum_scatter(
            g.reshape(g.shape[0], -1, g.shape[3]), ("dpx", "ctx"), scatter_dimension=1, tiled=True
        ).astype(jnp.float32)
        for g in (gate_half, core_reduce(grad_up, 9), core_reduce(grad_down, 10))
    ]
    gate_pair = jnp.sum(
        jnp.where(picked_onehot, jnp.transpose(gate_parts)[:, None, :], 0.0), axis=2
    )
    moe_summed = sum_axis(grad_rows_all.astype(bf16), "tensor", 4)
    gate_summed = sum_axis(gate_pair.astype(bf16), "tensor", 5)
    grad_picked = gate_probs * (
        gate_summed - jnp.sum(gate_probs * gate_summed, axis=1, keepdims=True)
    )
    grad_logits = jnp.sum(jnp.where(picked_onehot, grad_picked[:, :, None], 0.0), axis=1).astype(
        bf16
    )
    grad_router = contract_rows(normed_two, grad_logits)
    grad_normed_two = moe_summed + contract_cols(grad_logits, router_weight)
    grad_two_rows, grad_moe_gain = norm_backward(resid, scale_two, moe_gain, grad_normed_two)
    grad_resid = cot_f32 + grad_two_rows
    grad_mix = grad_resid.astype(bf16)
    grad_o = contract_rows(grad_mix, attn_bf)
    grad_attn = jnp.dot(grad_mix, o_weight, preferred_element_type=f32).astype(bf16)
    grad_attn_grouped = jnp.transpose(
        grad_attn.reshape(token_count, kv_local, group_size, HEAD_SIZE), (1, 2, 0, 3)
    )
    row_delta = jnp.sum(grad_attn_grouped.astype(f32) * attn_grouped, axis=-1)
    allowed = piece_mask(piece_rows)
    scores = (
        jnp.einsum("tkgd,nkd->kgtn", query_grouped, key_piece, preferred_element_type=f32)
        * score_scale
    )
    probability = jnp.where(allowed, jnp.exp(scores - log_sum[..., None]), 0.0)
    grad_probs = jnp.einsum(
        "kgtd,nkd->kgtn", grad_attn_grouped, value_piece, preferred_element_type=f32
    )
    grad_scores = (probability * (grad_probs - row_delta[..., None])).astype(bf16)
    grad_query = score_scale * jnp.einsum(
        "kgtn,nkd->kgtd", grad_scores, key_piece, preferred_element_type=f32
    )
    key_part = score_scale * jnp.einsum(
        "kgtn,tkgd->nkd", grad_scores, query_grouped, preferred_element_type=f32
    )
    value_part = jnp.einsum(
        "kgtn,kgtd->nkd", probability.astype(bf16), grad_attn_grouped, preferred_element_type=f32
    )
    grad_keys_all = key_part.reshape(piece_rows, kv_local * HEAD_SIZE)
    grad_values_all = value_part.reshape(piece_rows, kv_local * HEAD_SIZE)
    back_state = (grad_query, grad_keys_all, grad_values_all)
    grad_query, grad_keys_all, grad_values_all = back_state
    grad_kv_here = scatter_sum_axis(
        jnp.concatenate([grad_keys_all, grad_values_all], axis=1)
        .astype(bf16)
        .reshape(ctx_count, token_count, 2 * kv_width),
        "ctx",
        ctx_count,
        6,
    )
    grad_keys_here = grad_kv_here[:, :kv_width]
    grad_values_here = grad_kv_here[:, kv_width:]
    grad_query_rows = jnp.transpose(grad_query, (2, 0, 1, 3)).reshape(
        token_count, heads_local, HEAD_SIZE
    )
    grad_query_bf = (
        apply_rotary(grad_query_rows, token_positions, -1.0)
        .reshape(token_count, heads_local * HEAD_SIZE)
        .astype(bf16)
    )
    grad_key_bf = (
        apply_rotary(
            grad_keys_here.reshape(token_count, kv_local, HEAD_SIZE), token_positions, -1.0
        )
        .reshape(token_count, kv_local * HEAD_SIZE)
        .astype(bf16)
    )
    grad_value_bf = grad_values_here.astype(bf16)
    grad_q = contract_rows(normed_one, grad_query_bf)
    grad_k = contract_rows(normed_one, grad_key_bf)
    grad_v = contract_rows(normed_one, grad_value_bf)
    partial_one = (
        contract_cols(grad_query_bf, q_weight)
        + contract_cols(grad_key_bf, key_matrix)
        + contract_cols(grad_value_bf, value_matrix)
    )
    grad_normed_one = sum_axis(partial_one.astype(bf16), "tensor", 7)
    grad_one_rows, grad_attn_gain = norm_backward(inputs_f32, scale_one, attn_gain, grad_normed_one)
    input_grad = grad_resid + grad_one_rows
    q_cols, o_cols, k_cols = grad_q.shape[1], grad_o.shape[1], grad_k.shape[1]
    small = jnp.concatenate(
        [
            grad_router,
            grad_attn_gain[:, None],
            grad_moe_gain[:, None],
            jnp.zeros((grad_router.shape[0], 128 - grad_router.shape[1] - 2), f32),
        ],
        axis=1,
    )
    dense_all = jnp.concatenate(
        [grad_q, grad_o, grad_k, grad_v, small], axis=1
    ).astype(bf16)
    width = dense_all.shape[0]
    dense_all = jnp.transpose(
        dense_all.reshape(dpx_count, 2, width // (2 * dpx_count), dense_all.shape[1]), (1, 0, 2, 3)
    )
    dense_all, grad_gate_out, grad_up_out, grad_down_out = lax.optimization_barrier(
        (dense_all, grad_gate_out, grad_up_out, grad_down_out)
    )
    dense_half = core_reduce(dense_all, 11)
    dense_here = lax.psum_scatter(
        dense_half.reshape(-1, dense_half.shape[-1]), ("dpx", "ctx"), scatter_dimension=0, tiled=True
    ).astype(f32)
    spans = [q_cols, o_cols, k_cols, k_cols, router_weight.shape[1], 1, 1]
    cuts = [sum(spans[:i]) for i in range(len(spans) + 1)]
    pieces_out = [dense_here[:, cuts[i] : cuts[i + 1]] for i in range(len(spans))]
    dense_out = (
        pieces_out[5][:, 0],
        pieces_out[0],
        pieces_out[2],
        pieces_out[3],
        pieces_out[1],
        pieces_out[6][:, 0],
        pieces_out[4],
    )
    return (
        output,
        input_grad,
        dense_out[0],
        dense_out[1],
        dense_out[2],
        dense_out[3],
        dense_out[4],
        dense_out[5],
        dense_out[6],
        grad_gate_out,
        grad_up_out,
        grad_down_out,
    )


def solution(mesh):
    dp_count, ctx_count, tensor_count = (mesh.shape[a] for a in ("dp", "ctx", "tensor"))
    split_mesh = jax.sharding.Mesh(
        mesh.devices.reshape(dp_count // 2, 2, ctx_count, tensor_count), ("dpx", "core", "ctx", "tensor")
    )
    return jax.shard_map(
        functools.partial(per_device, dp_count // 2),
        mesh=split_mesh,
        in_specs=(
            P(("dpx", "core", "ctx"), None),
            P(),
            P(None, "tensor"),
            P(None, "tensor"),
            P(None, "tensor"),
            P(None, "tensor"),
            P(),
            P(),
            P(None, None, "tensor"),
            P(None, None, "tensor"),
            P(None, None, "tensor"),
            P(("dpx", "core")),
            P(("dpx", "core", "ctx"), None),
            P(("dpx", "core", "ctx"), None),
        ),
        out_specs=(
            P(("dpx", "core", "ctx"), None),
            P(("dpx", "core", "ctx"), None),
            P(("dpx", "core", "ctx")),
            P(("dpx", "core", "ctx"), "tensor"),
            P(("dpx", "core", "ctx"), "tensor"),
            P(("dpx", "core", "ctx"), "tensor"),
            P(("dpx", "core", "ctx"), "tensor"),
            P(("dpx", "core", "ctx")),
            P(("dpx", "core", "ctx"), None),
            P(None, ("dpx", "core", "ctx"), "tensor"),
            P(None, ("dpx", "core", "ctx"), "tensor"),
            P(None, ("dpx", "core", "ctx"), "tensor"),
        ),
        check_vma=False,
    )
```

```python
import functools
import math

import jax
import jax.numpy as jnp
from jax import lax
from jax.experimental import pallas as pl
from jax.experimental.pallas import tpu as pltpu
from jax.sharding import PartitionSpec as P

HEAD_SIZE = 64
NEXP = 24
CAP = 341


EPSILON = 1e-06
ROPE_BASE = 10000.0
NEGATIVE = -1e30
HIGHEST = lax.Precision.HIGHEST


def normalize(rows, gain):
    scale_inv = lax.rsqrt(jnp.mean(rows * rows, axis=-1, keepdims=True) + EPSILON)
    return (rows * scale_inv * gain, scale_inv)


def norm_backward(rows, scale_inv, gain, grad_normed):
    weighted = gain * grad_normed
    grad_gain = jnp.sum(grad_normed * rows * scale_inv, axis=0)
    inner_mean = jnp.mean(weighted * rows, axis=-1, keepdims=True)
    grad_rows = scale_inv * weighted - rows * scale_inv * scale_inv * scale_inv * inner_mean
    return (grad_rows, grad_gain)


def apply_rotary(value_rows, token_positions, direction):
    half_dim = value_rows.shape[-1] // 2
    frequency = ROPE_BASE ** (-jnp.arange(half_dim, dtype=jnp.float32) / half_dim)
    angles = token_positions.astype(jnp.float32)[:, None] * frequency[None, :]
    cosine = jnp.cos(angles)[:, None, :]
    sine_part = direction * jnp.sin(angles)[:, None, :]
    first_half = value_rows[..., :half_dim]
    second = value_rows[..., half_dim:]
    return jnp.concatenate(
        [first_half * cosine - second * sine_part, second * cosine + first_half * sine_part],
        axis=-1,
    )


def contract_rows(left, right):
    return lax.dot_general(
        left, right, (((0,), (0,)), ((), ())), preferred_element_type=jnp.float32
    )


def contract_rows_exact(left, right):
    return lax.dot_general(
        left, right, (((0,), (0,)), ((), ())), precision=HIGHEST, preferred_element_type=jnp.float32
    )


def contract_cols(left, right):
    return lax.dot_general(
        left, right, (((1,), (1,)), ((), ())), preferred_element_type=jnp.float32
    )


def _store_split(out_ref, value):
    cores, _, groups, rows, _ = out_ref.shape
    for x in range(groups):
        for c in range(cores):
            start = (x * cores + c) * rows
            out_ref[c, 0, x] = value[start : start + rows].astype(out_ref.dtype)


def _grad_body(
    n2_ref, n2t_ref, dy_ref, dyt_ref, gcol_ref, grow_ref, wg_ref, wu_ref, wd_ref,
    gg_ref, gu_ref, gd_ref, hid_ref, dga_ref, dua_ref,
):
    f32 = jnp.float32
    bf16 = jnp.bfloat16
    n2 = n2_ref[...]
    wd = wd_ref[0]
    gate_act = jnp.dot(n2, wg_ref[0], preferred_element_type=f32)
    up_act = jnp.dot(n2, wu_ref[0], preferred_element_type=f32)
    sig = 1.0 / (1.0 + jnp.exp(-gate_act))
    silu = gate_act * sig
    hidden = (silu * up_act).astype(bf16)
    hid_ref[0] = hidden
    deo = (gcol_ref[0] * dy_ref[...].astype(f32)).astype(bf16)
    grad_hidden = jnp.dot(deo, wd, preferred_element_type=f32)
    deo_t = (grow_ref[0] * dyt_ref[...].astype(f32)).astype(bf16)
    _store_split(gd_ref, jnp.dot(deo_t, hidden, preferred_element_type=f32))
    grad_gate_act = (grad_hidden * up_act * sig * (1.0 + gate_act * (1.0 - sig))).astype(bf16)
    grad_up_act = (grad_hidden * silu).astype(bf16)
    dga_ref[0] = grad_gate_act
    dua_ref[0] = grad_up_act
    n2t = n2t_ref[...]
    _store_split(gg_ref, jnp.dot(n2t, grad_gate_act, preferred_element_type=f32))
    _store_split(gu_ref, jnp.dot(n2t, grad_up_act, preferred_element_type=f32))


def _rows_body(hid_ref, dga_ref, dua_ref, dy_ref, gcol_ref, wg_ref, wu_ref, wd_ref, acc_ref, dgate_ref, dn2_ref):
    f32 = jnp.float32
    nt = (((1,), (1,)), ((), ()))

    @pl.when(pl.program_id(0) == 0)
    def _():
        acc_ref[...] = jnp.zeros_like(acc_ref)
        dn2_ref[...] = jnp.zeros_like(dn2_ref)

    expert_out = lax.dot_general(hid_ref[0], wd_ref[0], nt, preferred_element_type=f32)
    acc_ref[...] += gcol_ref[0] * expert_out
    dgate_ref[0] = jnp.sum(expert_out * dy_ref[...].astype(f32), axis=1, keepdims=True)
    dn2_ref[...] += lax.dot_general(
        dga_ref[0], wg_ref[0], nt, preferred_element_type=f32
    ) + lax.dot_general(dua_ref[0], wu_ref[0], nt, preferred_element_type=f32)


def expert_grad_kernel(n2, n2t, dy, dyt, gcol, grow, wg, wu, wd, groups):
    tokens, width = n2.shape
    experts, _, hidden = wg.shape
    bf16 = jnp.bfloat16
    whole = lambda shape: pl.BlockSpec(shape, lambda e: (0,) * len(shape))
    per_expert = lambda shape: pl.BlockSpec((1,) + shape, lambda e: (e,) + (0,) * len(shape))
    split_rows = width // (groups * 2)
    split = pl.BlockSpec((2, 1, groups, split_rows, hidden), lambda e: (0, e, 0, 0, 0))
    split_shape = jax.ShapeDtypeStruct((2, experts, groups, split_rows, hidden), bf16)
    act_shape = jax.ShapeDtypeStruct((experts, tokens, hidden), bf16)
    return pl.pallas_call(
        _grad_body,
        grid=(experts,),
        in_specs=[
            whole((tokens, width)),
            whole((width, tokens)),
            whole((tokens, width)),
            whole((width, tokens)),
            per_expert((tokens, 1)),
            per_expert((1, tokens)),
            per_expert((width, hidden)),
            per_expert((width, hidden)),
            per_expert((width, hidden)),
        ],
        out_specs=[split, split, split]
        + [per_expert((tokens, hidden))] * 3,
        out_shape=[split_shape] * 3 + [act_shape] * 3,
        compiler_params=pltpu.CompilerParams(
            dimension_semantics=("arbitrary",), vmem_limit_bytes=64 * 1024 * 1024
        ),
        cost_estimate=pl.CostEstimate(
            flops=experts * tokens * width * hidden * 2 * 6,
            transcendentals=experts * tokens * hidden,
            bytes_accessed=experts * width * hidden * 12 + tokens * width * 8 + experts * tokens * hidden * 6,
        ),
    )(n2, n2t, dy, dyt, gcol, grow, wg, wu, wd)


def expert_rows_kernel(hid, dga, dua, dy, gcol, wg, wu, wd):
    experts, tokens, hidden = hid.shape
    width = dy.shape[1]
    f32 = jnp.float32
    whole = lambda shape: pl.BlockSpec(shape, lambda e: (0,) * len(shape))
    per_expert = lambda shape: pl.BlockSpec((1,) + shape, lambda e: (e,) + (0,) * len(shape))
    return pl.pallas_call(
        _rows_body,
        grid=(experts,),
        in_specs=[
            per_expert((tokens, hidden)),
            per_expert((tokens, hidden)),
            per_expert((tokens, hidden)),
            whole((tokens, width)),
            per_expert((tokens, 1)),
            per_expert((width, hidden)),
            per_expert((width, hidden)),
            per_expert((width, hidden)),
        ],
        out_specs=[whole((tokens, width)), per_expert((tokens, 1)), whole((tokens, width))],
        out_shape=[
            jax.ShapeDtypeStruct((tokens, width), f32),
            jax.ShapeDtypeStruct((experts, tokens, 1), f32),
            jax.ShapeDtypeStruct((tokens, width), f32),
        ],
        compiler_params=pltpu.CompilerParams(
            dimension_semantics=("arbitrary",), vmem_limit_bytes=64 * 1024 * 1024
        ),
        cost_estimate=pl.CostEstimate(
            flops=experts * tokens * width * hidden * 2 * 3,
            transcendentals=0,
            bytes_accessed=experts * width * hidden * 6 + tokens * width * 10 + experts * tokens * hidden * 6,
        ),
    )(hid, dga, dua, dy, gcol, wg, wu, wd)

MESH = pl.DeviceIdType.MESH


def _exchange_body(axis, n, per_peer, downward, src_ref, out_ref, send_sems, recv_sems):
    me = lax.axis_index(axis)
    barrier = pltpu.get_barrier_semaphore()
    for k in range(1, n):
        peer = lax.rem(me + k, n)
        pl.semaphore_signal(barrier, 1, device_id={axis: peer}, device_id_type=MESH)
    pl.semaphore_wait(barrier, n - 1)
    sends = []
    for k in range(1, n):
        peer = lax.rem(me + k, n)
        copy = pltpu.make_async_remote_copy(
            src_ref=src_ref.at[peer] if per_peer else src_ref,
            dst_ref=out_ref.at[me],
            send_sem=send_sems.at[k - 1],
            recv_sem=recv_sems.at[k - 1],
            device_id={axis: peer},
            device_id_type=MESH,
        )
        sends.append((peer, copy))
        if downward:
            pl.when(peer < me)(copy.start)
        else:
            copy.start()
    for k in range(1, n):
        source = lax.rem(me + n - k, n)
        incoming = pltpu.make_async_remote_copy(
            src_ref=src_ref.at[source] if per_peer else src_ref,
            dst_ref=out_ref.at[source],
            send_sem=send_sems.at[k - 1],
            recv_sem=recv_sems.at[k - 1],
            device_id={axis: source},
            device_id_type=MESH,
        )
        if downward:
            pl.when(source > me)(incoming.wait_recv)
        else:
            incoming.wait_recv()
    for peer, copy in sends:
        if downward:
            pl.when(peer < me)(copy.wait_send)
        else:
            copy.wait_send()


def exchange(x, axis, n, per_peer, collective_id, downward=False):
    block = x.shape[1:] if per_peer else x.shape
    nbytes = math.prod(block) * x.dtype.itemsize
    return pl.pallas_call(
        functools.partial(_exchange_body, axis, n, per_peer, downward),
        out_shape=jax.ShapeDtypeStruct((n,) + tuple(block), x.dtype),
        in_specs=[pl.BlockSpec(memory_space=pl.ANY)],
        out_specs=pl.BlockSpec(memory_space=pl.ANY),
        scratch_shapes=[pltpu.SemaphoreType.DMA((n - 1,)), pltpu.SemaphoreType.DMA((n - 1,))],
        compiler_params=pltpu.CompilerParams(collective_id=collective_id, has_side_effects=True),
        cost_estimate=pl.CostEstimate(flops=0, transcendentals=0, bytes_accessed=2 * (n - 1) * nbytes),
    )(x)


def gather_axis(x, axis, n, collective_id):
    got = exchange(x, axis, n, False, collective_id)
    return lax.dynamic_update_slice_in_dim(got, x[None], lax.axis_index(axis), 0)


def sum_axis(x, axis, collective_id):
    got = exchange(x, axis, 2, False, collective_id)
    me = lax.axis_index(axis)
    other = lax.dynamic_index_in_dim(got, 1 - me, 0, keepdims=False)
    return x.astype(jnp.float32) + other.astype(jnp.float32)


def core_reduce(x, collective_id):
    got = exchange(x, "core", 2, True, collective_id)
    me = lax.axis_index("core")
    own = lax.dynamic_index_in_dim(x, me, 0, keepdims=False)
    other = lax.dynamic_index_in_dim(got, 1 - me, 0, keepdims=False)
    return (own.astype(jnp.float32) + other.astype(jnp.float32)).astype(jnp.bfloat16)


def scatter_sum_downward(x, axis, n, collective_id):
    got = exchange(x, axis, n, True, collective_id, downward=True)
    me = lax.axis_index(axis)
    own = lax.dynamic_index_in_dim(x, me, 0, keepdims=False).astype(jnp.float32)
    above = (jnp.arange(n, dtype=jnp.int32) > me).reshape((n,) + (1,) * (x.ndim - 1))
    return own + jnp.sum(jnp.where(above, got.astype(jnp.float32), 0.0), axis=0)


def _flash_body(ctx_ref, q_ref, k_ref, v_ref, qseg_ref, qpos_ref, kseg_ref, o_ref, lse_ref, m_sc, l_sc, acc_sc):
    f32 = jnp.float32
    block = pl.program_id(1)

    @pl.when(block == 0)
    def _():
        m_sc[...] = jnp.full_like(m_sc, NEGATIVE)
        l_sc[...] = jnp.zeros_like(l_sc)
        acc_sc[...] = jnp.zeros_like(acc_sc)

    @pl.when(block <= ctx_ref[0])
    def _():
        keys = k_ref[0]
        width = keys.shape[0]
        scores = lax.dot_general(
            q_ref[0], keys, (((1,), (1,)), ((), ())), preferred_element_type=f32
        ) * (1.0 / math.sqrt(HEAD_SIZE))
        key_pos = block * width + lax.broadcasted_iota(jnp.int32, (1, width), 1)
        allowed = (qseg_ref[...] == kseg_ref[...]) & (key_pos <= qpos_ref[...])
        scores = jnp.where(allowed, scores, NEGATIVE)
        m_old = m_sc[...]
        m_new = jnp.maximum(m_old, jnp.max(scores, axis=1, keepdims=True))
        alpha = jnp.exp(m_old - m_new)
        weights = jnp.where(allowed, jnp.exp(scores - m_new), 0.0)
        l_sc[...] = alpha * l_sc[...] + jnp.sum(weights, axis=1, keepdims=True)
        acc_sc[...] = alpha * acc_sc[...] + jnp.dot(
            weights.astype(jnp.bfloat16), v_ref[0], preferred_element_type=f32
        )
        m_sc[...] = m_new

    @pl.when(block == pl.num_programs(1) - 1)
    def _():
        o_ref[0] = acc_sc[...] / l_sc[...]
        lse_ref[0] = m_sc[...] + jnp.log(l_sc[...])


def flash_forward(ctx_index, q, k, v, qseg, qpos, kseg, width):
    heads, rows, depth = q.shape
    blocks = k.shape[1] // width
    f32 = jnp.float32
    capped = lambda h, b, c: (h, jnp.minimum(b, c[0]), 0)
    grid_spec = pltpu.PrefetchScalarGridSpec(
        num_scalar_prefetch=1,
        grid=(heads, blocks),
        in_specs=[
            pl.BlockSpec((1, rows, depth), lambda h, b, c: (h, 0, 0)),
            pl.BlockSpec((1, width, depth), capped),
            pl.BlockSpec((1, width, depth), capped),
            pl.BlockSpec((rows, 1), lambda h, b, c: (0, 0)),
            pl.BlockSpec((rows, 1), lambda h, b, c: (0, 0)),
            pl.BlockSpec((1, width), lambda h, b, c: (0, jnp.minimum(b, c[0]))),
        ],
        out_specs=[
            pl.BlockSpec((1, rows, depth), lambda h, b, c: (h, 0, 0)),
            pl.BlockSpec((1, rows, 1), lambda h, b, c: (h, 0, 0)),
        ],
        scratch_shapes=[
            pltpu.VMEM((rows, 1), f32),
            pltpu.VMEM((rows, 1), f32),
            pltpu.VMEM((rows, depth), f32),
        ],
    )
    return pl.pallas_call(
        _flash_body,
        grid_spec=grid_spec,
        out_shape=[
            jax.ShapeDtypeStruct((heads, rows, depth), f32),
            jax.ShapeDtypeStruct((heads, rows, 1), f32),
        ],
        compiler_params=pltpu.CompilerParams(
            dimension_semantics=("arbitrary", "arbitrary"), vmem_limit_bytes=48 * 1024 * 1024
        ),
        cost_estimate=pl.CostEstimate(
            flops=heads * rows * k.shape[1] * depth * 4,
            transcendentals=heads * rows * k.shape[1],
            bytes_accessed=(q.size + k.size + v.size) * 2 + heads * rows * depth * 4,
        ),
    )(jnp.reshape(ctx_index, (1,)).astype(jnp.int32), q, k, v, qseg, qpos, kseg)


def per_device(
    dpx_count,
    hidden_in,
    attn_gain,
    q_weight,
    key_matrix,
    value_matrix,
    o_weight,
    moe_gain,
    router_weight,
    gate_weight,
    up_weight,
    down_weight,
    segments,
    expert_picks,
    output_grad,
):
    bf16 = jnp.bfloat16
    f32 = jnp.float32
    token_count = hidden_in.shape[0]
    ctx_index = lax.axis_index("ctx")
    heads_local = q_weight.shape[1] // HEAD_SIZE
    kv_local = key_matrix.shape[1] // HEAD_SIZE
    group_size = heads_local // kv_local
    score_scale = 1.0 / math.sqrt(HEAD_SIZE)
    token_positions = ctx_index * token_count + jnp.arange(token_count, dtype=jnp.int32)
    segment_here = lax.dynamic_slice_in_dim(segments, ctx_index * token_count, token_count)
    inputs_f32 = hidden_in.astype(f32)
    o_full = lax.all_gather(o_weight, "tensor", axis=1, tiled=True)
    normed_f32, scale_one = normalize(inputs_f32, attn_gain)
    normed_one = normed_f32.astype(bf16)
    query_rows = jnp.dot(normed_one, q_weight, preferred_element_type=f32).reshape(
        token_count, heads_local, HEAD_SIZE
    )
    keys_raw = jnp.dot(normed_one, key_matrix, preferred_element_type=f32).reshape(
        token_count, kv_local, HEAD_SIZE
    )
    values_raw = jnp.dot(normed_one, value_matrix, preferred_element_type=f32)
    query_grouped = (
        apply_rotary(query_rows, token_positions, 1.0)
        .astype(bf16)
        .reshape(token_count, kv_local, group_size, HEAD_SIZE)
    )
    key_flat = (
        apply_rotary(keys_raw, token_positions, 1.0)
        .astype(bf16)
        .reshape(token_count, kv_local * HEAD_SIZE)
    )
    value_flat = values_raw.astype(bf16)

    def piece_mask(piece_rows):
        key_pos = jnp.arange(piece_rows, dtype=jnp.int32)
        return (segment_here[:, None] == segments[None, :]) & (
            key_pos[None, :] <= token_positions[:, None]
        )

    ctx_count = segments.shape[0] // token_count
    kv_both = gather_axis(jnp.concatenate([key_flat, value_flat], axis=1), "ctx", ctx_count, 1)
    piece_rows = ctx_count * token_count
    kv_width = kv_local * HEAD_SIZE
    key_piece = kv_both[:, :, :kv_width].reshape(piece_rows, kv_local, HEAD_SIZE)
    value_piece = kv_both[:, :, kv_width:].reshape(piece_rows, kv_local, HEAD_SIZE)
    row_segments = jnp.tile(segment_here, group_size)[:, None]
    row_positions = jnp.tile(token_positions, group_size)[:, None]
    attn_rows, lse_rows = flash_forward(
        ctx_index,
        jnp.transpose(query_grouped, (1, 2, 0, 3)).reshape(kv_local, group_size * token_count, HEAD_SIZE),
        jnp.transpose(key_piece, (1, 0, 2)),
        jnp.transpose(value_piece, (1, 0, 2)),
        row_segments,
        row_positions,
        segments[None, :],
        token_count,
    )
    attn_grouped = attn_rows.reshape(kv_local, group_size, token_count, HEAD_SIZE)
    log_sum = lse_rows.reshape(kv_local, group_size, token_count)
    attn_bf = (
        jnp.transpose(attn_grouped, (2, 0, 1, 3))
        .reshape(token_count, heads_local * HEAD_SIZE)
        .astype(bf16)
    )
    tensor_count = o_weight.shape[0] // o_weight.shape[1]
    attn_all = gather_axis(attn_bf, "tensor", tensor_count, 2)
    attn_full = jnp.transpose(attn_all, (1, 0, 2)).reshape(token_count, tensor_count * attn_bf.shape[1])
    mixed_attn = contract_cols(attn_full, o_full)
    resid = inputs_f32 + mixed_attn
    normed_two_f32, scale_two = normalize(resid, moe_gain)
    normed_two = normed_two_f32.astype(bf16)
    logits = jnp.dot(normed_two, router_weight, preferred_element_type=f32)
    expert_range = jnp.arange(NEXP, dtype=jnp.int32)
    picked_onehot = expert_picks[:, :, None] == expert_range[None, None, :]
    picked = jnp.sum(jnp.where(picked_onehot, logits[:, None, :], 0.0), axis=2)
    gate_probs = jax.nn.softmax(picked, axis=-1)
    gates_dense = jnp.sum(jnp.where(picked_onehot, gate_probs[:, :, None], 0.0), axis=1)
    gates_by_expert = jnp.transpose(gates_dense)
    cot_bf = output_grad
    gcol = gates_by_expert[:, :, None]
    grad_gate, grad_up, grad_down, hid_all, dga_all, dua_all = expert_grad_kernel(
        normed_two,
        jnp.transpose(normed_two),
        cot_bf,
        jnp.transpose(cot_bf),
        gcol,
        gates_by_expert[:, None, :],
        gate_weight,
        up_weight,
        down_weight,
        dpx_count,
    )
    gate_half = core_reduce(grad_gate, 8)
    gate_half, hid_all, dga_all, dua_all = lax.optimization_barrier(
        (gate_half, hid_all, dga_all, dua_all)
    )
    moe_acc, gate_parts, moe_grad_rows = expert_rows_kernel(
        hid_all, dga_all, dua_all, cot_bf, gcol, gate_weight, up_weight, down_weight
    )
    cot_f32 = output_grad.astype(f32)
    moe_total = sum_axis(moe_acc.astype(bf16), "tensor", 3)
    output = (resid + moe_total).astype(bf16)
    grad_rows_all = moe_grad_rows
    gate_parts = gate_parts[:, :, 0]
    grad_gate_out, grad_up_out, grad_down_out = [
        lax.psum_scatter(
            g.reshape(g.shape[0], -1, g.shape[3]), ("dpx", "ctx"), scatter_dimension=1, tiled=True
        ).astype(jnp.float32)
        for g in (gate_half, core_reduce(grad_up, 9), core_reduce(grad_down, 10))
    ]
    gate_pair = jnp.sum(
        jnp.where(picked_onehot, jnp.transpose(gate_parts)[:, None, :], 0.0), axis=2
    )
    moe_summed = sum_axis(grad_rows_all.astype(bf16), "tensor", 4)
    gate_summed = sum_axis(gate_pair.astype(bf16), "tensor", 5)
    grad_picked = gate_probs * (
        gate_summed - jnp.sum(gate_probs * gate_summed, axis=1, keepdims=True)
    )
    grad_logits = jnp.sum(jnp.where(picked_onehot, grad_picked[:, :, None], 0.0), axis=1).astype(
        bf16
    )
    grad_router = contract_rows(normed_two, grad_logits)
    grad_normed_two = moe_summed + contract_cols(grad_logits, router_weight)
    grad_two_rows, grad_moe_gain = norm_backward(resid, scale_two, moe_gain, grad_normed_two)
    grad_resid = cot_f32 + grad_two_rows
    grad_mix = grad_resid.astype(bf16)
    grad_o = contract_rows(grad_mix, attn_bf)
    grad_attn = jnp.dot(grad_mix, o_weight, preferred_element_type=f32).astype(bf16)
    grad_attn_grouped = jnp.transpose(
        grad_attn.reshape(token_count, kv_local, group_size, HEAD_SIZE), (1, 2, 0, 3)
    )
    row_delta = jnp.sum(grad_attn_grouped.astype(f32) * attn_grouped, axis=-1)
    allowed = piece_mask(piece_rows)
    scores = (
        jnp.einsum("tkgd,nkd->kgtn", query_grouped, key_piece, preferred_element_type=f32)
        * score_scale
    )
    probability = jnp.where(allowed, jnp.exp(scores - log_sum[..., None]), 0.0)
    grad_probs = jnp.einsum(
        "kgtd,nkd->kgtn", grad_attn_grouped, value_piece, preferred_element_type=f32
    )
    grad_scores = (probability * (grad_probs - row_delta[..., None])).astype(bf16)
    grad_query = score_scale * jnp.einsum(
        "kgtn,nkd->kgtd", grad_scores, key_piece, preferred_element_type=f32
    )
    key_part = score_scale * jnp.einsum(
        "kgtn,tkgd->nkd", grad_scores, query_grouped, preferred_element_type=f32
    )
    value_part = jnp.einsum(
        "kgtn,kgtd->nkd", probability.astype(bf16), grad_attn_grouped, preferred_element_type=f32
    )
    grad_keys_all = key_part.reshape(piece_rows, kv_local * HEAD_SIZE)
    grad_values_all = value_part.reshape(piece_rows, kv_local * HEAD_SIZE)
    back_state = (grad_query, grad_keys_all, grad_values_all)
    grad_query, grad_keys_all, grad_values_all = back_state
    grad_kv_here = scatter_sum_downward(
        jnp.concatenate([grad_keys_all, grad_values_all], axis=1)
        .astype(bf16)
        .reshape(ctx_count, token_count, 2 * kv_width),
        "ctx",
        ctx_count,
        6,
    )
    grad_keys_here = grad_kv_here[:, :kv_width]
    grad_values_here = grad_kv_here[:, kv_width:]
    grad_query_rows = jnp.transpose(grad_query, (2, 0, 1, 3)).reshape(
        token_count, heads_local, HEAD_SIZE
    )
    grad_query_bf = (
        apply_rotary(grad_query_rows, token_positions, -1.0)
        .reshape(token_count, heads_local * HEAD_SIZE)
        .astype(bf16)
    )
    grad_key_bf = (
        apply_rotary(
            grad_keys_here.reshape(token_count, kv_local, HEAD_SIZE), token_positions, -1.0
        )
        .reshape(token_count, kv_local * HEAD_SIZE)
        .astype(bf16)
    )
    grad_value_bf = grad_values_here.astype(bf16)
    grad_q = contract_rows(normed_one, grad_query_bf)
    grad_k = contract_rows(normed_one, grad_key_bf)
    grad_v = contract_rows(normed_one, grad_value_bf)
    partial_one = (
        contract_cols(grad_query_bf, q_weight)
        + contract_cols(grad_key_bf, key_matrix)
        + contract_cols(grad_value_bf, value_matrix)
    )
    grad_normed_one = sum_axis(partial_one.astype(bf16), "tensor", 7)
    grad_one_rows, grad_attn_gain = norm_backward(inputs_f32, scale_one, attn_gain, grad_normed_one)
    input_grad = grad_resid + grad_one_rows
    q_cols, o_cols, k_cols = grad_q.shape[1], grad_o.shape[1], grad_k.shape[1]
    small = jnp.concatenate(
        [
            grad_router,
            grad_attn_gain[:, None],
            grad_moe_gain[:, None],
            jnp.zeros((grad_router.shape[0], 128 - grad_router.shape[1] - 2), f32),
        ],
        axis=1,
    )
    dense_all = jnp.concatenate(
        [grad_q, grad_o, grad_k, grad_v, small], axis=1
    ).astype(bf16)
    width = dense_all.shape[0]
    dense_all = jnp.transpose(
        dense_all.reshape(dpx_count, 2, width // (2 * dpx_count), dense_all.shape[1]), (1, 0, 2, 3)
    )
    dense_all, grad_gate_out, grad_up_out, grad_down_out = lax.optimization_barrier(
        (dense_all, grad_gate_out, grad_up_out, grad_down_out)
    )
    dense_half = core_reduce(dense_all, 11)
    dense_here = lax.psum_scatter(
        dense_half.reshape(-1, dense_half.shape[-1]), ("dpx", "ctx"), scatter_dimension=0, tiled=True
    ).astype(f32)
    spans = [q_cols, o_cols, k_cols, k_cols, router_weight.shape[1], 1, 1]
    cuts = [sum(spans[:i]) for i in range(len(spans) + 1)]
    pieces_out = [dense_here[:, cuts[i] : cuts[i + 1]] for i in range(len(spans))]
    dense_out = (
        pieces_out[5][:, 0],
        pieces_out[0],
        pieces_out[2],
        pieces_out[3],
        pieces_out[1],
        pieces_out[6][:, 0],
        pieces_out[4],
    )
    return (
        output,
        input_grad,
        dense_out[0],
        dense_out[1],
        dense_out[2],
        dense_out[3],
        dense_out[4],
        dense_out[5],
        dense_out[6],
        grad_gate_out,
        grad_up_out,
        grad_down_out,
    )


def solution(mesh):
    dp_count, ctx_count, tensor_count = (mesh.shape[a] for a in ("dp", "ctx", "tensor"))
    split_mesh = jax.sharding.Mesh(
        mesh.devices.reshape(dp_count // 2, 2, ctx_count, tensor_count), ("dpx", "core", "ctx", "tensor")
    )
    return jax.shard_map(
        functools.partial(per_device, dp_count // 2),
        mesh=split_mesh,
        in_specs=(
            P(("dpx", "core", "ctx"), None),
            P(),
            P(None, "tensor"),
            P(None, "tensor"),
            P(None, "tensor"),
            P(None, "tensor"),
            P(),
            P(),
            P(None, None, "tensor"),
            P(None, None, "tensor"),
            P(None, None, "tensor"),
            P(("dpx", "core")),
            P(("dpx", "core", "ctx"), None),
            P(("dpx", "core", "ctx"), None),
        ),
        out_specs=(
            P(("dpx", "core", "ctx"), None),
            P(("dpx", "core", "ctx"), None),
            P(("dpx", "core", "ctx")),
            P(("dpx", "core", "ctx"), "tensor"),
            P(("dpx", "core", "ctx"), "tensor"),
            P(("dpx", "core", "ctx"), "tensor"),
            P(("dpx", "core", "ctx"), "tensor"),
            P(("dpx", "core", "ctx")),
            P(("dpx", "core", "ctx"), None),
            P(None, ("dpx", "core", "ctx"), "tensor"),
            P(None, ("dpx", "core", "ctx"), "tensor"),
            P(None, ("dpx", "core", "ctx"), "tensor"),
        ),
        check_vma=False,
    )
```

```python
import functools
import math

import jax
import jax.numpy as jnp
from jax import lax
from jax.experimental import pallas as pl
from jax.experimental.pallas import tpu as pltpu
from jax.sharding import PartitionSpec as P

HEAD_SIZE = 64
NEXP = 24
CAP = 341


EPSILON = 1e-06
ROPE_BASE = 10000.0
NEGATIVE = -1e30
HIGHEST = lax.Precision.HIGHEST


def normalize(rows, gain):
    scale_inv = lax.rsqrt(jnp.mean(rows * rows, axis=-1, keepdims=True) + EPSILON)
    return (rows * scale_inv * gain, scale_inv)


def norm_backward(rows, scale_inv, gain, grad_normed):
    weighted = gain * grad_normed
    grad_gain = jnp.sum(grad_normed * rows * scale_inv, axis=0)
    inner_mean = jnp.mean(weighted * rows, axis=-1, keepdims=True)
    grad_rows = scale_inv * weighted - rows * scale_inv * scale_inv * scale_inv * inner_mean
    return (grad_rows, grad_gain)


def apply_rotary(value_rows, token_positions, direction):
    half_dim = value_rows.shape[-1] // 2
    frequency = ROPE_BASE ** (-jnp.arange(half_dim, dtype=jnp.float32) / half_dim)
    angles = token_positions.astype(jnp.float32)[:, None] * frequency[None, :]
    cosine = jnp.cos(angles)[:, None, :]
    sine_part = direction * jnp.sin(angles)[:, None, :]
    first_half = value_rows[..., :half_dim]
    second = value_rows[..., half_dim:]
    return jnp.concatenate(
        [first_half * cosine - second * sine_part, second * cosine + first_half * sine_part],
        axis=-1,
    )


def contract_rows(left, right):
    return lax.dot_general(
        left, right, (((0,), (0,)), ((), ())), preferred_element_type=jnp.float32
    )


def contract_rows_exact(left, right):
    return lax.dot_general(
        left, right, (((0,), (0,)), ((), ())), precision=HIGHEST, preferred_element_type=jnp.float32
    )


def contract_cols(left, right):
    return lax.dot_general(
        left, right, (((1,), (1,)), ((), ())), preferred_element_type=jnp.float32
    )


def _store_split(out_ref, value):
    cores, _, groups, rows, _ = out_ref.shape
    for x in range(groups):
        for c in range(cores):
            start = (x * cores + c) * rows
            out_ref[c, 0, x] = value[start : start + rows].astype(out_ref.dtype)


def _gate_column(gates_ref):
    gates = gates_ref[...]
    lane = lax.broadcasted_iota(jnp.int32, gates.shape, 1)
    return jnp.sum(jnp.where(lane == pl.program_id(0), gates, 0.0), axis=1, keepdims=True)


def _grad_body(
    n2_ref, n2t_ref, dy_ref, dyt_ref, gcol_ref, grow_ref, wg_ref, wu_ref, wd_ref,
    gg_ref, gu_ref, gd_ref, hid_ref, dga_ref, dua_ref,
):
    f32 = jnp.float32
    bf16 = jnp.bfloat16
    n2 = n2_ref[...]
    wd = wd_ref[0]
    gate_act = jnp.dot(n2, wg_ref[0], preferred_element_type=f32)
    up_act = jnp.dot(n2, wu_ref[0], preferred_element_type=f32)
    sig = 1.0 / (1.0 + jnp.exp(-gate_act))
    silu = gate_act * sig
    hidden = (silu * up_act).astype(bf16)
    hid_ref[0] = hidden
    deo = (_gate_column(gcol_ref) * dy_ref[...].astype(f32)).astype(bf16)
    grad_hidden = jnp.dot(deo, wd, preferred_element_type=f32)
    deo_t = (grow_ref[0] * dyt_ref[...].astype(f32)).astype(bf16)
    _store_split(gd_ref, jnp.dot(deo_t, hidden, preferred_element_type=f32))
    grad_gate_act = (grad_hidden * up_act * sig * (1.0 + gate_act * (1.0 - sig))).astype(bf16)
    grad_up_act = (grad_hidden * silu).astype(bf16)
    dga_ref[0] = grad_gate_act
    dua_ref[0] = grad_up_act
    n2t = n2t_ref[...]
    _store_split(gg_ref, jnp.dot(n2t, grad_gate_act, preferred_element_type=f32))
    _store_split(gu_ref, jnp.dot(n2t, grad_up_act, preferred_element_type=f32))


def _rows_body(hid_ref, dga_ref, dua_ref, dy_ref, gcol_ref, wg_ref, wu_ref, wd_ref, acc_ref, dgate_ref, dn2_ref):
    f32 = jnp.float32
    nt = (((1,), (1,)), ((), ()))

    @pl.when(pl.program_id(0) == 0)
    def _():
        acc_ref[...] = jnp.zeros_like(acc_ref)
        dn2_ref[...] = jnp.zeros_like(dn2_ref)

    expert_out = lax.dot_general(hid_ref[0], wd_ref[0], nt, preferred_element_type=f32)
    acc_ref[...] += _gate_column(gcol_ref) * expert_out
    dgate_ref[0] = jnp.sum(expert_out * dy_ref[...].astype(f32), axis=1, keepdims=True)
    dn2_ref[...] += lax.dot_general(
        dga_ref[0], wg_ref[0], nt, preferred_element_type=f32
    ) + lax.dot_general(dua_ref[0], wu_ref[0], nt, preferred_element_type=f32)


def expert_grad_kernel(n2, n2t, dy, dyt, gcol, grow, wg, wu, wd, groups):
    tokens, width = n2.shape
    experts, _, hidden = wg.shape
    bf16 = jnp.bfloat16
    whole = lambda shape: pl.BlockSpec(shape, lambda e: (0,) * len(shape))
    per_expert = lambda shape: pl.BlockSpec((1,) + shape, lambda e: (e,) + (0,) * len(shape))
    split_rows = width // (groups * 2)
    split = pl.BlockSpec((2, 1, groups, split_rows, hidden), lambda e: (0, e, 0, 0, 0))
    split_shape = jax.ShapeDtypeStruct((2, experts, groups, split_rows, hidden), bf16)
    act_shape = jax.ShapeDtypeStruct((experts, tokens, hidden), bf16)
    return pl.pallas_call(
        _grad_body,
        grid=(experts,),
        in_specs=[
            whole((tokens, width)),
            whole((width, tokens)),
            whole((tokens, width)),
            whole((width, tokens)),
            whole((tokens, experts)),
            per_expert((1, tokens)),
            per_expert((width, hidden)),
            per_expert((width, hidden)),
            per_expert((width, hidden)),
        ],
        out_specs=[split, split, split]
        + [per_expert((tokens, hidden))] * 3,
        out_shape=[split_shape] * 3 + [act_shape] * 3,
        compiler_params=pltpu.CompilerParams(
            dimension_semantics=("arbitrary",), vmem_limit_bytes=64 * 1024 * 1024
        ),
        cost_estimate=pl.CostEstimate(
            flops=experts * tokens * width * hidden * 2 * 6,
            transcendentals=experts * tokens * hidden,
            bytes_accessed=experts * width * hidden * 12 + tokens * width * 8 + experts * tokens * hidden * 6,
        ),
    )(n2, n2t, dy, dyt, gcol, grow, wg, wu, wd)


def expert_rows_kernel(hid, dga, dua, dy, gcol, wg, wu, wd):
    experts, tokens, hidden = hid.shape
    width = dy.shape[1]
    f32 = jnp.float32
    whole = lambda shape: pl.BlockSpec(shape, lambda e: (0,) * len(shape))
    per_expert = lambda shape: pl.BlockSpec((1,) + shape, lambda e: (e,) + (0,) * len(shape))
    return pl.pallas_call(
        _rows_body,
        grid=(experts,),
        in_specs=[
            per_expert((tokens, hidden)),
            per_expert((tokens, hidden)),
            per_expert((tokens, hidden)),
            whole((tokens, width)),
            whole((tokens, experts)),
            per_expert((width, hidden)),
            per_expert((width, hidden)),
            per_expert((width, hidden)),
        ],
        out_specs=[whole((tokens, width)), per_expert((tokens, 1)), whole((tokens, width))],
        out_shape=[
            jax.ShapeDtypeStruct((tokens, width), f32),
            jax.ShapeDtypeStruct((experts, tokens, 1), f32),
            jax.ShapeDtypeStruct((tokens, width), f32),
        ],
        compiler_params=pltpu.CompilerParams(
            dimension_semantics=("arbitrary",), vmem_limit_bytes=64 * 1024 * 1024
        ),
        cost_estimate=pl.CostEstimate(
            flops=experts * tokens * width * hidden * 2 * 3,
            transcendentals=0,
            bytes_accessed=experts * width * hidden * 6 + tokens * width * 10 + experts * tokens * hidden * 6,
        ),
    )(hid, dga, dua, dy, gcol, wg, wu, wd)

MESH = pl.DeviceIdType.MESH


def _exchange_body(axis, n, per_peer, downward, src_ref, out_ref, send_sems, recv_sems):
    me = lax.axis_index(axis)
    barrier = pltpu.get_barrier_semaphore()
    for k in range(1, n):
        peer = lax.rem(me + k, n)
        pl.semaphore_signal(barrier, 1, device_id={axis: peer}, device_id_type=MESH)
    pl.semaphore_wait(barrier, n - 1)
    sends = []
    for k in range(1, n):
        peer = lax.rem(me + k, n)
        copy = pltpu.make_async_remote_copy(
            src_ref=src_ref.at[peer] if per_peer else src_ref,
            dst_ref=out_ref.at[me],
            send_sem=send_sems.at[k - 1],
            recv_sem=recv_sems.at[k - 1],
            device_id={axis: peer},
            device_id_type=MESH,
        )
        sends.append((peer, copy))
        if downward:
            pl.when(peer < me)(copy.start)
        else:
            copy.start()
    for k in range(1, n):
        source = lax.rem(me + n - k, n)
        incoming = pltpu.make_async_remote_copy(
            src_ref=src_ref.at[source] if per_peer else src_ref,
            dst_ref=out_ref.at[source],
            send_sem=send_sems.at[k - 1],
            recv_sem=recv_sems.at[k - 1],
            device_id={axis: source},
            device_id_type=MESH,
        )
        if downward:
            pl.when(source > me)(incoming.wait_recv)
        else:
            incoming.wait_recv()
    for peer, copy in sends:
        if downward:
            pl.when(peer < me)(copy.wait_send)
        else:
            copy.wait_send()


def exchange(x, axis, n, per_peer, collective_id, downward=False):
    block = x.shape[1:] if per_peer else x.shape
    nbytes = math.prod(block) * x.dtype.itemsize
    return pl.pallas_call(
        functools.partial(_exchange_body, axis, n, per_peer, downward),
        out_shape=jax.ShapeDtypeStruct((n,) + tuple(block), x.dtype),
        in_specs=[pl.BlockSpec(memory_space=pl.ANY)],
        out_specs=pl.BlockSpec(memory_space=pl.ANY),
        scratch_shapes=[pltpu.SemaphoreType.DMA((n - 1,)), pltpu.SemaphoreType.DMA((n - 1,))],
        compiler_params=pltpu.CompilerParams(collective_id=collective_id, has_side_effects=True),
        cost_estimate=pl.CostEstimate(flops=0, transcendentals=0, bytes_accessed=2 * (n - 1) * nbytes),
    )(x)


def gather_axis(x, axis, n, collective_id):
    got = exchange(x, axis, n, False, collective_id)
    return lax.dynamic_update_slice_in_dim(got, x[None], lax.axis_index(axis), 0)


def sum_axis(x, axis, collective_id):
    got = exchange(x, axis, 2, False, collective_id)
    me = lax.axis_index(axis)
    other = lax.dynamic_index_in_dim(got, 1 - me, 0, keepdims=False)
    return x.astype(jnp.float32) + other.astype(jnp.float32)


def _pair_add_body(me_ref, own_ref, other_ref, out_ref):
    out_ref[...] = (own_ref[...].astype(jnp.float32) + other_ref[...].astype(jnp.float32)).astype(out_ref.dtype)


def core_reduce(x, collective_id):
    got = exchange(x, "core", 2, True, collective_id)
    me = lax.axis_index("core")
    count = x.shape[1]
    rest = x.shape[2:]
    zeros = (0,) * len(rest)
    grid_spec = pltpu.PrefetchScalarGridSpec(
        num_scalar_prefetch=1,
        grid=(count,),
        in_specs=[
            pl.BlockSpec((None, None) + rest, lambda i, c: (c[0], i) + zeros),
            pl.BlockSpec((None, None) + rest, lambda i, c: (1 - c[0], i) + zeros),
        ],
        out_specs=pl.BlockSpec((None,) + rest, lambda i, c: (i,) + zeros),
    )
    return pl.pallas_call(
        _pair_add_body,
        grid_spec=grid_spec,
        out_shape=jax.ShapeDtypeStruct(x.shape[1:], jnp.bfloat16),
        cost_estimate=pl.CostEstimate(flops=x.size // 2, transcendentals=0, bytes_accessed=x.size * 3),
    )(jnp.reshape(me, (1,)).astype(jnp.int32), x, got)


def scatter_sum_downward(x, axis, n, collective_id):
    got = exchange(x, axis, n, True, collective_id, downward=True)
    me = lax.axis_index(axis)
    own = lax.dynamic_index_in_dim(x, me, 0, keepdims=False).astype(jnp.float32)
    above = (jnp.arange(n, dtype=jnp.int32) > me).reshape((n,) + (1,) * (x.ndim - 1))
    return own + jnp.sum(jnp.where(above, got.astype(jnp.float32), 0.0), axis=0)


def _flash_body(ctx_ref, q_ref, k_ref, v_ref, qseg_ref, qpos_ref, kseg_ref, o_ref, lse_ref, m_sc, l_sc, acc_sc):
    f32 = jnp.float32
    block = pl.program_id(1)

    @pl.when(block == 0)
    def _():
        m_sc[...] = jnp.full_like(m_sc, NEGATIVE)
        l_sc[...] = jnp.zeros_like(l_sc)
        acc_sc[...] = jnp.zeros_like(acc_sc)

    @pl.when(block <= ctx_ref[0])
    def _():
        keys = k_ref[0]
        width = keys.shape[0]
        scores = lax.dot_general(
            q_ref[0], keys, (((1,), (1,)), ((), ())), preferred_element_type=f32
        ) * (1.0 / math.sqrt(HEAD_SIZE))
        key_pos = block * width + lax.broadcasted_iota(jnp.int32, (1, width), 1)
        allowed = (qseg_ref[...] == kseg_ref[...]) & (key_pos <= qpos_ref[...])
        scores = jnp.where(allowed, scores, NEGATIVE)
        m_old = m_sc[...]
        m_new = jnp.maximum(m_old, jnp.max(scores, axis=1, keepdims=True))
        alpha = jnp.exp(m_old - m_new)
        weights = jnp.where(allowed, jnp.exp(scores - m_new), 0.0)
        l_sc[...] = alpha * l_sc[...] + jnp.sum(weights, axis=1, keepdims=True)
        acc_sc[...] = alpha * acc_sc[...] + jnp.dot(
            weights.astype(jnp.bfloat16), v_ref[0], preferred_element_type=f32
        )
        m_sc[...] = m_new

    @pl.when(block == pl.num_programs(1) - 1)
    def _():
        o_ref[0] = acc_sc[...] / l_sc[...]
        lse_ref[0] = m_sc[...] + jnp.log(l_sc[...])


def flash_forward(ctx_index, q, k, v, qseg, qpos, kseg, width):
    heads, rows, depth = q.shape
    blocks = k.shape[1] // width
    f32 = jnp.float32
    capped = lambda h, b, c: (h, jnp.minimum(b, c[0]), 0)
    grid_spec = pltpu.PrefetchScalarGridSpec(
        num_scalar_prefetch=1,
        grid=(heads, blocks),
        in_specs=[
            pl.BlockSpec((1, rows, depth), lambda h, b, c: (h, 0, 0)),
            pl.BlockSpec((1, width, depth), capped),
            pl.BlockSpec((1, width, depth), capped),
            pl.BlockSpec((rows, 1), lambda h, b, c: (0, 0)),
            pl.BlockSpec((rows, 1), lambda h, b, c: (0, 0)),
            pl.BlockSpec((1, width), lambda h, b, c: (0, jnp.minimum(b, c[0]))),
        ],
        out_specs=[
            pl.BlockSpec((1, rows, depth), lambda h, b, c: (h, 0, 0)),
            pl.BlockSpec((1, rows, 1), lambda h, b, c: (h, 0, 0)),
        ],
        scratch_shapes=[
            pltpu.VMEM((rows, 1), f32),
            pltpu.VMEM((rows, 1), f32),
            pltpu.VMEM((rows, depth), f32),
        ],
    )
    return pl.pallas_call(
        _flash_body,
        grid_spec=grid_spec,
        out_shape=[
            jax.ShapeDtypeStruct((heads, rows, depth), f32),
            jax.ShapeDtypeStruct((heads, rows, 1), f32),
        ],
        compiler_params=pltpu.CompilerParams(
            dimension_semantics=("arbitrary", "arbitrary"), vmem_limit_bytes=48 * 1024 * 1024
        ),
        cost_estimate=pl.CostEstimate(
            flops=heads * rows * k.shape[1] * depth * 4,
            transcendentals=heads * rows * k.shape[1],
            bytes_accessed=(q.size + k.size + v.size) * 2 + heads * rows * depth * 4,
        ),
    )(jnp.reshape(ctx_index, (1,)).astype(jnp.int32), q, k, v, qseg, qpos, kseg)


def per_device(
    dpx_count,
    hidden_in,
    attn_gain,
    q_weight,
    key_matrix,
    value_matrix,
    o_weight,
    moe_gain,
    router_weight,
    gate_weight,
    up_weight,
    down_weight,
    segments,
    expert_picks,
    output_grad,
):
    bf16 = jnp.bfloat16
    f32 = jnp.float32
    token_count = hidden_in.shape[0]
    ctx_index = lax.axis_index("ctx")
    heads_local = q_weight.shape[1] // HEAD_SIZE
    kv_local = key_matrix.shape[1] // HEAD_SIZE
    group_size = heads_local // kv_local
    score_scale = 1.0 / math.sqrt(HEAD_SIZE)
    token_positions = ctx_index * token_count + jnp.arange(token_count, dtype=jnp.int32)
    segment_here = lax.dynamic_slice_in_dim(segments, ctx_index * token_count, token_count)
    inputs_f32 = hidden_in.astype(f32)
    o_full = lax.all_gather(o_weight, "tensor", axis=1, tiled=True)
    normed_f32, scale_one = normalize(inputs_f32, attn_gain)
    normed_one = normed_f32.astype(bf16)
    query_rows = jnp.dot(normed_one, q_weight, preferred_element_type=f32).reshape(
        token_count, heads_local, HEAD_SIZE
    )
    keys_raw = jnp.dot(normed_one, key_matrix, preferred_element_type=f32).reshape(
        token_count, kv_local, HEAD_SIZE
    )
    values_raw = jnp.dot(normed_one, value_matrix, preferred_element_type=f32)
    query_grouped = (
        apply_rotary(query_rows, token_positions, 1.0)
        .astype(bf16)
        .reshape(token_count, kv_local, group_size, HEAD_SIZE)
    )
    key_flat = (
        apply_rotary(keys_raw, token_positions, 1.0)
        .astype(bf16)
        .reshape(token_count, kv_local * HEAD_SIZE)
    )
    value_flat = values_raw.astype(bf16)

    def piece_mask(piece_rows):
        key_pos = jnp.arange(piece_rows, dtype=jnp.int32)
        return (segment_here[:, None] == segments[None, :]) & (
            key_pos[None, :] <= token_positions[:, None]
        )

    ctx_count = segments.shape[0] // token_count
    kv_both = gather_axis(jnp.concatenate([key_flat, value_flat], axis=1), "ctx", ctx_count, 1)
    piece_rows = ctx_count * token_count
    kv_width = kv_local * HEAD_SIZE
    key_piece = kv_both[:, :, :kv_width].reshape(piece_rows, kv_local, HEAD_SIZE)
    value_piece = kv_both[:, :, kv_width:].reshape(piece_rows, kv_local, HEAD_SIZE)
    row_segments = jnp.tile(segment_here, group_size)[:, None]
    row_positions = jnp.tile(token_positions, group_size)[:, None]
    attn_rows, lse_rows = flash_forward(
        ctx_index,
        jnp.transpose(query_grouped, (1, 2, 0, 3)).reshape(kv_local, group_size * token_count, HEAD_SIZE),
        jnp.transpose(key_piece, (1, 0, 2)),
        jnp.transpose(value_piece, (1, 0, 2)),
        row_segments,
        row_positions,
        segments[None, :],
        token_count,
    )
    attn_grouped = attn_rows.reshape(kv_local, group_size, token_count, HEAD_SIZE)
    log_sum = lse_rows.reshape(kv_local, group_size, token_count)
    attn_bf = (
        jnp.transpose(attn_grouped, (2, 0, 1, 3))
        .reshape(token_count, heads_local * HEAD_SIZE)
        .astype(bf16)
    )
    tensor_count = o_weight.shape[0] // o_weight.shape[1]
    attn_all = gather_axis(attn_bf, "tensor", tensor_count, 2)
    attn_full = jnp.transpose(attn_all, (1, 0, 2)).reshape(token_count, tensor_count * attn_bf.shape[1])
    mixed_attn = contract_cols(attn_full, o_full)
    resid = inputs_f32 + mixed_attn
    normed_two_f32, scale_two = normalize(resid, moe_gain)
    normed_two = normed_two_f32.astype(bf16)
    logits = jnp.dot(normed_two, router_weight, preferred_element_type=f32)
    expert_range = jnp.arange(NEXP, dtype=jnp.int32)
    picked_onehot = expert_picks[:, :, None] == expert_range[None, None, :]
    picked = jnp.sum(jnp.where(picked_onehot, logits[:, None, :], 0.0), axis=2)
    gate_probs = jax.nn.softmax(picked, axis=-1)
    gates_dense = jnp.sum(jnp.where(picked_onehot, gate_probs[:, :, None], 0.0), axis=1)
    gates_by_expert = jnp.transpose(gates_dense)
    cot_bf = output_grad
    gcol = gates_dense
    grad_gate, grad_up, grad_down, hid_all, dga_all, dua_all = expert_grad_kernel(
        normed_two,
        jnp.transpose(normed_two),
        cot_bf,
        jnp.transpose(cot_bf),
        gcol,
        gates_by_expert[:, None, :],
        gate_weight,
        up_weight,
        down_weight,
        dpx_count,
    )
    gate_half = core_reduce(grad_gate, 8)
    gate_half, hid_all, dga_all, dua_all = lax.optimization_barrier(
        (gate_half, hid_all, dga_all, dua_all)
    )
    moe_acc, gate_parts, moe_grad_rows = expert_rows_kernel(
        hid_all, dga_all, dua_all, cot_bf, gcol, gate_weight, up_weight, down_weight
    )
    cot_f32 = output_grad.astype(f32)
    moe_total = sum_axis(moe_acc.astype(bf16), "tensor", 3)
    output = (resid + moe_total).astype(bf16)
    grad_rows_all = moe_grad_rows
    gate_parts = gate_parts[:, :, 0]
    grad_gate_out, grad_up_out, grad_down_out = [
        lax.psum_scatter(
            g.reshape(g.shape[0], -1, g.shape[3]), ("dpx", "ctx"), scatter_dimension=1, tiled=True
        ).astype(jnp.float32)
        for g in (gate_half, core_reduce(grad_up, 9), core_reduce(grad_down, 10))
    ]
    gate_pair = jnp.sum(
        jnp.where(picked_onehot, jnp.transpose(gate_parts)[:, None, :], 0.0), axis=2
    )
    moe_summed = sum_axis(grad_rows_all.astype(bf16), "tensor", 4)
    gate_summed = sum_axis(gate_pair.astype(bf16), "tensor", 5)
    grad_picked = gate_probs * (
        gate_summed - jnp.sum(gate_probs * gate_summed, axis=1, keepdims=True)
    )
    grad_logits = jnp.sum(jnp.where(picked_onehot, grad_picked[:, :, None], 0.0), axis=1).astype(
        bf16
    )
    grad_router = contract_rows(normed_two, grad_logits)
    grad_normed_two = moe_summed + contract_cols(grad_logits, router_weight)
    grad_two_rows, grad_moe_gain = norm_backward(resid, scale_two, moe_gain, grad_normed_two)
    grad_resid = cot_f32 + grad_two_rows
    grad_mix = grad_resid.astype(bf16)
    grad_o = contract_rows(grad_mix, attn_bf)
    grad_attn = jnp.dot(grad_mix, o_weight, preferred_element_type=f32).astype(bf16)
    grad_attn_grouped = jnp.transpose(
        grad_attn.reshape(token_count, kv_local, group_size, HEAD_SIZE), (1, 2, 0, 3)
    )
    row_delta = jnp.sum(grad_attn_grouped.astype(f32) * attn_grouped, axis=-1)
    allowed = piece_mask(piece_rows)
    scores = (
        jnp.einsum("tkgd,nkd->kgtn", query_grouped, key_piece, preferred_element_type=f32)
        * score_scale
    )
    probability = jnp.where(allowed, jnp.exp(scores - log_sum[..., None]), 0.0)
    grad_probs = jnp.einsum(
        "kgtd,nkd->kgtn", grad_attn_grouped, value_piece, preferred_element_type=f32
    )
    grad_scores = (probability * (grad_probs - row_delta[..., None])).astype(bf16)
    grad_query = score_scale * jnp.einsum(
        "kgtn,nkd->kgtd", grad_scores, key_piece, preferred_element_type=f32
    )
    key_part = score_scale * jnp.einsum(
        "kgtn,tkgd->nkd", grad_scores, query_grouped, preferred_element_type=f32
    )
    value_part = jnp.einsum(
        "kgtn,kgtd->nkd", probability.astype(bf16), grad_attn_grouped, preferred_element_type=f32
    )
    grad_keys_all = key_part.reshape(piece_rows, kv_local * HEAD_SIZE)
    grad_values_all = value_part.reshape(piece_rows, kv_local * HEAD_SIZE)
    back_state = (grad_query, grad_keys_all, grad_values_all)
    grad_query, grad_keys_all, grad_values_all = back_state
    grad_kv_here = scatter_sum_downward(
        jnp.concatenate([grad_keys_all, grad_values_all], axis=1)
        .astype(bf16)
        .reshape(ctx_count, token_count, 2 * kv_width),
        "ctx",
        ctx_count,
        6,
    )
    grad_keys_here = grad_kv_here[:, :kv_width]
    grad_values_here = grad_kv_here[:, kv_width:]
    grad_query_rows = jnp.transpose(grad_query, (2, 0, 1, 3)).reshape(
        token_count, heads_local, HEAD_SIZE
    )
    grad_query_bf = (
        apply_rotary(grad_query_rows, token_positions, -1.0)
        .reshape(token_count, heads_local * HEAD_SIZE)
        .astype(bf16)
    )
    grad_key_bf = (
        apply_rotary(
            grad_keys_here.reshape(token_count, kv_local, HEAD_SIZE), token_positions, -1.0
        )
        .reshape(token_count, kv_local * HEAD_SIZE)
        .astype(bf16)
    )
    grad_value_bf = grad_values_here.astype(bf16)
    grad_q = contract_rows(normed_one, grad_query_bf)
    grad_k = contract_rows(normed_one, grad_key_bf)
    grad_v = contract_rows(normed_one, grad_value_bf)
    partial_one = (
        contract_cols(grad_query_bf, q_weight)
        + contract_cols(grad_key_bf, key_matrix)
        + contract_cols(grad_value_bf, value_matrix)
    )
    grad_normed_one = sum_axis(partial_one.astype(bf16), "tensor", 7)
    grad_one_rows, grad_attn_gain = norm_backward(inputs_f32, scale_one, attn_gain, grad_normed_one)
    input_grad = grad_resid + grad_one_rows
    q_cols, o_cols, k_cols = grad_q.shape[1], grad_o.shape[1], grad_k.shape[1]
    small = jnp.concatenate(
        [
            grad_router,
            grad_attn_gain[:, None],
            grad_moe_gain[:, None],
            jnp.zeros((grad_router.shape[0], 128 - grad_router.shape[1] - 2), f32),
        ],
        axis=1,
    )
    dense_all = jnp.concatenate(
        [grad_q, grad_o, grad_k, grad_v, small], axis=1
    ).astype(bf16)
    width = dense_all.shape[0]
    dense_all = jnp.transpose(
        dense_all.reshape(dpx_count, 2, width // (2 * dpx_count), dense_all.shape[1]), (1, 0, 2, 3)
    )
    dense_all, grad_gate_out, grad_up_out, grad_down_out = lax.optimization_barrier(
        (dense_all, grad_gate_out, grad_up_out, grad_down_out)
    )
    dense_half = core_reduce(dense_all, 11)
    dense_here = lax.psum_scatter(
        dense_half.reshape(-1, dense_half.shape[-1]), ("dpx", "ctx"), scatter_dimension=0, tiled=True
    ).astype(f32)
    spans = [q_cols, o_cols, k_cols, k_cols, router_weight.shape[1], 1, 1]
    cuts = [sum(spans[:i]) for i in range(len(spans) + 1)]
    pieces_out = [dense_here[:, cuts[i] : cuts[i + 1]] for i in range(len(spans))]
    dense_out = (
        pieces_out[5][:, 0],
        pieces_out[0],
        pieces_out[2],
        pieces_out[3],
        pieces_out[1],
        pieces_out[6][:, 0],
        pieces_out[4],
    )
    return (
        output,
        input_grad,
        dense_out[0],
        dense_out[1],
        dense_out[2],
        dense_out[3],
        dense_out[4],
        dense_out[5],
        dense_out[6],
        grad_gate_out,
        grad_up_out,
        grad_down_out,
    )


def solution(mesh):
    dp_count, ctx_count, tensor_count = (mesh.shape[a] for a in ("dp", "ctx", "tensor"))
    split_mesh = jax.sharding.Mesh(
        mesh.devices.reshape(dp_count // 2, 2, ctx_count, tensor_count), ("dpx", "core", "ctx", "tensor")
    )
    return jax.shard_map(
        functools.partial(per_device, dp_count // 2),
        mesh=split_mesh,
        in_specs=(
            P(("dpx", "core", "ctx"), None),
            P(),
            P(None, "tensor"),
            P(None, "tensor"),
            P(None, "tensor"),
            P(None, "tensor"),
            P(),
            P(),
            P(None, None, "tensor"),
            P(None, None, "tensor"),
            P(None, None, "tensor"),
            P(("dpx", "core")),
            P(("dpx", "core", "ctx"), None),
            P(("dpx", "core", "ctx"), None),
        ),
        out_specs=(
            P(("dpx", "core", "ctx"), None),
            P(("dpx", "core", "ctx"), None),
            P(("dpx", "core", "ctx")),
            P(("dpx", "core", "ctx"), "tensor"),
            P(("dpx", "core", "ctx"), "tensor"),
            P(("dpx", "core", "ctx"), "tensor"),
            P(("dpx", "core", "ctx"), "tensor"),
            P(("dpx", "core", "ctx")),
            P(("dpx", "core", "ctx"), None),
            P(None, ("dpx", "core", "ctx"), "tensor"),
            P(None, ("dpx", "core", "ctx"), "tensor"),
            P(None, ("dpx", "core", "ctx"), "tensor"),
        ),
        check_vma=False,
    )
```

```python
import functools
import math

import jax
import jax.numpy as jnp
from jax import lax
from jax.experimental import pallas as pl
from jax.experimental.pallas import tpu as pltpu
from jax.sharding import PartitionSpec as P

HEAD_SIZE = 64
NEXP = 24
CAP = 341


EPSILON = 1e-06
ROPE_BASE = 10000.0
NEGATIVE = -1e30
HIGHEST = lax.Precision.HIGHEST


def normalize(rows, gain):
    scale_inv = lax.rsqrt(jnp.mean(rows * rows, axis=-1, keepdims=True) + EPSILON)
    return (rows * scale_inv * gain, scale_inv)


def norm_backward(rows, scale_inv, gain, grad_normed):
    weighted = gain * grad_normed
    grad_gain = jnp.sum(grad_normed * rows * scale_inv, axis=0)
    inner_mean = jnp.mean(weighted * rows, axis=-1, keepdims=True)
    grad_rows = scale_inv * weighted - rows * scale_inv * scale_inv * scale_inv * inner_mean
    return (grad_rows, grad_gain)


def apply_rotary(value_rows, token_positions, direction):
    half_dim = value_rows.shape[-1] // 2
    frequency = ROPE_BASE ** (-jnp.arange(half_dim, dtype=jnp.float32) / half_dim)
    angles = token_positions.astype(jnp.float32)[:, None] * frequency[None, :]
    cosine = jnp.cos(angles)[:, None, :]
    sine_part = direction * jnp.sin(angles)[:, None, :]
    first_half = value_rows[..., :half_dim]
    second = value_rows[..., half_dim:]
    return jnp.concatenate(
        [first_half * cosine - second * sine_part, second * cosine + first_half * sine_part],
        axis=-1,
    )


def contract_rows(left, right):
    return lax.dot_general(
        left, right, (((0,), (0,)), ((), ())), preferred_element_type=jnp.float32
    )


def contract_rows_exact(left, right):
    return lax.dot_general(
        left, right, (((0,), (0,)), ((), ())), precision=HIGHEST, preferred_element_type=jnp.float32
    )


def contract_cols(left, right):
    return lax.dot_general(
        left, right, (((1,), (1,)), ((), ())), preferred_element_type=jnp.float32
    )


def _store_split(out_ref, value):
    cores, _, groups, rows, _ = out_ref.shape
    for x in range(groups):
        for c in range(cores):
            start = (x * cores + c) * rows
            out_ref[c, 0, x] = value[start : start + rows].astype(out_ref.dtype)


def _gate_column(gates_ref):
    gates = gates_ref[...]
    lane = lax.broadcasted_iota(jnp.int32, gates.shape, 1)
    return jnp.sum(jnp.where(lane == pl.program_id(0), gates, 0.0), axis=1, keepdims=True)


def _grad_body(
    n2_ref, n2t_ref, dy_ref, dyt_ref, gcol_ref, grow_ref, wg_ref, wu_ref, wd_ref,
    gg_ref, gu_ref, gd_ref, hid_ref, dga_ref, dua_ref,
):
    f32 = jnp.float32
    bf16 = jnp.bfloat16
    n2 = n2_ref[...]
    wd = wd_ref[0]
    gate_act = jnp.dot(n2, wg_ref[0], preferred_element_type=f32)
    up_act = jnp.dot(n2, wu_ref[0], preferred_element_type=f32)
    sig = 1.0 / (1.0 + jnp.exp(-gate_act))
    silu = gate_act * sig
    hidden = (silu * up_act).astype(bf16)
    hid_ref[0] = hidden
    deo = (_gate_column(gcol_ref) * dy_ref[...].astype(f32)).astype(bf16)
    grad_hidden = jnp.dot(deo, wd, preferred_element_type=f32)
    deo_t = (grow_ref[0] * dyt_ref[...].astype(f32)).astype(bf16)
    _store_split(gd_ref, jnp.dot(deo_t, hidden, preferred_element_type=f32))
    grad_gate_act = (grad_hidden * up_act * sig * (1.0 + gate_act * (1.0 - sig))).astype(bf16)
    grad_up_act = (grad_hidden * silu).astype(bf16)
    dga_ref[0] = grad_gate_act
    dua_ref[0] = grad_up_act
    n2t = n2t_ref[...]
    _store_split(gg_ref, jnp.dot(n2t, grad_gate_act, preferred_element_type=f32))
    _store_split(gu_ref, jnp.dot(n2t, grad_up_act, preferred_element_type=f32))


def _rows_body(hid_ref, dga_ref, dua_ref, dy_ref, gcol_ref, wg_ref, wu_ref, wd_ref, acc_ref, dgate_ref, dn2_ref):
    f32 = jnp.float32
    nt = (((1,), (1,)), ((), ()))

    @pl.when(pl.program_id(0) == 0)
    def _():
        acc_ref[...] = jnp.zeros_like(acc_ref)
        dn2_ref[...] = jnp.zeros_like(dn2_ref)

    expert_out = lax.dot_general(hid_ref[0], wd_ref[0], nt, preferred_element_type=f32)
    acc_ref[...] += _gate_column(gcol_ref) * expert_out
    dgate_ref[0] = jnp.sum(expert_out * dy_ref[...].astype(f32), axis=1, keepdims=True)
    dn2_ref[...] += lax.dot_general(
        dga_ref[0], wg_ref[0], nt, preferred_element_type=f32
    ) + lax.dot_general(dua_ref[0], wu_ref[0], nt, preferred_element_type=f32)


def expert_grad_kernel(n2, n2t, dy, dyt, gcol, grow, wg, wu, wd, groups):
    tokens, width = n2.shape
    experts, _, hidden = wg.shape
    bf16 = jnp.bfloat16
    whole = lambda shape: pl.BlockSpec(shape, lambda e: (0,) * len(shape))
    per_expert = lambda shape: pl.BlockSpec((1,) + shape, lambda e: (e,) + (0,) * len(shape))
    split_rows = width // (groups * 2)
    split = pl.BlockSpec((2, 1, groups, split_rows, hidden), lambda e: (0, e, 0, 0, 0))
    split_shape = jax.ShapeDtypeStruct((2, experts, groups, split_rows, hidden), bf16)
    act_shape = jax.ShapeDtypeStruct((experts, tokens, hidden), bf16)
    return pl.pallas_call(
        _grad_body,
        grid=(experts,),
        in_specs=[
            whole((tokens, width)),
            whole((width, tokens)),
            whole((tokens, width)),
            whole((width, tokens)),
            whole((tokens, experts)),
            per_expert((1, tokens)),
            per_expert((width, hidden)),
            per_expert((width, hidden)),
            per_expert((width, hidden)),
        ],
        out_specs=[split, split, split]
        + [per_expert((tokens, hidden))] * 3,
        out_shape=[split_shape] * 3 + [act_shape] * 3,
        compiler_params=pltpu.CompilerParams(
            dimension_semantics=("arbitrary",), vmem_limit_bytes=64 * 1024 * 1024
        ),
        cost_estimate=pl.CostEstimate(
            flops=experts * tokens * width * hidden * 2 * 6,
            transcendentals=experts * tokens * hidden,
            bytes_accessed=experts * width * hidden * 12 + tokens * width * 8 + experts * tokens * hidden * 6,
        ),
    )(n2, n2t, dy, dyt, gcol, grow, wg, wu, wd)


def expert_rows_kernel(hid, dga, dua, dy, gcol, wg, wu, wd):
    experts, tokens, hidden = hid.shape
    width = dy.shape[1]
    f32 = jnp.float32
    whole = lambda shape: pl.BlockSpec(shape, lambda e: (0,) * len(shape))
    per_expert = lambda shape: pl.BlockSpec((1,) + shape, lambda e: (e,) + (0,) * len(shape))
    return pl.pallas_call(
        _rows_body,
        grid=(experts,),
        in_specs=[
            per_expert((tokens, hidden)),
            per_expert((tokens, hidden)),
            per_expert((tokens, hidden)),
            whole((tokens, width)),
            whole((tokens, experts)),
            per_expert((width, hidden)),
            per_expert((width, hidden)),
            per_expert((width, hidden)),
        ],
        out_specs=[whole((tokens, width)), per_expert((tokens, 1)), whole((tokens, width))],
        out_shape=[
            jax.ShapeDtypeStruct((tokens, width), f32),
            jax.ShapeDtypeStruct((experts, tokens, 1), f32),
            jax.ShapeDtypeStruct((tokens, width), f32),
        ],
        compiler_params=pltpu.CompilerParams(
            dimension_semantics=("arbitrary",), vmem_limit_bytes=64 * 1024 * 1024
        ),
        cost_estimate=pl.CostEstimate(
            flops=experts * tokens * width * hidden * 2 * 3,
            transcendentals=0,
            bytes_accessed=experts * width * hidden * 6 + tokens * width * 10 + experts * tokens * hidden * 6,
        ),
    )(hid, dga, dua, dy, gcol, wg, wu, wd)

MESH = pl.DeviceIdType.MESH


def _exchange_body(axis, n, per_peer, downward, src_ref, out_ref, send_sems, recv_sems):
    me = lax.axis_index(axis)
    barrier = pltpu.get_barrier_semaphore()
    for k in range(1, n):
        peer = lax.rem(me + k, n)
        pl.semaphore_signal(barrier, 1, device_id={axis: peer}, device_id_type=MESH)
    pl.semaphore_wait(barrier, n - 1)
    sends = []
    for k in range(1, n):
        peer = lax.rem(me + k, n)
        copy = pltpu.make_async_remote_copy(
            src_ref=src_ref.at[peer] if per_peer else src_ref,
            dst_ref=out_ref.at[me],
            send_sem=send_sems.at[k - 1],
            recv_sem=recv_sems.at[k - 1],
            device_id={axis: peer},
            device_id_type=MESH,
        )
        sends.append((peer, copy))
        if downward:
            pl.when(peer < me)(copy.start)
        else:
            copy.start()
    for k in range(1, n):
        source = lax.rem(me + n - k, n)
        incoming = pltpu.make_async_remote_copy(
            src_ref=src_ref.at[source] if per_peer else src_ref,
            dst_ref=out_ref.at[source],
            send_sem=send_sems.at[k - 1],
            recv_sem=recv_sems.at[k - 1],
            device_id={axis: source},
            device_id_type=MESH,
        )
        if downward:
            pl.when(source > me)(incoming.wait_recv)
        else:
            incoming.wait_recv()
    for peer, copy in sends:
        if downward:
            pl.when(peer < me)(copy.wait_send)
        else:
            copy.wait_send()


def exchange(x, axis, n, per_peer, collective_id, downward=False):
    block = x.shape[1:] if per_peer else x.shape
    nbytes = math.prod(block) * x.dtype.itemsize
    return pl.pallas_call(
        functools.partial(_exchange_body, axis, n, per_peer, downward),
        out_shape=jax.ShapeDtypeStruct((n,) + tuple(block), x.dtype),
        in_specs=[pl.BlockSpec(memory_space=pl.ANY)],
        out_specs=pl.BlockSpec(memory_space=pl.ANY),
        scratch_shapes=[pltpu.SemaphoreType.DMA((n - 1,)), pltpu.SemaphoreType.DMA((n - 1,))],
        compiler_params=pltpu.CompilerParams(collective_id=collective_id, has_side_effects=True),
        cost_estimate=pl.CostEstimate(flops=0, transcendentals=0, bytes_accessed=2 * (n - 1) * nbytes),
    )(x)


def gather_axis(x, axis, n, collective_id):
    got = exchange(x, axis, n, False, collective_id)
    return lax.dynamic_update_slice_in_dim(got, x[None], lax.axis_index(axis), 0)


def sum_axis(x, axis, collective_id):
    got = exchange(x, axis, 2, False, collective_id)
    me = lax.axis_index(axis)
    other = lax.dynamic_index_in_dim(got, 1 - me, 0, keepdims=False)
    return x.astype(jnp.float32) + other.astype(jnp.float32)


def _pair_add_body(me_ref, own_ref, other_ref, out_ref):
    out_ref[...] = (own_ref[...].astype(jnp.float32) + other_ref[...].astype(jnp.float32)).astype(out_ref.dtype)


def core_reduce(x, collective_id):
    got = exchange(x, "core", 2, True, collective_id)
    me = lax.axis_index("core")
    count = x.shape[1]
    rest = x.shape[2:]
    zeros = (0,) * len(rest)
    item_bytes = math.prod(rest) * x.dtype.itemsize
    step = max(d for d in range(1, count + 1) if count % d == 0 and d * item_bytes <= 4 * 1024 * 1024)
    grid_spec = pltpu.PrefetchScalarGridSpec(
        num_scalar_prefetch=1,
        grid=(count // step,),
        in_specs=[
            pl.BlockSpec((None, step) + rest, lambda i, c: (c[0], i) + zeros),
            pl.BlockSpec((None, step) + rest, lambda i, c: (1 - c[0], i) + zeros),
        ],
        out_specs=pl.BlockSpec((step,) + rest, lambda i, c: (i,) + zeros),
    )
    return pl.pallas_call(
        _pair_add_body,
        grid_spec=grid_spec,
        out_shape=jax.ShapeDtypeStruct(x.shape[1:], jnp.bfloat16),
        compiler_params=pltpu.CompilerParams(vmem_limit_bytes=56 * 1024 * 1024),
        cost_estimate=pl.CostEstimate(flops=x.size // 2, transcendentals=0, bytes_accessed=x.size * 3),
    )(jnp.reshape(me, (1,)).astype(jnp.int32), x, got)


def scatter_sum_downward(x, axis, n, collective_id):
    got = exchange(x, axis, n, True, collective_id, downward=True)
    me = lax.axis_index(axis)
    own = lax.dynamic_index_in_dim(x, me, 0, keepdims=False).astype(jnp.float32)
    above = (jnp.arange(n, dtype=jnp.int32) > me).reshape((n,) + (1,) * (x.ndim - 1))
    return own + jnp.sum(jnp.where(above, got.astype(jnp.float32), 0.0), axis=0)


def _flash_body(ctx_ref, q_ref, k_ref, v_ref, qseg_ref, qpos_ref, kseg_ref, o_ref, lse_ref, m_sc, l_sc, acc_sc):
    f32 = jnp.float32
    block = pl.program_id(1)

    @pl.when(block == 0)
    def _():
        m_sc[...] = jnp.full_like(m_sc, NEGATIVE)
        l_sc[...] = jnp.zeros_like(l_sc)
        acc_sc[...] = jnp.zeros_like(acc_sc)

    @pl.when(block <= ctx_ref[0])
    def _():
        keys = k_ref[0]
        width = keys.shape[0]
        scores = lax.dot_general(
            q_ref[0], keys, (((1,), (1,)), ((), ())), preferred_element_type=f32
        ) * (1.0 / math.sqrt(HEAD_SIZE))
        key_pos = block * width + lax.broadcasted_iota(jnp.int32, (1, width), 1)
        allowed = (qseg_ref[...] == kseg_ref[...]) & (key_pos <= qpos_ref[...])
        scores = jnp.where(allowed, scores, NEGATIVE)
        m_old = m_sc[...]
        m_new = jnp.maximum(m_old, jnp.max(scores, axis=1, keepdims=True))
        alpha = jnp.exp(m_old - m_new)
        weights = jnp.where(allowed, jnp.exp(scores - m_new), 0.0)
        l_sc[...] = alpha * l_sc[...] + jnp.sum(weights, axis=1, keepdims=True)
        acc_sc[...] = alpha * acc_sc[...] + jnp.dot(
            weights.astype(jnp.bfloat16), v_ref[0], preferred_element_type=f32
        )
        m_sc[...] = m_new

    @pl.when(block == pl.num_programs(1) - 1)
    def _():
        o_ref[0] = acc_sc[...] / l_sc[...]
        lse_ref[0] = m_sc[...] + jnp.log(l_sc[...])


def flash_forward(ctx_index, q, k, v, qseg, qpos, kseg, width):
    heads, rows, depth = q.shape
    blocks = k.shape[1] // width
    f32 = jnp.float32
    capped = lambda h, b, c: (h, jnp.minimum(b, c[0]), 0)
    grid_spec = pltpu.PrefetchScalarGridSpec(
        num_scalar_prefetch=1,
        grid=(heads, blocks),
        in_specs=[
            pl.BlockSpec((1, rows, depth), lambda h, b, c: (h, 0, 0)),
            pl.BlockSpec((1, width, depth), capped),
            pl.BlockSpec((1, width, depth), capped),
            pl.BlockSpec((rows, 1), lambda h, b, c: (0, 0)),
            pl.BlockSpec((rows, 1), lambda h, b, c: (0, 0)),
            pl.BlockSpec((1, width), lambda h, b, c: (0, jnp.minimum(b, c[0]))),
        ],
        out_specs=[
            pl.BlockSpec((1, rows, depth), lambda h, b, c: (h, 0, 0)),
            pl.BlockSpec((1, rows, 1), lambda h, b, c: (h, 0, 0)),
        ],
        scratch_shapes=[
            pltpu.VMEM((rows, 1), f32),
            pltpu.VMEM((rows, 1), f32),
            pltpu.VMEM((rows, depth), f32),
        ],
    )
    return pl.pallas_call(
        _flash_body,
        grid_spec=grid_spec,
        out_shape=[
            jax.ShapeDtypeStruct((heads, rows, depth), f32),
            jax.ShapeDtypeStruct((heads, rows, 1), f32),
        ],
        compiler_params=pltpu.CompilerParams(
            dimension_semantics=("arbitrary", "arbitrary"), vmem_limit_bytes=48 * 1024 * 1024
        ),
        cost_estimate=pl.CostEstimate(
            flops=heads * rows * k.shape[1] * depth * 4,
            transcendentals=heads * rows * k.shape[1],
            bytes_accessed=(q.size + k.size + v.size) * 2 + heads * rows * depth * 4,
        ),
    )(jnp.reshape(ctx_index, (1,)).astype(jnp.int32), q, k, v, qseg, qpos, kseg)


def per_device(
    dpx_count,
    hidden_in,
    attn_gain,
    q_weight,
    key_matrix,
    value_matrix,
    o_weight,
    moe_gain,
    router_weight,
    gate_weight,
    up_weight,
    down_weight,
    segments,
    expert_picks,
    output_grad,
):
    bf16 = jnp.bfloat16
    f32 = jnp.float32
    token_count = hidden_in.shape[0]
    ctx_index = lax.axis_index("ctx")
    heads_local = q_weight.shape[1] // HEAD_SIZE
    kv_local = key_matrix.shape[1] // HEAD_SIZE
    group_size = heads_local // kv_local
    score_scale = 1.0 / math.sqrt(HEAD_SIZE)
    token_positions = ctx_index * token_count + jnp.arange(token_count, dtype=jnp.int32)
    segment_here = lax.dynamic_slice_in_dim(segments, ctx_index * token_count, token_count)
    inputs_f32 = hidden_in.astype(f32)
    o_full = lax.all_gather(o_weight, "tensor", axis=1, tiled=True)
    normed_f32, scale_one = normalize(inputs_f32, attn_gain)
    normed_one = normed_f32.astype(bf16)
    query_rows = jnp.dot(normed_one, q_weight, preferred_element_type=f32).reshape(
        token_count, heads_local, HEAD_SIZE
    )
    keys_raw = jnp.dot(normed_one, key_matrix, preferred_element_type=f32).reshape(
        token_count, kv_local, HEAD_SIZE
    )
    values_raw = jnp.dot(normed_one, value_matrix, preferred_element_type=f32)
    query_grouped = (
        apply_rotary(query_rows, token_positions, 1.0)
        .astype(bf16)
        .reshape(token_count, kv_local, group_size, HEAD_SIZE)
    )
    key_flat = (
        apply_rotary(keys_raw, token_positions, 1.0)
        .astype(bf16)
        .reshape(token_count, kv_local * HEAD_SIZE)
    )
    value_flat = values_raw.astype(bf16)

    def piece_mask(piece_rows):
        key_pos = jnp.arange(piece_rows, dtype=jnp.int32)
        return (segment_here[:, None] == segments[None, :]) & (
            key_pos[None, :] <= token_positions[:, None]
        )

    ctx_count = segments.shape[0] // token_count
    kv_both = gather_axis(jnp.concatenate([key_flat, value_flat], axis=1), "ctx", ctx_count, 1)
    piece_rows = ctx_count * token_count
    kv_width = kv_local * HEAD_SIZE
    key_piece = kv_both[:, :, :kv_width].reshape(piece_rows, kv_local, HEAD_SIZE)
    value_piece = kv_both[:, :, kv_width:].reshape(piece_rows, kv_local, HEAD_SIZE)
    row_segments = jnp.tile(segment_here, group_size)[:, None]
    row_positions = jnp.tile(token_positions, group_size)[:, None]
    attn_rows, lse_rows = flash_forward(
        ctx_index,
        jnp.transpose(query_grouped, (1, 2, 0, 3)).reshape(kv_local, group_size * token_count, HEAD_SIZE),
        jnp.transpose(key_piece, (1, 0, 2)),
        jnp.transpose(value_piece, (1, 0, 2)),
        row_segments,
        row_positions,
        segments[None, :],
        token_count,
    )
    attn_grouped = attn_rows.reshape(kv_local, group_size, token_count, HEAD_SIZE)
    log_sum = lse_rows.reshape(kv_local, group_size, token_count)
    attn_bf = (
        jnp.transpose(attn_grouped, (2, 0, 1, 3))
        .reshape(token_count, heads_local * HEAD_SIZE)
        .astype(bf16)
    )
    tensor_count = o_weight.shape[0] // o_weight.shape[1]
    attn_all = gather_axis(attn_bf, "tensor", tensor_count, 2)
    attn_full = jnp.transpose(attn_all, (1, 0, 2)).reshape(token_count, tensor_count * attn_bf.shape[1])
    mixed_attn = contract_cols(attn_full, o_full)
    resid = inputs_f32 + mixed_attn
    normed_two_f32, scale_two = normalize(resid, moe_gain)
    normed_two = normed_two_f32.astype(bf16)
    logits = jnp.dot(normed_two, router_weight, preferred_element_type=f32)
    expert_range = jnp.arange(NEXP, dtype=jnp.int32)
    picked_onehot = expert_picks[:, :, None] == expert_range[None, None, :]
    picked = jnp.sum(jnp.where(picked_onehot, logits[:, None, :], 0.0), axis=2)
    gate_probs = jax.nn.softmax(picked, axis=-1)
    gates_dense = jnp.sum(jnp.where(picked_onehot, gate_probs[:, :, None], 0.0), axis=1)
    gates_by_expert = jnp.transpose(gates_dense)
    cot_bf = output_grad
    gcol = gates_dense
    grad_gate, grad_up, grad_down, hid_all, dga_all, dua_all = expert_grad_kernel(
        normed_two,
        jnp.transpose(normed_two),
        cot_bf,
        jnp.transpose(cot_bf),
        gcol,
        gates_by_expert[:, None, :],
        gate_weight,
        up_weight,
        down_weight,
        dpx_count,
    )
    gate_half = core_reduce(grad_gate, 8)
    gate_half, hid_all, dga_all, dua_all = lax.optimization_barrier(
        (gate_half, hid_all, dga_all, dua_all)
    )
    moe_acc, gate_parts, moe_grad_rows = expert_rows_kernel(
        hid_all, dga_all, dua_all, cot_bf, gcol, gate_weight, up_weight, down_weight
    )
    cot_f32 = output_grad.astype(f32)
    moe_total = sum_axis(moe_acc.astype(bf16), "tensor", 3)
    output = (resid + moe_total).astype(bf16)
    grad_rows_all = moe_grad_rows
    gate_parts = gate_parts[:, :, 0]
    grad_gate_out, grad_up_out, grad_down_out = [
        lax.psum_scatter(
            g.reshape(g.shape[0], -1, g.shape[3]), ("dpx", "ctx"), scatter_dimension=1, tiled=True
        ).astype(jnp.float32)
        for g in (gate_half, core_reduce(grad_up, 9), core_reduce(grad_down, 10))
    ]
    gate_pair = jnp.sum(
        jnp.where(picked_onehot, jnp.transpose(gate_parts)[:, None, :], 0.0), axis=2
    )
    moe_summed = sum_axis(grad_rows_all.astype(bf16), "tensor", 4)
    gate_summed = sum_axis(gate_pair.astype(bf16), "tensor", 5)
    grad_picked = gate_probs * (
        gate_summed - jnp.sum(gate_probs * gate_summed, axis=1, keepdims=True)
    )
    grad_logits = jnp.sum(jnp.where(picked_onehot, grad_picked[:, :, None], 0.0), axis=1).astype(
        bf16
    )
    grad_router = contract_rows(normed_two, grad_logits)
    grad_normed_two = moe_summed + contract_cols(grad_logits, router_weight)
    grad_two_rows, grad_moe_gain = norm_backward(resid, scale_two, moe_gain, grad_normed_two)
    grad_resid = cot_f32 + grad_two_rows
    grad_mix = grad_resid.astype(bf16)
    grad_o = contract_rows(grad_mix, attn_bf)
    grad_attn = jnp.dot(grad_mix, o_weight, preferred_element_type=f32).astype(bf16)
    grad_attn_grouped = jnp.transpose(
        grad_attn.reshape(token_count, kv_local, group_size, HEAD_SIZE), (1, 2, 0, 3)
    )
    row_delta = jnp.sum(grad_attn_grouped.astype(f32) * attn_grouped, axis=-1)
    allowed = piece_mask(piece_rows)
    scores = (
        jnp.einsum("tkgd,nkd->kgtn", query_grouped, key_piece, preferred_element_type=f32)
        * score_scale
    )
    probability = jnp.where(allowed, jnp.exp(scores - log_sum[..., None]), 0.0)
    grad_probs = jnp.einsum(
        "kgtd,nkd->kgtn", grad_attn_grouped, value_piece, preferred_element_type=f32
    )
    grad_scores = (probability * (grad_probs - row_delta[..., None])).astype(bf16)
    grad_query = score_scale * jnp.einsum(
        "kgtn,nkd->kgtd", grad_scores, key_piece, preferred_element_type=f32
    )
    key_part = score_scale * jnp.einsum(
        "kgtn,tkgd->nkd", grad_scores, query_grouped, preferred_element_type=f32
    )
    value_part = jnp.einsum(
        "kgtn,kgtd->nkd", probability.astype(bf16), grad_attn_grouped, preferred_element_type=f32
    )
    grad_keys_all = key_part.reshape(piece_rows, kv_local * HEAD_SIZE)
    grad_values_all = value_part.reshape(piece_rows, kv_local * HEAD_SIZE)
    back_state = (grad_query, grad_keys_all, grad_values_all)
    grad_query, grad_keys_all, grad_values_all = back_state
    grad_kv_here = scatter_sum_downward(
        jnp.concatenate([grad_keys_all, grad_values_all], axis=1)
        .astype(bf16)
        .reshape(ctx_count, token_count, 2 * kv_width),
        "ctx",
        ctx_count,
        6,
    )
    grad_keys_here = grad_kv_here[:, :kv_width]
    grad_values_here = grad_kv_here[:, kv_width:]
    grad_query_rows = jnp.transpose(grad_query, (2, 0, 1, 3)).reshape(
        token_count, heads_local, HEAD_SIZE
    )
    grad_query_bf = (
        apply_rotary(grad_query_rows, token_positions, -1.0)
        .reshape(token_count, heads_local * HEAD_SIZE)
        .astype(bf16)
    )
    grad_key_bf = (
        apply_rotary(
            grad_keys_here.reshape(token_count, kv_local, HEAD_SIZE), token_positions, -1.0
        )
        .reshape(token_count, kv_local * HEAD_SIZE)
        .astype(bf16)
    )
    grad_value_bf = grad_values_here.astype(bf16)
    grad_q = contract_rows(normed_one, grad_query_bf)
    grad_k = contract_rows(normed_one, grad_key_bf)
    grad_v = contract_rows(normed_one, grad_value_bf)
    partial_one = (
        contract_cols(grad_query_bf, q_weight)
        + contract_cols(grad_key_bf, key_matrix)
        + contract_cols(grad_value_bf, value_matrix)
    )
    grad_normed_one = sum_axis(partial_one.astype(bf16), "tensor", 7)
    grad_one_rows, grad_attn_gain = norm_backward(inputs_f32, scale_one, attn_gain, grad_normed_one)
    input_grad = grad_resid + grad_one_rows
    q_cols, o_cols, k_cols = grad_q.shape[1], grad_o.shape[1], grad_k.shape[1]
    small = jnp.concatenate(
        [
            grad_router,
            grad_attn_gain[:, None],
            grad_moe_gain[:, None],
            jnp.zeros((grad_router.shape[0], 128 - grad_router.shape[1] - 2), f32),
        ],
        axis=1,
    )
    dense_all = jnp.concatenate(
        [grad_q, grad_o, grad_k, grad_v, small], axis=1
    ).astype(bf16)
    width = dense_all.shape[0]
    dense_all = jnp.transpose(
        dense_all.reshape(dpx_count, 2, width // (2 * dpx_count), dense_all.shape[1]), (1, 0, 2, 3)
    )
    dense_all, grad_gate_out, grad_up_out, grad_down_out = lax.optimization_barrier(
        (dense_all, grad_gate_out, grad_up_out, grad_down_out)
    )
    dense_half = core_reduce(dense_all, 11)
    dense_here = lax.psum_scatter(
        dense_half.reshape(-1, dense_half.shape[-1]), ("dpx", "ctx"), scatter_dimension=0, tiled=True
    ).astype(f32)
    spans = [q_cols, o_cols, k_cols, k_cols, router_weight.shape[1], 1, 1]
    cuts = [sum(spans[:i]) for i in range(len(spans) + 1)]
    pieces_out = [dense_here[:, cuts[i] : cuts[i + 1]] for i in range(len(spans))]
    dense_out = (
        pieces_out[5][:, 0],
        pieces_out[0],
        pieces_out[2],
        pieces_out[3],
        pieces_out[1],
        pieces_out[6][:, 0],
        pieces_out[4],
    )
    return (
        output,
        input_grad,
        dense_out[0],
        dense_out[1],
        dense_out[2],
        dense_out[3],
        dense_out[4],
        dense_out[5],
        dense_out[6],
        grad_gate_out,
        grad_up_out,
        grad_down_out,
    )


def solution(mesh):
    dp_count, ctx_count, tensor_count = (mesh.shape[a] for a in ("dp", "ctx", "tensor"))
    split_mesh = jax.sharding.Mesh(
        mesh.devices.reshape(dp_count // 2, 2, ctx_count, tensor_count), ("dpx", "core", "ctx", "tensor")
    )
    return jax.shard_map(
        functools.partial(per_device, dp_count // 2),
        mesh=split_mesh,
        in_specs=(
            P(("dpx", "core", "ctx"), None),
            P(),
            P(None, "tensor"),
            P(None, "tensor"),
            P(None, "tensor"),
            P(None, "tensor"),
            P(),
            P(),
            P(None, None, "tensor"),
            P(None, None, "tensor"),
            P(None, None, "tensor"),
            P(("dpx", "core")),
            P(("dpx", "core", "ctx"), None),
            P(("dpx", "core", "ctx"), None),
        ),
        out_specs=(
            P(("dpx", "core", "ctx"), None),
            P(("dpx", "core", "ctx"), None),
            P(("dpx", "core", "ctx")),
            P(("dpx", "core", "ctx"), "tensor"),
            P(("dpx", "core", "ctx"), "tensor"),
            P(("dpx", "core", "ctx"), "tensor"),
            P(("dpx", "core", "ctx"), "tensor"),
            P(("dpx", "core", "ctx")),
            P(("dpx", "core", "ctx"), None),
            P(None, ("dpx", "core", "ctx"), "tensor"),
            P(None, ("dpx", "core", "ctx"), "tensor"),
            P(None, ("dpx", "core", "ctx"), "tensor"),
        ),
        check_vma=False,
    )
```

```python
import functools
import math

import jax
import jax.numpy as jnp
from jax import lax
from jax.experimental import pallas as pl
from jax.experimental.pallas import tpu as pltpu
from jax.sharding import PartitionSpec as P

HEAD_SIZE = 64
NEXP = 24
CAP = 341


EPSILON = 1e-06
ROPE_BASE = 10000.0
NEGATIVE = -1e30
HIGHEST = lax.Precision.HIGHEST


def normalize(rows, gain):
    scale_inv = lax.rsqrt(jnp.mean(rows * rows, axis=-1, keepdims=True) + EPSILON)
    return (rows * scale_inv * gain, scale_inv)


def norm_backward(rows, scale_inv, gain, grad_normed):
    weighted = gain * grad_normed
    grad_gain = jnp.sum(grad_normed * rows * scale_inv, axis=0)
    inner_mean = jnp.mean(weighted * rows, axis=-1, keepdims=True)
    grad_rows = scale_inv * weighted - rows * scale_inv * scale_inv * scale_inv * inner_mean
    return (grad_rows, grad_gain)


def apply_rotary(value_rows, token_positions, direction):
    half_dim = value_rows.shape[-1] // 2
    frequency = ROPE_BASE ** (-jnp.arange(half_dim, dtype=jnp.float32) / half_dim)
    angles = token_positions.astype(jnp.float32)[:, None] * frequency[None, :]
    cosine = jnp.cos(angles)[:, None, :]
    sine_part = direction * jnp.sin(angles)[:, None, :]
    first_half = value_rows[..., :half_dim]
    second = value_rows[..., half_dim:]
    return jnp.concatenate(
        [first_half * cosine - second * sine_part, second * cosine + first_half * sine_part],
        axis=-1,
    )


def contract_rows(left, right):
    return lax.dot_general(
        left, right, (((0,), (0,)), ((), ())), preferred_element_type=jnp.float32
    )


def contract_rows_exact(left, right):
    return lax.dot_general(
        left, right, (((0,), (0,)), ((), ())), precision=HIGHEST, preferred_element_type=jnp.float32
    )


def contract_cols(left, right):
    return lax.dot_general(
        left, right, (((1,), (1,)), ((), ())), preferred_element_type=jnp.float32
    )


def _store_split(out_ref, value):
    cores, _, groups, rows, _ = out_ref.shape
    for x in range(groups):
        for c in range(cores):
            start = (x * cores + c) * rows
            out_ref[c, 0, x] = value[start : start + rows].astype(out_ref.dtype)


def _gate_column(gates_ref):
    gates = gates_ref[...]
    lane = lax.broadcasted_iota(jnp.int32, gates.shape, 1)
    return jnp.sum(jnp.where(lane == pl.program_id(0), gates, 0.0), axis=1, keepdims=True)


def _grad_body(
    n2_ref, n2t_ref, dy_ref, dyt_ref, gcol_ref, grow_ref, wg_ref, wu_ref, wd_ref,
    gg_ref, gu_ref, gd_ref, hid_ref, dga_ref, dua_ref,
):
    f32 = jnp.float32
    bf16 = jnp.bfloat16
    n2 = n2_ref[...]
    wd = wd_ref[0]
    gate_act = jnp.dot(n2, wg_ref[0], preferred_element_type=f32)
    up_act = jnp.dot(n2, wu_ref[0], preferred_element_type=f32)
    sig = 1.0 / (1.0 + jnp.exp(-gate_act))
    silu = gate_act * sig
    hidden = (silu * up_act).astype(bf16)
    hid_ref[0] = hidden
    deo = (_gate_column(gcol_ref) * dy_ref[...].astype(f32)).astype(bf16)
    grad_hidden = jnp.dot(deo, wd, preferred_element_type=f32)
    deo_t = (grow_ref[0] * dyt_ref[...].astype(f32)).astype(bf16)
    _store_split(gd_ref, jnp.dot(deo_t, hidden, preferred_element_type=f32))
    grad_gate_act = (grad_hidden * up_act * sig * (1.0 + gate_act * (1.0 - sig))).astype(bf16)
    grad_up_act = (grad_hidden * silu).astype(bf16)
    dga_ref[0] = grad_gate_act
    dua_ref[0] = grad_up_act
    n2t = n2t_ref[...]
    _store_split(gg_ref, jnp.dot(n2t, grad_gate_act, preferred_element_type=f32))
    _store_split(gu_ref, jnp.dot(n2t, grad_up_act, preferred_element_type=f32))


def _rows_body(hid_ref, dga_ref, dua_ref, dy_ref, gcol_ref, wg_ref, wu_ref, wd_ref, acc_ref, dgate_ref, dn2_ref):
    f32 = jnp.float32
    nt = (((1,), (1,)), ((), ()))

    @pl.when(pl.program_id(0) == 0)
    def _():
        acc_ref[...] = jnp.zeros_like(acc_ref)
        dn2_ref[...] = jnp.zeros_like(dn2_ref)

    expert_out = lax.dot_general(hid_ref[0], wd_ref[0], nt, preferred_element_type=f32)
    acc_ref[...] += _gate_column(gcol_ref) * expert_out
    dgate_ref[0] = jnp.sum(expert_out * dy_ref[...].astype(f32), axis=1, keepdims=True)
    dn2_ref[...] += lax.dot_general(
        dga_ref[0], wg_ref[0], nt, preferred_element_type=f32
    ) + lax.dot_general(dua_ref[0], wu_ref[0], nt, preferred_element_type=f32)


def expert_grad_kernel(n2, n2t, dy, dyt, gcol, grow, wg, wu, wd, groups):
    tokens, width = n2.shape
    experts, _, hidden = wg.shape
    bf16 = jnp.bfloat16
    whole = lambda shape: pl.BlockSpec(shape, lambda e: (0,) * len(shape))
    per_expert = lambda shape: pl.BlockSpec((1,) + shape, lambda e: (e,) + (0,) * len(shape))
    split_rows = width // (groups * 2)
    split = pl.BlockSpec((2, 1, groups, split_rows, hidden), lambda e: (0, e, 0, 0, 0))
    split_shape = jax.ShapeDtypeStruct((2, experts, groups, split_rows, hidden), bf16)
    act_shape = jax.ShapeDtypeStruct((experts, tokens, hidden), bf16)
    return pl.pallas_call(
        _grad_body,
        grid=(experts,),
        in_specs=[
            whole((tokens, width)),
            whole((width, tokens)),
            whole((tokens, width)),
            whole((width, tokens)),
            whole((tokens, experts)),
            per_expert((1, tokens)),
            per_expert((width, hidden)),
            per_expert((width, hidden)),
            per_expert((width, hidden)),
        ],
        out_specs=[split, split, split]
        + [per_expert((tokens, hidden))] * 3,
        out_shape=[split_shape] * 3 + [act_shape] * 3,
        compiler_params=pltpu.CompilerParams(
            dimension_semantics=("arbitrary",), vmem_limit_bytes=64 * 1024 * 1024
        ),
        cost_estimate=pl.CostEstimate(
            flops=experts * tokens * width * hidden * 2 * 6,
            transcendentals=experts * tokens * hidden,
            bytes_accessed=experts * width * hidden * 12 + tokens * width * 8 + experts * tokens * hidden * 6,
        ),
    )(n2, n2t, dy, dyt, gcol, grow, wg, wu, wd)


def expert_rows_kernel(hid, dga, dua, dy, gcol, wg, wu, wd):
    experts, tokens, hidden = hid.shape
    width = dy.shape[1]
    f32 = jnp.float32
    whole = lambda shape: pl.BlockSpec(shape, lambda e: (0,) * len(shape))
    per_expert = lambda shape: pl.BlockSpec((1,) + shape, lambda e: (e,) + (0,) * len(shape))
    return pl.pallas_call(
        _rows_body,
        grid=(experts,),
        in_specs=[
            per_expert((tokens, hidden)),
            per_expert((tokens, hidden)),
            per_expert((tokens, hidden)),
            whole((tokens, width)),
            whole((tokens, experts)),
            per_expert((width, hidden)),
            per_expert((width, hidden)),
            per_expert((width, hidden)),
        ],
        out_specs=[whole((tokens, width)), per_expert((tokens, 1)), whole((tokens, width))],
        out_shape=[
            jax.ShapeDtypeStruct((tokens, width), f32),
            jax.ShapeDtypeStruct((experts, tokens, 1), f32),
            jax.ShapeDtypeStruct((tokens, width), f32),
        ],
        compiler_params=pltpu.CompilerParams(
            dimension_semantics=("arbitrary",), vmem_limit_bytes=64 * 1024 * 1024
        ),
        cost_estimate=pl.CostEstimate(
            flops=experts * tokens * width * hidden * 2 * 3,
            transcendentals=0,
            bytes_accessed=experts * width * hidden * 6 + tokens * width * 10 + experts * tokens * hidden * 6,
        ),
    )(hid, dga, dua, dy, gcol, wg, wu, wd)

MESH = pl.DeviceIdType.MESH


def _exchange_body(axis, n, per_peer, downward, src_ref, out_ref, send_sems, recv_sems):
    me = lax.axis_index(axis)
    barrier = pltpu.get_barrier_semaphore()
    for k in range(1, n):
        peer = lax.rem(me + k, n)
        pl.semaphore_signal(barrier, 1, device_id={axis: peer}, device_id_type=MESH)
    pl.semaphore_wait(barrier, n - 1)
    sends = []
    for k in range(1, n):
        peer = lax.rem(me + k, n)
        copy = pltpu.make_async_remote_copy(
            src_ref=src_ref.at[peer] if per_peer else src_ref,
            dst_ref=out_ref.at[me],
            send_sem=send_sems.at[k - 1],
            recv_sem=recv_sems.at[k - 1],
            device_id={axis: peer},
            device_id_type=MESH,
        )
        sends.append((peer, copy))
        if downward:
            pl.when(peer < me)(copy.start)
        else:
            copy.start()
    for k in range(1, n):
        source = lax.rem(me + n - k, n)
        incoming = pltpu.make_async_remote_copy(
            src_ref=src_ref.at[source] if per_peer else src_ref,
            dst_ref=out_ref.at[source],
            send_sem=send_sems.at[k - 1],
            recv_sem=recv_sems.at[k - 1],
            device_id={axis: source},
            device_id_type=MESH,
        )
        if downward:
            pl.when(source > me)(incoming.wait_recv)
        else:
            incoming.wait_recv()
    for peer, copy in sends:
        if downward:
            pl.when(peer < me)(copy.wait_send)
        else:
            copy.wait_send()


def exchange(x, axis, n, per_peer, collective_id, downward=False):
    block = x.shape[1:] if per_peer else x.shape
    nbytes = math.prod(block) * x.dtype.itemsize
    return pl.pallas_call(
        functools.partial(_exchange_body, axis, n, per_peer, downward),
        out_shape=jax.ShapeDtypeStruct((n,) + tuple(block), x.dtype),
        in_specs=[pl.BlockSpec(memory_space=pl.ANY)],
        out_specs=pl.BlockSpec(memory_space=pl.ANY),
        scratch_shapes=[pltpu.SemaphoreType.DMA((n - 1,)), pltpu.SemaphoreType.DMA((n - 1,))],
        compiler_params=pltpu.CompilerParams(collective_id=collective_id, has_side_effects=True),
        cost_estimate=pl.CostEstimate(flops=0, transcendentals=0, bytes_accessed=2 * (n - 1) * nbytes),
    )(x)


def gather_axis(x, axis, n, collective_id):
    got = exchange(x, axis, n, False, collective_id)
    return lax.dynamic_update_slice_in_dim(got, x[None], lax.axis_index(axis), 0)


def sum_axis(x, axis, collective_id):
    got = exchange(x, axis, 2, False, collective_id)
    me = lax.axis_index(axis)
    other = lax.dynamic_index_in_dim(got, 1 - me, 0, keepdims=False)
    return x.astype(jnp.float32) + other.astype(jnp.float32)


def _pair_add_body(me_ref, own_ref, other_ref, out_ref):
    out_ref[...] = (own_ref[...].astype(jnp.float32) + other_ref[...].astype(jnp.float32)).astype(out_ref.dtype)


def core_reduce(x, collective_id):
    got = exchange(x, "core", 2, True, collective_id)
    me = lax.axis_index("core")
    count = x.shape[1]
    rest = x.shape[2:]
    zeros = (0,) * len(rest)
    item_bytes = math.prod(rest) * x.dtype.itemsize
    step = max(d for d in range(1, count + 1) if count % d == 0 and d * item_bytes <= 4 * 1024 * 1024)
    grid_spec = pltpu.PrefetchScalarGridSpec(
        num_scalar_prefetch=1,
        grid=(count // step,),
        in_specs=[
            pl.BlockSpec((None, step) + rest, lambda i, c: (c[0], i) + zeros),
            pl.BlockSpec((None, step) + rest, lambda i, c: (1 - c[0], i) + zeros),
        ],
        out_specs=pl.BlockSpec((step,) + rest, lambda i, c: (i,) + zeros),
    )
    return pl.pallas_call(
        _pair_add_body,
        grid_spec=grid_spec,
        out_shape=jax.ShapeDtypeStruct(x.shape[1:], jnp.bfloat16),
        compiler_params=pltpu.CompilerParams(vmem_limit_bytes=56 * 1024 * 1024),
        cost_estimate=pl.CostEstimate(flops=x.size // 2, transcendentals=0, bytes_accessed=x.size * 3),
    )(jnp.reshape(me, (1,)).astype(jnp.int32), x, got)


def scatter_sum_downward(x, axis, n, collective_id):
    got = exchange(x, axis, n, True, collective_id, downward=True)
    me = lax.axis_index(axis)
    own = lax.dynamic_index_in_dim(x, me, 0, keepdims=False).astype(jnp.float32)
    above = (jnp.arange(n, dtype=jnp.int32) > me).reshape((n,) + (1,) * (x.ndim - 1))
    return own + jnp.sum(jnp.where(above, got.astype(jnp.float32), 0.0), axis=0)


def _flash_body(groups, ctx_ref, q_ref, k_ref, v_ref, qseg_ref, qpos_ref, kseg_ref, o_ref, lse_ref, m_sc, l_sc, acc_sc):
    f32 = jnp.float32
    block = pl.program_id(1)
    depth = HEAD_SIZE
    pair = k_ref.shape[2] // depth

    @pl.when(block == 0)
    def _():
        m_sc[...] = jnp.full_like(m_sc, NEGATIVE)
        l_sc[...] = jnp.zeros_like(l_sc)
        acc_sc[...] = jnp.zeros_like(acc_sc)

    @pl.when(block <= ctx_ref[0])
    def _():
        width = k_ref.shape[1]
        key_pos = block * width + lax.broadcasted_iota(jnp.int32, (1, width), 1)
        allowed = (qseg_ref[...] == kseg_ref[...]) & (key_pos <= qpos_ref[...])
        for kk in range(pair):
            keys = k_ref[0, :, kk * depth : (kk + 1) * depth]
            values = v_ref[0, :, kk * depth : (kk + 1) * depth]
            for gi in range(groups):
                i = kk * groups + gi
                cols = slice(i * depth, (i + 1) * depth)
                scores = lax.dot_general(
                    q_ref[:, cols], keys, (((1,), (1,)), ((), ())), preferred_element_type=f32
                ) * (1.0 / math.sqrt(HEAD_SIZE))
                scores = jnp.where(allowed, scores, NEGATIVE)
                m_old = m_sc[i]
                m_new = jnp.maximum(m_old, jnp.max(scores, axis=1, keepdims=True))
                alpha = jnp.exp(m_old - m_new)
                weights = jnp.where(allowed, jnp.exp(scores - m_new), 0.0)
                l_sc[i] = alpha * l_sc[i] + jnp.sum(weights, axis=1, keepdims=True)
                acc_sc[:, cols] = alpha * acc_sc[:, cols] + jnp.dot(
                    weights.astype(jnp.bfloat16), values, preferred_element_type=f32
                )
                m_sc[i] = m_new

    @pl.when(block == pl.num_programs(1) - 1)
    def _():
        for i in range(m_sc.shape[0]):
            cols = slice(i * depth, (i + 1) * depth)
            o_ref[:, cols] = acc_sc[:, cols] / l_sc[i]
            lse_ref[0, :, i : i + 1] = m_sc[i] + jnp.log(l_sc[i])


def flash_forward(ctx_index, q, kv, qseg, qpos, kseg, groups):
    tokens, q_width = q.shape
    blocks, width, kv_width = kv.shape
    pair = 2
    pairs = kv_width // (2 * pair * HEAD_SIZE)
    heads_step = pair * groups
    f32 = jnp.float32
    capped = lambda p, b, c: (jnp.minimum(b, c[0]), 0, p)
    grid_spec = pltpu.PrefetchScalarGridSpec(
        num_scalar_prefetch=1,
        grid=(pairs, blocks),
        in_specs=[
            pl.BlockSpec((tokens, heads_step * HEAD_SIZE), lambda p, b, c: (0, p)),
            pl.BlockSpec((1, width, pair * HEAD_SIZE), capped),
            pl.BlockSpec((1, width, pair * HEAD_SIZE), lambda p, b, c: (jnp.minimum(b, c[0]), 0, pairs + p)),
            pl.BlockSpec((tokens, 1), lambda p, b, c: (0, 0)),
            pl.BlockSpec((tokens, 1), lambda p, b, c: (0, 0)),
            pl.BlockSpec((1, width), lambda p, b, c: (0, jnp.minimum(b, c[0]))),
        ],
        out_specs=[
            pl.BlockSpec((tokens, heads_step * HEAD_SIZE), lambda p, b, c: (0, p)),
            pl.BlockSpec((1, tokens, heads_step), lambda p, b, c: (p, 0, 0)),
        ],
        scratch_shapes=[
            pltpu.VMEM((heads_step, tokens, 1), f32),
            pltpu.VMEM((heads_step, tokens, 1), f32),
            pltpu.VMEM((tokens, heads_step * HEAD_SIZE), f32),
        ],
    )
    return pl.pallas_call(
        functools.partial(_flash_body, groups),
        grid_spec=grid_spec,
        out_shape=[
            jax.ShapeDtypeStruct((tokens, q_width), f32),
            jax.ShapeDtypeStruct((pairs, tokens, heads_step), f32),
        ],
        compiler_params=pltpu.CompilerParams(
            dimension_semantics=("arbitrary", "arbitrary"), vmem_limit_bytes=48 * 1024 * 1024
        ),
        cost_estimate=pl.CostEstimate(
            flops=tokens * q_width * blocks * width * 4,
            transcendentals=tokens * (q_width // HEAD_SIZE) * blocks * width,
            bytes_accessed=(q.size + kv.size) * 2 + tokens * q_width * 4,
        ),
    )(jnp.reshape(ctx_index, (1,)).astype(jnp.int32), q, kv, kv, qseg, qpos, kseg)

def per_device(
    dpx_count,
    hidden_in,
    attn_gain,
    q_weight,
    key_matrix,
    value_matrix,
    o_weight,
    moe_gain,
    router_weight,
    gate_weight,
    up_weight,
    down_weight,
    segments,
    expert_picks,
    output_grad,
):
    bf16 = jnp.bfloat16
    f32 = jnp.float32
    token_count = hidden_in.shape[0]
    ctx_index = lax.axis_index("ctx")
    heads_local = q_weight.shape[1] // HEAD_SIZE
    kv_local = key_matrix.shape[1] // HEAD_SIZE
    group_size = heads_local // kv_local
    score_scale = 1.0 / math.sqrt(HEAD_SIZE)
    token_positions = ctx_index * token_count + jnp.arange(token_count, dtype=jnp.int32)
    segment_here = lax.dynamic_slice_in_dim(segments, ctx_index * token_count, token_count)
    inputs_f32 = hidden_in.astype(f32)
    o_full = lax.all_gather(o_weight, "tensor", axis=1, tiled=True)
    normed_f32, scale_one = normalize(inputs_f32, attn_gain)
    normed_one = normed_f32.astype(bf16)
    query_rows = jnp.dot(normed_one, q_weight, preferred_element_type=f32).reshape(
        token_count, heads_local, HEAD_SIZE
    )
    keys_raw = jnp.dot(normed_one, key_matrix, preferred_element_type=f32).reshape(
        token_count, kv_local, HEAD_SIZE
    )
    values_raw = jnp.dot(normed_one, value_matrix, preferred_element_type=f32)
    query_grouped = (
        apply_rotary(query_rows, token_positions, 1.0)
        .astype(bf16)
        .reshape(token_count, kv_local, group_size, HEAD_SIZE)
    )
    key_flat = (
        apply_rotary(keys_raw, token_positions, 1.0)
        .astype(bf16)
        .reshape(token_count, kv_local * HEAD_SIZE)
    )
    value_flat = values_raw.astype(bf16)

    def piece_mask(piece_rows):
        key_pos = jnp.arange(piece_rows, dtype=jnp.int32)
        return (segment_here[:, None] == segments[None, :]) & (
            key_pos[None, :] <= token_positions[:, None]
        )

    ctx_count = segments.shape[0] // token_count
    kv_both = gather_axis(jnp.concatenate([key_flat, value_flat], axis=1), "ctx", ctx_count, 1)
    piece_rows = ctx_count * token_count
    kv_width = kv_local * HEAD_SIZE
    key_piece = kv_both[:, :, :kv_width].reshape(piece_rows, kv_local, HEAD_SIZE)
    value_piece = kv_both[:, :, kv_width:].reshape(piece_rows, kv_local, HEAD_SIZE)
    attn_flat, lse_pairs = flash_forward(
        ctx_index,
        query_grouped.reshape(token_count, heads_local * HEAD_SIZE),
        kv_both,
        segment_here[:, None],
        token_positions[:, None],
        segments[None, :],
        group_size,
    )
    attn_grouped = jnp.transpose(
        attn_flat.reshape(token_count, kv_local, group_size, HEAD_SIZE), (1, 2, 0, 3)
    )
    log_sum = jnp.transpose(
        lse_pairs.reshape(kv_local // 2, token_count, 2, group_size), (0, 2, 3, 1)
    ).reshape(kv_local, group_size, token_count)
    attn_bf = attn_flat.astype(bf16)
    tensor_count = o_weight.shape[0] // o_weight.shape[1]
    attn_all = gather_axis(attn_bf, "tensor", tensor_count, 2)
    attn_full = jnp.transpose(attn_all, (1, 0, 2)).reshape(token_count, tensor_count * attn_bf.shape[1])
    mixed_attn = contract_cols(attn_full, o_full)
    resid = inputs_f32 + mixed_attn
    normed_two_f32, scale_two = normalize(resid, moe_gain)
    normed_two = normed_two_f32.astype(bf16)
    logits = jnp.dot(normed_two, router_weight, preferred_element_type=f32)
    expert_range = jnp.arange(NEXP, dtype=jnp.int32)
    picked_onehot = expert_picks[:, :, None] == expert_range[None, None, :]
    picked = jnp.sum(jnp.where(picked_onehot, logits[:, None, :], 0.0), axis=2)
    gate_probs = jax.nn.softmax(picked, axis=-1)
    gates_dense = jnp.sum(jnp.where(picked_onehot, gate_probs[:, :, None], 0.0), axis=1)
    gates_by_expert = jnp.transpose(gates_dense)
    cot_bf = output_grad
    gcol = gates_dense
    grad_gate, grad_up, grad_down, hid_all, dga_all, dua_all = expert_grad_kernel(
        normed_two,
        jnp.transpose(normed_two),
        cot_bf,
        jnp.transpose(cot_bf),
        gcol,
        gates_by_expert[:, None, :],
        gate_weight,
        up_weight,
        down_weight,
        dpx_count,
    )
    gate_half = core_reduce(grad_gate, 8)
    gate_half, hid_all, dga_all, dua_all = lax.optimization_barrier(
        (gate_half, hid_all, dga_all, dua_all)
    )
    moe_acc, gate_parts, moe_grad_rows = expert_rows_kernel(
        hid_all, dga_all, dua_all, cot_bf, gcol, gate_weight, up_weight, down_weight
    )
    cot_f32 = output_grad.astype(f32)
    moe_total = sum_axis(moe_acc.astype(bf16), "tensor", 3)
    output = (resid + moe_total).astype(bf16)
    grad_rows_all = moe_grad_rows
    gate_parts = gate_parts[:, :, 0]
    grad_gate_out, grad_up_out, grad_down_out = [
        lax.psum_scatter(
            g.reshape(g.shape[0], -1, g.shape[3]), ("dpx", "ctx"), scatter_dimension=1, tiled=True
        ).astype(jnp.float32)
        for g in (gate_half, core_reduce(grad_up, 9), core_reduce(grad_down, 10))
    ]
    gate_pair = jnp.sum(
        jnp.where(picked_onehot, jnp.transpose(gate_parts)[:, None, :], 0.0), axis=2
    )
    moe_summed = sum_axis(grad_rows_all.astype(bf16), "tensor", 4)
    gate_summed = sum_axis(gate_pair.astype(bf16), "tensor", 5)
    grad_picked = gate_probs * (
        gate_summed - jnp.sum(gate_probs * gate_summed, axis=1, keepdims=True)
    )
    grad_logits = jnp.sum(jnp.where(picked_onehot, grad_picked[:, :, None], 0.0), axis=1).astype(
        bf16
    )
    grad_router = contract_rows(normed_two, grad_logits)
    grad_normed_two = moe_summed + contract_cols(grad_logits, router_weight)
    grad_two_rows, grad_moe_gain = norm_backward(resid, scale_two, moe_gain, grad_normed_two)
    grad_resid = cot_f32 + grad_two_rows
    grad_mix = grad_resid.astype(bf16)
    grad_o = contract_rows(grad_mix, attn_bf)
    grad_attn = jnp.dot(grad_mix, o_weight, preferred_element_type=f32).astype(bf16)
    grad_attn_grouped = jnp.transpose(
        grad_attn.reshape(token_count, kv_local, group_size, HEAD_SIZE), (1, 2, 0, 3)
    )
    row_delta = jnp.sum(grad_attn_grouped.astype(f32) * attn_grouped, axis=-1)
    allowed = piece_mask(piece_rows)
    scores = (
        jnp.einsum("tkgd,nkd->kgtn", query_grouped, key_piece, preferred_element_type=f32)
        * score_scale
    )
    probability = jnp.where(allowed, jnp.exp(scores - log_sum[..., None]), 0.0)
    grad_probs = jnp.einsum(
        "kgtd,nkd->kgtn", grad_attn_grouped, value_piece, preferred_element_type=f32
    )
    grad_scores = (probability * (grad_probs - row_delta[..., None])).astype(bf16)
    grad_query = score_scale * jnp.einsum(
        "kgtn,nkd->kgtd", grad_scores, key_piece, preferred_element_type=f32
    )
    key_part = score_scale * jnp.einsum(
        "kgtn,tkgd->nkd", grad_scores, query_grouped, preferred_element_type=f32
    )
    value_part = jnp.einsum(
        "kgtn,kgtd->nkd", probability.astype(bf16), grad_attn_grouped, preferred_element_type=f32
    )
    grad_keys_all = key_part.reshape(piece_rows, kv_local * HEAD_SIZE)
    grad_values_all = value_part.reshape(piece_rows, kv_local * HEAD_SIZE)
    back_state = (grad_query, grad_keys_all, grad_values_all)
    grad_query, grad_keys_all, grad_values_all = back_state
    grad_kv_here = scatter_sum_downward(
        jnp.concatenate([grad_keys_all, grad_values_all], axis=1)
        .astype(bf16)
        .reshape(ctx_count, token_count, 2 * kv_width),
        "ctx",
        ctx_count,
        6,
    )
    grad_keys_here = grad_kv_here[:, :kv_width]
    grad_values_here = grad_kv_here[:, kv_width:]
    grad_query_rows = jnp.transpose(grad_query, (2, 0, 1, 3)).reshape(
        token_count, heads_local, HEAD_SIZE
    )
    grad_query_bf = (
        apply_rotary(grad_query_rows, token_positions, -1.0)
        .reshape(token_count, heads_local * HEAD_SIZE)
        .astype(bf16)
    )
    grad_key_bf = (
        apply_rotary(
            grad_keys_here.reshape(token_count, kv_local, HEAD_SIZE), token_positions, -1.0
        )
        .reshape(token_count, kv_local * HEAD_SIZE)
        .astype(bf16)
    )
    grad_value_bf = grad_values_here.astype(bf16)
    grad_q = contract_rows(normed_one, grad_query_bf)
    grad_k = contract_rows(normed_one, grad_key_bf)
    grad_v = contract_rows(normed_one, grad_value_bf)
    partial_one = (
        contract_cols(grad_query_bf, q_weight)
        + contract_cols(grad_key_bf, key_matrix)
        + contract_cols(grad_value_bf, value_matrix)
    )
    grad_normed_one = sum_axis(partial_one.astype(bf16), "tensor", 7)
    grad_one_rows, grad_attn_gain = norm_backward(inputs_f32, scale_one, attn_gain, grad_normed_one)
    input_grad = grad_resid + grad_one_rows
    q_cols, o_cols, k_cols = grad_q.shape[1], grad_o.shape[1], grad_k.shape[1]
    small = jnp.concatenate(
        [
            grad_router,
            grad_attn_gain[:, None],
            grad_moe_gain[:, None],
            jnp.zeros((grad_router.shape[0], 128 - grad_router.shape[1] - 2), f32),
        ],
        axis=1,
    )
    dense_all = jnp.concatenate(
        [grad_q, grad_o, grad_k, grad_v, small], axis=1
    ).astype(bf16)
    width = dense_all.shape[0]
    dense_all = jnp.transpose(
        dense_all.reshape(dpx_count, 2, width // (2 * dpx_count), dense_all.shape[1]), (1, 0, 2, 3)
    )
    dense_all, grad_gate_out, grad_up_out, grad_down_out = lax.optimization_barrier(
        (dense_all, grad_gate_out, grad_up_out, grad_down_out)
    )
    dense_half = core_reduce(dense_all, 11)
    dense_here = lax.psum_scatter(
        dense_half.reshape(-1, dense_half.shape[-1]), ("dpx", "ctx"), scatter_dimension=0, tiled=True
    ).astype(f32)
    spans = [q_cols, o_cols, k_cols, k_cols, router_weight.shape[1], 1, 1]
    cuts = [sum(spans[:i]) for i in range(len(spans) + 1)]
    pieces_out = [dense_here[:, cuts[i] : cuts[i + 1]] for i in range(len(spans))]
    dense_out = (
        pieces_out[5][:, 0],
        pieces_out[0],
        pieces_out[2],
        pieces_out[3],
        pieces_out[1],
        pieces_out[6][:, 0],
        pieces_out[4],
    )
    return (
        output,
        input_grad,
        dense_out[0],
        dense_out[1],
        dense_out[2],
        dense_out[3],
        dense_out[4],
        dense_out[5],
        dense_out[6],
        grad_gate_out,
        grad_up_out,
        grad_down_out,
    )


def solution(mesh):
    dp_count, ctx_count, tensor_count = (mesh.shape[a] for a in ("dp", "ctx", "tensor"))
    split_mesh = jax.sharding.Mesh(
        mesh.devices.reshape(dp_count // 2, 2, ctx_count, tensor_count), ("dpx", "core", "ctx", "tensor")
    )
    return jax.shard_map(
        functools.partial(per_device, dp_count // 2),
        mesh=split_mesh,
        in_specs=(
            P(("dpx", "core", "ctx"), None),
            P(),
            P(None, "tensor"),
            P(None, "tensor"),
            P(None, "tensor"),
            P(None, "tensor"),
            P(),
            P(),
            P(None, None, "tensor"),
            P(None, None, "tensor"),
            P(None, None, "tensor"),
            P(("dpx", "core")),
            P(("dpx", "core", "ctx"), None),
            P(("dpx", "core", "ctx"), None),
        ),
        out_specs=(
            P(("dpx", "core", "ctx"), None),
            P(("dpx", "core", "ctx"), None),
            P(("dpx", "core", "ctx")),
            P(("dpx", "core", "ctx"), "tensor"),
            P(("dpx", "core", "ctx"), "tensor"),
            P(("dpx", "core", "ctx"), "tensor"),
            P(("dpx", "core", "ctx"), "tensor"),
            P(("dpx", "core", "ctx")),
            P(("dpx", "core", "ctx"), None),
            P(None, ("dpx", "core", "ctx"), "tensor"),
            P(None, ("dpx", "core", "ctx"), "tensor"),
            P(None, ("dpx", "core", "ctx"), "tensor"),
        ),
        check_vma=False,
    )
```

```python
import functools
import math

import jax
import jax.numpy as jnp
from jax import lax
from jax.experimental import pallas as pl
from jax.experimental.pallas import tpu as pltpu
from jax.sharding import PartitionSpec as P

HEAD_SIZE = 64
NEXP = 24
CAP = 341


EPSILON = 1e-06
ROPE_BASE = 10000.0
NEGATIVE = -1e30
HIGHEST = lax.Precision.HIGHEST


def normalize(rows, gain):
    scale_inv = lax.rsqrt(jnp.mean(rows * rows, axis=-1, keepdims=True) + EPSILON)
    return (rows * scale_inv * gain, scale_inv)


def norm_backward(rows, scale_inv, gain, grad_normed):
    weighted = gain * grad_normed
    grad_gain = jnp.sum(grad_normed * rows * scale_inv, axis=0)
    inner_mean = jnp.mean(weighted * rows, axis=-1, keepdims=True)
    grad_rows = scale_inv * weighted - rows * scale_inv * scale_inv * scale_inv * inner_mean
    return (grad_rows, grad_gain)


def apply_rotary(value_rows, token_positions, direction):
    half_dim = value_rows.shape[-1] // 2
    frequency = ROPE_BASE ** (-jnp.arange(half_dim, dtype=jnp.float32) / half_dim)
    angles = token_positions.astype(jnp.float32)[:, None] * frequency[None, :]
    cosine = jnp.cos(angles)[:, None, :]
    sine_part = direction * jnp.sin(angles)[:, None, :]
    first_half = value_rows[..., :half_dim]
    second = value_rows[..., half_dim:]
    return jnp.concatenate(
        [first_half * cosine - second * sine_part, second * cosine + first_half * sine_part],
        axis=-1,
    )


def contract_rows(left, right):
    return lax.dot_general(
        left, right, (((0,), (0,)), ((), ())), preferred_element_type=jnp.float32
    )


def contract_rows_exact(left, right):
    return lax.dot_general(
        left, right, (((0,), (0,)), ((), ())), precision=HIGHEST, preferred_element_type=jnp.float32
    )


def contract_cols(left, right):
    return lax.dot_general(
        left, right, (((1,), (1,)), ((), ())), preferred_element_type=jnp.float32
    )


def _store_split(out_ref, value):
    cores, _, groups, rows, _ = out_ref.shape
    for x in range(groups):
        for c in range(cores):
            start = (x * cores + c) * rows
            out_ref[c, 0, x] = value[start : start + rows].astype(out_ref.dtype)


def _gate_column(gates_ref):
    gates = gates_ref[...]
    lane = lax.broadcasted_iota(jnp.int32, gates.shape, 1)
    return jnp.sum(jnp.where(lane == pl.program_id(0), gates, 0.0), axis=1, keepdims=True)


def _grad_body(
    n2_ref, n2t_ref, dy_ref, dyt_ref, gcol_ref, grow_ref, wg_ref, wu_ref, wd_ref,
    gg_ref, gu_ref, gd_ref, hid_ref, dga_ref, dua_ref,
):
    f32 = jnp.float32
    bf16 = jnp.bfloat16
    n2 = n2_ref[...]
    wd = wd_ref[0]
    gate_act = jnp.dot(n2, wg_ref[0], preferred_element_type=f32)
    up_act = jnp.dot(n2, wu_ref[0], preferred_element_type=f32)
    sig = 1.0 / (1.0 + jnp.exp(-gate_act))
    silu = gate_act * sig
    hidden = (silu * up_act).astype(bf16)
    hid_ref[0] = hidden
    deo = (_gate_column(gcol_ref) * dy_ref[...].astype(f32)).astype(bf16)
    grad_hidden = jnp.dot(deo, wd, preferred_element_type=f32)
    deo_t = (grow_ref[0] * dyt_ref[...].astype(f32)).astype(bf16)
    _store_split(gd_ref, jnp.dot(deo_t, hidden, preferred_element_type=f32))
    grad_gate_act = (grad_hidden * up_act * sig * (1.0 + gate_act * (1.0 - sig))).astype(bf16)
    grad_up_act = (grad_hidden * silu).astype(bf16)
    dga_ref[0] = grad_gate_act
    dua_ref[0] = grad_up_act
    n2t = n2t_ref[...]
    _store_split(gg_ref, jnp.dot(n2t, grad_gate_act, preferred_element_type=f32))
    _store_split(gu_ref, jnp.dot(n2t, grad_up_act, preferred_element_type=f32))


def _rows_body(hid_ref, dga_ref, dua_ref, dy_ref, gcol_ref, wg_ref, wu_ref, wd_ref, acc_ref, dgate_ref, dn2_ref):
    f32 = jnp.float32
    nt = (((1,), (1,)), ((), ()))

    @pl.when(pl.program_id(0) == 0)
    def _():
        acc_ref[...] = jnp.zeros_like(acc_ref)
        dn2_ref[...] = jnp.zeros_like(dn2_ref)

    expert_out = lax.dot_general(hid_ref[0], wd_ref[0], nt, preferred_element_type=f32)
    acc_ref[...] += _gate_column(gcol_ref) * expert_out
    dgate_ref[0] = jnp.sum(expert_out * dy_ref[...].astype(f32), axis=1, keepdims=True)
    dn2_ref[...] += lax.dot_general(
        dga_ref[0], wg_ref[0], nt, preferred_element_type=f32
    ) + lax.dot_general(dua_ref[0], wu_ref[0], nt, preferred_element_type=f32)


def expert_grad_kernel(n2, n2t, dy, dyt, gcol, grow, wg, wu, wd, groups):
    tokens, width = n2.shape
    experts, _, hidden = wg.shape
    bf16 = jnp.bfloat16
    whole = lambda shape: pl.BlockSpec(shape, lambda e: (0,) * len(shape))
    per_expert = lambda shape: pl.BlockSpec((1,) + shape, lambda e: (e,) + (0,) * len(shape))
    split_rows = width // (groups * 2)
    split = pl.BlockSpec((2, 1, groups, split_rows, hidden), lambda e: (0, e, 0, 0, 0))
    split_shape = jax.ShapeDtypeStruct((2, experts, groups, split_rows, hidden), bf16)
    act_shape = jax.ShapeDtypeStruct((experts, tokens, hidden), bf16)
    return pl.pallas_call(
        _grad_body,
        grid=(experts,),
        in_specs=[
            whole((tokens, width)),
            whole((width, tokens)),
            whole((tokens, width)),
            whole((width, tokens)),
            whole((tokens, experts)),
            per_expert((1, tokens)),
            per_expert((width, hidden)),
            per_expert((width, hidden)),
            per_expert((width, hidden)),
        ],
        out_specs=[split, split, split]
        + [per_expert((tokens, hidden))] * 3,
        out_shape=[split_shape] * 3 + [act_shape] * 3,
        compiler_params=pltpu.CompilerParams(
            dimension_semantics=("arbitrary",), vmem_limit_bytes=64 * 1024 * 1024
        ),
        cost_estimate=pl.CostEstimate(
            flops=experts * tokens * width * hidden * 2 * 6,
            transcendentals=experts * tokens * hidden,
            bytes_accessed=experts * width * hidden * 12 + tokens * width * 8 + experts * tokens * hidden * 6,
        ),
    )(n2, n2t, dy, dyt, gcol, grow, wg, wu, wd)


def expert_rows_kernel(hid, dga, dua, dy, gcol, wg, wu, wd):
    experts, tokens, hidden = hid.shape
    width = dy.shape[1]
    f32 = jnp.float32
    whole = lambda shape: pl.BlockSpec(shape, lambda e: (0,) * len(shape))
    per_expert = lambda shape: pl.BlockSpec((1,) + shape, lambda e: (e,) + (0,) * len(shape))
    return pl.pallas_call(
        _rows_body,
        grid=(experts,),
        in_specs=[
            per_expert((tokens, hidden)),
            per_expert((tokens, hidden)),
            per_expert((tokens, hidden)),
            whole((tokens, width)),
            whole((tokens, experts)),
            per_expert((width, hidden)),
            per_expert((width, hidden)),
            per_expert((width, hidden)),
        ],
        out_specs=[whole((tokens, width)), per_expert((tokens, 1)), whole((tokens, width))],
        out_shape=[
            jax.ShapeDtypeStruct((tokens, width), f32),
            jax.ShapeDtypeStruct((experts, tokens, 1), f32),
            jax.ShapeDtypeStruct((tokens, width), f32),
        ],
        compiler_params=pltpu.CompilerParams(
            dimension_semantics=("arbitrary",), vmem_limit_bytes=64 * 1024 * 1024
        ),
        cost_estimate=pl.CostEstimate(
            flops=experts * tokens * width * hidden * 2 * 3,
            transcendentals=0,
            bytes_accessed=experts * width * hidden * 6 + tokens * width * 10 + experts * tokens * hidden * 6,
        ),
    )(hid, dga, dua, dy, gcol, wg, wu, wd)

MESH = pl.DeviceIdType.MESH


def _exchange_body(axis, n, per_peer, downward, src_ref, out_ref, send_sems, recv_sems):
    me = lax.axis_index(axis)
    barrier = pltpu.get_barrier_semaphore()
    for k in range(1, n):
        peer = lax.rem(me + k, n)
        pl.semaphore_signal(barrier, 1, device_id={axis: peer}, device_id_type=MESH)
    pl.semaphore_wait(barrier, n - 1)
    sends = []
    for k in range(1, n):
        peer = lax.rem(me + k, n)
        copy = pltpu.make_async_remote_copy(
            src_ref=src_ref.at[peer] if per_peer else src_ref,
            dst_ref=out_ref.at[me],
            send_sem=send_sems.at[k - 1],
            recv_sem=recv_sems.at[k - 1],
            device_id={axis: peer},
            device_id_type=MESH,
        )
        sends.append((peer, copy))
        if downward:
            pl.when(peer < me)(copy.start)
        else:
            copy.start()
    for k in range(1, n):
        source = lax.rem(me + n - k, n)
        incoming = pltpu.make_async_remote_copy(
            src_ref=src_ref.at[source] if per_peer else src_ref,
            dst_ref=out_ref.at[source],
            send_sem=send_sems.at[k - 1],
            recv_sem=recv_sems.at[k - 1],
            device_id={axis: source},
            device_id_type=MESH,
        )
        if downward:
            pl.when(source > me)(incoming.wait_recv)
        else:
            incoming.wait_recv()
    for peer, copy in sends:
        if downward:
            pl.when(peer < me)(copy.wait_send)
        else:
            copy.wait_send()


def exchange(x, axis, n, per_peer, collective_id, downward=False):
    block = x.shape[1:] if per_peer else x.shape
    nbytes = math.prod(block) * x.dtype.itemsize
    return pl.pallas_call(
        functools.partial(_exchange_body, axis, n, per_peer, downward),
        out_shape=jax.ShapeDtypeStruct((n,) + tuple(block), x.dtype),
        in_specs=[pl.BlockSpec(memory_space=pl.ANY)],
        out_specs=pl.BlockSpec(memory_space=pl.ANY),
        scratch_shapes=[pltpu.SemaphoreType.DMA((n - 1,)), pltpu.SemaphoreType.DMA((n - 1,))],
        compiler_params=pltpu.CompilerParams(collective_id=collective_id, has_side_effects=True),
        cost_estimate=pl.CostEstimate(flops=0, transcendentals=0, bytes_accessed=2 * (n - 1) * nbytes),
    )(x)


def gather_axis(x, axis, n, collective_id):
    got = exchange(x, axis, n, False, collective_id)
    return lax.dynamic_update_slice_in_dim(got, x[None], lax.axis_index(axis), 0)


def sum_axis(x, axis, collective_id):
    got = exchange(x, axis, 2, False, collective_id)
    me = lax.axis_index(axis)
    other = lax.dynamic_index_in_dim(got, 1 - me, 0, keepdims=False)
    return x.astype(jnp.float32) + other.astype(jnp.float32)


def _pair_add_body(me_ref, own_ref, other_ref, out_ref):
    out_ref[...] = (own_ref[...].astype(jnp.float32) + other_ref[...].astype(jnp.float32)).astype(out_ref.dtype)


def core_reduce(x, collective_id):
    got = exchange(x, "core", 2, True, collective_id)
    me = lax.axis_index("core")
    count = x.shape[1]
    rest = x.shape[2:]
    zeros = (0,) * len(rest)
    item_bytes = math.prod(rest) * x.dtype.itemsize
    step = max(d for d in range(1, count + 1) if count % d == 0 and d * item_bytes <= 4 * 1024 * 1024)
    grid_spec = pltpu.PrefetchScalarGridSpec(
        num_scalar_prefetch=1,
        grid=(count // step,),
        in_specs=[
            pl.BlockSpec((None, step) + rest, lambda i, c: (c[0], i) + zeros),
            pl.BlockSpec((None, step) + rest, lambda i, c: (1 - c[0], i) + zeros),
        ],
        out_specs=pl.BlockSpec((step,) + rest, lambda i, c: (i,) + zeros),
    )
    return pl.pallas_call(
        _pair_add_body,
        grid_spec=grid_spec,
        out_shape=jax.ShapeDtypeStruct(x.shape[1:], jnp.bfloat16),
        compiler_params=pltpu.CompilerParams(vmem_limit_bytes=56 * 1024 * 1024),
        cost_estimate=pl.CostEstimate(flops=x.size // 2, transcendentals=0, bytes_accessed=x.size * 3),
    )(jnp.reshape(me, (1,)).astype(jnp.int32), x, got)


def scatter_sum_downward(x, axis, n, collective_id):
    got = exchange(x, axis, n, True, collective_id, downward=True)
    me = lax.axis_index(axis)
    own = lax.dynamic_index_in_dim(x, me, 0, keepdims=False).astype(jnp.float32)
    above = (jnp.arange(n, dtype=jnp.int32) > me).reshape((n,) + (1,) * (x.ndim - 1))
    return own + jnp.sum(jnp.where(above, got.astype(jnp.float32), 0.0), axis=0)


def _flash_body(groups, ctx_ref, q_ref, k_ref, v_ref, qseg_ref, qpos_ref, kseg_ref, o_ref, lse_ref, m_sc, l_sc, acc_sc):
    f32 = jnp.float32
    block = pl.program_id(1)
    depth = HEAD_SIZE
    pair = k_ref.shape[2] // depth

    @pl.when(block == 0)
    def _():
        m_sc[...] = jnp.full_like(m_sc, NEGATIVE)
        l_sc[...] = jnp.zeros_like(l_sc)
        acc_sc[...] = jnp.zeros_like(acc_sc)

    @pl.when(block <= ctx_ref[0])
    def _():
        width = k_ref.shape[1]
        key_pos = block * width + lax.broadcasted_iota(jnp.int32, (1, width), 1)
        allowed = (qseg_ref[...] == kseg_ref[...]) & (key_pos <= qpos_ref[...])
        for kk in range(pair):
            keys = k_ref[0, :, kk * depth : (kk + 1) * depth]
            values = v_ref[0, :, kk * depth : (kk + 1) * depth]
            for gi in range(groups):
                i = kk * groups + gi
                cols = slice(i * depth, (i + 1) * depth)
                scores = lax.dot_general(
                    q_ref[:, cols], keys, (((1,), (1,)), ((), ())), preferred_element_type=f32
                ) * (1.0 / math.sqrt(HEAD_SIZE))
                scores = jnp.where(allowed, scores, NEGATIVE)
                m_old = m_sc[i]
                m_new = jnp.maximum(m_old, jnp.max(scores, axis=1, keepdims=True))
                alpha = jnp.exp(m_old - m_new)
                weights = jnp.where(allowed, jnp.exp(scores - m_new), 0.0)
                l_sc[i] = alpha * l_sc[i] + jnp.sum(weights, axis=1, keepdims=True)
                acc_sc[:, cols] = alpha * acc_sc[:, cols] + jnp.dot(
                    weights.astype(jnp.bfloat16), values, preferred_element_type=f32
                )
                m_sc[i] = m_new

    @pl.when(block == pl.num_programs(1) - 1)
    def _():
        for i in range(m_sc.shape[0]):
            cols = slice(i * depth, (i + 1) * depth)
            o_ref[:, cols] = acc_sc[:, cols] / l_sc[i]
            lse_ref[0, :, i : i + 1] = m_sc[i] + jnp.log(l_sc[i])


def flash_forward(ctx_index, q, kv, qseg, qpos, kseg, groups):
    tokens, q_width = q.shape
    blocks, width, kv_width = kv.shape
    pair = 2
    pairs = kv_width // (2 * pair * HEAD_SIZE)
    heads_step = pair * groups
    f32 = jnp.float32
    capped = lambda p, b, c: (jnp.minimum(b, c[0]), 0, p)
    grid_spec = pltpu.PrefetchScalarGridSpec(
        num_scalar_prefetch=1,
        grid=(pairs, blocks),
        in_specs=[
            pl.BlockSpec((tokens, heads_step * HEAD_SIZE), lambda p, b, c: (0, p)),
            pl.BlockSpec((1, width, pair * HEAD_SIZE), capped),
            pl.BlockSpec((1, width, pair * HEAD_SIZE), lambda p, b, c: (jnp.minimum(b, c[0]), 0, pairs + p)),
            pl.BlockSpec((tokens, 1), lambda p, b, c: (0, 0)),
            pl.BlockSpec((tokens, 1), lambda p, b, c: (0, 0)),
            pl.BlockSpec((1, width), lambda p, b, c: (0, jnp.minimum(b, c[0]))),
        ],
        out_specs=[
            pl.BlockSpec((tokens, heads_step * HEAD_SIZE), lambda p, b, c: (0, p)),
            pl.BlockSpec((1, tokens, heads_step), lambda p, b, c: (p, 0, 0)),
        ],
        scratch_shapes=[
            pltpu.VMEM((heads_step, tokens, 1), f32),
            pltpu.VMEM((heads_step, tokens, 1), f32),
            pltpu.VMEM((tokens, heads_step * HEAD_SIZE), f32),
        ],
    )
    return pl.pallas_call(
        functools.partial(_flash_body, groups),
        grid_spec=grid_spec,
        out_shape=[
            jax.ShapeDtypeStruct((tokens, q_width), f32),
            jax.ShapeDtypeStruct((pairs, tokens, heads_step), f32),
        ],
        compiler_params=pltpu.CompilerParams(
            dimension_semantics=("arbitrary", "arbitrary"), vmem_limit_bytes=48 * 1024 * 1024
        ),
        cost_estimate=pl.CostEstimate(
            flops=tokens * q_width * blocks * width * 4,
            transcendentals=tokens * (q_width // HEAD_SIZE) * blocks * width,
            bytes_accessed=(q.size + kv.size) * 2 + tokens * q_width * 4,
        ),
    )(jnp.reshape(ctx_index, (1,)).astype(jnp.int32), q, kv, kv, qseg, qpos, kseg)

def per_device(
    dpx_count,
    hidden_in,
    attn_gain,
    q_weight,
    key_matrix,
    value_matrix,
    o_weight,
    moe_gain,
    router_weight,
    gate_weight,
    up_weight,
    down_weight,
    segments,
    expert_picks,
    output_grad,
):
    bf16 = jnp.bfloat16
    f32 = jnp.float32
    token_count = hidden_in.shape[0]
    ctx_index = lax.axis_index("ctx")
    heads_local = q_weight.shape[1] // HEAD_SIZE
    kv_local = key_matrix.shape[1] // HEAD_SIZE
    group_size = heads_local // kv_local
    score_scale = 1.0 / math.sqrt(HEAD_SIZE)
    token_positions = ctx_index * token_count + jnp.arange(token_count, dtype=jnp.int32)
    segment_here = lax.dynamic_slice_in_dim(segments, ctx_index * token_count, token_count)
    inputs_f32 = hidden_in.astype(f32)
    o_full = lax.all_gather(o_weight, "tensor", axis=1, tiled=True)
    normed_f32, scale_one = normalize(inputs_f32, attn_gain)
    normed_one = normed_f32.astype(bf16)
    query_rows = jnp.dot(normed_one, q_weight, preferred_element_type=f32).reshape(
        token_count, heads_local, HEAD_SIZE
    )
    keys_raw = jnp.dot(normed_one, key_matrix, preferred_element_type=f32).reshape(
        token_count, kv_local, HEAD_SIZE
    )
    values_raw = jnp.dot(normed_one, value_matrix, preferred_element_type=f32)
    query_grouped = (
        apply_rotary(query_rows, token_positions, 1.0)
        .astype(bf16)
        .reshape(token_count, kv_local, group_size, HEAD_SIZE)
    )
    key_flat = (
        apply_rotary(keys_raw, token_positions, 1.0)
        .astype(bf16)
        .reshape(token_count, kv_local * HEAD_SIZE)
    )
    value_flat = values_raw.astype(bf16)

    def piece_mask(piece_rows):
        key_pos = jnp.arange(piece_rows, dtype=jnp.int32)
        return (segment_here[:, None] == segments[None, :]) & (
            key_pos[None, :] <= token_positions[:, None]
        )

    ctx_count = segments.shape[0] // token_count
    kv_both = gather_axis(jnp.concatenate([key_flat, value_flat], axis=1), "ctx", ctx_count, 1)
    piece_rows = ctx_count * token_count
    kv_width = kv_local * HEAD_SIZE
    key_piece = kv_both[:, :, :kv_width].reshape(piece_rows, kv_local, HEAD_SIZE)
    value_piece = kv_both[:, :, kv_width:].reshape(piece_rows, kv_local, HEAD_SIZE)
    attn_flat, lse_pairs = flash_forward(
        ctx_index,
        query_grouped.reshape(token_count, heads_local * HEAD_SIZE),
        kv_both,
        segment_here[:, None],
        token_positions[:, None],
        segments[None, :],
        group_size,
    )
    attn_grouped = jnp.transpose(
        attn_flat.reshape(token_count, kv_local, group_size, HEAD_SIZE), (1, 2, 0, 3)
    )
    log_sum = jnp.transpose(
        lse_pairs.reshape(kv_local // 2, token_count, 2, group_size), (0, 2, 3, 1)
    ).reshape(kv_local, group_size, token_count)
    attn_bf = attn_flat.astype(bf16)
    tensor_count = o_weight.shape[0] // o_weight.shape[1]
    attn_all = gather_axis(attn_bf, "tensor", tensor_count, 2)
    attn_full = jnp.transpose(attn_all, (1, 0, 2)).reshape(token_count, tensor_count * attn_bf.shape[1])
    mixed_attn = contract_cols(attn_full, o_full)
    resid = inputs_f32 + mixed_attn
    normed_two_f32, scale_two = normalize(resid, moe_gain)
    normed_two = normed_two_f32.astype(bf16)
    logits = jnp.dot(normed_two, router_weight, preferred_element_type=f32)
    expert_range = jnp.arange(NEXP, dtype=jnp.int32)
    picked_onehot = expert_picks[:, :, None] == expert_range[None, None, :]
    picked = jnp.sum(jnp.where(picked_onehot, logits[:, None, :], 0.0), axis=2)
    gate_probs = jax.nn.softmax(picked, axis=-1)
    gates_dense = jnp.sum(jnp.where(picked_onehot, gate_probs[:, :, None], 0.0), axis=1)
    gates_by_expert = jnp.transpose(gates_dense)
    cot_bf = output_grad
    gcol = gates_dense
    grad_gate, grad_up, grad_down, hid_all, dga_all, dua_all = expert_grad_kernel(
        normed_two,
        jnp.transpose(normed_two),
        cot_bf,
        jnp.transpose(cot_bf),
        gcol,
        gates_by_expert[:, None, :],
        gate_weight,
        up_weight,
        down_weight,
        dpx_count,
    )
    gate_half = core_reduce(grad_gate, 8)
    gate_half, hid_all, dga_all, dua_all = lax.optimization_barrier(
        (gate_half, hid_all, dga_all, dua_all)
    )
    moe_acc, gate_parts, moe_grad_rows = expert_rows_kernel(
        hid_all, dga_all, dua_all, cot_bf, gcol, gate_weight, up_weight, down_weight
    )
    cot_f32 = output_grad.astype(f32)
    moe_acc_bf = moe_acc.astype(bf16)
    grad_rows_all = moe_grad_rows
    gate_parts = gate_parts[:, :, 0]
    grad_gate_out, grad_up_out, grad_down_out = [
        lax.psum_scatter(
            g.reshape(g.shape[0], -1, g.shape[3]), ("dpx", "ctx"), scatter_dimension=1, tiled=True
        ).astype(jnp.float32)
        for g in (gate_half, core_reduce(grad_up, 9), core_reduce(grad_down, 10))
    ]
    gate_pair = jnp.sum(
        jnp.where(picked_onehot, jnp.transpose(gate_parts)[:, None, :], 0.0), axis=2
    )
    moe_summed = sum_axis(grad_rows_all.astype(bf16), "tensor", 4)
    gate_summed = sum_axis(gate_pair.astype(bf16), "tensor", 5)
    grad_picked = gate_probs * (
        gate_summed - jnp.sum(gate_probs * gate_summed, axis=1, keepdims=True)
    )
    grad_logits = jnp.sum(jnp.where(picked_onehot, grad_picked[:, :, None], 0.0), axis=1).astype(
        bf16
    )
    grad_router = contract_rows(normed_two, grad_logits)
    grad_normed_two = moe_summed + contract_cols(grad_logits, router_weight)
    grad_two_rows, grad_moe_gain = norm_backward(resid, scale_two, moe_gain, grad_normed_two)
    grad_resid = cot_f32 + grad_two_rows
    grad_mix = grad_resid.astype(bf16)
    grad_o = contract_rows(grad_mix, attn_bf)
    grad_attn = jnp.dot(grad_mix, o_weight, preferred_element_type=f32).astype(bf16)
    grad_attn_grouped = jnp.transpose(
        grad_attn.reshape(token_count, kv_local, group_size, HEAD_SIZE), (1, 2, 0, 3)
    )
    row_delta = jnp.sum(grad_attn_grouped.astype(f32) * attn_grouped, axis=-1)
    allowed = piece_mask(piece_rows)
    scores = (
        jnp.einsum("tkgd,nkd->kgtn", query_grouped, key_piece, preferred_element_type=f32)
        * score_scale
    )
    probability = jnp.where(allowed, jnp.exp(scores - log_sum[..., None]), 0.0)
    grad_probs = jnp.einsum(
        "kgtd,nkd->kgtn", grad_attn_grouped, value_piece, preferred_element_type=f32
    )
    grad_scores = (probability * (grad_probs - row_delta[..., None])).astype(bf16)
    grad_query = score_scale * jnp.einsum(
        "kgtn,nkd->kgtd", grad_scores, key_piece, preferred_element_type=f32
    )
    key_part = score_scale * jnp.einsum(
        "kgtn,tkgd->nkd", grad_scores, query_grouped, preferred_element_type=f32
    )
    value_part = jnp.einsum(
        "kgtn,kgtd->nkd", probability.astype(bf16), grad_attn_grouped, preferred_element_type=f32
    )
    grad_keys_all = key_part.reshape(piece_rows, kv_local * HEAD_SIZE)
    grad_values_all = value_part.reshape(piece_rows, kv_local * HEAD_SIZE)
    back_state = (grad_query, grad_keys_all, grad_values_all)
    grad_query, grad_keys_all, grad_values_all = back_state
    grad_kv_here = scatter_sum_downward(
        jnp.concatenate([grad_keys_all, grad_values_all], axis=1)
        .astype(bf16)
        .reshape(ctx_count, token_count, 2 * kv_width),
        "ctx",
        ctx_count,
        6,
    )
    grad_keys_here = grad_kv_here[:, :kv_width]
    grad_values_here = grad_kv_here[:, kv_width:]
    grad_query_rows = jnp.transpose(grad_query, (2, 0, 1, 3)).reshape(
        token_count, heads_local, HEAD_SIZE
    )
    grad_query_bf = (
        apply_rotary(grad_query_rows, token_positions, -1.0)
        .reshape(token_count, heads_local * HEAD_SIZE)
        .astype(bf16)
    )
    grad_key_bf = (
        apply_rotary(
            grad_keys_here.reshape(token_count, kv_local, HEAD_SIZE), token_positions, -1.0
        )
        .reshape(token_count, kv_local * HEAD_SIZE)
        .astype(bf16)
    )
    grad_value_bf = grad_values_here.astype(bf16)
    grad_q = contract_rows(normed_one, grad_query_bf)
    grad_k = contract_rows(normed_one, grad_key_bf)
    grad_v = contract_rows(normed_one, grad_value_bf)
    partial_one = (
        contract_cols(grad_query_bf, q_weight)
        + contract_cols(grad_key_bf, key_matrix)
        + contract_cols(grad_value_bf, value_matrix)
    )
    grad_normed_one = sum_axis(partial_one.astype(bf16), "tensor", 7)
    grad_one_rows, grad_attn_gain = norm_backward(inputs_f32, scale_one, attn_gain, grad_normed_one)
    input_grad = grad_resid + grad_one_rows
    q_cols, o_cols, k_cols = grad_q.shape[1], grad_o.shape[1], grad_k.shape[1]
    small = jnp.concatenate(
        [
            grad_router,
            grad_attn_gain[:, None],
            grad_moe_gain[:, None],
            jnp.zeros((grad_router.shape[0], 128 - grad_router.shape[1] - 2), f32),
        ],
        axis=1,
    )
    dense_all = jnp.concatenate(
        [grad_q, grad_o, grad_k, grad_v, small], axis=1
    ).astype(bf16)
    width = dense_all.shape[0]
    dense_all = jnp.transpose(
        dense_all.reshape(dpx_count, 2, width // (2 * dpx_count), dense_all.shape[1]), (1, 0, 2, 3)
    )
    dense_all, grad_gate_out, grad_up_out, grad_down_out = lax.optimization_barrier(
        (dense_all, grad_gate_out, grad_up_out, grad_down_out)
    )
    moe_acc_bf, dense_all = lax.optimization_barrier((moe_acc_bf, dense_all))
    output = (resid + sum_axis(moe_acc_bf, "tensor", 3)).astype(bf16)
    dense_half = core_reduce(dense_all, 11)
    dense_here = lax.psum_scatter(
        dense_half.reshape(-1, dense_half.shape[-1]), ("dpx", "ctx"), scatter_dimension=0, tiled=True
    ).astype(f32)
    spans = [q_cols, o_cols, k_cols, k_cols, router_weight.shape[1], 1, 1]
    cuts = [sum(spans[:i]) for i in range(len(spans) + 1)]
    pieces_out = [dense_here[:, cuts[i] : cuts[i + 1]] for i in range(len(spans))]
    dense_out = (
        pieces_out[5][:, 0],
        pieces_out[0],
        pieces_out[2],
        pieces_out[3],
        pieces_out[1],
        pieces_out[6][:, 0],
        pieces_out[4],
    )
    return (
        output,
        input_grad,
        dense_out[0],
        dense_out[1],
        dense_out[2],
        dense_out[3],
        dense_out[4],
        dense_out[5],
        dense_out[6],
        grad_gate_out,
        grad_up_out,
        grad_down_out,
    )


def solution(mesh):
    dp_count, ctx_count, tensor_count = (mesh.shape[a] for a in ("dp", "ctx", "tensor"))
    split_mesh = jax.sharding.Mesh(
        mesh.devices.reshape(dp_count // 2, 2, ctx_count, tensor_count), ("dpx", "core", "ctx", "tensor")
    )
    return jax.shard_map(
        functools.partial(per_device, dp_count // 2),
        mesh=split_mesh,
        in_specs=(
            P(("dpx", "core", "ctx"), None),
            P(),
            P(None, "tensor"),
            P(None, "tensor"),
            P(None, "tensor"),
            P(None, "tensor"),
            P(),
            P(),
            P(None, None, "tensor"),
            P(None, None, "tensor"),
            P(None, None, "tensor"),
            P(("dpx", "core")),
            P(("dpx", "core", "ctx"), None),
            P(("dpx", "core", "ctx"), None),
        ),
        out_specs=(
            P(("dpx", "core", "ctx"), None),
            P(("dpx", "core", "ctx"), None),
            P(("dpx", "core", "ctx")),
            P(("dpx", "core", "ctx"), "tensor"),
            P(("dpx", "core", "ctx"), "tensor"),
            P(("dpx", "core", "ctx"), "tensor"),
            P(("dpx", "core", "ctx"), "tensor"),
            P(("dpx", "core", "ctx")),
            P(("dpx", "core", "ctx"), None),
            P(None, ("dpx", "core", "ctx"), "tensor"),
            P(None, ("dpx", "core", "ctx"), "tensor"),
            P(None, ("dpx", "core", "ctx"), "tensor"),
        ),
        check_vma=False,
    )
```

```python
import functools
import math

import jax
import jax.numpy as jnp
from jax import lax
from jax.experimental import pallas as pl
from jax.experimental.pallas import tpu as pltpu
from jax.sharding import PartitionSpec as P

HEAD_SIZE = 64
NEXP = 24
CAP = 341


EPSILON = 1e-06
ROPE_BASE = 10000.0
NEGATIVE = -1e30
HIGHEST = lax.Precision.HIGHEST


def normalize(rows, gain):
    scale_inv = lax.rsqrt(jnp.mean(rows * rows, axis=-1, keepdims=True) + EPSILON)
    return (rows * scale_inv * gain, scale_inv)


def norm_backward(rows, scale_inv, gain, grad_normed):
    weighted = gain * grad_normed
    grad_gain = jnp.sum(grad_normed * rows * scale_inv, axis=0)
    inner_mean = jnp.mean(weighted * rows, axis=-1, keepdims=True)
    grad_rows = scale_inv * weighted - rows * scale_inv * scale_inv * scale_inv * inner_mean
    return (grad_rows, grad_gain)


def apply_rotary(value_rows, token_positions, direction):
    half_dim = value_rows.shape[-1] // 2
    frequency = ROPE_BASE ** (-jnp.arange(half_dim, dtype=jnp.float32) / half_dim)
    angles = token_positions.astype(jnp.float32)[:, None] * frequency[None, :]
    cosine = jnp.cos(angles)[:, None, :]
    sine_part = direction * jnp.sin(angles)[:, None, :]
    first_half = value_rows[..., :half_dim]
    second = value_rows[..., half_dim:]
    return jnp.concatenate(
        [first_half * cosine - second * sine_part, second * cosine + first_half * sine_part],
        axis=-1,
    )


def contract_rows(left, right):
    return lax.dot_general(
        left, right, (((0,), (0,)), ((), ())), preferred_element_type=jnp.float32
    )


def contract_rows_exact(left, right):
    return lax.dot_general(
        left, right, (((0,), (0,)), ((), ())), precision=HIGHEST, preferred_element_type=jnp.float32
    )


def contract_cols(left, right):
    return lax.dot_general(
        left, right, (((1,), (1,)), ((), ())), preferred_element_type=jnp.float32
    )


def _store_split(out_ref, value):
    cores, _, groups, rows, _ = out_ref.shape
    for x in range(groups):
        for c in range(cores):
            start = (x * cores + c) * rows
            out_ref[c, 0, x] = value[start : start + rows].astype(out_ref.dtype)


def _gate_column(gates_ref):
    gates = gates_ref[...]
    lane = lax.broadcasted_iota(jnp.int32, gates.shape, 1)
    return jnp.sum(jnp.where(lane == pl.program_id(0), gates, 0.0), axis=1, keepdims=True)


def _grad_body(
    n2_ref, n2t_ref, dy_ref, dyt_ref, gcol_ref, grow_ref, wg_ref, wu_ref, wd_ref,
    gg_ref, gu_ref, gd_ref, hid_ref, dga_ref, dua_ref,
):
    f32 = jnp.float32
    bf16 = jnp.bfloat16
    n2 = n2_ref[...]
    wd = wd_ref[0]
    gate_act = jnp.dot(n2, wg_ref[0], preferred_element_type=f32)
    up_act = jnp.dot(n2, wu_ref[0], preferred_element_type=f32)
    sig = 1.0 / (1.0 + jnp.exp(-gate_act))
    silu = gate_act * sig
    hidden = (silu * up_act).astype(bf16)
    hid_ref[0] = hidden
    deo = (_gate_column(gcol_ref) * dy_ref[...].astype(f32)).astype(bf16)
    grad_hidden = jnp.dot(deo, wd, preferred_element_type=f32)
    deo_t = (grow_ref[0] * dyt_ref[...].astype(f32)).astype(bf16)
    _store_split(gd_ref, jnp.dot(deo_t, hidden, preferred_element_type=f32))
    grad_gate_act = (grad_hidden * up_act * sig * (1.0 + gate_act * (1.0 - sig))).astype(bf16)
    grad_up_act = (grad_hidden * silu).astype(bf16)
    dga_ref[0] = grad_gate_act
    dua_ref[0] = grad_up_act
    n2t = n2t_ref[...]
    _store_split(gg_ref, jnp.dot(n2t, grad_gate_act, preferred_element_type=f32))
    _store_split(gu_ref, jnp.dot(n2t, grad_up_act, preferred_element_type=f32))


def _rows_body(hid_ref, dga_ref, dua_ref, dy_ref, gcol_ref, wg_ref, wu_ref, wd_ref, acc_ref, dgate_ref, dn2_ref):
    f32 = jnp.float32
    nt = (((1,), (1,)), ((), ()))

    @pl.when(pl.program_id(0) == 0)
    def _():
        acc_ref[...] = jnp.zeros_like(acc_ref)
        dn2_ref[...] = jnp.zeros_like(dn2_ref)

    expert_out = lax.dot_general(hid_ref[0], wd_ref[0], nt, preferred_element_type=f32)
    acc_ref[...] += _gate_column(gcol_ref) * expert_out
    dgate_ref[0] = jnp.sum(expert_out * dy_ref[...].astype(f32), axis=1, keepdims=True)
    dn2_ref[...] += lax.dot_general(
        dga_ref[0], wg_ref[0], nt, preferred_element_type=f32
    ) + lax.dot_general(dua_ref[0], wu_ref[0], nt, preferred_element_type=f32)


def expert_grad_kernel(n2, n2t, dy, dyt, gcol, grow, wg, wu, wd, groups):
    tokens, width = n2.shape
    experts, _, hidden = wg.shape
    bf16 = jnp.bfloat16
    whole = lambda shape: pl.BlockSpec(shape, lambda e: (0,) * len(shape))
    per_expert = lambda shape: pl.BlockSpec((1,) + shape, lambda e: (e,) + (0,) * len(shape))
    split_rows = width // (groups * 2)
    split = pl.BlockSpec((2, 1, groups, split_rows, hidden), lambda e: (0, e, 0, 0, 0))
    split_shape = jax.ShapeDtypeStruct((2, experts, groups, split_rows, hidden), bf16)
    act_shape = jax.ShapeDtypeStruct((experts, tokens, hidden), bf16)
    return pl.pallas_call(
        _grad_body,
        grid=(experts,),
        in_specs=[
            whole((tokens, width)),
            whole((width, tokens)),
            whole((tokens, width)),
            whole((width, tokens)),
            whole((tokens, experts)),
            per_expert((1, tokens)),
            per_expert((width, hidden)),
            per_expert((width, hidden)),
            per_expert((width, hidden)),
        ],
        out_specs=[split, split, split]
        + [per_expert((tokens, hidden))] * 3,
        out_shape=[split_shape] * 3 + [act_shape] * 3,
        compiler_params=pltpu.CompilerParams(
            dimension_semantics=("arbitrary",), vmem_limit_bytes=64 * 1024 * 1024
        ),
        cost_estimate=pl.CostEstimate(
            flops=experts * tokens * width * hidden * 2 * 6,
            transcendentals=experts * tokens * hidden,
            bytes_accessed=experts * width * hidden * 12 + tokens * width * 8 + experts * tokens * hidden * 6,
        ),
    )(n2, n2t, dy, dyt, gcol, grow, wg, wu, wd)


def expert_rows_kernel(hid, dga, dua, dy, gcol, wg, wu, wd):
    experts, tokens, hidden = hid.shape
    width = dy.shape[1]
    f32 = jnp.float32
    whole = lambda shape: pl.BlockSpec(shape, lambda e: (0,) * len(shape))
    per_expert = lambda shape: pl.BlockSpec((1,) + shape, lambda e: (e,) + (0,) * len(shape))
    return pl.pallas_call(
        _rows_body,
        grid=(experts,),
        in_specs=[
            per_expert((tokens, hidden)),
            per_expert((tokens, hidden)),
            per_expert((tokens, hidden)),
            whole((tokens, width)),
            whole((tokens, experts)),
            per_expert((width, hidden)),
            per_expert((width, hidden)),
            per_expert((width, hidden)),
        ],
        out_specs=[whole((tokens, width)), per_expert((tokens, 1)), whole((tokens, width))],
        out_shape=[
            jax.ShapeDtypeStruct((tokens, width), f32),
            jax.ShapeDtypeStruct((experts, tokens, 1), f32),
            jax.ShapeDtypeStruct((tokens, width), f32),
        ],
        compiler_params=pltpu.CompilerParams(
            dimension_semantics=("arbitrary",), vmem_limit_bytes=64 * 1024 * 1024
        ),
        cost_estimate=pl.CostEstimate(
            flops=experts * tokens * width * hidden * 2 * 3,
            transcendentals=0,
            bytes_accessed=experts * width * hidden * 6 + tokens * width * 10 + experts * tokens * hidden * 6,
        ),
    )(hid, dga, dua, dy, gcol, wg, wu, wd)

MESH = pl.DeviceIdType.MESH


def _exchange_body(axis, n, per_peer, downward, src_ref, out_ref, send_sems, recv_sems):
    me = lax.axis_index(axis)
    barrier = pltpu.get_barrier_semaphore()
    for k in range(1, n):
        peer = lax.rem(me + k, n)
        pl.semaphore_signal(barrier, 1, device_id={axis: peer}, device_id_type=MESH)
    pl.semaphore_wait(barrier, n - 1)
    sends = []
    for k in range(1, n):
        peer = lax.rem(me + k, n)
        copy = pltpu.make_async_remote_copy(
            src_ref=src_ref.at[peer] if per_peer else src_ref,
            dst_ref=out_ref.at[me],
            send_sem=send_sems.at[k - 1],
            recv_sem=recv_sems.at[k - 1],
            device_id={axis: peer},
            device_id_type=MESH,
        )
        sends.append((peer, copy))
        if downward:
            pl.when(peer < me)(copy.start)
        else:
            copy.start()
    for k in range(1, n):
        source = lax.rem(me + n - k, n)
        incoming = pltpu.make_async_remote_copy(
            src_ref=src_ref.at[source] if per_peer else src_ref,
            dst_ref=out_ref.at[source],
            send_sem=send_sems.at[k - 1],
            recv_sem=recv_sems.at[k - 1],
            device_id={axis: source},
            device_id_type=MESH,
        )
        if downward:
            pl.when(source > me)(incoming.wait_recv)
        else:
            incoming.wait_recv()
    for peer, copy in sends:
        if downward:
            pl.when(peer < me)(copy.wait_send)
        else:
            copy.wait_send()


def exchange(x, axis, n, per_peer, collective_id, downward=False):
    block = x.shape[1:] if per_peer else x.shape
    nbytes = math.prod(block) * x.dtype.itemsize
    return pl.pallas_call(
        functools.partial(_exchange_body, axis, n, per_peer, downward),
        out_shape=jax.ShapeDtypeStruct((n,) + tuple(block), x.dtype),
        in_specs=[pl.BlockSpec(memory_space=pl.ANY)],
        out_specs=pl.BlockSpec(memory_space=pl.ANY),
        scratch_shapes=[pltpu.SemaphoreType.DMA((n - 1,)), pltpu.SemaphoreType.DMA((n - 1,))],
        compiler_params=pltpu.CompilerParams(collective_id=collective_id, has_side_effects=True),
        cost_estimate=pl.CostEstimate(flops=0, transcendentals=0, bytes_accessed=2 * (n - 1) * nbytes),
    )(x)


def gather_axis(x, axis, n, collective_id):
    got = exchange(x, axis, n, False, collective_id)
    return lax.dynamic_update_slice_in_dim(got, x[None], lax.axis_index(axis), 0)


def sum_axis(x, axis, collective_id):
    got = exchange(x, axis, 2, False, collective_id)
    me = lax.axis_index(axis)
    other = lax.dynamic_index_in_dim(got, 1 - me, 0, keepdims=False)
    return x.astype(jnp.float32) + other.astype(jnp.float32)


def _pair_add_body(me_ref, own_ref, other_ref, out_ref):
    out_ref[...] = (own_ref[...].astype(jnp.float32) + other_ref[...].astype(jnp.float32)).astype(out_ref.dtype)


def core_reduce(x, collective_id):
    got = exchange(x, "core", 2, True, collective_id)
    me = lax.axis_index("core")
    count = x.shape[1]
    rest = x.shape[2:]
    zeros = (0,) * len(rest)
    item_bytes = math.prod(rest) * x.dtype.itemsize
    step = max(d for d in range(1, count + 1) if count % d == 0 and d * item_bytes <= 4 * 1024 * 1024)
    grid_spec = pltpu.PrefetchScalarGridSpec(
        num_scalar_prefetch=1,
        grid=(count // step,),
        in_specs=[
            pl.BlockSpec((None, step) + rest, lambda i, c: (c[0], i) + zeros),
            pl.BlockSpec((None, step) + rest, lambda i, c: (1 - c[0], i) + zeros),
        ],
        out_specs=pl.BlockSpec((step,) + rest, lambda i, c: (i,) + zeros),
    )
    return pl.pallas_call(
        _pair_add_body,
        grid_spec=grid_spec,
        out_shape=jax.ShapeDtypeStruct(x.shape[1:], jnp.bfloat16),
        compiler_params=pltpu.CompilerParams(vmem_limit_bytes=56 * 1024 * 1024),
        cost_estimate=pl.CostEstimate(flops=x.size // 2, transcendentals=0, bytes_accessed=x.size * 3),
    )(jnp.reshape(me, (1,)).astype(jnp.int32), x, got)


def scatter_sum_downward(x, axis, n, collective_id):
    got = exchange(x, axis, n, True, collective_id, downward=True)
    me = lax.axis_index(axis)
    own = lax.dynamic_index_in_dim(x, me, 0, keepdims=False).astype(jnp.float32)
    above = (jnp.arange(n, dtype=jnp.int32) > me).reshape((n,) + (1,) * (x.ndim - 1))
    return own + jnp.sum(jnp.where(above, got.astype(jnp.float32), 0.0), axis=0)


def _flash_body(groups, ctx_ref, q_ref, k_ref, v_ref, qseg_ref, qpos_ref, kseg_ref, o_ref, lse_ref, m_sc, l_sc, acc_sc):
    f32 = jnp.float32
    block = pl.program_id(1)
    depth = HEAD_SIZE
    pair = k_ref.shape[2] // depth

    @pl.when(block == 0)
    def _():
        m_sc[...] = jnp.full_like(m_sc, NEGATIVE)
        l_sc[...] = jnp.zeros_like(l_sc)
        acc_sc[...] = jnp.zeros_like(acc_sc)

    @pl.when(block <= ctx_ref[0])
    def _():
        width = k_ref.shape[1]
        key_pos = block * width + lax.broadcasted_iota(jnp.int32, (1, width), 1)
        allowed = (qseg_ref[...] == kseg_ref[...]) & (key_pos <= qpos_ref[...])
        for kk in range(pair):
            keys = k_ref[0, :, kk * depth : (kk + 1) * depth]
            values = v_ref[0, :, kk * depth : (kk + 1) * depth]
            for gi in range(groups):
                i = kk * groups + gi
                cols = slice(i * depth, (i + 1) * depth)
                scores = lax.dot_general(
                    q_ref[:, cols], keys, (((1,), (1,)), ((), ())), preferred_element_type=f32
                ) * (1.0 / math.sqrt(HEAD_SIZE))
                scores = jnp.where(allowed, scores, NEGATIVE)
                m_old = m_sc[i]
                m_new = jnp.maximum(m_old, jnp.max(scores, axis=1, keepdims=True))
                alpha = jnp.exp(m_old - m_new)
                weights = jnp.where(allowed, jnp.exp(scores - m_new), 0.0)
                l_sc[i] = alpha * l_sc[i] + jnp.sum(weights, axis=1, keepdims=True)
                acc_sc[:, cols] = alpha * acc_sc[:, cols] + jnp.dot(
                    weights.astype(jnp.bfloat16), values, preferred_element_type=f32
                )
                m_sc[i] = m_new

    @pl.when(block == pl.num_programs(1) - 1)
    def _():
        for i in range(m_sc.shape[0]):
            cols = slice(i * depth, (i + 1) * depth)
            o_ref[:, cols] = acc_sc[:, cols] / l_sc[i]
            lse_ref[0, :, i : i + 1] = m_sc[i] + jnp.log(l_sc[i])


def flash_forward(ctx_index, q, kv, qseg, qpos, kseg, groups):
    tokens, q_width = q.shape
    blocks, width, kv_width = kv.shape
    pair = 2
    pairs = kv_width // (2 * pair * HEAD_SIZE)
    heads_step = pair * groups
    f32 = jnp.float32
    capped = lambda p, b, c: (jnp.minimum(b, c[0]), 0, p)
    grid_spec = pltpu.PrefetchScalarGridSpec(
        num_scalar_prefetch=1,
        grid=(pairs, blocks),
        in_specs=[
            pl.BlockSpec((tokens, heads_step * HEAD_SIZE), lambda p, b, c: (0, p)),
            pl.BlockSpec((1, width, pair * HEAD_SIZE), capped),
            pl.BlockSpec((1, width, pair * HEAD_SIZE), lambda p, b, c: (jnp.minimum(b, c[0]), 0, pairs + p)),
            pl.BlockSpec((tokens, 1), lambda p, b, c: (0, 0)),
            pl.BlockSpec((tokens, 1), lambda p, b, c: (0, 0)),
            pl.BlockSpec((1, width), lambda p, b, c: (0, jnp.minimum(b, c[0]))),
        ],
        out_specs=[
            pl.BlockSpec((tokens, heads_step * HEAD_SIZE), lambda p, b, c: (0, p)),
            pl.BlockSpec((1, tokens, heads_step), lambda p, b, c: (p, 0, 0)),
        ],
        scratch_shapes=[
            pltpu.VMEM((heads_step, tokens, 1), f32),
            pltpu.VMEM((heads_step, tokens, 1), f32),
            pltpu.VMEM((tokens, heads_step * HEAD_SIZE), f32),
        ],
    )
    return pl.pallas_call(
        functools.partial(_flash_body, groups),
        grid_spec=grid_spec,
        out_shape=[
            jax.ShapeDtypeStruct((tokens, q_width), f32),
            jax.ShapeDtypeStruct((pairs, tokens, heads_step), f32),
        ],
        compiler_params=pltpu.CompilerParams(
            dimension_semantics=("arbitrary", "arbitrary"), vmem_limit_bytes=48 * 1024 * 1024
        ),
        cost_estimate=pl.CostEstimate(
            flops=tokens * q_width * blocks * width * 4,
            transcendentals=tokens * (q_width // HEAD_SIZE) * blocks * width,
            bytes_accessed=(q.size + kv.size) * 2 + tokens * q_width * 4,
        ),
    )(jnp.reshape(ctx_index, (1,)).astype(jnp.int32), q, kv, kv, qseg, qpos, kseg)

def per_device(
    dpx_count,
    hidden_in,
    attn_gain,
    q_weight,
    key_matrix,
    value_matrix,
    o_weight,
    moe_gain,
    router_weight,
    gate_weight,
    up_weight,
    down_weight,
    segments,
    expert_picks,
    output_grad,
):
    bf16 = jnp.bfloat16
    f32 = jnp.float32
    token_count = hidden_in.shape[0]
    ctx_index = lax.axis_index("ctx")
    heads_local = q_weight.shape[1] // HEAD_SIZE
    kv_local = key_matrix.shape[1] // HEAD_SIZE
    group_size = heads_local // kv_local
    score_scale = 1.0 / math.sqrt(HEAD_SIZE)
    token_positions = ctx_index * token_count + jnp.arange(token_count, dtype=jnp.int32)
    segment_here = lax.dynamic_slice_in_dim(segments, ctx_index * token_count, token_count)
    inputs_f32 = hidden_in.astype(f32)
    o_full = lax.all_gather(o_weight, "tensor", axis=1, tiled=True)
    normed_f32, scale_one = normalize(inputs_f32, attn_gain)
    normed_one = normed_f32.astype(bf16)
    query_rows = jnp.dot(normed_one, q_weight, preferred_element_type=f32).reshape(
        token_count, heads_local, HEAD_SIZE
    )
    keys_raw = jnp.dot(normed_one, key_matrix, preferred_element_type=f32).reshape(
        token_count, kv_local, HEAD_SIZE
    )
    values_raw = jnp.dot(normed_one, value_matrix, preferred_element_type=f32)
    query_grouped = (
        apply_rotary(query_rows, token_positions, 1.0)
        .astype(bf16)
        .reshape(token_count, kv_local, group_size, HEAD_SIZE)
    )
    key_flat = (
        apply_rotary(keys_raw, token_positions, 1.0)
        .astype(bf16)
        .reshape(token_count, kv_local * HEAD_SIZE)
    )
    value_flat = values_raw.astype(bf16)

    def piece_mask(piece_rows):
        key_pos = jnp.arange(piece_rows, dtype=jnp.int32)
        return (segment_here[:, None] == segments[None, :]) & (
            key_pos[None, :] <= token_positions[:, None]
        )

    ctx_count = segments.shape[0] // token_count
    kv_both = gather_axis(jnp.concatenate([key_flat, value_flat], axis=1), "ctx", ctx_count, 1)
    piece_rows = ctx_count * token_count
    kv_width = kv_local * HEAD_SIZE
    key_piece = kv_both[:, :, :kv_width].reshape(piece_rows, kv_local, HEAD_SIZE)
    value_piece = kv_both[:, :, kv_width:].reshape(piece_rows, kv_local, HEAD_SIZE)
    attn_flat, lse_pairs = flash_forward(
        ctx_index,
        query_grouped.reshape(token_count, heads_local * HEAD_SIZE),
        kv_both,
        segment_here[:, None],
        token_positions[:, None],
        segments[None, :],
        group_size,
    )
    attn_grouped = jnp.transpose(
        attn_flat.reshape(token_count, kv_local, group_size, HEAD_SIZE), (1, 2, 0, 3)
    )
    log_sum = jnp.transpose(
        lse_pairs.reshape(kv_local // 2, token_count, 2, group_size), (0, 2, 3, 1)
    ).reshape(kv_local, group_size, token_count)
    attn_bf = attn_flat.astype(bf16)
    tensor_count = o_weight.shape[0] // o_weight.shape[1]
    attn_all = gather_axis(attn_bf, "tensor", tensor_count, 2)
    attn_full = jnp.transpose(attn_all, (1, 0, 2)).reshape(token_count, tensor_count * attn_bf.shape[1])
    mixed_attn = contract_cols(attn_full, o_full)
    resid = inputs_f32 + mixed_attn
    normed_two_f32, scale_two = normalize(resid, moe_gain)
    normed_two = normed_two_f32.astype(bf16)
    logits = jnp.dot(normed_two, router_weight, preferred_element_type=f32)
    expert_range = jnp.arange(NEXP, dtype=jnp.int32)
    picked_onehot = expert_picks[:, :, None] == expert_range[None, None, :]
    picked = jnp.sum(jnp.where(picked_onehot, logits[:, None, :], 0.0), axis=2)
    gate_probs = jax.nn.softmax(picked, axis=-1)
    gates_dense = jnp.sum(jnp.where(picked_onehot, gate_probs[:, :, None], 0.0), axis=1)
    gates_by_expert = jnp.transpose(gates_dense)
    cot_bf = output_grad
    gcol = gates_dense
    grad_gate, grad_up, grad_down, hid_all, dga_all, dua_all = expert_grad_kernel(
        normed_two,
        jnp.transpose(normed_two),
        cot_bf,
        jnp.transpose(cot_bf),
        gcol,
        gates_by_expert[:, None, :],
        gate_weight,
        up_weight,
        down_weight,
        dpx_count,
    )
    gate_half = core_reduce(grad_gate, 8)
    gate_half, hid_all, dga_all, dua_all = lax.optimization_barrier(
        (gate_half, hid_all, dga_all, dua_all)
    )
    moe_acc, gate_parts, moe_grad_rows = expert_rows_kernel(
        hid_all, dga_all, dua_all, cot_bf, gcol, gate_weight, up_weight, down_weight
    )
    cot_f32 = output_grad.astype(f32)
    moe_total = sum_axis(moe_acc.astype(bf16), "tensor", 3)
    output = (resid + moe_total).astype(bf16)
    grad_rows_all = moe_grad_rows
    gate_parts = gate_parts[:, :, 0]
    grad_gate_out, grad_up_out, grad_down_out = [
        lax.psum_scatter(
            g.reshape(g.shape[0], -1, g.shape[3]), ("dpx", "ctx"), scatter_dimension=1, tiled=True
        ).astype(jnp.float32)
        for g in (gate_half, core_reduce(grad_up, 9), core_reduce(grad_down, 10))
    ]
    gate_pair = jnp.sum(
        jnp.where(picked_onehot, jnp.transpose(gate_parts)[:, None, :], 0.0), axis=2
    )
    moe_summed = sum_axis(grad_rows_all.astype(bf16), "tensor", 4)
    gate_summed = sum_axis(gate_pair.astype(bf16), "tensor", 5)
    grad_picked = gate_probs * (
        gate_summed - jnp.sum(gate_probs * gate_summed, axis=1, keepdims=True)
    )
    grad_logits = jnp.sum(jnp.where(picked_onehot, grad_picked[:, :, None], 0.0), axis=1).astype(
        bf16
    )
    grad_router = contract_rows(normed_two, grad_logits)
    grad_normed_two = moe_summed + contract_cols(grad_logits, router_weight)
    grad_two_rows, grad_moe_gain = norm_backward(resid, scale_two, moe_gain, grad_normed_two)
    grad_resid = cot_f32 + grad_two_rows
    grad_mix = grad_resid.astype(bf16)
    grad_o = contract_rows(grad_mix, attn_bf)
    grad_attn = jnp.dot(grad_mix, o_weight, preferred_element_type=f32).astype(bf16)
    grad_attn_grouped = jnp.transpose(
        grad_attn.reshape(token_count, kv_local, group_size, HEAD_SIZE), (1, 2, 0, 3)
    )
    row_delta = jnp.sum(grad_attn_grouped.astype(f32) * attn_grouped, axis=-1)
    allowed = piece_mask(piece_rows)
    scores = (
        jnp.einsum("tkgd,nkd->kgtn", query_grouped, key_piece, preferred_element_type=f32)
        * score_scale
    )
    probability = jnp.where(allowed, jnp.exp(scores - log_sum[..., None]), 0.0)
    grad_probs = jnp.einsum(
        "kgtd,nkd->kgtn", grad_attn_grouped, value_piece, preferred_element_type=f32
    )
    grad_scores = (probability * (grad_probs - row_delta[..., None])).astype(bf16)
    grad_query = score_scale * jnp.einsum(
        "kgtn,nkd->kgtd", grad_scores, key_piece, preferred_element_type=f32
    )
    key_part = score_scale * jnp.einsum(
        "kgtn,tkgd->nkd", grad_scores, query_grouped, preferred_element_type=f32
    )
    value_part = jnp.einsum(
        "kgtn,kgtd->nkd", probability.astype(bf16), grad_attn_grouped, preferred_element_type=f32
    )
    grad_keys_all = key_part.reshape(piece_rows, kv_local * HEAD_SIZE)
    grad_values_all = value_part.reshape(piece_rows, kv_local * HEAD_SIZE)
    back_state = (grad_query, grad_keys_all, grad_values_all)
    grad_query, grad_keys_all, grad_values_all = back_state
    grad_kv_here = scatter_sum_downward(
        jnp.concatenate([grad_keys_all, grad_values_all], axis=1)
        .astype(bf16)
        .reshape(ctx_count, token_count, 2 * kv_width),
        "ctx",
        ctx_count,
        6,
    )
    grad_keys_here = grad_kv_here[:, :kv_width]
    grad_values_here = grad_kv_here[:, kv_width:]
    grad_query_rows = jnp.transpose(grad_query, (2, 0, 1, 3)).reshape(
        token_count, heads_local, HEAD_SIZE
    )
    grad_query_bf = (
        apply_rotary(grad_query_rows, token_positions, -1.0)
        .reshape(token_count, heads_local * HEAD_SIZE)
        .astype(bf16)
    )
    grad_key_bf = (
        apply_rotary(
            grad_keys_here.reshape(token_count, kv_local, HEAD_SIZE), token_positions, -1.0
        )
        .reshape(token_count, kv_local * HEAD_SIZE)
        .astype(bf16)
    )
    grad_value_bf = grad_values_here.astype(bf16)
    grad_q = contract_rows(normed_one, grad_query_bf)
    grad_k = contract_rows(normed_one, grad_key_bf)
    grad_v = contract_rows(normed_one, grad_value_bf)
    partial_one = (
        contract_cols(grad_query_bf, q_weight)
        + contract_cols(grad_key_bf, key_matrix)
        + contract_cols(grad_value_bf, value_matrix)
    )
    grad_normed_one = sum_axis(partial_one.astype(bf16), "tensor", 7)
    grad_one_rows, grad_attn_gain = norm_backward(inputs_f32, scale_one, attn_gain, grad_normed_one)
    input_grad = grad_resid + grad_one_rows
    q_cols, o_cols, k_cols = grad_q.shape[1], grad_o.shape[1], grad_k.shape[1]
    small = jnp.concatenate(
        [
            grad_router,
            grad_attn_gain[:, None],
            grad_moe_gain[:, None],
            jnp.zeros((grad_router.shape[0], 128 - grad_router.shape[1] - 2), f32),
        ],
        axis=1,
    )
    dense_all = jnp.concatenate(
        [grad_q, grad_o, grad_k, grad_v, small], axis=1
    ).astype(bf16)
    width = dense_all.shape[0]
    dense_all = jnp.transpose(
        dense_all.reshape(dpx_count, 2, width // (2 * dpx_count), dense_all.shape[1]), (1, 0, 2, 3)
    )
    dense_half = core_reduce(dense_all, 11)
    dense_half, grad_gate_out, grad_up_out, grad_down_out = lax.optimization_barrier(
        (dense_half, grad_gate_out, grad_up_out, grad_down_out)
    )
    dense_here = lax.psum_scatter(
        dense_half.reshape(-1, dense_half.shape[-1]), ("dpx", "ctx"), scatter_dimension=0, tiled=True
    ).astype(f32)
    spans = [q_cols, o_cols, k_cols, k_cols, router_weight.shape[1], 1, 1]
    cuts = [sum(spans[:i]) for i in range(len(spans) + 1)]
    pieces_out = [dense_here[:, cuts[i] : cuts[i + 1]] for i in range(len(spans))]
    dense_out = (
        pieces_out[5][:, 0],
        pieces_out[0],
        pieces_out[2],
        pieces_out[3],
        pieces_out[1],
        pieces_out[6][:, 0],
        pieces_out[4],
    )
    return (
        output,
        input_grad,
        dense_out[0],
        dense_out[1],
        dense_out[2],
        dense_out[3],
        dense_out[4],
        dense_out[5],
        dense_out[6],
        grad_gate_out,
        grad_up_out,
        grad_down_out,
    )


def solution(mesh):
    dp_count, ctx_count, tensor_count = (mesh.shape[a] for a in ("dp", "ctx", "tensor"))
    split_mesh = jax.sharding.Mesh(
        mesh.devices.reshape(dp_count // 2, 2, ctx_count, tensor_count), ("dpx", "core", "ctx", "tensor")
    )
    return jax.shard_map(
        functools.partial(per_device, dp_count // 2),
        mesh=split_mesh,
        in_specs=(
            P(("dpx", "core", "ctx"), None),
            P(),
            P(None, "tensor"),
            P(None, "tensor"),
            P(None, "tensor"),
            P(None, "tensor"),
            P(),
            P(),
            P(None, None, "tensor"),
            P(None, None, "tensor"),
            P(None, None, "tensor"),
            P(("dpx", "core")),
            P(("dpx", "core", "ctx"), None),
            P(("dpx", "core", "ctx"), None),
        ),
        out_specs=(
            P(("dpx", "core", "ctx"), None),
            P(("dpx", "core", "ctx"), None),
            P(("dpx", "core", "ctx")),
            P(("dpx", "core", "ctx"), "tensor"),
            P(("dpx", "core", "ctx"), "tensor"),
            P(("dpx", "core", "ctx"), "tensor"),
            P(("dpx", "core", "ctx"), "tensor"),
            P(("dpx", "core", "ctx")),
            P(("dpx", "core", "ctx"), None),
            P(None, ("dpx", "core", "ctx"), "tensor"),
            P(None, ("dpx", "core", "ctx"), "tensor"),
            P(None, ("dpx", "core", "ctx"), "tensor"),
        ),
        check_vma=False,
    )
```

```python
import functools
import math

import jax
import jax.numpy as jnp
from jax import lax
from jax.experimental import pallas as pl
from jax.experimental.pallas import tpu as pltpu
from jax.sharding import PartitionSpec as P

HEAD_SIZE = 64
NEXP = 24
CAP = 341


EPSILON = 1e-06
ROPE_BASE = 10000.0
NEGATIVE = -1e30
HIGHEST = lax.Precision.HIGHEST


def normalize(rows, gain):
    scale_inv = lax.rsqrt(jnp.mean(rows * rows, axis=-1, keepdims=True) + EPSILON)
    return (rows * scale_inv * gain, scale_inv)


def norm_backward(rows, scale_inv, gain, grad_normed):
    weighted = gain * grad_normed
    grad_gain = jnp.sum(grad_normed * rows * scale_inv, axis=0)
    inner_mean = jnp.mean(weighted * rows, axis=-1, keepdims=True)
    grad_rows = scale_inv * weighted - rows * scale_inv * scale_inv * scale_inv * inner_mean
    return (grad_rows, grad_gain)


def apply_rotary(value_rows, token_positions, direction):
    half_dim = value_rows.shape[-1] // 2
    frequency = ROPE_BASE ** (-jnp.arange(half_dim, dtype=jnp.float32) / half_dim)
    angles = token_positions.astype(jnp.float32)[:, None] * frequency[None, :]
    cosine = jnp.cos(angles)[:, None, :]
    sine_part = direction * jnp.sin(angles)[:, None, :]
    first_half = value_rows[..., :half_dim]
    second = value_rows[..., half_dim:]
    return jnp.concatenate(
        [first_half * cosine - second * sine_part, second * cosine + first_half * sine_part],
        axis=-1,
    )


def contract_rows(left, right):
    return lax.dot_general(
        left, right, (((0,), (0,)), ((), ())), preferred_element_type=jnp.float32
    )


def contract_rows_exact(left, right):
    return lax.dot_general(
        left, right, (((0,), (0,)), ((), ())), precision=HIGHEST, preferred_element_type=jnp.float32
    )


def contract_cols(left, right):
    return lax.dot_general(
        left, right, (((1,), (1,)), ((), ())), preferred_element_type=jnp.float32
    )


def _store_split(out_ref, value):
    cores, _, groups, rows, _ = out_ref.shape
    for x in range(groups):
        for c in range(cores):
            start = (x * cores + c) * rows
            out_ref[c, 0, x] = value[start : start + rows].astype(out_ref.dtype)


def _gate_column(gates_ref):
    gates = gates_ref[...]
    lane = lax.broadcasted_iota(jnp.int32, gates.shape, 1)
    return jnp.sum(jnp.where(lane == pl.program_id(0), gates, 0.0), axis=1, keepdims=True)


def _grad_body(
    n2_ref, n2t_ref, dy_ref, dyt_ref, gcol_ref, grow_ref, wg_ref, wu_ref, wd_ref,
    gg_ref, gu_ref, gd_ref, hid_ref, dga_ref, dua_ref,
):
    f32 = jnp.float32
    bf16 = jnp.bfloat16
    n2 = n2_ref[...]
    wd = wd_ref[0]
    gate_act = jnp.dot(n2, wg_ref[0], preferred_element_type=f32)
    up_act = jnp.dot(n2, wu_ref[0], preferred_element_type=f32)
    sig = 1.0 / (1.0 + jnp.exp(-gate_act))
    silu = gate_act * sig
    hidden = (silu * up_act).astype(bf16)
    hid_ref[0] = hidden
    deo = (_gate_column(gcol_ref) * dy_ref[...].astype(f32)).astype(bf16)
    grad_hidden = jnp.dot(deo, wd, preferred_element_type=f32)
    deo_t = (grow_ref[0] * dyt_ref[...].astype(f32)).astype(bf16)
    _store_split(gd_ref, jnp.dot(deo_t, hidden, preferred_element_type=f32))
    grad_gate_act = (grad_hidden * up_act * sig * (1.0 + gate_act * (1.0 - sig))).astype(bf16)
    grad_up_act = (grad_hidden * silu).astype(bf16)
    dga_ref[0] = grad_gate_act
    dua_ref[0] = grad_up_act
    n2t = n2t_ref[...]
    _store_split(gg_ref, jnp.dot(n2t, grad_gate_act, preferred_element_type=f32))
    _store_split(gu_ref, jnp.dot(n2t, grad_up_act, preferred_element_type=f32))


def _rows_body(hid_ref, dga_ref, dua_ref, dy_ref, gcol_ref, wg_ref, wu_ref, wd_ref, acc_ref, dgate_ref, dn2_ref):
    f32 = jnp.float32
    nt = (((1,), (1,)), ((), ()))

    @pl.when(pl.program_id(0) == 0)
    def _():
        acc_ref[...] = jnp.zeros_like(acc_ref)
        dn2_ref[...] = jnp.zeros_like(dn2_ref)

    expert_out = lax.dot_general(hid_ref[0], wd_ref[0], nt, preferred_element_type=f32)
    acc_ref[...] += _gate_column(gcol_ref) * expert_out
    dgate_ref[0] = jnp.sum(expert_out * dy_ref[...].astype(f32), axis=1, keepdims=True)
    dn2_ref[...] += lax.dot_general(
        dga_ref[0], wg_ref[0], nt, preferred_element_type=f32
    ) + lax.dot_general(dua_ref[0], wu_ref[0], nt, preferred_element_type=f32)


def expert_grad_kernel(n2, n2t, dy, dyt, gcol, grow, wg, wu, wd, groups):
    tokens, width = n2.shape
    experts, _, hidden = wg.shape
    bf16 = jnp.bfloat16
    whole = lambda shape: pl.BlockSpec(shape, lambda e: (0,) * len(shape))
    per_expert = lambda shape: pl.BlockSpec((1,) + shape, lambda e: (e,) + (0,) * len(shape))
    split_rows = width // (groups * 2)
    split = pl.BlockSpec((2, 1, groups, split_rows, hidden), lambda e: (0, e, 0, 0, 0))
    split_shape = jax.ShapeDtypeStruct((2, experts, groups, split_rows, hidden), bf16)
    act_shape = jax.ShapeDtypeStruct((experts, tokens, hidden), bf16)
    return pl.pallas_call(
        _grad_body,
        grid=(experts,),
        in_specs=[
            whole((tokens, width)),
            whole((width, tokens)),
            whole((tokens, width)),
            whole((width, tokens)),
            whole((tokens, experts)),
            per_expert((1, tokens)),
            per_expert((width, hidden)),
            per_expert((width, hidden)),
            per_expert((width, hidden)),
        ],
        out_specs=[split, split, split]
        + [per_expert((tokens, hidden))] * 3,
        out_shape=[split_shape] * 3 + [act_shape] * 3,
        compiler_params=pltpu.CompilerParams(
            dimension_semantics=("arbitrary",), vmem_limit_bytes=64 * 1024 * 1024
        ),
        cost_estimate=pl.CostEstimate(
            flops=experts * tokens * width * hidden * 2 * 6,
            transcendentals=experts * tokens * hidden,
            bytes_accessed=experts * width * hidden * 12 + tokens * width * 8 + experts * tokens * hidden * 6,
        ),
    )(n2, n2t, dy, dyt, gcol, grow, wg, wu, wd)


def expert_rows_kernel(hid, dga, dua, dy, gcol, wg, wu, wd):
    experts, tokens, hidden = hid.shape
    width = dy.shape[1]
    f32 = jnp.float32
    whole = lambda shape: pl.BlockSpec(shape, lambda e: (0,) * len(shape))
    per_expert = lambda shape: pl.BlockSpec((1,) + shape, lambda e: (e,) + (0,) * len(shape))
    return pl.pallas_call(
        _rows_body,
        grid=(experts,),
        in_specs=[
            per_expert((tokens, hidden)),
            per_expert((tokens, hidden)),
            per_expert((tokens, hidden)),
            whole((tokens, width)),
            whole((tokens, experts)),
            per_expert((width, hidden)),
            per_expert((width, hidden)),
            per_expert((width, hidden)),
        ],
        out_specs=[whole((tokens, width)), per_expert((tokens, 1)), whole((tokens, width))],
        out_shape=[
            jax.ShapeDtypeStruct((tokens, width), f32),
            jax.ShapeDtypeStruct((experts, tokens, 1), f32),
            jax.ShapeDtypeStruct((tokens, width), f32),
        ],
        compiler_params=pltpu.CompilerParams(
            dimension_semantics=("arbitrary",), vmem_limit_bytes=64 * 1024 * 1024
        ),
        cost_estimate=pl.CostEstimate(
            flops=experts * tokens * width * hidden * 2 * 3,
            transcendentals=0,
            bytes_accessed=experts * width * hidden * 6 + tokens * width * 10 + experts * tokens * hidden * 6,
        ),
    )(hid, dga, dua, dy, gcol, wg, wu, wd)

MESH = pl.DeviceIdType.MESH


def _exchange_body(axis, n, per_peer, downward, src_ref, out_ref, send_sems, recv_sems):
    me = lax.axis_index(axis)
    barrier = pltpu.get_barrier_semaphore()
    for k in range(1, n):
        peer = lax.rem(me + k, n)
        pl.semaphore_signal(barrier, 1, device_id={axis: peer}, device_id_type=MESH)
    pl.semaphore_wait(barrier, n - 1)
    sends = []
    for k in range(1, n):
        peer = lax.rem(me + k, n)
        copy = pltpu.make_async_remote_copy(
            src_ref=src_ref.at[peer] if per_peer else src_ref,
            dst_ref=out_ref.at[me],
            send_sem=send_sems.at[k - 1],
            recv_sem=recv_sems.at[k - 1],
            device_id={axis: peer},
            device_id_type=MESH,
        )
        sends.append((peer, copy))
        if downward:
            pl.when(peer < me)(copy.start)
        else:
            copy.start()
    for k in range(1, n):
        source = lax.rem(me + n - k, n)
        incoming = pltpu.make_async_remote_copy(
            src_ref=src_ref.at[source] if per_peer else src_ref,
            dst_ref=out_ref.at[source],
            send_sem=send_sems.at[k - 1],
            recv_sem=recv_sems.at[k - 1],
            device_id={axis: source},
            device_id_type=MESH,
        )
        if downward:
            pl.when(source > me)(incoming.wait_recv)
        else:
            incoming.wait_recv()
    for peer, copy in sends:
        if downward:
            pl.when(peer < me)(copy.wait_send)
        else:
            copy.wait_send()


def exchange(x, axis, n, per_peer, collective_id, downward=False):
    block = x.shape[1:] if per_peer else x.shape
    nbytes = math.prod(block) * x.dtype.itemsize
    return pl.pallas_call(
        functools.partial(_exchange_body, axis, n, per_peer, downward),
        out_shape=jax.ShapeDtypeStruct((n,) + tuple(block), x.dtype),
        in_specs=[pl.BlockSpec(memory_space=pl.ANY)],
        out_specs=pl.BlockSpec(memory_space=pl.ANY),
        scratch_shapes=[pltpu.SemaphoreType.DMA((n - 1,)), pltpu.SemaphoreType.DMA((n - 1,))],
        compiler_params=pltpu.CompilerParams(collective_id=collective_id, has_side_effects=True),
        cost_estimate=pl.CostEstimate(flops=0, transcendentals=0, bytes_accessed=2 * (n - 1) * nbytes),
    )(x)


def gather_axis(x, axis, n, collective_id):
    got = exchange(x, axis, n, False, collective_id)
    return lax.dynamic_update_slice_in_dim(got, x[None], lax.axis_index(axis), 0)


def sum_axis(x, axis, collective_id):
    got = exchange(x, axis, 2, False, collective_id)
    me = lax.axis_index(axis)
    other = lax.dynamic_index_in_dim(got, 1 - me, 0, keepdims=False)
    return x.astype(jnp.float32) + other.astype(jnp.float32)


def _pair_add_body(me_ref, own_ref, other_ref, out_ref):
    out_ref[...] = (own_ref[...].astype(jnp.float32) + other_ref[...].astype(jnp.float32)).astype(out_ref.dtype)


def core_reduce(x, collective_id):
    got = exchange(x, "core", 2, True, collective_id)
    me = lax.axis_index("core")
    count = x.shape[1]
    rest = x.shape[2:]
    zeros = (0,) * len(rest)
    item_bytes = math.prod(rest) * x.dtype.itemsize
    step = max(d for d in range(1, count + 1) if count % d == 0 and d * item_bytes <= 4 * 1024 * 1024)
    grid_spec = pltpu.PrefetchScalarGridSpec(
        num_scalar_prefetch=1,
        grid=(count // step,),
        in_specs=[
            pl.BlockSpec((None, step) + rest, lambda i, c: (c[0], i) + zeros),
            pl.BlockSpec((None, step) + rest, lambda i, c: (1 - c[0], i) + zeros),
        ],
        out_specs=pl.BlockSpec((step,) + rest, lambda i, c: (i,) + zeros),
    )
    return pl.pallas_call(
        _pair_add_body,
        grid_spec=grid_spec,
        out_shape=jax.ShapeDtypeStruct(x.shape[1:], jnp.bfloat16),
        compiler_params=pltpu.CompilerParams(vmem_limit_bytes=56 * 1024 * 1024),
        cost_estimate=pl.CostEstimate(flops=x.size // 2, transcendentals=0, bytes_accessed=x.size * 3),
    )(jnp.reshape(me, (1,)).astype(jnp.int32), x, got)


def scatter_sum_downward(x, axis, n, collective_id):
    got = exchange(x, axis, n, True, collective_id, downward=True)
    me = lax.axis_index(axis)
    own = lax.dynamic_index_in_dim(x, me, 0, keepdims=False).astype(jnp.float32)
    above = (jnp.arange(n, dtype=jnp.int32) > me).reshape((n,) + (1,) * (x.ndim - 1))
    return own + jnp.sum(jnp.where(above, got.astype(jnp.float32), 0.0), axis=0)


def _flash_body(groups, ctx_ref, q_ref, k_ref, v_ref, qseg_ref, qpos_ref, kseg_ref, o_ref, lse_ref, m_sc, l_sc, acc_sc):
    f32 = jnp.float32
    block = pl.program_id(1)
    depth = HEAD_SIZE
    pair = k_ref.shape[2] // depth

    @pl.when(block == 0)
    def _():
        m_sc[...] = jnp.full_like(m_sc, NEGATIVE)
        l_sc[...] = jnp.zeros_like(l_sc)
        acc_sc[...] = jnp.zeros_like(acc_sc)

    @pl.when(block <= ctx_ref[0])
    def _():
        width = k_ref.shape[1]
        key_pos = block * width + lax.broadcasted_iota(jnp.int32, (1, width), 1)
        allowed = (qseg_ref[...] == kseg_ref[...]) & (key_pos <= qpos_ref[...])
        for kk in range(pair):
            keys = k_ref[0, :, kk * depth : (kk + 1) * depth]
            values = v_ref[0, :, kk * depth : (kk + 1) * depth]
            for gi in range(groups):
                i = kk * groups + gi
                cols = slice(i * depth, (i + 1) * depth)
                scores = lax.dot_general(
                    q_ref[:, cols], keys, (((1,), (1,)), ((), ())), preferred_element_type=f32
                ) * (1.0 / math.sqrt(HEAD_SIZE))
                scores = jnp.where(allowed, scores, NEGATIVE)
                m_old = m_sc[i]
                m_new = jnp.maximum(m_old, jnp.max(scores, axis=1, keepdims=True))
                alpha = jnp.exp(m_old - m_new)
                weights = jnp.where(allowed, jnp.exp(scores - m_new), 0.0)
                l_sc[i] = alpha * l_sc[i] + jnp.sum(weights, axis=1, keepdims=True)
                acc_sc[:, cols] = alpha * acc_sc[:, cols] + jnp.dot(
                    weights.astype(jnp.bfloat16), values, preferred_element_type=f32
                )
                m_sc[i] = m_new

    @pl.when(block == pl.num_programs(1) - 1)
    def _():
        for i in range(m_sc.shape[0]):
            cols = slice(i * depth, (i + 1) * depth)
            o_ref[:, cols] = acc_sc[:, cols] / l_sc[i]
            lse_ref[0, :, i : i + 1] = m_sc[i] + jnp.log(l_sc[i])


def flash_forward(ctx_index, q, kv, qseg, qpos, kseg, groups):
    tokens, q_width = q.shape
    blocks, width, kv_width = kv.shape
    pair = 2
    pairs = kv_width // (2 * pair * HEAD_SIZE)
    heads_step = pair * groups
    f32 = jnp.float32
    capped = lambda p, b, c: (jnp.minimum(b, c[0]), 0, p)
    grid_spec = pltpu.PrefetchScalarGridSpec(
        num_scalar_prefetch=1,
        grid=(pairs, blocks),
        in_specs=[
            pl.BlockSpec((tokens, heads_step * HEAD_SIZE), lambda p, b, c: (0, p)),
            pl.BlockSpec((1, width, pair * HEAD_SIZE), capped),
            pl.BlockSpec((1, width, pair * HEAD_SIZE), lambda p, b, c: (jnp.minimum(b, c[0]), 0, pairs + p)),
            pl.BlockSpec((tokens, 1), lambda p, b, c: (0, 0)),
            pl.BlockSpec((tokens, 1), lambda p, b, c: (0, 0)),
            pl.BlockSpec((1, width), lambda p, b, c: (0, jnp.minimum(b, c[0]))),
        ],
        out_specs=[
            pl.BlockSpec((tokens, heads_step * HEAD_SIZE), lambda p, b, c: (0, p)),
            pl.BlockSpec((1, tokens, heads_step), lambda p, b, c: (p, 0, 0)),
        ],
        scratch_shapes=[
            pltpu.VMEM((heads_step, tokens, 1), f32),
            pltpu.VMEM((heads_step, tokens, 1), f32),
            pltpu.VMEM((tokens, heads_step * HEAD_SIZE), f32),
        ],
    )
    return pl.pallas_call(
        functools.partial(_flash_body, groups),
        grid_spec=grid_spec,
        out_shape=[
            jax.ShapeDtypeStruct((tokens, q_width), f32),
            jax.ShapeDtypeStruct((pairs, tokens, heads_step), f32),
        ],
        compiler_params=pltpu.CompilerParams(
            dimension_semantics=("arbitrary", "arbitrary"), vmem_limit_bytes=48 * 1024 * 1024
        ),
        cost_estimate=pl.CostEstimate(
            flops=tokens * q_width * blocks * width * 4,
            transcendentals=tokens * (q_width // HEAD_SIZE) * blocks * width,
            bytes_accessed=(q.size + kv.size) * 2 + tokens * q_width * 4,
        ),
    )(jnp.reshape(ctx_index, (1,)).astype(jnp.int32), q, kv, kv, qseg, qpos, kseg)

def _chain_down_body(axis, n, x_ref, out_ref, recv, send, send_sems, recv_sems):
    f32 = jnp.float32
    me = lax.axis_index(axis)
    below = lax.rem(me + n - 1, n)
    above = lax.rem(me + 1, n)
    barrier = pltpu.get_barrier_semaphore()
    pl.semaphore_signal(barrier, 1, device_id={axis: below}, device_id_type=MESH)
    pl.semaphore_signal(barrier, 1, device_id={axis: above}, device_id_type=MESH)
    pl.semaphore_wait(barrier, 2)
    copies = []
    for j in range(n - 1):
        copy = pltpu.make_async_remote_copy(
            src_ref=send.at[j],
            dst_ref=recv.at[j],
            send_sem=send_sems.at[j],
            recv_sem=recv_sems.at[j],
            device_id={axis: below},
            device_id_type=MESH,
        )
        copies.append(copy)

        @pl.when((j < me) & (me < n - 1))
        def _():
            copy.wait_recv()
            send[j] = (x_ref[j].astype(f32) + recv[j].astype(f32)).astype(send.dtype)

        @pl.when((j < me) & (me == n - 1))
        def _():
            send[j] = x_ref[j]

        @pl.when(j < me)
        def _():
            copy.start()

        @pl.when(j == me)
        def _():
            copy.wait_recv()
            out_ref[...] = x_ref[j].astype(f32) + recv[j].astype(f32)

    @pl.when(me == n - 1)
    def _():
        out_ref[...] = x_ref[n - 1].astype(f32)

    for j in range(n - 1):
        pl.when(j < me)(copies[j].wait_send)


def chain_sum_down(x, axis, n, collective_id):
    _, rows, cols = x.shape
    return pl.pallas_call(
        functools.partial(_chain_down_body, axis, n),
        out_shape=jax.ShapeDtypeStruct((rows, cols), jnp.float32),
        in_specs=[pl.BlockSpec(memory_space=pltpu.VMEM)],
        out_specs=pl.BlockSpec(memory_space=pltpu.VMEM),
        scratch_shapes=[
            pltpu.VMEM((n - 1, rows, cols), x.dtype),
            pltpu.VMEM((n - 1, rows, cols), x.dtype),
            pltpu.SemaphoreType.DMA((n - 1,)),
            pltpu.SemaphoreType.DMA((n - 1,)),
        ],
        compiler_params=pltpu.CompilerParams(
            collective_id=collective_id, has_side_effects=True, vmem_limit_bytes=32 * 1024 * 1024
        ),
        cost_estimate=pl.CostEstimate(
            flops=(n - 1) * rows * cols, transcendentals=0, bytes_accessed=3 * n * rows * cols * 2
        ),
    )(x)


def per_device(
    dpx_count,
    hidden_in,
    attn_gain,
    q_weight,
    key_matrix,
    value_matrix,
    o_weight,
    moe_gain,
    router_weight,
    gate_weight,
    up_weight,
    down_weight,
    segments,
    expert_picks,
    output_grad,
):
    bf16 = jnp.bfloat16
    f32 = jnp.float32
    token_count = hidden_in.shape[0]
    ctx_index = lax.axis_index("ctx")
    heads_local = q_weight.shape[1] // HEAD_SIZE
    kv_local = key_matrix.shape[1] // HEAD_SIZE
    group_size = heads_local // kv_local
    score_scale = 1.0 / math.sqrt(HEAD_SIZE)
    token_positions = ctx_index * token_count + jnp.arange(token_count, dtype=jnp.int32)
    segment_here = lax.dynamic_slice_in_dim(segments, ctx_index * token_count, token_count)
    inputs_f32 = hidden_in.astype(f32)
    o_full = lax.all_gather(o_weight, "tensor", axis=1, tiled=True)
    normed_f32, scale_one = normalize(inputs_f32, attn_gain)
    normed_one = normed_f32.astype(bf16)
    query_rows = jnp.dot(normed_one, q_weight, preferred_element_type=f32).reshape(
        token_count, heads_local, HEAD_SIZE
    )
    keys_raw = jnp.dot(normed_one, key_matrix, preferred_element_type=f32).reshape(
        token_count, kv_local, HEAD_SIZE
    )
    values_raw = jnp.dot(normed_one, value_matrix, preferred_element_type=f32)
    query_grouped = (
        apply_rotary(query_rows, token_positions, 1.0)
        .astype(bf16)
        .reshape(token_count, kv_local, group_size, HEAD_SIZE)
    )
    key_flat = (
        apply_rotary(keys_raw, token_positions, 1.0)
        .astype(bf16)
        .reshape(token_count, kv_local * HEAD_SIZE)
    )
    value_flat = values_raw.astype(bf16)

    def piece_mask(piece_rows):
        key_pos = jnp.arange(piece_rows, dtype=jnp.int32)
        return (segment_here[:, None] == segments[None, :]) & (
            key_pos[None, :] <= token_positions[:, None]
        )

    ctx_count = segments.shape[0] // token_count
    kv_both = gather_axis(jnp.concatenate([key_flat, value_flat], axis=1), "ctx", ctx_count, 1)
    piece_rows = ctx_count * token_count
    kv_width = kv_local * HEAD_SIZE
    key_piece = kv_both[:, :, :kv_width].reshape(piece_rows, kv_local, HEAD_SIZE)
    value_piece = kv_both[:, :, kv_width:].reshape(piece_rows, kv_local, HEAD_SIZE)
    attn_flat, lse_pairs = flash_forward(
        ctx_index,
        query_grouped.reshape(token_count, heads_local * HEAD_SIZE),
        kv_both,
        segment_here[:, None],
        token_positions[:, None],
        segments[None, :],
        group_size,
    )
    attn_grouped = jnp.transpose(
        attn_flat.reshape(token_count, kv_local, group_size, HEAD_SIZE), (1, 2, 0, 3)
    )
    log_sum = jnp.transpose(
        lse_pairs.reshape(kv_local // 2, token_count, 2, group_size), (0, 2, 3, 1)
    ).reshape(kv_local, group_size, token_count)
    attn_bf = attn_flat.astype(bf16)
    tensor_count = o_weight.shape[0] // o_weight.shape[1]
    attn_all = gather_axis(attn_bf, "tensor", tensor_count, 2)
    attn_full = jnp.transpose(attn_all, (1, 0, 2)).reshape(token_count, tensor_count * attn_bf.shape[1])
    mixed_attn = contract_cols(attn_full, o_full)
    resid = inputs_f32 + mixed_attn
    normed_two_f32, scale_two = normalize(resid, moe_gain)
    normed_two = normed_two_f32.astype(bf16)
    logits = jnp.dot(normed_two, router_weight, preferred_element_type=f32)
    expert_range = jnp.arange(NEXP, dtype=jnp.int32)
    picked_onehot = expert_picks[:, :, None] == expert_range[None, None, :]
    picked = jnp.sum(jnp.where(picked_onehot, logits[:, None, :], 0.0), axis=2)
    gate_probs = jax.nn.softmax(picked, axis=-1)
    gates_dense = jnp.sum(jnp.where(picked_onehot, gate_probs[:, :, None], 0.0), axis=1)
    gates_by_expert = jnp.transpose(gates_dense)
    cot_bf = output_grad
    gcol = gates_dense
    grad_gate, grad_up, grad_down, hid_all, dga_all, dua_all = expert_grad_kernel(
        normed_two,
        jnp.transpose(normed_two),
        cot_bf,
        jnp.transpose(cot_bf),
        gcol,
        gates_by_expert[:, None, :],
        gate_weight,
        up_weight,
        down_weight,
        dpx_count,
    )
    gate_half = core_reduce(grad_gate, 8)
    gate_half, hid_all, dga_all, dua_all = lax.optimization_barrier(
        (gate_half, hid_all, dga_all, dua_all)
    )
    moe_acc, gate_parts, moe_grad_rows = expert_rows_kernel(
        hid_all, dga_all, dua_all, cot_bf, gcol, gate_weight, up_weight, down_weight
    )
    cot_f32 = output_grad.astype(f32)
    moe_total = sum_axis(moe_acc.astype(bf16), "tensor", 3)
    output = (resid + moe_total).astype(bf16)
    grad_rows_all = moe_grad_rows
    gate_parts = gate_parts[:, :, 0]
    grad_gate_out, grad_up_out, grad_down_out = [
        lax.psum_scatter(
            g.reshape(g.shape[0], -1, g.shape[3]), ("dpx", "ctx"), scatter_dimension=1, tiled=True
        ).astype(jnp.float32)
        for g in (gate_half, core_reduce(grad_up, 9), core_reduce(grad_down, 10))
    ]
    gate_pair = jnp.sum(
        jnp.where(picked_onehot, jnp.transpose(gate_parts)[:, None, :], 0.0), axis=2
    )
    moe_summed = sum_axis(grad_rows_all.astype(bf16), "tensor", 4)
    gate_summed = sum_axis(gate_pair.astype(bf16), "tensor", 5)
    grad_picked = gate_probs * (
        gate_summed - jnp.sum(gate_probs * gate_summed, axis=1, keepdims=True)
    )
    grad_logits = jnp.sum(jnp.where(picked_onehot, grad_picked[:, :, None], 0.0), axis=1).astype(
        bf16
    )
    grad_router = contract_rows(normed_two, grad_logits)
    grad_normed_two = moe_summed + contract_cols(grad_logits, router_weight)
    grad_two_rows, grad_moe_gain = norm_backward(resid, scale_two, moe_gain, grad_normed_two)
    grad_resid = cot_f32 + grad_two_rows
    grad_mix = grad_resid.astype(bf16)
    grad_o = contract_rows(grad_mix, attn_bf)
    grad_attn = jnp.dot(grad_mix, o_weight, preferred_element_type=f32).astype(bf16)
    grad_attn_grouped = jnp.transpose(
        grad_attn.reshape(token_count, kv_local, group_size, HEAD_SIZE), (1, 2, 0, 3)
    )
    row_delta = jnp.sum(grad_attn_grouped.astype(f32) * attn_grouped, axis=-1)
    allowed = piece_mask(piece_rows)
    scores = (
        jnp.einsum("tkgd,nkd->kgtn", query_grouped, key_piece, preferred_element_type=f32)
        * score_scale
    )
    probability = jnp.where(allowed, jnp.exp(scores - log_sum[..., None]), 0.0)
    grad_probs = jnp.einsum(
        "kgtd,nkd->kgtn", grad_attn_grouped, value_piece, preferred_element_type=f32
    )
    grad_scores = (probability * (grad_probs - row_delta[..., None])).astype(bf16)
    grad_query = score_scale * jnp.einsum(
        "kgtn,nkd->kgtd", grad_scores, key_piece, preferred_element_type=f32
    )
    key_part = score_scale * jnp.einsum(
        "kgtn,tkgd->nkd", grad_scores, query_grouped, preferred_element_type=f32
    )
    value_part = jnp.einsum(
        "kgtn,kgtd->nkd", probability.astype(bf16), grad_attn_grouped, preferred_element_type=f32
    )
    grad_keys_all = key_part.reshape(piece_rows, kv_local * HEAD_SIZE)
    grad_values_all = value_part.reshape(piece_rows, kv_local * HEAD_SIZE)
    back_state = (grad_query, grad_keys_all, grad_values_all)
    grad_query, grad_keys_all, grad_values_all = back_state
    grad_kv_here = chain_sum_down(
        jnp.concatenate([grad_keys_all, grad_values_all], axis=1)
        .astype(bf16)
        .reshape(ctx_count, token_count, 2 * kv_width),
        "ctx",
        ctx_count,
        6,
    )
    grad_keys_here = grad_kv_here[:, :kv_width]
    grad_values_here = grad_kv_here[:, kv_width:]
    grad_query_rows = jnp.transpose(grad_query, (2, 0, 1, 3)).reshape(
        token_count, heads_local, HEAD_SIZE
    )
    grad_query_bf = (
        apply_rotary(grad_query_rows, token_positions, -1.0)
        .reshape(token_count, heads_local * HEAD_SIZE)
        .astype(bf16)
    )
    grad_key_bf = (
        apply_rotary(
            grad_keys_here.reshape(token_count, kv_local, HEAD_SIZE), token_positions, -1.0
        )
        .reshape(token_count, kv_local * HEAD_SIZE)
        .astype(bf16)
    )
    grad_value_bf = grad_values_here.astype(bf16)
    grad_q = contract_rows(normed_one, grad_query_bf)
    grad_k = contract_rows(normed_one, grad_key_bf)
    grad_v = contract_rows(normed_one, grad_value_bf)
    partial_one = (
        contract_cols(grad_query_bf, q_weight)
        + contract_cols(grad_key_bf, key_matrix)
        + contract_cols(grad_value_bf, value_matrix)
    )
    grad_normed_one = sum_axis(partial_one.astype(bf16), "tensor", 7)
    grad_one_rows, grad_attn_gain = norm_backward(inputs_f32, scale_one, attn_gain, grad_normed_one)
    input_grad = grad_resid + grad_one_rows
    q_cols, o_cols, k_cols = grad_q.shape[1], grad_o.shape[1], grad_k.shape[1]
    small = jnp.concatenate(
        [
            grad_router,
            grad_attn_gain[:, None],
            grad_moe_gain[:, None],
            jnp.zeros((grad_router.shape[0], 128 - grad_router.shape[1] - 2), f32),
        ],
        axis=1,
    )
    dense_all = jnp.concatenate(
        [grad_q, grad_o, grad_k, grad_v, small], axis=1
    ).astype(bf16)
    width = dense_all.shape[0]
    dense_all = jnp.transpose(
        dense_all.reshape(dpx_count, 2, width // (2 * dpx_count), dense_all.shape[1]), (1, 0, 2, 3)
    )
    dense_half = core_reduce(dense_all, 11)
    dense_half, grad_gate_out, grad_up_out, grad_down_out = lax.optimization_barrier(
        (dense_half, grad_gate_out, grad_up_out, grad_down_out)
    )
    dense_here = lax.psum_scatter(
        dense_half.reshape(-1, dense_half.shape[-1]), ("dpx", "ctx"), scatter_dimension=0, tiled=True
    ).astype(f32)
    spans = [q_cols, o_cols, k_cols, k_cols, router_weight.shape[1], 1, 1]
    cuts = [sum(spans[:i]) for i in range(len(spans) + 1)]
    pieces_out = [dense_here[:, cuts[i] : cuts[i + 1]] for i in range(len(spans))]
    dense_out = (
        pieces_out[5][:, 0],
        pieces_out[0],
        pieces_out[2],
        pieces_out[3],
        pieces_out[1],
        pieces_out[6][:, 0],
        pieces_out[4],
    )
    return (
        output,
        input_grad,
        dense_out[0],
        dense_out[1],
        dense_out[2],
        dense_out[3],
        dense_out[4],
        dense_out[5],
        dense_out[6],
        grad_gate_out,
        grad_up_out,
        grad_down_out,
    )


def solution(mesh):
    dp_count, ctx_count, tensor_count = (mesh.shape[a] for a in ("dp", "ctx", "tensor"))
    split_mesh = jax.sharding.Mesh(
        mesh.devices.reshape(dp_count // 2, 2, ctx_count, tensor_count), ("dpx", "core", "ctx", "tensor")
    )
    return jax.shard_map(
        functools.partial(per_device, dp_count // 2),
        mesh=split_mesh,
        in_specs=(
            P(("dpx", "core", "ctx"), None),
            P(),
            P(None, "tensor"),
            P(None, "tensor"),
            P(None, "tensor"),
            P(None, "tensor"),
            P(),
            P(),
            P(None, None, "tensor"),
            P(None, None, "tensor"),
            P(None, None, "tensor"),
            P(("dpx", "core")),
            P(("dpx", "core", "ctx"), None),
            P(("dpx", "core", "ctx"), None),
        ),
        out_specs=(
            P(("dpx", "core", "ctx"), None),
            P(("dpx", "core", "ctx"), None),
            P(("dpx", "core", "ctx")),
            P(("dpx", "core", "ctx"), "tensor"),
            P(("dpx", "core", "ctx"), "tensor"),
            P(("dpx", "core", "ctx"), "tensor"),
            P(("dpx", "core", "ctx"), "tensor"),
            P(("dpx", "core", "ctx")),
            P(("dpx", "core", "ctx"), None),
            P(None, ("dpx", "core", "ctx"), "tensor"),
            P(None, ("dpx", "core", "ctx"), "tensor"),
            P(None, ("dpx", "core", "ctx"), "tensor"),
        ),
        check_vma=False,
    )
```

```python
import functools
import math

import jax
import jax.numpy as jnp
from jax import lax
from jax.experimental import pallas as pl
from jax.experimental.pallas import tpu as pltpu
from jax.sharding import PartitionSpec as P

HEAD_SIZE = 64
NEXP = 24
CAP = 341


EPSILON = 1e-06
ROPE_BASE = 10000.0
NEGATIVE = -1e30
HIGHEST = lax.Precision.HIGHEST


def normalize(rows, gain):
    scale_inv = lax.rsqrt(jnp.mean(rows * rows, axis=-1, keepdims=True) + EPSILON)
    return (rows * scale_inv * gain, scale_inv)


def norm_backward(rows, scale_inv, gain, grad_normed):
    weighted = gain * grad_normed
    grad_gain = jnp.sum(grad_normed * rows * scale_inv, axis=0)
    inner_mean = jnp.mean(weighted * rows, axis=-1, keepdims=True)
    grad_rows = scale_inv * weighted - rows * scale_inv * scale_inv * scale_inv * inner_mean
    return (grad_rows, grad_gain)


def apply_rotary(value_rows, token_positions, direction):
    half_dim = value_rows.shape[-1] // 2
    frequency = ROPE_BASE ** (-jnp.arange(half_dim, dtype=jnp.float32) / half_dim)
    angles = token_positions.astype(jnp.float32)[:, None] * frequency[None, :]
    cosine = jnp.cos(angles)[:, None, :]
    sine_part = direction * jnp.sin(angles)[:, None, :]
    first_half = value_rows[..., :half_dim]
    second = value_rows[..., half_dim:]
    return jnp.concatenate(
        [first_half * cosine - second * sine_part, second * cosine + first_half * sine_part],
        axis=-1,
    )


def contract_rows(left, right):
    return lax.dot_general(
        left, right, (((0,), (0,)), ((), ())), preferred_element_type=jnp.float32
    )


def contract_rows_exact(left, right):
    return lax.dot_general(
        left, right, (((0,), (0,)), ((), ())), precision=HIGHEST, preferred_element_type=jnp.float32
    )


def contract_cols(left, right):
    return lax.dot_general(
        left, right, (((1,), (1,)), ((), ())), preferred_element_type=jnp.float32
    )


def _store_split(out_ref, value):
    cores, _, groups, rows, _ = out_ref.shape
    for x in range(groups):
        for c in range(cores):
            start = (x * cores + c) * rows
            out_ref[c, 0, x] = value[start : start + rows].astype(out_ref.dtype)


def _gate_column(gates_ref):
    gates = gates_ref[...]
    lane = lax.broadcasted_iota(jnp.int32, gates.shape, 1)
    return jnp.sum(jnp.where(lane == pl.program_id(0), gates, 0.0), axis=1, keepdims=True)


def _grad_body(
    n2_ref, n2t_ref, dy_ref, dyt_ref, gcol_ref, grow_ref, wg_ref, wu_ref, wd_ref,
    gg_ref, gu_ref, gd_ref, hid_ref, dga_ref, dua_ref,
):
    f32 = jnp.float32
    bf16 = jnp.bfloat16
    n2 = n2_ref[...]
    wd = wd_ref[0]
    gate_act = jnp.dot(n2, wg_ref[0], preferred_element_type=f32)
    up_act = jnp.dot(n2, wu_ref[0], preferred_element_type=f32)
    sig = 1.0 / (1.0 + jnp.exp(-gate_act))
    silu = gate_act * sig
    hidden = (silu * up_act).astype(bf16)
    hid_ref[0] = hidden
    deo = (_gate_column(gcol_ref) * dy_ref[...].astype(f32)).astype(bf16)
    grad_hidden = jnp.dot(deo, wd, preferred_element_type=f32)
    deo_t = (grow_ref[0] * dyt_ref[...].astype(f32)).astype(bf16)
    _store_split(gd_ref, jnp.dot(deo_t, hidden, preferred_element_type=f32))
    grad_gate_act = (grad_hidden * up_act * sig * (1.0 + gate_act * (1.0 - sig))).astype(bf16)
    grad_up_act = (grad_hidden * silu).astype(bf16)
    dga_ref[0] = grad_gate_act
    dua_ref[0] = grad_up_act
    n2t = n2t_ref[...]
    _store_split(gg_ref, jnp.dot(n2t, grad_gate_act, preferred_element_type=f32))
    _store_split(gu_ref, jnp.dot(n2t, grad_up_act, preferred_element_type=f32))


def _rows_body(hid_ref, dga_ref, dua_ref, dy_ref, gcol_ref, wg_ref, wu_ref, wd_ref, acc_ref, dgate_ref, dn2_ref):
    f32 = jnp.float32
    nt = (((1,), (1,)), ((), ()))

    @pl.when(pl.program_id(0) == 0)
    def _():
        acc_ref[...] = jnp.zeros_like(acc_ref)
        dn2_ref[...] = jnp.zeros_like(dn2_ref)

    expert_out = lax.dot_general(hid_ref[0], wd_ref[0], nt, preferred_element_type=f32)
    acc_ref[...] += _gate_column(gcol_ref) * expert_out
    dgate_ref[0] = jnp.sum(expert_out * dy_ref[...].astype(f32), axis=1, keepdims=True)
    dn2_ref[...] += lax.dot_general(
        dga_ref[0], wg_ref[0], nt, preferred_element_type=f32
    ) + lax.dot_general(dua_ref[0], wu_ref[0], nt, preferred_element_type=f32)


def expert_grad_kernel(n2, n2t, dy, dyt, gcol, grow, wg, wu, wd, groups):
    tokens, width = n2.shape
    experts, _, hidden = wg.shape
    bf16 = jnp.bfloat16
    whole = lambda shape: pl.BlockSpec(shape, lambda e: (0,) * len(shape))
    per_expert = lambda shape: pl.BlockSpec((1,) + shape, lambda e: (e,) + (0,) * len(shape))
    split_rows = width // (groups * 2)
    split = pl.BlockSpec((2, 1, groups, split_rows, hidden), lambda e: (0, e, 0, 0, 0))
    split_shape = jax.ShapeDtypeStruct((2, experts, groups, split_rows, hidden), bf16)
    act_shape = jax.ShapeDtypeStruct((experts, tokens, hidden), bf16)
    return pl.pallas_call(
        _grad_body,
        grid=(experts,),
        in_specs=[
            whole((tokens, width)),
            whole((width, tokens)),
            whole((tokens, width)),
            whole((width, tokens)),
            whole((tokens, experts)),
            per_expert((1, tokens)),
            per_expert((width, hidden)),
            per_expert((width, hidden)),
            per_expert((width, hidden)),
        ],
        out_specs=[split, split, split]
        + [per_expert((tokens, hidden))] * 3,
        out_shape=[split_shape] * 3 + [act_shape] * 3,
        compiler_params=pltpu.CompilerParams(
            dimension_semantics=("arbitrary",), vmem_limit_bytes=64 * 1024 * 1024
        ),
        cost_estimate=pl.CostEstimate(
            flops=experts * tokens * width * hidden * 2 * 6,
            transcendentals=experts * tokens * hidden,
            bytes_accessed=experts * width * hidden * 12 + tokens * width * 8 + experts * tokens * hidden * 6,
        ),
    )(n2, n2t, dy, dyt, gcol, grow, wg, wu, wd)


def expert_rows_kernel(hid, dga, dua, dy, gcol, wg, wu, wd):
    experts, tokens, hidden = hid.shape
    width = dy.shape[1]
    f32 = jnp.float32
    whole = lambda shape: pl.BlockSpec(shape, lambda e: (0,) * len(shape))
    per_expert = lambda shape: pl.BlockSpec((1,) + shape, lambda e: (e,) + (0,) * len(shape))
    return pl.pallas_call(
        _rows_body,
        grid=(experts,),
        in_specs=[
            per_expert((tokens, hidden)),
            per_expert((tokens, hidden)),
            per_expert((tokens, hidden)),
            whole((tokens, width)),
            whole((tokens, experts)),
            per_expert((width, hidden)),
            per_expert((width, hidden)),
            per_expert((width, hidden)),
        ],
        out_specs=[whole((tokens, width)), per_expert((tokens, 1)), whole((tokens, width))],
        out_shape=[
            jax.ShapeDtypeStruct((tokens, width), f32),
            jax.ShapeDtypeStruct((experts, tokens, 1), f32),
            jax.ShapeDtypeStruct((tokens, width), f32),
        ],
        compiler_params=pltpu.CompilerParams(
            dimension_semantics=("arbitrary",), vmem_limit_bytes=64 * 1024 * 1024
        ),
        cost_estimate=pl.CostEstimate(
            flops=experts * tokens * width * hidden * 2 * 3,
            transcendentals=0,
            bytes_accessed=experts * width * hidden * 6 + tokens * width * 10 + experts * tokens * hidden * 6,
        ),
    )(hid, dga, dua, dy, gcol, wg, wu, wd)

MESH = pl.DeviceIdType.MESH


def _exchange_body(axis, n, per_peer, downward, src_ref, out_ref, send_sems, recv_sems):
    me = lax.axis_index(axis)
    barrier = pltpu.get_barrier_semaphore()
    for k in range(1, n):
        peer = lax.rem(me + k, n)
        pl.semaphore_signal(barrier, 1, device_id={axis: peer}, device_id_type=MESH)
    pl.semaphore_wait(barrier, n - 1)
    sends = []
    for k in range(1, n):
        peer = lax.rem(me + k, n)
        copy = pltpu.make_async_remote_copy(
            src_ref=src_ref.at[peer] if per_peer else src_ref,
            dst_ref=out_ref.at[me],
            send_sem=send_sems.at[k - 1],
            recv_sem=recv_sems.at[k - 1],
            device_id={axis: peer},
            device_id_type=MESH,
        )
        sends.append((peer, copy))
        if downward:
            pl.when(peer < me)(copy.start)
        else:
            copy.start()
    for k in range(1, n):
        source = lax.rem(me + n - k, n)
        incoming = pltpu.make_async_remote_copy(
            src_ref=src_ref.at[source] if per_peer else src_ref,
            dst_ref=out_ref.at[source],
            send_sem=send_sems.at[k - 1],
            recv_sem=recv_sems.at[k - 1],
            device_id={axis: source},
            device_id_type=MESH,
        )
        if downward:
            pl.when(source > me)(incoming.wait_recv)
        else:
            incoming.wait_recv()
    for peer, copy in sends:
        if downward:
            pl.when(peer < me)(copy.wait_send)
        else:
            copy.wait_send()


def exchange(x, axis, n, per_peer, collective_id, downward=False):
    block = x.shape[1:] if per_peer else x.shape
    nbytes = math.prod(block) * x.dtype.itemsize
    return pl.pallas_call(
        functools.partial(_exchange_body, axis, n, per_peer, downward),
        out_shape=jax.ShapeDtypeStruct((n,) + tuple(block), x.dtype),
        in_specs=[pl.BlockSpec(memory_space=pl.ANY)],
        out_specs=pl.BlockSpec(memory_space=pl.ANY),
        scratch_shapes=[pltpu.SemaphoreType.DMA((n - 1,)), pltpu.SemaphoreType.DMA((n - 1,))],
        compiler_params=pltpu.CompilerParams(collective_id=collective_id, has_side_effects=True),
        cost_estimate=pl.CostEstimate(flops=0, transcendentals=0, bytes_accessed=2 * (n - 1) * nbytes),
    )(x)


def gather_axis(x, axis, n, collective_id):
    got = exchange(x, axis, n, False, collective_id)
    return lax.dynamic_update_slice_in_dim(got, x[None], lax.axis_index(axis), 0)


def sum_axis(x, axis, collective_id):
    got = exchange(x, axis, 2, False, collective_id)
    me = lax.axis_index(axis)
    other = lax.dynamic_index_in_dim(got, 1 - me, 0, keepdims=False)
    return x.astype(jnp.float32) + other.astype(jnp.float32)


def _pair_add_body(me_ref, own_ref, other_ref, out_ref):
    out_ref[...] = (own_ref[...].astype(jnp.float32) + other_ref[...].astype(jnp.float32)).astype(out_ref.dtype)


def core_reduce(x, collective_id):
    got = exchange(x, "core", 2, True, collective_id)
    me = lax.axis_index("core")
    count = x.shape[1]
    rest = x.shape[2:]
    zeros = (0,) * len(rest)
    item_bytes = math.prod(rest) * x.dtype.itemsize
    step = max(d for d in range(1, count + 1) if count % d == 0 and d * item_bytes <= 4 * 1024 * 1024)
    grid_spec = pltpu.PrefetchScalarGridSpec(
        num_scalar_prefetch=1,
        grid=(count // step,),
        in_specs=[
            pl.BlockSpec((None, step) + rest, lambda i, c: (c[0], i) + zeros),
            pl.BlockSpec((None, step) + rest, lambda i, c: (1 - c[0], i) + zeros),
        ],
        out_specs=pl.BlockSpec((step,) + rest, lambda i, c: (i,) + zeros),
    )
    return pl.pallas_call(
        _pair_add_body,
        grid_spec=grid_spec,
        out_shape=jax.ShapeDtypeStruct(x.shape[1:], jnp.bfloat16),
        compiler_params=pltpu.CompilerParams(vmem_limit_bytes=56 * 1024 * 1024),
        cost_estimate=pl.CostEstimate(flops=x.size // 2, transcendentals=0, bytes_accessed=x.size * 3),
    )(jnp.reshape(me, (1,)).astype(jnp.int32), x, got)


def scatter_sum_downward(x, axis, n, collective_id):
    got = exchange(x, axis, n, True, collective_id, downward=True)
    me = lax.axis_index(axis)
    own = lax.dynamic_index_in_dim(x, me, 0, keepdims=False).astype(jnp.float32)
    above = (jnp.arange(n, dtype=jnp.int32) > me).reshape((n,) + (1,) * (x.ndim - 1))
    return own + jnp.sum(jnp.where(above, got.astype(jnp.float32), 0.0), axis=0)


def _flash_body(groups, ctx_ref, live_ref, q_ref, k_ref, v_ref, qseg_ref, qpos_ref, kseg_ref, o_ref, lse_ref, m_sc, l_sc, acc_sc):
    f32 = jnp.float32
    block = pl.program_id(1)
    depth = HEAD_SIZE
    pair = k_ref.shape[2] // depth

    @pl.when(block == 0)
    def _():
        m_sc[...] = jnp.full_like(m_sc, NEGATIVE)
        l_sc[...] = jnp.zeros_like(l_sc)
        acc_sc[...] = jnp.zeros_like(acc_sc)

    @pl.when((block <= ctx_ref[0]) & (live_ref[block] != 0))
    def _():
        width = k_ref.shape[1]
        key_pos = block * width + lax.broadcasted_iota(jnp.int32, (1, width), 1)
        allowed = (qseg_ref[...] == kseg_ref[...]) & (key_pos <= qpos_ref[...])
        for kk in range(pair):
            keys = k_ref[0, :, kk * depth : (kk + 1) * depth]
            values = v_ref[0, :, kk * depth : (kk + 1) * depth]
            for gi in range(groups):
                i = kk * groups + gi
                cols = slice(i * depth, (i + 1) * depth)
                queries = q_ref[:, cols] * jnp.asarray(1.0 / math.sqrt(HEAD_SIZE), q_ref.dtype)
                scores = lax.dot_general(
                    queries, keys, (((1,), (1,)), ((), ())), preferred_element_type=f32
                )
                scores = jnp.where(allowed, scores, NEGATIVE)
                m_old = m_sc[i]
                m_new = jnp.maximum(m_old, jnp.max(scores, axis=1, keepdims=True))
                alpha = jnp.exp(m_old - m_new)
                weights = jnp.exp(scores - m_new)
                l_sc[i] = alpha * l_sc[i] + jnp.sum(weights, axis=1, keepdims=True)
                acc_sc[:, cols] = alpha * acc_sc[:, cols] + jnp.dot(
                    weights.astype(jnp.bfloat16), values, preferred_element_type=f32
                )
                m_sc[i] = m_new

    @pl.when(block == pl.num_programs(1) - 1)
    def _():
        for i in range(m_sc.shape[0]):
            cols = slice(i * depth, (i + 1) * depth)
            o_ref[:, cols] = acc_sc[:, cols] / l_sc[i]
            lse_ref[0, :, i : i + 1] = m_sc[i] + jnp.log(l_sc[i])


def flash_forward(ctx_index, live, q, kv, qseg, qpos, kseg, groups):
    tokens, q_width = q.shape
    blocks, width, kv_width = kv.shape
    pair = 2
    pairs = kv_width // (2 * pair * HEAD_SIZE)
    heads_step = pair * groups
    f32 = jnp.float32
    capped = lambda p, b, c, f: (jnp.minimum(b, c[0]), 0, p)
    grid_spec = pltpu.PrefetchScalarGridSpec(
        num_scalar_prefetch=2,
        grid=(pairs, blocks),
        in_specs=[
            pl.BlockSpec((tokens, heads_step * HEAD_SIZE), lambda p, b, c, f: (0, p)),
            pl.BlockSpec((1, width, pair * HEAD_SIZE), capped),
            pl.BlockSpec(
                (1, width, pair * HEAD_SIZE), lambda p, b, c, f: (jnp.minimum(b, c[0]), 0, pairs + p)
            ),
            pl.BlockSpec((tokens, 1), lambda p, b, c, f: (0, 0)),
            pl.BlockSpec((tokens, 1), lambda p, b, c, f: (0, 0)),
            pl.BlockSpec((1, width), lambda p, b, c, f: (0, jnp.minimum(b, c[0]))),
        ],
        out_specs=[
            pl.BlockSpec((tokens, heads_step * HEAD_SIZE), lambda p, b, c, f: (0, p)),
            pl.BlockSpec((1, tokens, heads_step), lambda p, b, c, f: (p, 0, 0)),
        ],
        scratch_shapes=[
            pltpu.VMEM((heads_step, tokens, 1), f32),
            pltpu.VMEM((heads_step, tokens, 1), f32),
            pltpu.VMEM((tokens, heads_step * HEAD_SIZE), f32),
        ],
    )
    return pl.pallas_call(
        functools.partial(_flash_body, groups),
        grid_spec=grid_spec,
        out_shape=[
            jax.ShapeDtypeStruct((tokens, q_width), f32),
            jax.ShapeDtypeStruct((pairs, tokens, heads_step), f32),
        ],
        compiler_params=pltpu.CompilerParams(
            dimension_semantics=("arbitrary", "arbitrary"), vmem_limit_bytes=48 * 1024 * 1024
        ),
        cost_estimate=pl.CostEstimate(
            flops=tokens * q_width * blocks * width * 4,
            transcendentals=tokens * (q_width // HEAD_SIZE) * blocks * width,
            bytes_accessed=(q.size + kv.size) * 2 + tokens * q_width * 4,
        ),
    )(jnp.reshape(ctx_index, (1,)).astype(jnp.int32), live, q, kv, kv, qseg, qpos, kseg)

def _chain_down_body(axis, n, x_ref, out_ref, recv, send, send_sems, recv_sems):
    f32 = jnp.float32
    me = lax.axis_index(axis)
    below = lax.rem(me + n - 1, n)
    above = lax.rem(me + 1, n)
    barrier = pltpu.get_barrier_semaphore()
    pl.semaphore_signal(barrier, 1, device_id={axis: below}, device_id_type=MESH)
    pl.semaphore_signal(barrier, 1, device_id={axis: above}, device_id_type=MESH)
    pl.semaphore_wait(barrier, 2)
    copies = []
    for j in range(n - 1):
        copy = pltpu.make_async_remote_copy(
            src_ref=send.at[j],
            dst_ref=recv.at[j],
            send_sem=send_sems.at[j],
            recv_sem=recv_sems.at[j],
            device_id={axis: below},
            device_id_type=MESH,
        )
        copies.append(copy)

        @pl.when((j < me) & (me < n - 1))
        def _():
            copy.wait_recv()
            send[j] = (x_ref[j].astype(f32) + recv[j].astype(f32)).astype(send.dtype)

        @pl.when((j < me) & (me == n - 1))
        def _():
            send[j] = x_ref[j]

        @pl.when(j < me)
        def _():
            copy.start()

        @pl.when(j == me)
        def _():
            copy.wait_recv()
            out_ref[...] = x_ref[j].astype(f32) + recv[j].astype(f32)

    @pl.when(me == n - 1)
    def _():
        out_ref[...] = x_ref[n - 1].astype(f32)

    for j in range(n - 1):
        pl.when(j < me)(copies[j].wait_send)


def chain_sum_down(x, axis, n, collective_id):
    _, rows, cols = x.shape
    return pl.pallas_call(
        functools.partial(_chain_down_body, axis, n),
        out_shape=jax.ShapeDtypeStruct((rows, cols), jnp.float32),
        in_specs=[pl.BlockSpec(memory_space=pltpu.VMEM)],
        out_specs=pl.BlockSpec(memory_space=pltpu.VMEM),
        scratch_shapes=[
            pltpu.VMEM((n - 1, rows, cols), x.dtype),
            pltpu.VMEM((n - 1, rows, cols), x.dtype),
            pltpu.SemaphoreType.DMA((n - 1,)),
            pltpu.SemaphoreType.DMA((n - 1,)),
        ],
        compiler_params=pltpu.CompilerParams(
            collective_id=collective_id, has_side_effects=True, vmem_limit_bytes=32 * 1024 * 1024
        ),
        cost_estimate=pl.CostEstimate(
            flops=(n - 1) * rows * cols, transcendentals=0, bytes_accessed=3 * n * rows * cols * 2
        ),
    )(x)


def per_device(
    dpx_count,
    hidden_in,
    attn_gain,
    q_weight,
    key_matrix,
    value_matrix,
    o_weight,
    moe_gain,
    router_weight,
    gate_weight,
    up_weight,
    down_weight,
    segments,
    expert_picks,
    output_grad,
):
    bf16 = jnp.bfloat16
    f32 = jnp.float32
    token_count = hidden_in.shape[0]
    ctx_index = lax.axis_index("ctx")
    heads_local = q_weight.shape[1] // HEAD_SIZE
    kv_local = key_matrix.shape[1] // HEAD_SIZE
    group_size = heads_local // kv_local
    score_scale = 1.0 / math.sqrt(HEAD_SIZE)
    token_positions = ctx_index * token_count + jnp.arange(token_count, dtype=jnp.int32)
    segment_here = lax.dynamic_slice_in_dim(segments, ctx_index * token_count, token_count)
    inputs_f32 = hidden_in.astype(f32)
    o_full = lax.all_gather(o_weight, "tensor", axis=1, tiled=True)
    normed_f32, scale_one = normalize(inputs_f32, attn_gain)
    normed_one = normed_f32.astype(bf16)
    query_rows = jnp.dot(normed_one, q_weight, preferred_element_type=f32).reshape(
        token_count, heads_local, HEAD_SIZE
    )
    keys_raw = jnp.dot(normed_one, key_matrix, preferred_element_type=f32).reshape(
        token_count, kv_local, HEAD_SIZE
    )
    values_raw = jnp.dot(normed_one, value_matrix, preferred_element_type=f32)
    query_grouped = (
        apply_rotary(query_rows, token_positions, 1.0)
        .astype(bf16)
        .reshape(token_count, kv_local, group_size, HEAD_SIZE)
    )
    key_flat = (
        apply_rotary(keys_raw, token_positions, 1.0)
        .astype(bf16)
        .reshape(token_count, kv_local * HEAD_SIZE)
    )
    value_flat = values_raw.astype(bf16)

    def piece_mask(piece_rows):
        key_pos = jnp.arange(piece_rows, dtype=jnp.int32)
        return (segment_here[:, None] == segments[None, :]) & (
            key_pos[None, :] <= token_positions[:, None]
        )

    ctx_count = segments.shape[0] // token_count
    kv_both = gather_axis(jnp.concatenate([key_flat, value_flat], axis=1), "ctx", ctx_count, 1)
    piece_rows = ctx_count * token_count
    kv_width = kv_local * HEAD_SIZE
    key_piece = kv_both[:, :, :kv_width].reshape(piece_rows, kv_local, HEAD_SIZE)
    value_piece = kv_both[:, :, kv_width:].reshape(piece_rows, kv_local, HEAD_SIZE)
    key_blocks = segments.shape[0] // token_count
    live_blocks = jnp.any(
        (
            (segment_here[:, None] == segments[None, :])
            & (jnp.arange(segments.shape[0], dtype=jnp.int32)[None, :] <= token_positions[:, None])
        ).reshape(token_count, key_blocks, token_count),
        axis=(0, 2),
    ).astype(jnp.int32)
    attn_flat, lse_pairs = flash_forward(
        ctx_index,
        live_blocks,
        query_grouped.reshape(token_count, heads_local * HEAD_SIZE),
        kv_both,
        segment_here[:, None],
        token_positions[:, None],
        segments[None, :],
        group_size,
    )
    attn_grouped = jnp.transpose(
        attn_flat.reshape(token_count, kv_local, group_size, HEAD_SIZE), (1, 2, 0, 3)
    )
    log_sum = jnp.transpose(
        lse_pairs.reshape(kv_local // 2, token_count, 2, group_size), (0, 2, 3, 1)
    ).reshape(kv_local, group_size, token_count)
    attn_bf = attn_flat.astype(bf16)
    tensor_count = o_weight.shape[0] // o_weight.shape[1]
    attn_all = gather_axis(attn_bf, "tensor", tensor_count, 2)
    attn_full = jnp.transpose(attn_all, (1, 0, 2)).reshape(token_count, tensor_count * attn_bf.shape[1])
    mixed_attn = contract_cols(attn_full, o_full)
    resid = inputs_f32 + mixed_attn
    normed_two_f32, scale_two = normalize(resid, moe_gain)
    normed_two = normed_two_f32.astype(bf16)
    logits = jnp.dot(normed_two, router_weight, preferred_element_type=f32)
    expert_range = jnp.arange(NEXP, dtype=jnp.int32)
    picked_onehot = expert_picks[:, :, None] == expert_range[None, None, :]
    picked = jnp.sum(jnp.where(picked_onehot, logits[:, None, :], 0.0), axis=2)
    gate_probs = jax.nn.softmax(picked, axis=-1)
    gates_dense = jnp.sum(jnp.where(picked_onehot, gate_probs[:, :, None], 0.0), axis=1)
    gates_by_expert = jnp.transpose(gates_dense)
    cot_bf = output_grad
    gcol = gates_dense
    grad_gate, grad_up, grad_down, hid_all, dga_all, dua_all = expert_grad_kernel(
        normed_two,
        jnp.transpose(normed_two),
        cot_bf,
        jnp.transpose(cot_bf),
        gcol,
        gates_by_expert[:, None, :],
        gate_weight,
        up_weight,
        down_weight,
        dpx_count,
    )
    gate_half = core_reduce(grad_gate, 8)
    gate_half, hid_all, dga_all, dua_all = lax.optimization_barrier(
        (gate_half, hid_all, dga_all, dua_all)
    )
    moe_acc, gate_parts, moe_grad_rows = expert_rows_kernel(
        hid_all, dga_all, dua_all, cot_bf, gcol, gate_weight, up_weight, down_weight
    )
    cot_f32 = output_grad.astype(f32)
    moe_total = sum_axis(moe_acc.astype(bf16), "tensor", 3)
    output = (resid + moe_total).astype(bf16)
    grad_rows_all = moe_grad_rows
    gate_parts = gate_parts[:, :, 0]
    grad_gate_out, grad_up_out, grad_down_out = [
        lax.psum_scatter(
            g.reshape(g.shape[0], -1, g.shape[3]), ("dpx", "ctx"), scatter_dimension=1, tiled=True
        ).astype(jnp.float32)
        for g in (gate_half, core_reduce(grad_up, 9), core_reduce(grad_down, 10))
    ]
    gate_pair = jnp.sum(
        jnp.where(picked_onehot, jnp.transpose(gate_parts)[:, None, :], 0.0), axis=2
    )
    moe_summed = sum_axis(grad_rows_all.astype(bf16), "tensor", 4)
    gate_summed = sum_axis(gate_pair.astype(bf16), "tensor", 5)
    grad_picked = gate_probs * (
        gate_summed - jnp.sum(gate_probs * gate_summed, axis=1, keepdims=True)
    )
    grad_logits = jnp.sum(jnp.where(picked_onehot, grad_picked[:, :, None], 0.0), axis=1).astype(
        bf16
    )
    grad_router = contract_rows(normed_two, grad_logits)
    grad_normed_two = moe_summed + contract_cols(grad_logits, router_weight)
    grad_two_rows, grad_moe_gain = norm_backward(resid, scale_two, moe_gain, grad_normed_two)
    grad_resid = cot_f32 + grad_two_rows
    grad_mix = grad_resid.astype(bf16)
    grad_o = contract_rows(grad_mix, attn_bf)
    grad_attn = jnp.dot(grad_mix, o_weight, preferred_element_type=f32).astype(bf16)
    grad_attn_grouped = jnp.transpose(
        grad_attn.reshape(token_count, kv_local, group_size, HEAD_SIZE), (1, 2, 0, 3)
    )
    row_delta = jnp.sum(grad_attn_grouped.astype(f32) * attn_grouped, axis=-1)
    allowed = piece_mask(piece_rows)
    scores = (
        jnp.einsum("tkgd,nkd->kgtn", query_grouped, key_piece, preferred_element_type=f32)
        * score_scale
    )
    probability = jnp.where(allowed, jnp.exp(scores - log_sum[..., None]), 0.0)
    grad_probs = jnp.einsum(
        "kgtd,nkd->kgtn", grad_attn_grouped, value_piece, preferred_element_type=f32
    )
    grad_scores = (probability * (grad_probs - row_delta[..., None])).astype(bf16)
    grad_query = score_scale * jnp.einsum(
        "kgtn,nkd->kgtd", grad_scores, key_piece, preferred_element_type=f32
    )
    key_part = score_scale * jnp.einsum(
        "kgtn,tkgd->nkd", grad_scores, query_grouped, preferred_element_type=f32
    )
    value_part = jnp.einsum(
        "kgtn,kgtd->nkd", probability.astype(bf16), grad_attn_grouped, preferred_element_type=f32
    )
    grad_keys_all = key_part.reshape(piece_rows, kv_local * HEAD_SIZE)
    grad_values_all = value_part.reshape(piece_rows, kv_local * HEAD_SIZE)
    back_state = (grad_query, grad_keys_all, grad_values_all)
    grad_query, grad_keys_all, grad_values_all = back_state
    grad_kv_here = chain_sum_down(
        jnp.concatenate([grad_keys_all, grad_values_all], axis=1)
        .astype(bf16)
        .reshape(ctx_count, token_count, 2 * kv_width),
        "ctx",
        ctx_count,
        6,
    )
    grad_keys_here = grad_kv_here[:, :kv_width]
    grad_values_here = grad_kv_here[:, kv_width:]
    grad_query_rows = jnp.transpose(grad_query, (2, 0, 1, 3)).reshape(
        token_count, heads_local, HEAD_SIZE
    )
    grad_query_bf = (
        apply_rotary(grad_query_rows, token_positions, -1.0)
        .reshape(token_count, heads_local * HEAD_SIZE)
        .astype(bf16)
    )
    grad_key_bf = (
        apply_rotary(
            grad_keys_here.reshape(token_count, kv_local, HEAD_SIZE), token_positions, -1.0
        )
        .reshape(token_count, kv_local * HEAD_SIZE)
        .astype(bf16)
    )
    grad_value_bf = grad_values_here.astype(bf16)
    grad_q = contract_rows(normed_one, grad_query_bf)
    grad_k = contract_rows(normed_one, grad_key_bf)
    grad_v = contract_rows(normed_one, grad_value_bf)
    partial_one = (
        contract_cols(grad_query_bf, q_weight)
        + contract_cols(grad_key_bf, key_matrix)
        + contract_cols(grad_value_bf, value_matrix)
    )
    grad_normed_one = sum_axis(partial_one.astype(bf16), "tensor", 7)
    grad_one_rows, grad_attn_gain = norm_backward(inputs_f32, scale_one, attn_gain, grad_normed_one)
    input_grad = grad_resid + grad_one_rows
    q_cols, o_cols, k_cols = grad_q.shape[1], grad_o.shape[1], grad_k.shape[1]
    small = jnp.concatenate(
        [
            grad_router,
            grad_attn_gain[:, None],
            grad_moe_gain[:, None],
            jnp.zeros((grad_router.shape[0], 128 - grad_router.shape[1] - 2), f32),
        ],
        axis=1,
    )
    dense_all = jnp.concatenate(
        [grad_q, grad_o, grad_k, grad_v, small], axis=1
    ).astype(bf16)
    width = dense_all.shape[0]
    dense_all = jnp.transpose(
        dense_all.reshape(dpx_count, 2, width // (2 * dpx_count), dense_all.shape[1]), (1, 0, 2, 3)
    )
    dense_half = core_reduce(dense_all, 11)
    dense_half, grad_gate_out, grad_up_out, grad_down_out = lax.optimization_barrier(
        (dense_half, grad_gate_out, grad_up_out, grad_down_out)
    )
    dense_here = lax.psum_scatter(
        dense_half.reshape(-1, dense_half.shape[-1]), ("dpx", "ctx"), scatter_dimension=0, tiled=True
    ).astype(f32)
    spans = [q_cols, o_cols, k_cols, k_cols, router_weight.shape[1], 1, 1]
    cuts = [sum(spans[:i]) for i in range(len(spans) + 1)]
    pieces_out = [dense_here[:, cuts[i] : cuts[i + 1]] for i in range(len(spans))]
    dense_out = (
        pieces_out[5][:, 0],
        pieces_out[0],
        pieces_out[2],
        pieces_out[3],
        pieces_out[1],
        pieces_out[6][:, 0],
        pieces_out[4],
    )
    return (
        output,
        input_grad,
        dense_out[0],
        dense_out[1],
        dense_out[2],
        dense_out[3],
        dense_out[4],
        dense_out[5],
        dense_out[6],
        grad_gate_out,
        grad_up_out,
        grad_down_out,
    )


def solution(mesh):
    dp_count, ctx_count, tensor_count = (mesh.shape[a] for a in ("dp", "ctx", "tensor"))
    split_mesh = jax.sharding.Mesh(
        mesh.devices.reshape(dp_count // 2, 2, ctx_count, tensor_count), ("dpx", "core", "ctx", "tensor")
    )
    return jax.shard_map(
        functools.partial(per_device, dp_count // 2),
        mesh=split_mesh,
        in_specs=(
            P(("dpx", "core", "ctx"), None),
            P(),
            P(None, "tensor"),
            P(None, "tensor"),
            P(None, "tensor"),
            P(None, "tensor"),
            P(),
            P(),
            P(None, None, "tensor"),
            P(None, None, "tensor"),
            P(None, None, "tensor"),
            P(("dpx", "core")),
            P(("dpx", "core", "ctx"), None),
            P(("dpx", "core", "ctx"), None),
        ),
        out_specs=(
            P(("dpx", "core", "ctx"), None),
            P(("dpx", "core", "ctx"), None),
            P(("dpx", "core", "ctx")),
            P(("dpx", "core", "ctx"), "tensor"),
            P(("dpx", "core", "ctx"), "tensor"),
            P(("dpx", "core", "ctx"), "tensor"),
            P(("dpx", "core", "ctx"), "tensor"),
            P(("dpx", "core", "ctx")),
            P(("dpx", "core", "ctx"), None),
            P(None, ("dpx", "core", "ctx"), "tensor"),
            P(None, ("dpx", "core", "ctx"), "tensor"),
            P(None, ("dpx", "core", "ctx"), "tensor"),
        ),
        check_vma=False,
    )
```

```python
import functools
import math

import jax
import jax.numpy as jnp
from jax import lax
from jax.experimental import pallas as pl
from jax.experimental.pallas import tpu as pltpu
from jax.sharding import PartitionSpec as P

HEAD_SIZE = 64
NEXP = 24
CAP = 341


EPSILON = 1e-06
ROPE_BASE = 10000.0
NEGATIVE = -1e30
HIGHEST = lax.Precision.HIGHEST


def normalize(rows, gain):
    scale_inv = lax.rsqrt(jnp.mean(rows * rows, axis=-1, keepdims=True) + EPSILON)
    return (rows * scale_inv * gain, scale_inv)


def norm_backward(rows, scale_inv, gain, grad_normed):
    weighted = gain * grad_normed
    grad_gain = jnp.sum(grad_normed * rows * scale_inv, axis=0)
    inner_mean = jnp.mean(weighted * rows, axis=-1, keepdims=True)
    grad_rows = scale_inv * weighted - rows * scale_inv * scale_inv * scale_inv * inner_mean
    return (grad_rows, grad_gain)


def apply_rotary(value_rows, token_positions, direction):
    half_dim = value_rows.shape[-1] // 2
    frequency = ROPE_BASE ** (-jnp.arange(half_dim, dtype=jnp.float32) / half_dim)
    angles = token_positions.astype(jnp.float32)[:, None] * frequency[None, :]
    cosine = jnp.cos(angles)[:, None, :]
    sine_part = direction * jnp.sin(angles)[:, None, :]
    first_half = value_rows[..., :half_dim]
    second = value_rows[..., half_dim:]
    return jnp.concatenate(
        [first_half * cosine - second * sine_part, second * cosine + first_half * sine_part],
        axis=-1,
    )


def contract_rows(left, right):
    return lax.dot_general(
        left, right, (((0,), (0,)), ((), ())), preferred_element_type=jnp.float32
    )


def contract_rows_exact(left, right):
    return lax.dot_general(
        left, right, (((0,), (0,)), ((), ())), precision=HIGHEST, preferred_element_type=jnp.float32
    )


def contract_cols(left, right):
    return lax.dot_general(
        left, right, (((1,), (1,)), ((), ())), preferred_element_type=jnp.float32
    )


def _store_split(out_ref, value):
    cores, _, groups, rows, _ = out_ref.shape
    for x in range(groups):
        for c in range(cores):
            start = (x * cores + c) * rows
            out_ref[c, 0, x] = value[start : start + rows].astype(out_ref.dtype)


def _gate_column(gates_ref):
    gates = gates_ref[...]
    lane = lax.broadcasted_iota(jnp.int32, gates.shape, 1)
    return jnp.sum(jnp.where(lane == pl.program_id(0), gates, 0.0), axis=1, keepdims=True)


def _grad_body(
    n2_ref, n2t_ref, dy_ref, dyt_ref, gcol_ref, grow_ref, wg_ref, wu_ref, wd_ref,
    gg_ref, gu_ref, gd_ref, hid_ref, dga_ref, dua_ref,
):
    f32 = jnp.float32
    bf16 = jnp.bfloat16
    n2 = n2_ref[...]
    wd = wd_ref[0]
    gate_act = jnp.dot(n2, wg_ref[0], preferred_element_type=f32)
    up_act = jnp.dot(n2, wu_ref[0], preferred_element_type=f32)
    sig = 1.0 / (1.0 + jnp.exp(-gate_act))
    silu = gate_act * sig
    hidden = (silu * up_act).astype(bf16)
    hid_ref[0] = hidden
    deo = (_gate_column(gcol_ref) * dy_ref[...].astype(f32)).astype(bf16)
    grad_hidden = jnp.dot(deo, wd, preferred_element_type=f32)
    deo_t = (grow_ref[0] * dyt_ref[...].astype(f32)).astype(bf16)
    _store_split(gd_ref, jnp.dot(deo_t, hidden, preferred_element_type=f32))
    grad_gate_act = (grad_hidden * up_act * sig * (1.0 + gate_act * (1.0 - sig))).astype(bf16)
    grad_up_act = (grad_hidden * silu).astype(bf16)
    dga_ref[0] = grad_gate_act
    dua_ref[0] = grad_up_act
    n2t = n2t_ref[...]
    _store_split(gg_ref, jnp.dot(n2t, grad_gate_act, preferred_element_type=f32))
    _store_split(gu_ref, jnp.dot(n2t, grad_up_act, preferred_element_type=f32))


def _rows_body(hid_ref, dga_ref, dua_ref, dy_ref, gcol_ref, wg_ref, wu_ref, wd_ref, acc_ref, dgate_ref, dn2_ref):
    f32 = jnp.float32
    nt = (((1,), (1,)), ((), ()))

    @pl.when(pl.program_id(0) == 0)
    def _():
        acc_ref[...] = jnp.zeros_like(acc_ref)
        dn2_ref[...] = jnp.zeros_like(dn2_ref)

    expert_out = lax.dot_general(hid_ref[0], wd_ref[0], nt, preferred_element_type=f32)
    acc_ref[...] += _gate_column(gcol_ref) * expert_out
    dgate_ref[0] = jnp.sum(expert_out * dy_ref[...].astype(f32), axis=1, keepdims=True)
    dn2_ref[...] += lax.dot_general(
        dga_ref[0], wg_ref[0], nt, preferred_element_type=f32
    ) + lax.dot_general(dua_ref[0], wu_ref[0], nt, preferred_element_type=f32)


def expert_grad_kernel(n2, n2t, dy, dyt, gcol, grow, wg, wu, wd, groups):
    tokens, width = n2.shape
    experts, _, hidden = wg.shape
    bf16 = jnp.bfloat16
    whole = lambda shape: pl.BlockSpec(shape, lambda e: (0,) * len(shape))
    per_expert = lambda shape: pl.BlockSpec((1,) + shape, lambda e: (e,) + (0,) * len(shape))
    split_rows = width // (groups * 2)
    split = pl.BlockSpec((2, 1, groups, split_rows, hidden), lambda e: (0, e, 0, 0, 0))
    split_shape = jax.ShapeDtypeStruct((2, experts, groups, split_rows, hidden), bf16)
    act_shape = jax.ShapeDtypeStruct((experts, tokens, hidden), bf16)
    return pl.pallas_call(
        _grad_body,
        grid=(experts,),
        in_specs=[
            whole((tokens, width)),
            whole((width, tokens)),
            whole((tokens, width)),
            whole((width, tokens)),
            whole((tokens, experts)),
            per_expert((1, tokens)),
            per_expert((width, hidden)),
            per_expert((width, hidden)),
            per_expert((width, hidden)),
        ],
        out_specs=[split, split, split]
        + [per_expert((tokens, hidden))] * 3,
        out_shape=[split_shape] * 3 + [act_shape] * 3,
        compiler_params=pltpu.CompilerParams(
            dimension_semantics=("arbitrary",), vmem_limit_bytes=64 * 1024 * 1024
        ),
        cost_estimate=pl.CostEstimate(
            flops=experts * tokens * width * hidden * 2 * 6,
            transcendentals=experts * tokens * hidden,
            bytes_accessed=experts * width * hidden * 12 + tokens * width * 8 + experts * tokens * hidden * 6,
        ),
    )(n2, n2t, dy, dyt, gcol, grow, wg, wu, wd)


def expert_rows_kernel(hid, dga, dua, dy, gcol, wg, wu, wd):
    experts, tokens, hidden = hid.shape
    width = dy.shape[1]
    f32 = jnp.float32
    whole = lambda shape: pl.BlockSpec(shape, lambda e: (0,) * len(shape))
    per_expert = lambda shape: pl.BlockSpec((1,) + shape, lambda e: (e,) + (0,) * len(shape))
    return pl.pallas_call(
        _rows_body,
        grid=(experts,),
        in_specs=[
            per_expert((tokens, hidden)),
            per_expert((tokens, hidden)),
            per_expert((tokens, hidden)),
            whole((tokens, width)),
            whole((tokens, experts)),
            per_expert((width, hidden)),
            per_expert((width, hidden)),
            per_expert((width, hidden)),
        ],
        out_specs=[whole((tokens, width)), per_expert((tokens, 1)), whole((tokens, width))],
        out_shape=[
            jax.ShapeDtypeStruct((tokens, width), f32),
            jax.ShapeDtypeStruct((experts, tokens, 1), f32),
            jax.ShapeDtypeStruct((tokens, width), f32),
        ],
        compiler_params=pltpu.CompilerParams(
            dimension_semantics=("arbitrary",), vmem_limit_bytes=64 * 1024 * 1024
        ),
        cost_estimate=pl.CostEstimate(
            flops=experts * tokens * width * hidden * 2 * 3,
            transcendentals=0,
            bytes_accessed=experts * width * hidden * 6 + tokens * width * 10 + experts * tokens * hidden * 6,
        ),
    )(hid, dga, dua, dy, gcol, wg, wu, wd)

MESH = pl.DeviceIdType.MESH


def _exchange_body(axis, n, per_peer, downward, src_ref, out_ref, send_sems, recv_sems):
    me = lax.axis_index(axis)
    barrier = pltpu.get_barrier_semaphore()
    for k in range(1, n):
        peer = lax.rem(me + k, n)
        pl.semaphore_signal(barrier, 1, device_id={axis: peer}, device_id_type=MESH)
    pl.semaphore_wait(barrier, n - 1)
    sends = []
    for k in range(1, n):
        peer = lax.rem(me + k, n)
        copy = pltpu.make_async_remote_copy(
            src_ref=src_ref.at[peer] if per_peer else src_ref,
            dst_ref=out_ref.at[me],
            send_sem=send_sems.at[k - 1],
            recv_sem=recv_sems.at[k - 1],
            device_id={axis: peer},
            device_id_type=MESH,
        )
        sends.append((peer, copy))
        if downward:
            pl.when(peer < me)(copy.start)
        else:
            copy.start()
    for k in range(1, n):
        source = lax.rem(me + n - k, n)
        incoming = pltpu.make_async_remote_copy(
            src_ref=src_ref.at[source] if per_peer else src_ref,
            dst_ref=out_ref.at[source],
            send_sem=send_sems.at[k - 1],
            recv_sem=recv_sems.at[k - 1],
            device_id={axis: source},
            device_id_type=MESH,
        )
        if downward:
            pl.when(source > me)(incoming.wait_recv)
        else:
            incoming.wait_recv()
    for peer, copy in sends:
        if downward:
            pl.when(peer < me)(copy.wait_send)
        else:
            copy.wait_send()


def exchange(x, axis, n, per_peer, collective_id, downward=False):
    block = x.shape[1:] if per_peer else x.shape
    nbytes = math.prod(block) * x.dtype.itemsize
    return pl.pallas_call(
        functools.partial(_exchange_body, axis, n, per_peer, downward),
        out_shape=jax.ShapeDtypeStruct((n,) + tuple(block), x.dtype),
        in_specs=[pl.BlockSpec(memory_space=pl.ANY)],
        out_specs=pl.BlockSpec(memory_space=pl.ANY),
        scratch_shapes=[pltpu.SemaphoreType.DMA((n - 1,)), pltpu.SemaphoreType.DMA((n - 1,))],
        compiler_params=pltpu.CompilerParams(collective_id=collective_id, has_side_effects=True),
        cost_estimate=pl.CostEstimate(flops=0, transcendentals=0, bytes_accessed=2 * (n - 1) * nbytes),
    )(x)


def gather_axis(x, axis, n, collective_id):
    got = exchange(x, axis, n, False, collective_id)
    return lax.dynamic_update_slice_in_dim(got, x[None], lax.axis_index(axis), 0)


def sum_axis(x, axis, collective_id):
    got = exchange(x, axis, 2, False, collective_id)
    me = lax.axis_index(axis)
    other = lax.dynamic_index_in_dim(got, 1 - me, 0, keepdims=False)
    return x.astype(jnp.float32) + other.astype(jnp.float32)


def _pair_add_body(me_ref, own_ref, other_ref, out_ref):
    out_ref[...] = (own_ref[...].astype(jnp.float32) + other_ref[...].astype(jnp.float32)).astype(out_ref.dtype)


def core_reduce(x, collective_id):
    got = exchange(x, "core", 2, True, collective_id)
    me = lax.axis_index("core")
    count = x.shape[1]
    rest = x.shape[2:]
    zeros = (0,) * len(rest)
    item_bytes = math.prod(rest) * x.dtype.itemsize
    step = max(d for d in range(1, count + 1) if count % d == 0 and d * item_bytes <= 4 * 1024 * 1024)
    grid_spec = pltpu.PrefetchScalarGridSpec(
        num_scalar_prefetch=1,
        grid=(count // step,),
        in_specs=[
            pl.BlockSpec((None, step) + rest, lambda i, c: (c[0], i) + zeros),
            pl.BlockSpec((None, step) + rest, lambda i, c: (1 - c[0], i) + zeros),
        ],
        out_specs=pl.BlockSpec((step,) + rest, lambda i, c: (i,) + zeros),
    )
    return pl.pallas_call(
        _pair_add_body,
        grid_spec=grid_spec,
        out_shape=jax.ShapeDtypeStruct(x.shape[1:], jnp.bfloat16),
        compiler_params=pltpu.CompilerParams(vmem_limit_bytes=56 * 1024 * 1024),
        cost_estimate=pl.CostEstimate(flops=x.size // 2, transcendentals=0, bytes_accessed=x.size * 3),
    )(jnp.reshape(me, (1,)).astype(jnp.int32), x, got)


def scatter_sum_downward(x, axis, n, collective_id):
    got = exchange(x, axis, n, True, collective_id, downward=True)
    me = lax.axis_index(axis)
    own = lax.dynamic_index_in_dim(x, me, 0, keepdims=False).astype(jnp.float32)
    above = (jnp.arange(n, dtype=jnp.int32) > me).reshape((n,) + (1,) * (x.ndim - 1))
    return own + jnp.sum(jnp.where(above, got.astype(jnp.float32), 0.0), axis=0)


def _flash_body(groups, ctx_ref, q_ref, k_ref, v_ref, qseg_ref, qpos_ref, kseg_ref, o_ref, lse_ref, m_sc, l_sc, acc_sc):
    f32 = jnp.float32
    block = pl.program_id(1)
    depth = HEAD_SIZE
    pair = k_ref.shape[2] // depth

    @pl.when(block == 0)
    def _():
        m_sc[...] = jnp.full_like(m_sc, NEGATIVE)
        l_sc[...] = jnp.zeros_like(l_sc)
        acc_sc[...] = jnp.zeros_like(acc_sc)

    @pl.when(block <= ctx_ref[0])
    def _():
        width = k_ref.shape[1]
        key_pos = block * width + lax.broadcasted_iota(jnp.int32, (1, width), 1)
        allowed = (qseg_ref[...] == kseg_ref[...]) & (key_pos <= qpos_ref[...])
        for kk in range(pair):
            keys = k_ref[0, :, kk * depth : (kk + 1) * depth]
            values = v_ref[0, :, kk * depth : (kk + 1) * depth]
            for gi in range(groups):
                i = kk * groups + gi
                cols = slice(i * depth, (i + 1) * depth)
                scores = lax.dot_general(
                    q_ref[:, cols], keys, (((1,), (1,)), ((), ())), preferred_element_type=f32
                ) * (1.0 / math.sqrt(HEAD_SIZE))
                scores = jnp.where(allowed, scores, NEGATIVE)
                m_old = m_sc[i]
                m_new = jnp.maximum(m_old, jnp.max(scores, axis=1, keepdims=True))
                alpha = jnp.exp(m_old - m_new)
                weights = jnp.where(allowed, jnp.exp(scores - m_new), 0.0)
                l_sc[i] = alpha * l_sc[i] + jnp.sum(weights, axis=1, keepdims=True)
                acc_sc[:, cols] = alpha * acc_sc[:, cols] + jnp.dot(
                    weights.astype(jnp.bfloat16), values, preferred_element_type=f32
                )
                m_sc[i] = m_new

    @pl.when(block == pl.num_programs(1) - 1)
    def _():
        for i in range(m_sc.shape[0]):
            cols = slice(i * depth, (i + 1) * depth)
            o_ref[:, cols] = acc_sc[:, cols] / l_sc[i]
            lse_ref[0, :, i : i + 1] = m_sc[i] + jnp.log(l_sc[i])


def flash_forward(ctx_index, q, kv, qseg, qpos, kseg, groups):
    tokens, q_width = q.shape
    blocks, width, kv_width = kv.shape
    pair = 2
    pairs = kv_width // (2 * pair * HEAD_SIZE)
    heads_step = pair * groups
    f32 = jnp.float32
    capped = lambda p, b, c: (jnp.minimum(b, c[0]), 0, p)
    grid_spec = pltpu.PrefetchScalarGridSpec(
        num_scalar_prefetch=1,
        grid=(pairs, blocks),
        in_specs=[
            pl.BlockSpec((tokens, heads_step * HEAD_SIZE), lambda p, b, c: (0, p)),
            pl.BlockSpec((1, width, pair * HEAD_SIZE), capped),
            pl.BlockSpec((1, width, pair * HEAD_SIZE), lambda p, b, c: (jnp.minimum(b, c[0]), 0, pairs + p)),
            pl.BlockSpec((tokens, 1), lambda p, b, c: (0, 0)),
            pl.BlockSpec((tokens, 1), lambda p, b, c: (0, 0)),
            pl.BlockSpec((1, width), lambda p, b, c: (0, jnp.minimum(b, c[0]))),
        ],
        out_specs=[
            pl.BlockSpec((tokens, heads_step * HEAD_SIZE), lambda p, b, c: (0, p)),
            pl.BlockSpec((1, tokens, heads_step), lambda p, b, c: (p, 0, 0)),
        ],
        scratch_shapes=[
            pltpu.VMEM((heads_step, tokens, 1), f32),
            pltpu.VMEM((heads_step, tokens, 1), f32),
            pltpu.VMEM((tokens, heads_step * HEAD_SIZE), f32),
        ],
    )
    return pl.pallas_call(
        functools.partial(_flash_body, groups),
        grid_spec=grid_spec,
        out_shape=[
            jax.ShapeDtypeStruct((tokens, q_width), f32),
            jax.ShapeDtypeStruct((pairs, tokens, heads_step), f32),
        ],
        compiler_params=pltpu.CompilerParams(
            dimension_semantics=("arbitrary", "arbitrary"), vmem_limit_bytes=48 * 1024 * 1024
        ),
        cost_estimate=pl.CostEstimate(
            flops=tokens * q_width * blocks * width * 4,
            transcendentals=tokens * (q_width // HEAD_SIZE) * blocks * width,
            bytes_accessed=(q.size + kv.size) * 2 + tokens * q_width * 4,
        ),
    )(jnp.reshape(ctx_index, (1,)).astype(jnp.int32), q, kv, kv, qseg, qpos, kseg)

def _chain_down_body(axis, n, x_ref, out_ref, recv, send, send_sems, recv_sems):
    f32 = jnp.float32
    me = lax.axis_index(axis)
    below = lax.rem(me + n - 1, n)
    above = lax.rem(me + 1, n)
    barrier = pltpu.get_barrier_semaphore()
    pl.semaphore_signal(barrier, 1, device_id={axis: below}, device_id_type=MESH)
    pl.semaphore_signal(barrier, 1, device_id={axis: above}, device_id_type=MESH)
    pl.semaphore_wait(barrier, 2)
    copies = []
    for j in range(n - 1):
        copy = pltpu.make_async_remote_copy(
            src_ref=send.at[j],
            dst_ref=recv.at[j],
            send_sem=send_sems.at[j],
            recv_sem=recv_sems.at[j],
            device_id={axis: below},
            device_id_type=MESH,
        )
        copies.append(copy)

        @pl.when((j < me) & (me < n - 1))
        def _():
            copy.wait_recv()
            send[j] = (x_ref[j].astype(f32) + recv[j].astype(f32)).astype(send.dtype)

        @pl.when((j < me) & (me == n - 1))
        def _():
            send[j] = x_ref[j]

        @pl.when(j < me)
        def _():
            copy.start()

        @pl.when(j == me)
        def _():
            copy.wait_recv()
            out_ref[...] = x_ref[j].astype(f32) + recv[j].astype(f32)

    @pl.when(me == n - 1)
    def _():
        out_ref[...] = x_ref[n - 1].astype(f32)

    for j in range(n - 1):
        pl.when(j < me)(copies[j].wait_send)


def chain_sum_down(x, axis, n, collective_id):
    _, rows, cols = x.shape
    return pl.pallas_call(
        functools.partial(_chain_down_body, axis, n),
        out_shape=jax.ShapeDtypeStruct((rows, cols), jnp.float32),
        in_specs=[pl.BlockSpec(memory_space=pltpu.VMEM)],
        out_specs=pl.BlockSpec(memory_space=pltpu.VMEM),
        scratch_shapes=[
            pltpu.VMEM((n - 1, rows, cols), x.dtype),
            pltpu.VMEM((n - 1, rows, cols), x.dtype),
            pltpu.SemaphoreType.DMA((n - 1,)),
            pltpu.SemaphoreType.DMA((n - 1,)),
        ],
        compiler_params=pltpu.CompilerParams(
            collective_id=collective_id, has_side_effects=True, vmem_limit_bytes=32 * 1024 * 1024
        ),
        cost_estimate=pl.CostEstimate(
            flops=(n - 1) * rows * cols, transcendentals=0, bytes_accessed=3 * n * rows * cols * 2
        ),
    )(x)


def _chain_up_body(axis, n, x_ref, out_ref, send_sems, recv_sems):
    me = lax.axis_index(axis)
    below = lax.rem(me + n - 1, n)
    above = lax.rem(me + 1, n)
    barrier = pltpu.get_barrier_semaphore()
    pl.semaphore_signal(barrier, 1, device_id={axis: below}, device_id_type=MESH)
    pl.semaphore_signal(barrier, 1, device_id={axis: above}, device_id_type=MESH)
    pl.semaphore_wait(barrier, 2)
    own = pltpu.make_async_remote_copy(
        src_ref=x_ref,
        dst_ref=out_ref.at[me],
        send_sem=send_sems.at[me],
        recv_sem=recv_sems.at[me],
        device_id={axis: above},
        device_id_type=MESH,
    )
    pl.when(me < n - 1)(own.start)
    forwards = []
    for k in range(1, n):
        block = jnp.maximum(me - k, 0)
        incoming = pltpu.make_async_remote_copy(
            src_ref=out_ref.at[block],
            dst_ref=out_ref.at[block],
            send_sem=send_sems.at[block],
            recv_sem=recv_sems.at[block],
            device_id={axis: below},
            device_id_type=MESH,
        )
        forward = pltpu.make_async_remote_copy(
            src_ref=out_ref.at[block],
            dst_ref=out_ref.at[block],
            send_sem=send_sems.at[block],
            recv_sem=recv_sems.at[block],
            device_id={axis: above},
            device_id_type=MESH,
        )
        forwards.append((k, forward))
        pl.when(k <= me)(incoming.wait_recv)
        pl.when((k <= me) & (me < n - 1))(forward.start)
    pl.when(me < n - 1)(own.wait_send)
    for k, forward in forwards:
        pl.when((k <= me) & (me < n - 1))(forward.wait_send)


def gather_up(x, axis, n, collective_id):
    got = pl.pallas_call(
        functools.partial(_chain_up_body, axis, n),
        out_shape=jax.ShapeDtypeStruct((n,) + x.shape, x.dtype),
        in_specs=[pl.BlockSpec(memory_space=pl.ANY)],
        out_specs=pl.BlockSpec(memory_space=pl.ANY),
        scratch_shapes=[pltpu.SemaphoreType.DMA((n,)), pltpu.SemaphoreType.DMA((n,))],
        compiler_params=pltpu.CompilerParams(collective_id=collective_id, has_side_effects=True),
        cost_estimate=pl.CostEstimate(
            flops=0, transcendentals=0, bytes_accessed=2 * (n - 1) * x.size * x.dtype.itemsize
        ),
    )(x)
    me = lax.axis_index(axis)
    below = (jnp.arange(n, dtype=jnp.int32) < me).reshape((n,) + (1,) * x.ndim)
    got = jnp.where(below, got, jnp.zeros_like(got))
    return lax.dynamic_update_slice_in_dim(got, x[None], me, 0)


def per_device(
    dpx_count,
    hidden_in,
    attn_gain,
    q_weight,
    key_matrix,
    value_matrix,
    o_weight,
    moe_gain,
    router_weight,
    gate_weight,
    up_weight,
    down_weight,
    segments,
    expert_picks,
    output_grad,
):
    bf16 = jnp.bfloat16
    f32 = jnp.float32
    token_count = hidden_in.shape[0]
    ctx_index = lax.axis_index("ctx")
    heads_local = q_weight.shape[1] // HEAD_SIZE
    kv_local = key_matrix.shape[1] // HEAD_SIZE
    group_size = heads_local // kv_local
    score_scale = 1.0 / math.sqrt(HEAD_SIZE)
    token_positions = ctx_index * token_count + jnp.arange(token_count, dtype=jnp.int32)
    segment_here = lax.dynamic_slice_in_dim(segments, ctx_index * token_count, token_count)
    inputs_f32 = hidden_in.astype(f32)
    o_full = lax.all_gather(o_weight, "tensor", axis=1, tiled=True)
    normed_f32, scale_one = normalize(inputs_f32, attn_gain)
    normed_one = normed_f32.astype(bf16)
    query_rows = jnp.dot(normed_one, q_weight, preferred_element_type=f32).reshape(
        token_count, heads_local, HEAD_SIZE
    )
    keys_raw = jnp.dot(normed_one, key_matrix, preferred_element_type=f32).reshape(
        token_count, kv_local, HEAD_SIZE
    )
    values_raw = jnp.dot(normed_one, value_matrix, preferred_element_type=f32)
    query_grouped = (
        apply_rotary(query_rows, token_positions, 1.0)
        .astype(bf16)
        .reshape(token_count, kv_local, group_size, HEAD_SIZE)
    )
    key_flat = (
        apply_rotary(keys_raw, token_positions, 1.0)
        .astype(bf16)
        .reshape(token_count, kv_local * HEAD_SIZE)
    )
    value_flat = values_raw.astype(bf16)

    def piece_mask(piece_rows):
        key_pos = jnp.arange(piece_rows, dtype=jnp.int32)
        return (segment_here[:, None] == segments[None, :]) & (
            key_pos[None, :] <= token_positions[:, None]
        )

    ctx_count = segments.shape[0] // token_count
    kv_both = gather_up(jnp.concatenate([key_flat, value_flat], axis=1), "ctx", ctx_count, 1)
    piece_rows = ctx_count * token_count
    kv_width = kv_local * HEAD_SIZE
    key_piece = kv_both[:, :, :kv_width].reshape(piece_rows, kv_local, HEAD_SIZE)
    value_piece = kv_both[:, :, kv_width:].reshape(piece_rows, kv_local, HEAD_SIZE)
    attn_flat, lse_pairs = flash_forward(
        ctx_index,
        query_grouped.reshape(token_count, heads_local * HEAD_SIZE),
        kv_both,
        segment_here[:, None],
        token_positions[:, None],
        segments[None, :],
        group_size,
    )
    attn_grouped = jnp.transpose(
        attn_flat.reshape(token_count, kv_local, group_size, HEAD_SIZE), (1, 2, 0, 3)
    )
    log_sum = jnp.transpose(
        lse_pairs.reshape(kv_local // 2, token_count, 2, group_size), (0, 2, 3, 1)
    ).reshape(kv_local, group_size, token_count)
    attn_bf = attn_flat.astype(bf16)
    tensor_count = o_weight.shape[0] // o_weight.shape[1]
    attn_all = gather_axis(attn_bf, "tensor", tensor_count, 2)
    attn_full = jnp.transpose(attn_all, (1, 0, 2)).reshape(token_count, tensor_count * attn_bf.shape[1])
    mixed_attn = contract_cols(attn_full, o_full)
    resid = inputs_f32 + mixed_attn
    normed_two_f32, scale_two = normalize(resid, moe_gain)
    normed_two = normed_two_f32.astype(bf16)
    logits = jnp.dot(normed_two, router_weight, preferred_element_type=f32)
    expert_range = jnp.arange(NEXP, dtype=jnp.int32)
    picked_onehot = expert_picks[:, :, None] == expert_range[None, None, :]
    picked = jnp.sum(jnp.where(picked_onehot, logits[:, None, :], 0.0), axis=2)
    gate_probs = jax.nn.softmax(picked, axis=-1)
    gates_dense = jnp.sum(jnp.where(picked_onehot, gate_probs[:, :, None], 0.0), axis=1)
    gates_by_expert = jnp.transpose(gates_dense)
    cot_bf = output_grad
    gcol = gates_dense
    grad_gate, grad_up, grad_down, hid_all, dga_all, dua_all = expert_grad_kernel(
        normed_two,
        jnp.transpose(normed_two),
        cot_bf,
        jnp.transpose(cot_bf),
        gcol,
        gates_by_expert[:, None, :],
        gate_weight,
        up_weight,
        down_weight,
        dpx_count,
    )
    gate_half = core_reduce(grad_gate, 8)
    gate_half, hid_all, dga_all, dua_all = lax.optimization_barrier(
        (gate_half, hid_all, dga_all, dua_all)
    )
    moe_acc, gate_parts, moe_grad_rows = expert_rows_kernel(
        hid_all, dga_all, dua_all, cot_bf, gcol, gate_weight, up_weight, down_weight
    )
    cot_f32 = output_grad.astype(f32)
    moe_total = sum_axis(moe_acc.astype(bf16), "tensor", 3)
    output = (resid + moe_total).astype(bf16)
    grad_rows_all = moe_grad_rows
    gate_parts = gate_parts[:, :, 0]
    grad_gate_out, grad_up_out, grad_down_out = [
        lax.psum_scatter(
            g.reshape(g.shape[0], -1, g.shape[3]), ("dpx", "ctx"), scatter_dimension=1, tiled=True
        ).astype(jnp.float32)
        for g in (gate_half, core_reduce(grad_up, 9), core_reduce(grad_down, 10))
    ]
    gate_pair = jnp.sum(
        jnp.where(picked_onehot, jnp.transpose(gate_parts)[:, None, :], 0.0), axis=2
    )
    moe_summed = sum_axis(grad_rows_all.astype(bf16), "tensor", 4)
    gate_summed = sum_axis(gate_pair.astype(bf16), "tensor", 5)
    grad_picked = gate_probs * (
        gate_summed - jnp.sum(gate_probs * gate_summed, axis=1, keepdims=True)
    )
    grad_logits = jnp.sum(jnp.where(picked_onehot, grad_picked[:, :, None], 0.0), axis=1).astype(
        bf16
    )
    grad_router = contract_rows(normed_two, grad_logits)
    grad_normed_two = moe_summed + contract_cols(grad_logits, router_weight)
    grad_two_rows, grad_moe_gain = norm_backward(resid, scale_two, moe_gain, grad_normed_two)
    grad_resid = cot_f32 + grad_two_rows
    grad_mix = grad_resid.astype(bf16)
    grad_o = contract_rows(grad_mix, attn_bf)
    grad_attn = jnp.dot(grad_mix, o_weight, preferred_element_type=f32).astype(bf16)
    grad_attn_grouped = jnp.transpose(
        grad_attn.reshape(token_count, kv_local, group_size, HEAD_SIZE), (1, 2, 0, 3)
    )
    row_delta = jnp.sum(grad_attn_grouped.astype(f32) * attn_grouped, axis=-1)
    allowed = piece_mask(piece_rows)
    scores = (
        jnp.einsum("tkgd,nkd->kgtn", query_grouped, key_piece, preferred_element_type=f32)
        * score_scale
    )
    probability = jnp.where(allowed, jnp.exp(scores - log_sum[..., None]), 0.0)
    grad_probs = jnp.einsum(
        "kgtd,nkd->kgtn", grad_attn_grouped, value_piece, preferred_element_type=f32
    )
    grad_scores = (probability * (grad_probs - row_delta[..., None])).astype(bf16)
    grad_query = score_scale * jnp.einsum(
        "kgtn,nkd->kgtd", grad_scores, key_piece, preferred_element_type=f32
    )
    key_part = score_scale * jnp.einsum(
        "kgtn,tkgd->nkd", grad_scores, query_grouped, preferred_element_type=f32
    )
    value_part = jnp.einsum(
        "kgtn,kgtd->nkd", probability.astype(bf16), grad_attn_grouped, preferred_element_type=f32
    )
    grad_keys_all = key_part.reshape(piece_rows, kv_local * HEAD_SIZE)
    grad_values_all = value_part.reshape(piece_rows, kv_local * HEAD_SIZE)
    back_state = (grad_query, grad_keys_all, grad_values_all)
    grad_query, grad_keys_all, grad_values_all = back_state
    grad_kv_here = chain_sum_down(
        jnp.concatenate([grad_keys_all, grad_values_all], axis=1)
        .astype(bf16)
        .reshape(ctx_count, token_count, 2 * kv_width),
        "ctx",
        ctx_count,
        6,
    )
    grad_keys_here = grad_kv_here[:, :kv_width]
    grad_values_here = grad_kv_here[:, kv_width:]
    grad_query_rows = jnp.transpose(grad_query, (2, 0, 1, 3)).reshape(
        token_count, heads_local, HEAD_SIZE
    )
    grad_query_bf = (
        apply_rotary(grad_query_rows, token_positions, -1.0)
        .reshape(token_count, heads_local * HEAD_SIZE)
        .astype(bf16)
    )
    grad_key_bf = (
        apply_rotary(
            grad_keys_here.reshape(token_count, kv_local, HEAD_SIZE), token_positions, -1.0
        )
        .reshape(token_count, kv_local * HEAD_SIZE)
        .astype(bf16)
    )
    grad_value_bf = grad_values_here.astype(bf16)
    grad_q = contract_rows(normed_one, grad_query_bf)
    grad_k = contract_rows(normed_one, grad_key_bf)
    grad_v = contract_rows(normed_one, grad_value_bf)
    partial_one = (
        contract_cols(grad_query_bf, q_weight)
        + contract_cols(grad_key_bf, key_matrix)
        + contract_cols(grad_value_bf, value_matrix)
    )
    grad_normed_one = sum_axis(partial_one.astype(bf16), "tensor", 7)
    grad_one_rows, grad_attn_gain = norm_backward(inputs_f32, scale_one, attn_gain, grad_normed_one)
    input_grad = grad_resid + grad_one_rows
    q_cols, o_cols, k_cols = grad_q.shape[1], grad_o.shape[1], grad_k.shape[1]
    small = jnp.concatenate(
        [
            grad_router,
            grad_attn_gain[:, None],
            grad_moe_gain[:, None],
            jnp.zeros((grad_router.shape[0], 128 - grad_router.shape[1] - 2), f32),
        ],
        axis=1,
    )
    dense_all = jnp.concatenate(
        [grad_q, grad_o, grad_k, grad_v, small], axis=1
    ).astype(bf16)
    width = dense_all.shape[0]
    dense_all = jnp.transpose(
        dense_all.reshape(dpx_count, 2, width // (2 * dpx_count), dense_all.shape[1]), (1, 0, 2, 3)
    )
    dense_half = core_reduce(dense_all, 11)
    dense_half, grad_gate_out, grad_up_out, grad_down_out = lax.optimization_barrier(
        (dense_half, grad_gate_out, grad_up_out, grad_down_out)
    )
    dense_here = lax.psum_scatter(
        dense_half.reshape(-1, dense_half.shape[-1]), ("dpx", "ctx"), scatter_dimension=0, tiled=True
    ).astype(f32)
    spans = [q_cols, o_cols, k_cols, k_cols, router_weight.shape[1], 1, 1]
    cuts = [sum(spans[:i]) for i in range(len(spans) + 1)]
    pieces_out = [dense_here[:, cuts[i] : cuts[i + 1]] for i in range(len(spans))]
    dense_out = (
        pieces_out[5][:, 0],
        pieces_out[0],
        pieces_out[2],
        pieces_out[3],
        pieces_out[1],
        pieces_out[6][:, 0],
        pieces_out[4],
    )
    return (
        output,
        input_grad,
        dense_out[0],
        dense_out[1],
        dense_out[2],
        dense_out[3],
        dense_out[4],
        dense_out[5],
        dense_out[6],
        grad_gate_out,
        grad_up_out,
        grad_down_out,
    )


def solution(mesh):
    dp_count, ctx_count, tensor_count = (mesh.shape[a] for a in ("dp", "ctx", "tensor"))
    split_mesh = jax.sharding.Mesh(
        mesh.devices.reshape(dp_count // 2, 2, ctx_count, tensor_count), ("dpx", "core", "ctx", "tensor")
    )
    return jax.shard_map(
        functools.partial(per_device, dp_count // 2),
        mesh=split_mesh,
        in_specs=(
            P(("dpx", "core", "ctx"), None),
            P(),
            P(None, "tensor"),
            P(None, "tensor"),
            P(None, "tensor"),
            P(None, "tensor"),
            P(),
            P(),
            P(None, None, "tensor"),
            P(None, None, "tensor"),
            P(None, None, "tensor"),
            P(("dpx", "core")),
            P(("dpx", "core", "ctx"), None),
            P(("dpx", "core", "ctx"), None),
        ),
        out_specs=(
            P(("dpx", "core", "ctx"), None),
            P(("dpx", "core", "ctx"), None),
            P(("dpx", "core", "ctx")),
            P(("dpx", "core", "ctx"), "tensor"),
            P(("dpx", "core", "ctx"), "tensor"),
            P(("dpx", "core", "ctx"), "tensor"),
            P(("dpx", "core", "ctx"), "tensor"),
            P(("dpx", "core", "ctx")),
            P(("dpx", "core", "ctx"), None),
            P(None, ("dpx", "core", "ctx"), "tensor"),
            P(None, ("dpx", "core", "ctx"), "tensor"),
            P(None, ("dpx", "core", "ctx"), "tensor"),
        ),
        check_vma=False,
    )
```

```python
import functools
import math

import jax
import jax.numpy as jnp
from jax import lax
from jax.experimental import pallas as pl
from jax.experimental.pallas import tpu as pltpu
from jax.sharding import PartitionSpec as P

HEAD_SIZE = 64
NEXP = 24
CAP = 341


EPSILON = 1e-06
ROPE_BASE = 10000.0
NEGATIVE = -1e30
HIGHEST = lax.Precision.HIGHEST


def normalize(rows, gain):
    scale_inv = lax.rsqrt(jnp.mean(rows * rows, axis=-1, keepdims=True) + EPSILON)
    return (rows * scale_inv * gain, scale_inv)


def norm_backward(rows, scale_inv, gain, grad_normed):
    weighted = gain * grad_normed
    grad_gain = jnp.sum(grad_normed * rows * scale_inv, axis=0)
    inner_mean = jnp.mean(weighted * rows, axis=-1, keepdims=True)
    grad_rows = scale_inv * weighted - rows * scale_inv * scale_inv * scale_inv * inner_mean
    return (grad_rows, grad_gain)


def apply_rotary(value_rows, token_positions, direction):
    half_dim = value_rows.shape[-1] // 2
    frequency = ROPE_BASE ** (-jnp.arange(half_dim, dtype=jnp.float32) / half_dim)
    angles = token_positions.astype(jnp.float32)[:, None] * frequency[None, :]
    cosine = jnp.cos(angles)[:, None, :]
    sine_part = direction * jnp.sin(angles)[:, None, :]
    first_half = value_rows[..., :half_dim]
    second = value_rows[..., half_dim:]
    return jnp.concatenate(
        [first_half * cosine - second * sine_part, second * cosine + first_half * sine_part],
        axis=-1,
    )


def contract_rows(left, right):
    return lax.dot_general(
        left, right, (((0,), (0,)), ((), ())), preferred_element_type=jnp.float32
    )


def contract_rows_exact(left, right):
    return lax.dot_general(
        left, right, (((0,), (0,)), ((), ())), precision=HIGHEST, preferred_element_type=jnp.float32
    )


def contract_cols(left, right):
    return lax.dot_general(
        left, right, (((1,), (1,)), ((), ())), preferred_element_type=jnp.float32
    )


def _store_split(out_ref, value):
    cores, _, groups, rows, _ = out_ref.shape
    for x in range(groups):
        for c in range(cores):
            start = (x * cores + c) * rows
            out_ref[c, 0, x] = value[start : start + rows].astype(out_ref.dtype)


def _gate_column(gates_ref):
    gates = gates_ref[...]
    lane = lax.broadcasted_iota(jnp.int32, gates.shape, 1)
    return jnp.sum(jnp.where(lane == pl.program_id(0), gates, 0.0), axis=1, keepdims=True)


def _grad_body(
    n2_ref, n2t_ref, dy_ref, dyt_ref, gcol_ref, grow_ref, wg_ref, wu_ref, wd_ref,
    gg_ref, gu_ref, gd_ref, hid_ref, dga_ref, dua_ref,
):
    f32 = jnp.float32
    bf16 = jnp.bfloat16
    n2 = n2_ref[...]
    wd = wd_ref[0]
    gate_act = jnp.dot(n2, wg_ref[0], preferred_element_type=f32)
    up_act = jnp.dot(n2, wu_ref[0], preferred_element_type=f32)
    sig = 1.0 / (1.0 + jnp.exp(-gate_act))
    silu = gate_act * sig
    hidden = (silu * up_act).astype(bf16)
    hid_ref[0] = hidden
    deo = (_gate_column(gcol_ref) * dy_ref[...].astype(f32)).astype(bf16)
    grad_hidden = jnp.dot(deo, wd, preferred_element_type=f32)
    deo_t = (grow_ref[0] * dyt_ref[...].astype(f32)).astype(bf16)
    _store_split(gd_ref, jnp.dot(deo_t, hidden, preferred_element_type=f32))
    grad_gate_act = (grad_hidden * up_act * sig * (1.0 + gate_act * (1.0 - sig))).astype(bf16)
    grad_up_act = (grad_hidden * silu).astype(bf16)
    dga_ref[0] = grad_gate_act
    dua_ref[0] = grad_up_act
    n2t = n2t_ref[...]
    _store_split(gg_ref, jnp.dot(n2t, grad_gate_act, preferred_element_type=f32))
    _store_split(gu_ref, jnp.dot(n2t, grad_up_act, preferred_element_type=f32))


def _rows_body(hid_ref, dga_ref, dua_ref, dy_ref, gcol_ref, wg_ref, wu_ref, wd_ref, acc_ref, dgate_ref, dn2_ref):
    f32 = jnp.float32
    nt = (((1,), (1,)), ((), ()))

    @pl.when(pl.program_id(0) == 0)
    def _():
        acc_ref[...] = jnp.zeros_like(acc_ref)
        dn2_ref[...] = jnp.zeros_like(dn2_ref)

    expert_out = lax.dot_general(hid_ref[0], wd_ref[0], nt, preferred_element_type=f32)
    acc_ref[...] += _gate_column(gcol_ref) * expert_out
    dgate_ref[0] = jnp.sum(expert_out * dy_ref[...].astype(f32), axis=1, keepdims=True)
    dn2_ref[...] += lax.dot_general(
        dga_ref[0], wg_ref[0], nt, preferred_element_type=f32
    ) + lax.dot_general(dua_ref[0], wu_ref[0], nt, preferred_element_type=f32)


def expert_grad_kernel(n2, n2t, dy, dyt, gcol, grow, wg, wu, wd, groups):
    tokens, width = n2.shape
    experts, _, hidden = wg.shape
    bf16 = jnp.bfloat16
    whole = lambda shape: pl.BlockSpec(shape, lambda e: (0,) * len(shape))
    per_expert = lambda shape: pl.BlockSpec((1,) + shape, lambda e: (e,) + (0,) * len(shape))
    split_rows = width // (groups * 2)
    split = pl.BlockSpec((2, 1, groups, split_rows, hidden), lambda e: (0, e, 0, 0, 0))
    split_shape = jax.ShapeDtypeStruct((2, experts, groups, split_rows, hidden), bf16)
    act_shape = jax.ShapeDtypeStruct((experts, tokens, hidden), bf16)
    return pl.pallas_call(
        _grad_body,
        grid=(experts,),
        in_specs=[
            whole((tokens, width)),
            whole((width, tokens)),
            whole((tokens, width)),
            whole((width, tokens)),
            whole((tokens, experts)),
            per_expert((1, tokens)),
            per_expert((width, hidden)),
            per_expert((width, hidden)),
            per_expert((width, hidden)),
        ],
        out_specs=[split, split, split]
        + [per_expert((tokens, hidden))] * 3,
        out_shape=[split_shape] * 3 + [act_shape] * 3,
        compiler_params=pltpu.CompilerParams(
            dimension_semantics=("arbitrary",), vmem_limit_bytes=64 * 1024 * 1024
        ),
        cost_estimate=pl.CostEstimate(
            flops=experts * tokens * width * hidden * 2 * 6,
            transcendentals=experts * tokens * hidden,
            bytes_accessed=experts * width * hidden * 12 + tokens * width * 8 + experts * tokens * hidden * 6,
        ),
    )(n2, n2t, dy, dyt, gcol, grow, wg, wu, wd)


def expert_rows_kernel(hid, dga, dua, dy, gcol, wg, wu, wd):
    experts, tokens, hidden = hid.shape
    width = dy.shape[1]
    f32 = jnp.float32
    whole = lambda shape: pl.BlockSpec(shape, lambda e: (0,) * len(shape))
    per_expert = lambda shape: pl.BlockSpec((1,) + shape, lambda e: (e,) + (0,) * len(shape))
    return pl.pallas_call(
        _rows_body,
        grid=(experts,),
        in_specs=[
            per_expert((tokens, hidden)),
            per_expert((tokens, hidden)),
            per_expert((tokens, hidden)),
            whole((tokens, width)),
            whole((tokens, experts)),
            per_expert((width, hidden)),
            per_expert((width, hidden)),
            per_expert((width, hidden)),
        ],
        out_specs=[whole((tokens, width)), per_expert((tokens, 1)), whole((tokens, width))],
        out_shape=[
            jax.ShapeDtypeStruct((tokens, width), f32),
            jax.ShapeDtypeStruct((experts, tokens, 1), f32),
            jax.ShapeDtypeStruct((tokens, width), f32),
        ],
        compiler_params=pltpu.CompilerParams(
            dimension_semantics=("arbitrary",), vmem_limit_bytes=64 * 1024 * 1024
        ),
        cost_estimate=pl.CostEstimate(
            flops=experts * tokens * width * hidden * 2 * 3,
            transcendentals=0,
            bytes_accessed=experts * width * hidden * 6 + tokens * width * 10 + experts * tokens * hidden * 6,
        ),
    )(hid, dga, dua, dy, gcol, wg, wu, wd)

MESH = pl.DeviceIdType.MESH


def _exchange_body(axis, n, per_peer, downward, src_ref, out_ref, send_sems, recv_sems):
    me = lax.axis_index(axis)
    barrier = pltpu.get_barrier_semaphore()
    for k in range(1, n):
        peer = lax.rem(me + k, n)
        pl.semaphore_signal(barrier, 1, device_id={axis: peer}, device_id_type=MESH)
    pl.semaphore_wait(barrier, n - 1)
    sends = []
    for k in range(1, n):
        peer = lax.rem(me + k, n)
        copy = pltpu.make_async_remote_copy(
            src_ref=src_ref.at[peer] if per_peer else src_ref,
            dst_ref=out_ref.at[me],
            send_sem=send_sems.at[k - 1],
            recv_sem=recv_sems.at[k - 1],
            device_id={axis: peer},
            device_id_type=MESH,
        )
        sends.append((peer, copy))
        if downward:
            pl.when(peer < me)(copy.start)
        else:
            copy.start()
    for k in range(1, n):
        source = lax.rem(me + n - k, n)
        incoming = pltpu.make_async_remote_copy(
            src_ref=src_ref.at[source] if per_peer else src_ref,
            dst_ref=out_ref.at[source],
            send_sem=send_sems.at[k - 1],
            recv_sem=recv_sems.at[k - 1],
            device_id={axis: source},
            device_id_type=MESH,
        )
        if downward:
            pl.when(source > me)(incoming.wait_recv)
        else:
            incoming.wait_recv()
    for peer, copy in sends:
        if downward:
            pl.when(peer < me)(copy.wait_send)
        else:
            copy.wait_send()


def exchange(x, axis, n, per_peer, collective_id, downward=False):
    block = x.shape[1:] if per_peer else x.shape
    nbytes = math.prod(block) * x.dtype.itemsize
    return pl.pallas_call(
        functools.partial(_exchange_body, axis, n, per_peer, downward),
        out_shape=jax.ShapeDtypeStruct((n,) + tuple(block), x.dtype),
        in_specs=[pl.BlockSpec(memory_space=pl.ANY)],
        out_specs=pl.BlockSpec(memory_space=pl.ANY),
        scratch_shapes=[pltpu.SemaphoreType.DMA((n - 1,)), pltpu.SemaphoreType.DMA((n - 1,))],
        compiler_params=pltpu.CompilerParams(collective_id=collective_id, has_side_effects=True),
        cost_estimate=pl.CostEstimate(flops=0, transcendentals=0, bytes_accessed=2 * (n - 1) * nbytes),
    )(x)


def gather_axis(x, axis, n, collective_id):
    got = exchange(x, axis, n, False, collective_id)
    return lax.dynamic_update_slice_in_dim(got, x[None], lax.axis_index(axis), 0)


def sum_axis(x, axis, collective_id):
    got = exchange(x, axis, 2, False, collective_id)
    me = lax.axis_index(axis)
    other = lax.dynamic_index_in_dim(got, 1 - me, 0, keepdims=False)
    return x.astype(jnp.float32) + other.astype(jnp.float32)


def _pair_add_body(me_ref, own_ref, other_ref, out_ref):
    out_ref[...] = (own_ref[...].astype(jnp.float32) + other_ref[...].astype(jnp.float32)).astype(out_ref.dtype)


def core_reduce(x, collective_id):
    got = exchange(x, "core", 2, True, collective_id)
    me = lax.axis_index("core")
    count = x.shape[1]
    rest = x.shape[2:]
    zeros = (0,) * len(rest)
    item_bytes = math.prod(rest) * x.dtype.itemsize
    step = max(d for d in range(1, count + 1) if count % d == 0 and d * item_bytes <= 4 * 1024 * 1024)
    grid_spec = pltpu.PrefetchScalarGridSpec(
        num_scalar_prefetch=1,
        grid=(count // step,),
        in_specs=[
            pl.BlockSpec((None, step) + rest, lambda i, c: (c[0], i) + zeros),
            pl.BlockSpec((None, step) + rest, lambda i, c: (1 - c[0], i) + zeros),
        ],
        out_specs=pl.BlockSpec((step,) + rest, lambda i, c: (i,) + zeros),
    )
    return pl.pallas_call(
        _pair_add_body,
        grid_spec=grid_spec,
        out_shape=jax.ShapeDtypeStruct(x.shape[1:], jnp.bfloat16),
        compiler_params=pltpu.CompilerParams(vmem_limit_bytes=56 * 1024 * 1024),
        cost_estimate=pl.CostEstimate(flops=x.size // 2, transcendentals=0, bytes_accessed=x.size * 3),
    )(jnp.reshape(me, (1,)).astype(jnp.int32), x, got)


def scatter_sum_downward(x, axis, n, collective_id):
    got = exchange(x, axis, n, True, collective_id, downward=True)
    me = lax.axis_index(axis)
    own = lax.dynamic_index_in_dim(x, me, 0, keepdims=False).astype(jnp.float32)
    above = (jnp.arange(n, dtype=jnp.int32) > me).reshape((n,) + (1,) * (x.ndim - 1))
    return own + jnp.sum(jnp.where(above, got.astype(jnp.float32), 0.0), axis=0)


def _flash_body(groups, ctx_ref, q_ref, k_ref, v_ref, qseg_ref, qpos_ref, kseg_ref, o_ref, lse_ref, qs_sc, m_sc, l_sc, acc_sc):
    f32 = jnp.float32
    block = pl.program_id(1)
    depth = HEAD_SIZE
    pair = k_ref.shape[2] // depth
    tokens = q_ref.shape[0]

    @pl.when(block == 0)
    def _():
        m_sc[...] = jnp.full_like(m_sc, NEGATIVE)
        l_sc[...] = jnp.zeros_like(l_sc)
        acc_sc[...] = jnp.zeros_like(acc_sc)
        scale = jnp.asarray(1.0 / math.sqrt(HEAD_SIZE), q_ref.dtype)
        for kk in range(pair):
            for gi in range(groups):
                i = kk * groups + gi
                qs_sc[kk, gi * tokens : (gi + 1) * tokens, :] = q_ref[:, i * depth : (i + 1) * depth] * scale

    @pl.when(block <= ctx_ref[0])
    def _():
        width = k_ref.shape[1]
        key_pos = block * width + lax.broadcasted_iota(jnp.int32, (1, width), 1)
        allowed = (qseg_ref[...] == kseg_ref[...]) & (key_pos <= qpos_ref[...])
        for kk in range(pair):
            keys = k_ref[0, :, kk * depth : (kk + 1) * depth]
            values = v_ref[0, :, kk * depth : (kk + 1) * depth]
            scores = lax.dot_general(
                qs_sc[kk], keys, (((1,), (1,)), ((), ())), preferred_element_type=f32
            )
            scores = jnp.where(allowed, scores, NEGATIVE)
            m_old = m_sc[kk]
            m_new = jnp.maximum(m_old, jnp.max(scores, axis=1, keepdims=True))
            alpha = jnp.exp(m_old - m_new)
            weights = jnp.where(allowed, jnp.exp(scores - m_new), 0.0)
            l_sc[kk] = alpha * l_sc[kk] + jnp.sum(weights, axis=1, keepdims=True)
            acc_sc[kk] = alpha * acc_sc[kk] + jnp.dot(
                weights.astype(jnp.bfloat16), values, preferred_element_type=f32
            )
            m_sc[kk] = m_new

    @pl.when(block == pl.num_programs(1) - 1)
    def _():
        for kk in range(pair):
            for gi in range(groups):
                i = kk * groups + gi
                rows = slice(gi * tokens, (gi + 1) * tokens)
                o_ref[:, i * depth : (i + 1) * depth] = acc_sc[kk, rows, :] / l_sc[kk, rows, :]
                lse_ref[0, :, i : i + 1] = m_sc[kk, rows, :] + jnp.log(l_sc[kk, rows, :])


def flash_forward(ctx_index, q, kv, qseg, qpos, kseg, groups):
    tokens, q_width = q.shape
    blocks, width, kv_width = kv.shape
    pair = 2
    pairs = kv_width // (2 * pair * HEAD_SIZE)
    heads_step = pair * groups
    f32 = jnp.float32
    capped = lambda p, b, c: (jnp.minimum(b, c[0]), 0, p)
    grid_spec = pltpu.PrefetchScalarGridSpec(
        num_scalar_prefetch=1,
        grid=(pairs, blocks),
        in_specs=[
            pl.BlockSpec((tokens, heads_step * HEAD_SIZE), lambda p, b, c: (0, p)),
            pl.BlockSpec((1, width, pair * HEAD_SIZE), capped),
            pl.BlockSpec((1, width, pair * HEAD_SIZE), lambda p, b, c: (jnp.minimum(b, c[0]), 0, pairs + p)),
            pl.BlockSpec((groups * tokens, 1), lambda p, b, c: (0, 0)),
            pl.BlockSpec((groups * tokens, 1), lambda p, b, c: (0, 0)),
            pl.BlockSpec((1, width), lambda p, b, c: (0, jnp.minimum(b, c[0]))),
        ],
        out_specs=[
            pl.BlockSpec((tokens, heads_step * HEAD_SIZE), lambda p, b, c: (0, p)),
            pl.BlockSpec((1, tokens, heads_step), lambda p, b, c: (p, 0, 0)),
        ],
        scratch_shapes=[
            pltpu.VMEM((pair, groups * tokens, HEAD_SIZE), q.dtype),
            pltpu.VMEM((pair, groups * tokens, 1), f32),
            pltpu.VMEM((pair, groups * tokens, 1), f32),
            pltpu.VMEM((pair, groups * tokens, HEAD_SIZE), f32),
        ],
    )
    return pl.pallas_call(
        functools.partial(_flash_body, groups),
        grid_spec=grid_spec,
        out_shape=[
            jax.ShapeDtypeStruct((tokens, q_width), f32),
            jax.ShapeDtypeStruct((pairs, tokens, heads_step), f32),
        ],
        compiler_params=pltpu.CompilerParams(
            dimension_semantics=("arbitrary", "arbitrary"), vmem_limit_bytes=48 * 1024 * 1024
        ),
        cost_estimate=pl.CostEstimate(
            flops=tokens * q_width * blocks * width * 4,
            transcendentals=tokens * (q_width // HEAD_SIZE) * blocks * width,
            bytes_accessed=(q.size + kv.size) * 2 + tokens * q_width * 4,
        ),
    )(jnp.reshape(ctx_index, (1,)).astype(jnp.int32), q, kv, kv, qseg, qpos, kseg)

def _chain_down_body(axis, n, x_ref, out_ref, recv, send, send_sems, recv_sems):
    f32 = jnp.float32
    me = lax.axis_index(axis)
    below = lax.rem(me + n - 1, n)
    above = lax.rem(me + 1, n)
    barrier = pltpu.get_barrier_semaphore()
    pl.semaphore_signal(barrier, 1, device_id={axis: below}, device_id_type=MESH)
    pl.semaphore_signal(barrier, 1, device_id={axis: above}, device_id_type=MESH)
    pl.semaphore_wait(barrier, 2)
    copies = []
    for j in range(n - 1):
        copy = pltpu.make_async_remote_copy(
            src_ref=send.at[j],
            dst_ref=recv.at[j],
            send_sem=send_sems.at[j],
            recv_sem=recv_sems.at[j],
            device_id={axis: below},
            device_id_type=MESH,
        )
        copies.append(copy)

        @pl.when((j < me) & (me < n - 1))
        def _():
            copy.wait_recv()
            send[j] = (x_ref[j].astype(f32) + recv[j].astype(f32)).astype(send.dtype)

        @pl.when((j < me) & (me == n - 1))
        def _():
            send[j] = x_ref[j]

        @pl.when(j < me)
        def _():
            copy.start()

        @pl.when(j == me)
        def _():
            copy.wait_recv()
            out_ref[...] = x_ref[j].astype(f32) + recv[j].astype(f32)

    @pl.when(me == n - 1)
    def _():
        out_ref[...] = x_ref[n - 1].astype(f32)

    for j in range(n - 1):
        pl.when(j < me)(copies[j].wait_send)


def chain_sum_down(x, axis, n, collective_id):
    _, rows, cols = x.shape
    return pl.pallas_call(
        functools.partial(_chain_down_body, axis, n),
        out_shape=jax.ShapeDtypeStruct((rows, cols), jnp.float32),
        in_specs=[pl.BlockSpec(memory_space=pltpu.VMEM)],
        out_specs=pl.BlockSpec(memory_space=pltpu.VMEM),
        scratch_shapes=[
            pltpu.VMEM((n - 1, rows, cols), x.dtype),
            pltpu.VMEM((n - 1, rows, cols), x.dtype),
            pltpu.SemaphoreType.DMA((n - 1,)),
            pltpu.SemaphoreType.DMA((n - 1,)),
        ],
        compiler_params=pltpu.CompilerParams(
            collective_id=collective_id, has_side_effects=True, vmem_limit_bytes=32 * 1024 * 1024
        ),
        cost_estimate=pl.CostEstimate(
            flops=(n - 1) * rows * cols, transcendentals=0, bytes_accessed=3 * n * rows * cols * 2
        ),
    )(x)


def _chain_up_body(axis, n, x_ref, out_ref, send_sems, recv_sems):
    me = lax.axis_index(axis)
    below = lax.rem(me + n - 1, n)
    above = lax.rem(me + 1, n)
    barrier = pltpu.get_barrier_semaphore()
    pl.semaphore_signal(barrier, 1, device_id={axis: below}, device_id_type=MESH)
    pl.semaphore_signal(barrier, 1, device_id={axis: above}, device_id_type=MESH)
    pl.semaphore_wait(barrier, 2)
    own = pltpu.make_async_remote_copy(
        src_ref=x_ref,
        dst_ref=out_ref.at[me],
        send_sem=send_sems.at[me],
        recv_sem=recv_sems.at[me],
        device_id={axis: above},
        device_id_type=MESH,
    )
    pl.when(me < n - 1)(own.start)
    forwards = []
    for k in range(1, n):
        block = jnp.maximum(me - k, 0)
        incoming = pltpu.make_async_remote_copy(
            src_ref=out_ref.at[block],
            dst_ref=out_ref.at[block],
            send_sem=send_sems.at[block],
            recv_sem=recv_sems.at[block],
            device_id={axis: below},
            device_id_type=MESH,
        )
        forward = pltpu.make_async_remote_copy(
            src_ref=out_ref.at[block],
            dst_ref=out_ref.at[block],
            send_sem=send_sems.at[block],
            recv_sem=recv_sems.at[block],
            device_id={axis: above},
            device_id_type=MESH,
        )
        forwards.append((k, forward))
        pl.when(k <= me)(incoming.wait_recv)
        pl.when((k <= me) & (me < n - 1))(forward.start)
    pl.when(me < n - 1)(own.wait_send)
    for k, forward in forwards:
        pl.when((k <= me) & (me < n - 1))(forward.wait_send)


def gather_up(x, axis, n, collective_id):
    got = pl.pallas_call(
        functools.partial(_chain_up_body, axis, n),
        out_shape=jax.ShapeDtypeStruct((n,) + x.shape, x.dtype),
        in_specs=[pl.BlockSpec(memory_space=pl.ANY)],
        out_specs=pl.BlockSpec(memory_space=pl.ANY),
        scratch_shapes=[pltpu.SemaphoreType.DMA((n,)), pltpu.SemaphoreType.DMA((n,))],
        compiler_params=pltpu.CompilerParams(collective_id=collective_id, has_side_effects=True),
        cost_estimate=pl.CostEstimate(
            flops=0, transcendentals=0, bytes_accessed=2 * (n - 1) * x.size * x.dtype.itemsize
        ),
    )(x)
    me = lax.axis_index(axis)
    below = (jnp.arange(n, dtype=jnp.int32) < me).reshape((n,) + (1,) * x.ndim)
    got = jnp.where(below, got, jnp.zeros_like(got))
    return lax.dynamic_update_slice_in_dim(got, x[None], me, 0)


def per_device(
    dpx_count,
    hidden_in,
    attn_gain,
    q_weight,
    key_matrix,
    value_matrix,
    o_weight,
    moe_gain,
    router_weight,
    gate_weight,
    up_weight,
    down_weight,
    segments,
    expert_picks,
    output_grad,
):
    bf16 = jnp.bfloat16
    f32 = jnp.float32
    token_count = hidden_in.shape[0]
    ctx_index = lax.axis_index("ctx")
    heads_local = q_weight.shape[1] // HEAD_SIZE
    kv_local = key_matrix.shape[1] // HEAD_SIZE
    group_size = heads_local // kv_local
    score_scale = 1.0 / math.sqrt(HEAD_SIZE)
    token_positions = ctx_index * token_count + jnp.arange(token_count, dtype=jnp.int32)
    segment_here = lax.dynamic_slice_in_dim(segments, ctx_index * token_count, token_count)
    inputs_f32 = hidden_in.astype(f32)
    o_full = lax.all_gather(o_weight, "tensor", axis=1, tiled=True)
    normed_f32, scale_one = normalize(inputs_f32, attn_gain)
    normed_one = normed_f32.astype(bf16)
    query_rows = jnp.dot(normed_one, q_weight, preferred_element_type=f32).reshape(
        token_count, heads_local, HEAD_SIZE
    )
    keys_raw = jnp.dot(normed_one, key_matrix, preferred_element_type=f32).reshape(
        token_count, kv_local, HEAD_SIZE
    )
    values_raw = jnp.dot(normed_one, value_matrix, preferred_element_type=f32)
    query_grouped = (
        apply_rotary(query_rows, token_positions, 1.0)
        .astype(bf16)
        .reshape(token_count, kv_local, group_size, HEAD_SIZE)
    )
    key_flat = (
        apply_rotary(keys_raw, token_positions, 1.0)
        .astype(bf16)
        .reshape(token_count, kv_local * HEAD_SIZE)
    )
    value_flat = values_raw.astype(bf16)

    def piece_mask(piece_rows):
        key_pos = jnp.arange(piece_rows, dtype=jnp.int32)
        return (segment_here[:, None] == segments[None, :]) & (
            key_pos[None, :] <= token_positions[:, None]
        )

    ctx_count = segments.shape[0] // token_count
    kv_both = gather_up(jnp.concatenate([key_flat, value_flat], axis=1), "ctx", ctx_count, 1)
    piece_rows = ctx_count * token_count
    kv_width = kv_local * HEAD_SIZE
    key_piece = kv_both[:, :, :kv_width].reshape(piece_rows, kv_local, HEAD_SIZE)
    value_piece = kv_both[:, :, kv_width:].reshape(piece_rows, kv_local, HEAD_SIZE)
    attn_flat, lse_pairs = flash_forward(
        ctx_index,
        query_grouped.reshape(token_count, heads_local * HEAD_SIZE),
        kv_both,
        jnp.tile(segment_here, group_size)[:, None],
        jnp.tile(token_positions, group_size)[:, None],
        segments[None, :],
        group_size,
    )
    attn_grouped = jnp.transpose(
        attn_flat.reshape(token_count, kv_local, group_size, HEAD_SIZE), (1, 2, 0, 3)
    )
    log_sum = jnp.transpose(
        lse_pairs.reshape(kv_local // 2, token_count, 2, group_size), (0, 2, 3, 1)
    ).reshape(kv_local, group_size, token_count)
    attn_bf = attn_flat.astype(bf16)
    tensor_count = o_weight.shape[0] // o_weight.shape[1]
    attn_all = gather_axis(attn_bf, "tensor", tensor_count, 2)
    attn_full = jnp.transpose(attn_all, (1, 0, 2)).reshape(token_count, tensor_count * attn_bf.shape[1])
    mixed_attn = contract_cols(attn_full, o_full)
    resid = inputs_f32 + mixed_attn
    normed_two_f32, scale_two = normalize(resid, moe_gain)
    normed_two = normed_two_f32.astype(bf16)
    logits = jnp.dot(normed_two, router_weight, preferred_element_type=f32)
    expert_range = jnp.arange(NEXP, dtype=jnp.int32)
    picked_onehot = expert_picks[:, :, None] == expert_range[None, None, :]
    picked = jnp.sum(jnp.where(picked_onehot, logits[:, None, :], 0.0), axis=2)
    gate_probs = jax.nn.softmax(picked, axis=-1)
    gates_dense = jnp.sum(jnp.where(picked_onehot, gate_probs[:, :, None], 0.0), axis=1)
    gates_by_expert = jnp.transpose(gates_dense)
    cot_bf = output_grad
    gcol = gates_dense
    grad_gate, grad_up, grad_down, hid_all, dga_all, dua_all = expert_grad_kernel(
        normed_two,
        jnp.transpose(normed_two),
        cot_bf,
        jnp.transpose(cot_bf),
        gcol,
        gates_by_expert[:, None, :],
        gate_weight,
        up_weight,
        down_weight,
        dpx_count,
    )
    gate_half = core_reduce(grad_gate, 8)
    gate_half, hid_all, dga_all, dua_all = lax.optimization_barrier(
        (gate_half, hid_all, dga_all, dua_all)
    )
    moe_acc, gate_parts, moe_grad_rows = expert_rows_kernel(
        hid_all, dga_all, dua_all, cot_bf, gcol, gate_weight, up_weight, down_weight
    )
    cot_f32 = output_grad.astype(f32)
    moe_total = sum_axis(moe_acc.astype(bf16), "tensor", 3)
    output = (resid + moe_total).astype(bf16)
    grad_rows_all = moe_grad_rows
    gate_parts = gate_parts[:, :, 0]
    grad_gate_out, grad_up_out, grad_down_out = [
        lax.psum_scatter(
            g.reshape(g.shape[0], -1, g.shape[3]), ("dpx", "ctx"), scatter_dimension=1, tiled=True
        ).astype(jnp.float32)
        for g in (gate_half, core_reduce(grad_up, 9), core_reduce(grad_down, 10))
    ]
    gate_pair = jnp.sum(
        jnp.where(picked_onehot, jnp.transpose(gate_parts)[:, None, :], 0.0), axis=2
    )
    moe_summed = sum_axis(grad_rows_all.astype(bf16), "tensor", 4)
    gate_summed = sum_axis(gate_pair.astype(bf16), "tensor", 5)
    grad_picked = gate_probs * (
        gate_summed - jnp.sum(gate_probs * gate_summed, axis=1, keepdims=True)
    )
    grad_logits = jnp.sum(jnp.where(picked_onehot, grad_picked[:, :, None], 0.0), axis=1).astype(
        bf16
    )
    grad_router = contract_rows(normed_two, grad_logits)
    grad_normed_two = moe_summed + contract_cols(grad_logits, router_weight)
    grad_two_rows, grad_moe_gain = norm_backward(resid, scale_two, moe_gain, grad_normed_two)
    grad_resid = cot_f32 + grad_two_rows
    grad_mix = grad_resid.astype(bf16)
    grad_o = contract_rows(grad_mix, attn_bf)
    grad_attn = jnp.dot(grad_mix, o_weight, preferred_element_type=f32).astype(bf16)
    grad_attn_grouped = jnp.transpose(
        grad_attn.reshape(token_count, kv_local, group_size, HEAD_SIZE), (1, 2, 0, 3)
    )
    row_delta = jnp.sum(grad_attn_grouped.astype(f32) * attn_grouped, axis=-1)
    allowed = piece_mask(piece_rows)
    scores = (
        jnp.einsum("tkgd,nkd->kgtn", query_grouped, key_piece, preferred_element_type=f32)
        * score_scale
    )
    probability = jnp.where(allowed, jnp.exp(scores - log_sum[..., None]), 0.0)
    grad_probs = jnp.einsum(
        "kgtd,nkd->kgtn", grad_attn_grouped, value_piece, preferred_element_type=f32
    )
    grad_scores = (probability * (grad_probs - row_delta[..., None])).astype(bf16)
    grad_query = score_scale * jnp.einsum(
        "kgtn,nkd->kgtd", grad_scores, key_piece, preferred_element_type=f32
    )
    key_part = score_scale * jnp.einsum(
        "kgtn,tkgd->nkd", grad_scores, query_grouped, preferred_element_type=f32
    )
    value_part = jnp.einsum(
        "kgtn,kgtd->nkd", probability.astype(bf16), grad_attn_grouped, preferred_element_type=f32
    )
    grad_keys_all = key_part.reshape(piece_rows, kv_local * HEAD_SIZE)
    grad_values_all = value_part.reshape(piece_rows, kv_local * HEAD_SIZE)
    back_state = (grad_query, grad_keys_all, grad_values_all)
    grad_query, grad_keys_all, grad_values_all = back_state
    grad_kv_here = chain_sum_down(
        jnp.concatenate([grad_keys_all, grad_values_all], axis=1)
        .astype(bf16)
        .reshape(ctx_count, token_count, 2 * kv_width),
        "ctx",
        ctx_count,
        6,
    )
    grad_keys_here = grad_kv_here[:, :kv_width]
    grad_values_here = grad_kv_here[:, kv_width:]
    grad_query_rows = jnp.transpose(grad_query, (2, 0, 1, 3)).reshape(
        token_count, heads_local, HEAD_SIZE
    )
    grad_query_bf = (
        apply_rotary(grad_query_rows, token_positions, -1.0)
        .reshape(token_count, heads_local * HEAD_SIZE)
        .astype(bf16)
    )
    grad_key_bf = (
        apply_rotary(
            grad_keys_here.reshape(token_count, kv_local, HEAD_SIZE), token_positions, -1.0
        )
        .reshape(token_count, kv_local * HEAD_SIZE)
        .astype(bf16)
    )
    grad_value_bf = grad_values_here.astype(bf16)
    grad_q = contract_rows(normed_one, grad_query_bf)
    grad_k = contract_rows(normed_one, grad_key_bf)
    grad_v = contract_rows(normed_one, grad_value_bf)
    partial_one = (
        contract_cols(grad_query_bf, q_weight)
        + contract_cols(grad_key_bf, key_matrix)
        + contract_cols(grad_value_bf, value_matrix)
    )
    grad_normed_one = sum_axis(partial_one.astype(bf16), "tensor", 7)
    grad_one_rows, grad_attn_gain = norm_backward(inputs_f32, scale_one, attn_gain, grad_normed_one)
    input_grad = grad_resid + grad_one_rows
    q_cols, o_cols, k_cols = grad_q.shape[1], grad_o.shape[1], grad_k.shape[1]
    small = jnp.concatenate(
        [
            grad_router,
            grad_attn_gain[:, None],
            grad_moe_gain[:, None],
            jnp.zeros((grad_router.shape[0], 128 - grad_router.shape[1] - 2), f32),
        ],
        axis=1,
    )
    dense_all = jnp.concatenate(
        [grad_q, grad_o, grad_k, grad_v, small], axis=1
    ).astype(bf16)
    width = dense_all.shape[0]
    dense_all = jnp.transpose(
        dense_all.reshape(dpx_count, 2, width // (2 * dpx_count), dense_all.shape[1]), (1, 0, 2, 3)
    )
    dense_half = core_reduce(dense_all, 11)
    dense_half, grad_gate_out, grad_up_out, grad_down_out = lax.optimization_barrier(
        (dense_half, grad_gate_out, grad_up_out, grad_down_out)
    )
    dense_here = lax.psum_scatter(
        dense_half.reshape(-1, dense_half.shape[-1]), ("dpx", "ctx"), scatter_dimension=0, tiled=True
    ).astype(f32)
    spans = [q_cols, o_cols, k_cols, k_cols, router_weight.shape[1], 1, 1]
    cuts = [sum(spans[:i]) for i in range(len(spans) + 1)]
    pieces_out = [dense_here[:, cuts[i] : cuts[i + 1]] for i in range(len(spans))]
    dense_out = (
        pieces_out[5][:, 0],
        pieces_out[0],
        pieces_out[2],
        pieces_out[3],
        pieces_out[1],
        pieces_out[6][:, 0],
        pieces_out[4],
    )
    return (
        output,
        input_grad,
        dense_out[0],
        dense_out[1],
        dense_out[2],
        dense_out[3],
        dense_out[4],
        dense_out[5],
        dense_out[6],
        grad_gate_out,
        grad_up_out,
        grad_down_out,
    )


def solution(mesh):
    dp_count, ctx_count, tensor_count = (mesh.shape[a] for a in ("dp", "ctx", "tensor"))
    split_mesh = jax.sharding.Mesh(
        mesh.devices.reshape(dp_count // 2, 2, ctx_count, tensor_count), ("dpx", "core", "ctx", "tensor")
    )
    return jax.shard_map(
        functools.partial(per_device, dp_count // 2),
        mesh=split_mesh,
        in_specs=(
            P(("dpx", "core", "ctx"), None),
            P(),
            P(None, "tensor"),
            P(None, "tensor"),
            P(None, "tensor"),
            P(None, "tensor"),
            P(),
            P(),
            P(None, None, "tensor"),
            P(None, None, "tensor"),
            P(None, None, "tensor"),
            P(("dpx", "core")),
            P(("dpx", "core", "ctx"), None),
            P(("dpx", "core", "ctx"), None),
        ),
        out_specs=(
            P(("dpx", "core", "ctx"), None),
            P(("dpx", "core", "ctx"), None),
            P(("dpx", "core", "ctx")),
            P(("dpx", "core", "ctx"), "tensor"),
            P(("dpx", "core", "ctx"), "tensor"),
            P(("dpx", "core", "ctx"), "tensor"),
            P(("dpx", "core", "ctx"), "tensor"),
            P(("dpx", "core", "ctx")),
            P(("dpx", "core", "ctx"), None),
            P(None, ("dpx", "core", "ctx"), "tensor"),
            P(None, ("dpx", "core", "ctx"), "tensor"),
            P(None, ("dpx", "core", "ctx"), "tensor"),
        ),
        check_vma=False,
    )
```

```python
import functools
import math

import jax
import jax.numpy as jnp
from jax import lax
from jax.experimental import pallas as pl
from jax.experimental.pallas import tpu as pltpu
from jax.sharding import PartitionSpec as P

HEAD_SIZE = 64
NEXP = 24
CAP = 341


EPSILON = 1e-06
ROPE_BASE = 10000.0
NEGATIVE = -1e30
HIGHEST = lax.Precision.HIGHEST


def normalize(rows, gain):
    scale_inv = lax.rsqrt(jnp.mean(rows * rows, axis=-1, keepdims=True) + EPSILON)
    return (rows * scale_inv * gain, scale_inv)


def norm_backward(rows, scale_inv, gain, grad_normed):
    weighted = gain * grad_normed
    grad_gain = jnp.sum(grad_normed * rows * scale_inv, axis=0)
    inner_mean = jnp.mean(weighted * rows, axis=-1, keepdims=True)
    grad_rows = scale_inv * weighted - rows * scale_inv * scale_inv * scale_inv * inner_mean
    return (grad_rows, grad_gain)


def apply_rotary(value_rows, token_positions, direction):
    half_dim = value_rows.shape[-1] // 2
    frequency = ROPE_BASE ** (-jnp.arange(half_dim, dtype=jnp.float32) / half_dim)
    angles = token_positions.astype(jnp.float32)[:, None] * frequency[None, :]
    cosine = jnp.cos(angles)[:, None, :]
    sine_part = direction * jnp.sin(angles)[:, None, :]
    first_half = value_rows[..., :half_dim]
    second = value_rows[..., half_dim:]
    return jnp.concatenate(
        [first_half * cosine - second * sine_part, second * cosine + first_half * sine_part],
        axis=-1,
    )


def contract_rows(left, right):
    return lax.dot_general(
        left, right, (((0,), (0,)), ((), ())), preferred_element_type=jnp.float32
    )


def contract_rows_exact(left, right):
    return lax.dot_general(
        left, right, (((0,), (0,)), ((), ())), precision=HIGHEST, preferred_element_type=jnp.float32
    )


def contract_cols(left, right):
    return lax.dot_general(
        left, right, (((1,), (1,)), ((), ())), preferred_element_type=jnp.float32
    )


def _store_split(out_ref, value):
    cores, _, groups, rows, _ = out_ref.shape
    for x in range(groups):
        for c in range(cores):
            start = (x * cores + c) * rows
            out_ref[c, 0, x] = value[start : start + rows].astype(out_ref.dtype)


def _gate_column(gates_ref):
    gates = gates_ref[...]
    lane = lax.broadcasted_iota(jnp.int32, gates.shape, 1)
    return jnp.sum(jnp.where(lane == pl.program_id(0), gates, 0.0), axis=1, keepdims=True)


def _grad_body(
    n2_ref, n2t_ref, dy_ref, dyt_ref, gcol_ref, grow_ref, wg_ref, wu_ref, wd_ref,
    gg_ref, gu_ref, gd_ref, hid_ref, dga_ref, dua_ref,
):
    f32 = jnp.float32
    bf16 = jnp.bfloat16
    n2 = n2_ref[...]
    wd = wd_ref[0]
    gate_act = jnp.dot(n2, wg_ref[0], preferred_element_type=f32)
    up_act = jnp.dot(n2, wu_ref[0], preferred_element_type=f32)
    sig = 1.0 / (1.0 + jnp.exp(-gate_act))
    silu = gate_act * sig
    hidden = (silu * up_act).astype(bf16)
    hid_ref[0] = hidden
    deo = (_gate_column(gcol_ref) * dy_ref[...].astype(f32)).astype(bf16)
    grad_hidden = jnp.dot(deo, wd, preferred_element_type=f32)
    deo_t = (grow_ref[0] * dyt_ref[...].astype(f32)).astype(bf16)
    _store_split(gd_ref, jnp.dot(deo_t, hidden, preferred_element_type=f32))
    grad_gate_act = (grad_hidden * up_act * sig * (1.0 + gate_act * (1.0 - sig))).astype(bf16)
    grad_up_act = (grad_hidden * silu).astype(bf16)
    dga_ref[0] = grad_gate_act
    dua_ref[0] = grad_up_act
    n2t = n2t_ref[...]
    _store_split(gg_ref, jnp.dot(n2t, grad_gate_act, preferred_element_type=f32))
    _store_split(gu_ref, jnp.dot(n2t, grad_up_act, preferred_element_type=f32))


def _rows_body(hid_ref, dga_ref, dua_ref, dy_ref, gcol_ref, wg_ref, wu_ref, wd_ref, acc_ref, dgate_ref, dn2_ref):
    f32 = jnp.float32
    nt = (((1,), (1,)), ((), ()))

    @pl.when(pl.program_id(0) == 0)
    def _():
        acc_ref[...] = jnp.zeros_like(acc_ref)
        dn2_ref[...] = jnp.zeros_like(dn2_ref)

    expert_out = lax.dot_general(hid_ref[0], wd_ref[0], nt, preferred_element_type=f32)
    acc_ref[...] += _gate_column(gcol_ref) * expert_out
    dgate_ref[0] = jnp.sum(expert_out * dy_ref[...].astype(f32), axis=1, keepdims=True)
    dn2_ref[...] += lax.dot_general(
        dga_ref[0], wg_ref[0], nt, preferred_element_type=f32
    ) + lax.dot_general(dua_ref[0], wu_ref[0], nt, preferred_element_type=f32)


def expert_grad_kernel(n2, n2t, dy, dyt, gcol, grow, wg, wu, wd, groups):
    tokens, width = n2.shape
    experts, _, hidden = wg.shape
    bf16 = jnp.bfloat16
    whole = lambda shape: pl.BlockSpec(shape, lambda e: (0,) * len(shape))
    per_expert = lambda shape: pl.BlockSpec((1,) + shape, lambda e: (e,) + (0,) * len(shape))
    split_rows = width // (groups * 2)
    split = pl.BlockSpec((2, 1, groups, split_rows, hidden), lambda e: (0, e, 0, 0, 0))
    split_shape = jax.ShapeDtypeStruct((2, experts, groups, split_rows, hidden), bf16)
    act_shape = jax.ShapeDtypeStruct((experts, tokens, hidden), bf16)
    return pl.pallas_call(
        _grad_body,
        grid=(experts,),
        in_specs=[
            whole((tokens, width)),
            whole((width, tokens)),
            whole((tokens, width)),
            whole((width, tokens)),
            whole((tokens, experts)),
            per_expert((1, tokens)),
            per_expert((width, hidden)),
            per_expert((width, hidden)),
            per_expert((width, hidden)),
        ],
        out_specs=[split, split, split]
        + [per_expert((tokens, hidden))] * 3,
        out_shape=[split_shape] * 3 + [act_shape] * 3,
        compiler_params=pltpu.CompilerParams(
            dimension_semantics=("arbitrary",), vmem_limit_bytes=64 * 1024 * 1024
        ),
        cost_estimate=pl.CostEstimate(
            flops=experts * tokens * width * hidden * 2 * 6,
            transcendentals=experts * tokens * hidden,
            bytes_accessed=experts * width * hidden * 12 + tokens * width * 8 + experts * tokens * hidden * 6,
        ),
    )(n2, n2t, dy, dyt, gcol, grow, wg, wu, wd)


def expert_rows_kernel(hid, dga, dua, dy, gcol, wg, wu, wd):
    experts, tokens, hidden = hid.shape
    width = dy.shape[1]
    f32 = jnp.float32
    whole = lambda shape: pl.BlockSpec(shape, lambda e: (0,) * len(shape))
    per_expert = lambda shape: pl.BlockSpec((1,) + shape, lambda e: (e,) + (0,) * len(shape))
    return pl.pallas_call(
        _rows_body,
        grid=(experts,),
        in_specs=[
            per_expert((tokens, hidden)),
            per_expert((tokens, hidden)),
            per_expert((tokens, hidden)),
            whole((tokens, width)),
            whole((tokens, experts)),
            per_expert((width, hidden)),
            per_expert((width, hidden)),
            per_expert((width, hidden)),
        ],
        out_specs=[whole((tokens, width)), per_expert((tokens, 1)), whole((tokens, width))],
        out_shape=[
            jax.ShapeDtypeStruct((tokens, width), f32),
            jax.ShapeDtypeStruct((experts, tokens, 1), f32),
            jax.ShapeDtypeStruct((tokens, width), f32),
        ],
        compiler_params=pltpu.CompilerParams(
            dimension_semantics=("arbitrary",), vmem_limit_bytes=64 * 1024 * 1024
        ),
        cost_estimate=pl.CostEstimate(
            flops=experts * tokens * width * hidden * 2 * 3,
            transcendentals=0,
            bytes_accessed=experts * width * hidden * 6 + tokens * width * 10 + experts * tokens * hidden * 6,
        ),
    )(hid, dga, dua, dy, gcol, wg, wu, wd)

MESH = pl.DeviceIdType.MESH


def _exchange_body(axis, n, per_peer, downward, src_ref, out_ref, send_sems, recv_sems):
    me = lax.axis_index(axis)
    barrier = pltpu.get_barrier_semaphore()
    for k in range(1, n):
        peer = lax.rem(me + k, n)
        pl.semaphore_signal(barrier, 1, device_id={axis: peer}, device_id_type=MESH)
    pl.semaphore_wait(barrier, n - 1)
    sends = []
    for k in range(1, n):
        peer = lax.rem(me + k, n)
        copy = pltpu.make_async_remote_copy(
            src_ref=src_ref.at[peer] if per_peer else src_ref,
            dst_ref=out_ref.at[me],
            send_sem=send_sems.at[k - 1],
            recv_sem=recv_sems.at[k - 1],
            device_id={axis: peer},
            device_id_type=MESH,
        )
        sends.append((peer, copy))
        if downward:
            pl.when(peer < me)(copy.start)
        else:
            copy.start()
    for k in range(1, n):
        source = lax.rem(me + n - k, n)
        incoming = pltpu.make_async_remote_copy(
            src_ref=src_ref.at[source] if per_peer else src_ref,
            dst_ref=out_ref.at[source],
            send_sem=send_sems.at[k - 1],
            recv_sem=recv_sems.at[k - 1],
            device_id={axis: source},
            device_id_type=MESH,
        )
        if downward:
            pl.when(source > me)(incoming.wait_recv)
        else:
            incoming.wait_recv()
    for peer, copy in sends:
        if downward:
            pl.when(peer < me)(copy.wait_send)
        else:
            copy.wait_send()


def exchange(x, axis, n, per_peer, collective_id, downward=False):
    block = x.shape[1:] if per_peer else x.shape
    nbytes = math.prod(block) * x.dtype.itemsize
    return pl.pallas_call(
        functools.partial(_exchange_body, axis, n, per_peer, downward),
        out_shape=jax.ShapeDtypeStruct((n,) + tuple(block), x.dtype),
        in_specs=[pl.BlockSpec(memory_space=pl.ANY)],
        out_specs=pl.BlockSpec(memory_space=pl.ANY),
        scratch_shapes=[pltpu.SemaphoreType.DMA((n - 1,)), pltpu.SemaphoreType.DMA((n - 1,))],
        compiler_params=pltpu.CompilerParams(collective_id=collective_id, has_side_effects=True),
        cost_estimate=pl.CostEstimate(flops=0, transcendentals=0, bytes_accessed=2 * (n - 1) * nbytes),
    )(x)


def gather_axis(x, axis, n, collective_id):
    got = exchange(x, axis, n, False, collective_id)
    return lax.dynamic_update_slice_in_dim(got, x[None], lax.axis_index(axis), 0)


def sum_axis(x, axis, collective_id):
    got = exchange(x, axis, 2, False, collective_id)
    me = lax.axis_index(axis)
    other = lax.dynamic_index_in_dim(got, 1 - me, 0, keepdims=False)
    return x.astype(jnp.float32) + other.astype(jnp.float32)


def _pair_add_body(me_ref, own_ref, other_ref, out_ref):
    out_ref[...] = (own_ref[...].astype(jnp.float32) + other_ref[...].astype(jnp.float32)).astype(out_ref.dtype)


def core_reduce(x, collective_id):
    got = exchange(x, "core", 2, True, collective_id)
    me = lax.axis_index("core")
    count = x.shape[1]
    rest = x.shape[2:]
    zeros = (0,) * len(rest)
    item_bytes = math.prod(rest) * x.dtype.itemsize
    step = max(d for d in range(1, count + 1) if count % d == 0 and d * item_bytes <= 4 * 1024 * 1024)
    grid_spec = pltpu.PrefetchScalarGridSpec(
        num_scalar_prefetch=1,
        grid=(count // step,),
        in_specs=[
            pl.BlockSpec((None, step) + rest, lambda i, c: (c[0], i) + zeros),
            pl.BlockSpec((None, step) + rest, lambda i, c: (1 - c[0], i) + zeros),
        ],
        out_specs=pl.BlockSpec((step,) + rest, lambda i, c: (i,) + zeros),
    )
    return pl.pallas_call(
        _pair_add_body,
        grid_spec=grid_spec,
        out_shape=jax.ShapeDtypeStruct(x.shape[1:], jnp.bfloat16),
        compiler_params=pltpu.CompilerParams(vmem_limit_bytes=56 * 1024 * 1024),
        cost_estimate=pl.CostEstimate(flops=x.size // 2, transcendentals=0, bytes_accessed=x.size * 3),
    )(jnp.reshape(me, (1,)).astype(jnp.int32), x, got)


def scatter_sum_downward(x, axis, n, collective_id):
    got = exchange(x, axis, n, True, collective_id, downward=True)
    me = lax.axis_index(axis)
    own = lax.dynamic_index_in_dim(x, me, 0, keepdims=False).astype(jnp.float32)
    above = (jnp.arange(n, dtype=jnp.int32) > me).reshape((n,) + (1,) * (x.ndim - 1))
    return own + jnp.sum(jnp.where(above, got.astype(jnp.float32), 0.0), axis=0)


def _flash_body(groups, ctx_ref, q_ref, k_ref, v_ref, qseg_ref, qpos_ref, kseg_ref, o_ref, lse_ref, qs_sc, m_sc, l_sc, acc_sc):
    f32 = jnp.float32
    block = pl.program_id(1)
    depth = HEAD_SIZE
    pair = k_ref.shape[2] // depth
    tokens = q_ref.shape[0]

    @pl.when(block == 0)
    def _():
        m_sc[...] = jnp.full_like(m_sc, NEGATIVE)
        l_sc[...] = jnp.zeros_like(l_sc)
        acc_sc[...] = jnp.zeros_like(acc_sc)
        scale = jnp.asarray(1.0 / math.sqrt(HEAD_SIZE), q_ref.dtype)
        for kk in range(pair):
            for gi in range(groups):
                i = kk * groups + gi
                qs_sc[kk, gi * tokens : (gi + 1) * tokens, :] = q_ref[:, i * depth : (i + 1) * depth] * scale

    @pl.when(block <= ctx_ref[0])
    def _():
        width = k_ref.shape[1]
        key_pos = block * width + lax.broadcasted_iota(jnp.int32, (1, width), 1)
        allowed = (qseg_ref[...] == kseg_ref[...]) & (key_pos <= qpos_ref[...])
        for kk in range(pair):
            keys = k_ref[0, :, kk * depth : (kk + 1) * depth]
            values = v_ref[0, :, kk * depth : (kk + 1) * depth]
            scores = lax.dot_general(
                qs_sc[kk], keys, (((1,), (1,)), ((), ())), preferred_element_type=f32
            )
            scores = jnp.where(allowed, scores, NEGATIVE)
            m_old = m_sc[kk]
            m_new = jnp.maximum(m_old, jnp.max(scores, axis=1, keepdims=True))
            alpha = jnp.exp(m_old - m_new)
            weights = jnp.where(allowed, jnp.exp(scores - m_new), 0.0)
            l_sc[kk] = alpha * l_sc[kk] + jnp.sum(weights, axis=1, keepdims=True)
            acc_sc[kk] = alpha * acc_sc[kk] + jnp.dot(
                weights.astype(jnp.bfloat16), values, preferred_element_type=f32
            )
            m_sc[kk] = m_new

    @pl.when(block == pl.num_programs(1) - 1)
    def _():
        for kk in range(pair):
            for gi in range(groups):
                i = kk * groups + gi
                rows = slice(gi * tokens, (gi + 1) * tokens)
                o_ref[:, i * depth : (i + 1) * depth] = acc_sc[kk, rows, :] / l_sc[kk, rows, :]
                lse_ref[0, :, i : i + 1] = m_sc[kk, rows, :] + jnp.log(l_sc[kk, rows, :])


def flash_forward(ctx_index, q, kv, qseg, qpos, kseg, groups):
    tokens, q_width = q.shape
    blocks, width, kv_width = kv.shape
    pair = 2
    pairs = kv_width // (2 * pair * HEAD_SIZE)
    heads_step = pair * groups
    f32 = jnp.float32
    capped = lambda p, b, c: (jnp.minimum(b, c[0]), 0, p)
    grid_spec = pltpu.PrefetchScalarGridSpec(
        num_scalar_prefetch=1,
        grid=(pairs, blocks),
        in_specs=[
            pl.BlockSpec((tokens, heads_step * HEAD_SIZE), lambda p, b, c: (0, p)),
            pl.BlockSpec((1, width, pair * HEAD_SIZE), capped),
            pl.BlockSpec((1, width, pair * HEAD_SIZE), lambda p, b, c: (jnp.minimum(b, c[0]), 0, pairs + p)),
            pl.BlockSpec((groups * tokens, 1), lambda p, b, c: (0, 0)),
            pl.BlockSpec((groups * tokens, 1), lambda p, b, c: (0, 0)),
            pl.BlockSpec((1, width), lambda p, b, c: (0, jnp.minimum(b, c[0]))),
        ],
        out_specs=[
            pl.BlockSpec((tokens, heads_step * HEAD_SIZE), lambda p, b, c: (0, p)),
            pl.BlockSpec((1, tokens, heads_step), lambda p, b, c: (p, 0, 0)),
        ],
        scratch_shapes=[
            pltpu.VMEM((pair, groups * tokens, HEAD_SIZE), q.dtype),
            pltpu.VMEM((pair, groups * tokens, 1), f32),
            pltpu.VMEM((pair, groups * tokens, 1), f32),
            pltpu.VMEM((pair, groups * tokens, HEAD_SIZE), f32),
        ],
    )
    return pl.pallas_call(
        functools.partial(_flash_body, groups),
        grid_spec=grid_spec,
        out_shape=[
            jax.ShapeDtypeStruct((tokens, q_width), f32),
            jax.ShapeDtypeStruct((pairs, tokens, heads_step), f32),
        ],
        compiler_params=pltpu.CompilerParams(
            dimension_semantics=("arbitrary", "arbitrary"), vmem_limit_bytes=48 * 1024 * 1024
        ),
        cost_estimate=pl.CostEstimate(
            flops=tokens * q_width * blocks * width * 4,
            transcendentals=tokens * (q_width // HEAD_SIZE) * blocks * width,
            bytes_accessed=(q.size + kv.size) * 2 + tokens * q_width * 4,
        ),
    )(jnp.reshape(ctx_index, (1,)).astype(jnp.int32), q, kv, kv, qseg, qpos, kseg)

def _chain_down_body(axis, n, x_ref, out_ref, recv, send, send_sems, recv_sems):
    f32 = jnp.float32
    me = lax.axis_index(axis)
    below = lax.rem(me + n - 1, n)
    above = lax.rem(me + 1, n)
    barrier = pltpu.get_barrier_semaphore()
    pl.semaphore_signal(barrier, 1, device_id={axis: below}, device_id_type=MESH)
    pl.semaphore_signal(barrier, 1, device_id={axis: above}, device_id_type=MESH)
    pl.semaphore_wait(barrier, 2)
    copies = []
    for j in range(n - 1):
        copy = pltpu.make_async_remote_copy(
            src_ref=send.at[j],
            dst_ref=recv.at[j],
            send_sem=send_sems.at[j],
            recv_sem=recv_sems.at[j],
            device_id={axis: below},
            device_id_type=MESH,
        )
        copies.append(copy)

        @pl.when((j < me) & (me < n - 1))
        def _():
            copy.wait_recv()
            send[j] = (x_ref[j].astype(f32) + recv[j].astype(f32)).astype(send.dtype)

        @pl.when((j < me) & (me == n - 1))
        def _():
            send[j] = x_ref[j]

        @pl.when(j < me)
        def _():
            copy.start()

        @pl.when(j == me)
        def _():
            copy.wait_recv()
            out_ref[...] = x_ref[j].astype(f32) + recv[j].astype(f32)

    @pl.when(me == n - 1)
    def _():
        out_ref[...] = x_ref[n - 1].astype(f32)

    for j in range(n - 1):
        pl.when(j < me)(copies[j].wait_send)


def chain_sum_down(x, axis, n, collective_id):
    _, rows, cols = x.shape
    return pl.pallas_call(
        functools.partial(_chain_down_body, axis, n),
        out_shape=jax.ShapeDtypeStruct((rows, cols), jnp.float32),
        in_specs=[pl.BlockSpec(memory_space=pltpu.VMEM)],
        out_specs=pl.BlockSpec(memory_space=pltpu.VMEM),
        scratch_shapes=[
            pltpu.VMEM((n - 1, rows, cols), x.dtype),
            pltpu.VMEM((n - 1, rows, cols), x.dtype),
            pltpu.SemaphoreType.DMA((n - 1,)),
            pltpu.SemaphoreType.DMA((n - 1,)),
        ],
        compiler_params=pltpu.CompilerParams(
            collective_id=collective_id, has_side_effects=True, vmem_limit_bytes=32 * 1024 * 1024
        ),
        cost_estimate=pl.CostEstimate(
            flops=(n - 1) * rows * cols, transcendentals=0, bytes_accessed=3 * n * rows * cols * 2
        ),
    )(x)


def _chain_up_body(axis, n, x_ref, out_ref, send_sems, recv_sems):
    me = lax.axis_index(axis)
    below = lax.rem(me + n - 1, n)
    above = lax.rem(me + 1, n)
    barrier = pltpu.get_barrier_semaphore()
    pl.semaphore_signal(barrier, 1, device_id={axis: below}, device_id_type=MESH)
    pl.semaphore_signal(barrier, 1, device_id={axis: above}, device_id_type=MESH)
    pl.semaphore_wait(barrier, 2)
    own = pltpu.make_async_remote_copy(
        src_ref=x_ref,
        dst_ref=out_ref.at[me],
        send_sem=send_sems.at[me],
        recv_sem=recv_sems.at[me],
        device_id={axis: above},
        device_id_type=MESH,
    )
    pl.when(me < n - 1)(own.start)
    forwards = []
    for k in range(1, n):
        block = jnp.maximum(me - k, 0)
        incoming = pltpu.make_async_remote_copy(
            src_ref=out_ref.at[block],
            dst_ref=out_ref.at[block],
            send_sem=send_sems.at[block],
            recv_sem=recv_sems.at[block],
            device_id={axis: below},
            device_id_type=MESH,
        )
        forward = pltpu.make_async_remote_copy(
            src_ref=out_ref.at[block],
            dst_ref=out_ref.at[block],
            send_sem=send_sems.at[block],
            recv_sem=recv_sems.at[block],
            device_id={axis: above},
            device_id_type=MESH,
        )
        forwards.append((k, forward))
        pl.when(k <= me)(incoming.wait_recv)
        pl.when((k <= me) & (me < n - 1))(forward.start)
    pl.when(me < n - 1)(own.wait_send)
    for k, forward in forwards:
        pl.when((k <= me) & (me < n - 1))(forward.wait_send)


def gather_up(x, axis, n, collective_id):
    got = pl.pallas_call(
        functools.partial(_chain_up_body, axis, n),
        out_shape=jax.ShapeDtypeStruct((n,) + x.shape, x.dtype),
        in_specs=[pl.BlockSpec(memory_space=pl.ANY)],
        out_specs=pl.BlockSpec(memory_space=pl.ANY),
        scratch_shapes=[pltpu.SemaphoreType.DMA((n,)), pltpu.SemaphoreType.DMA((n,))],
        compiler_params=pltpu.CompilerParams(collective_id=collective_id, has_side_effects=True),
        cost_estimate=pl.CostEstimate(
            flops=0, transcendentals=0, bytes_accessed=2 * (n - 1) * x.size * x.dtype.itemsize
        ),
    )(x)
    me = lax.axis_index(axis)
    below = (jnp.arange(n, dtype=jnp.int32) < me).reshape((n,) + (1,) * x.ndim)
    got = jnp.where(below, got, jnp.zeros_like(got))
    return lax.dynamic_update_slice_in_dim(got, x[None], me, 0)


def _attend_block(groups, kv_heads, q_sc, kv_buf, qseg_ref, qpos_ref, kseg_ref, m_sc, l_sc, acc_sc, block):
    f32 = jnp.float32
    depth = HEAD_SIZE
    width = kv_buf.shape[0]
    start = pl.multiple_of(block * width, width)
    key_pos = start + lax.broadcasted_iota(jnp.int32, (1, width), 1)
    allowed = (qseg_ref[...] == kseg_ref[:, pl.ds(start, width)]) & (key_pos <= qpos_ref[...])
    for kk in range(kv_heads):
        keys = kv_buf[:, kk * depth : (kk + 1) * depth]
        values = kv_buf[:, (kv_heads + kk) * depth : (kv_heads + kk + 1) * depth]
        scores = lax.dot_general(q_sc[kk], keys, (((1,), (1,)), ((), ())), preferred_element_type=f32)
        scores = jnp.where(allowed, scores, NEGATIVE)
        m_old = m_sc[kk]
        m_new = jnp.maximum(m_old, jnp.max(scores, axis=1, keepdims=True))
        alpha = jnp.exp(m_old - m_new)
        weights = jnp.where(allowed, jnp.exp(scores - m_new), 0.0)
        l_sc[kk] = alpha * l_sc[kk] + jnp.sum(weights, axis=1, keepdims=True)
        acc_sc[kk] = alpha * acc_sc[kk] + jnp.dot(
            weights.astype(jnp.bfloat16), values, preferred_element_type=f32
        )
        m_sc[kk] = m_new


def _gather_attend_body(
    axis, n, groups, q_ref, own_ref, qseg_ref, qpos_ref, kseg_ref,
    kv_ref, o_ref, lse_ref,
    q_sc, m_sc, l_sc, acc_sc, kv_buf, send_sems, recv_sems, copy_sem,
):
    depth = HEAD_SIZE
    tokens = q_ref.shape[0]
    kv_heads = own_ref.shape[1] // (2 * depth)
    me = lax.axis_index(axis)
    below = lax.rem(me + n - 1, n)
    above = lax.rem(me + 1, n)
    barrier = pltpu.get_barrier_semaphore()
    pl.semaphore_signal(barrier, 1, device_id={axis: below}, device_id_type=MESH)
    pl.semaphore_signal(barrier, 1, device_id={axis: above}, device_id_type=MESH)
    pl.semaphore_wait(barrier, 2)
    own = pltpu.make_async_remote_copy(
        src_ref=own_ref,
        dst_ref=kv_ref.at[me],
        send_sem=send_sems.at[me],
        recv_sem=recv_sems.at[me],
        device_id={axis: above},
        device_id_type=MESH,
    )
    pl.when(me < n - 1)(own.start)

    m_sc[...] = jnp.full_like(m_sc, NEGATIVE)
    l_sc[...] = jnp.zeros_like(l_sc)
    acc_sc[...] = jnp.zeros_like(acc_sc)
    scale = jnp.asarray(1.0 / math.sqrt(HEAD_SIZE), q_ref.dtype)
    for kk in range(kv_heads):
        for gi in range(groups):
            i = kk * groups + gi
            q_sc[kk, gi * tokens : (gi + 1) * tokens, :] = q_ref[:, i * depth : (i + 1) * depth] * scale

    local = pltpu.make_async_copy(own_ref, kv_buf, copy_sem)
    local.start()
    local.wait()
    _attend_block(groups, kv_heads, q_sc, kv_buf, qseg_ref, qpos_ref, kseg_ref, m_sc, l_sc, acc_sc, me)

    def step(k, carry):
        block = me - k
        incoming = pltpu.make_async_remote_copy(
            src_ref=kv_ref.at[block],
            dst_ref=kv_ref.at[block],
            send_sem=send_sems.at[block],
            recv_sem=recv_sems.at[block],
            device_id={axis: below},
            device_id_type=MESH,
        )
        incoming.wait_recv()
        forward = pltpu.make_async_remote_copy(
            src_ref=kv_ref.at[block],
            dst_ref=kv_ref.at[block],
            send_sem=send_sems.at[block],
            recv_sem=recv_sems.at[block],
            device_id={axis: above},
            device_id_type=MESH,
        )
        pl.when(me < n - 1)(forward.start)
        fetch = pltpu.make_async_copy(kv_ref.at[block], kv_buf, copy_sem)
        fetch.start()
        fetch.wait()
        _attend_block(groups, kv_heads, q_sc, kv_buf, qseg_ref, qpos_ref, kseg_ref, m_sc, l_sc, acc_sc, block)
        return carry

    lax.fori_loop(1, me + 1, step, 0)

    for kk in range(kv_heads):
        for gi in range(groups):
            i = kk * groups + gi
            rows = slice(gi * tokens, (gi + 1) * tokens)
            o_ref[:, i * depth : (i + 1) * depth] = acc_sc[kk, rows, :] / l_sc[kk, rows, :]
            lse_ref[:, i : i + 1] = m_sc[kk, rows, :] + jnp.log(l_sc[kk, rows, :])

    pl.when(me < n - 1)(own.wait_send)

    def drain(k, carry):
        block = me - k
        pltpu.make_async_remote_copy(
            src_ref=kv_ref.at[block],
            dst_ref=kv_ref.at[block],
            send_sem=send_sems.at[block],
            recv_sem=recv_sems.at[block],
            device_id={axis: above},
            device_id_type=MESH,
        ).wait_send()
        return carry

    lax.fori_loop(1, jnp.where(me < n - 1, me + 1, 1), drain, 0)


def gather_attend(q, own, qseg, qpos, kseg, axis, n, groups, collective_id):
    tokens, q_width = q.shape
    rows, kv_width = own.shape
    heads = q_width // HEAD_SIZE
    kv_heads = kv_width // (2 * HEAD_SIZE)
    f32 = jnp.float32
    vmem = pl.BlockSpec(memory_space=pltpu.VMEM)
    anywhere = pl.BlockSpec(memory_space=pl.ANY)
    kv_all, attn, lse = pl.pallas_call(
        functools.partial(_gather_attend_body, axis, n, groups),
        out_shape=[
            jax.ShapeDtypeStruct((n, rows, kv_width), own.dtype),
            jax.ShapeDtypeStruct((tokens, q_width), f32),
            jax.ShapeDtypeStruct((tokens, heads), f32),
        ],
        in_specs=[vmem, anywhere, vmem, vmem, vmem],
        out_specs=[anywhere, vmem, vmem],
        scratch_shapes=[
            pltpu.VMEM((kv_heads, groups * tokens, HEAD_SIZE), q.dtype),
            pltpu.VMEM((kv_heads, groups * tokens, 1), f32),
            pltpu.VMEM((kv_heads, groups * tokens, 1), f32),
            pltpu.VMEM((kv_heads, groups * tokens, HEAD_SIZE), f32),
            pltpu.VMEM((rows, kv_width), own.dtype),
            pltpu.SemaphoreType.DMA((n,)),
            pltpu.SemaphoreType.DMA((n,)),
            pltpu.SemaphoreType.DMA(()),
        ],
        compiler_params=pltpu.CompilerParams(
            collective_id=collective_id, has_side_effects=True, vmem_limit_bytes=48 * 1024 * 1024
        ),
        cost_estimate=pl.CostEstimate(
            flops=tokens * q_width * n * rows * 4,
            transcendentals=tokens * heads * n * rows,
            bytes_accessed=2 * n * own.size * own.dtype.itemsize + tokens * q_width * 6,
        ),
    )(q, own, qseg, qpos, kseg)
    me = lax.axis_index(axis)
    below = (jnp.arange(n, dtype=jnp.int32) < me).reshape((n, 1, 1))
    kv_all = jnp.where(below, kv_all, jnp.zeros_like(kv_all))
    return attn, lse, lax.dynamic_update_slice_in_dim(kv_all, own[None], me, 0)


def per_device(
    dpx_count,
    hidden_in,
    attn_gain,
    q_weight,
    key_matrix,
    value_matrix,
    o_weight,
    moe_gain,
    router_weight,
    gate_weight,
    up_weight,
    down_weight,
    segments,
    expert_picks,
    output_grad,
):
    bf16 = jnp.bfloat16
    f32 = jnp.float32
    token_count = hidden_in.shape[0]
    ctx_index = lax.axis_index("ctx")
    heads_local = q_weight.shape[1] // HEAD_SIZE
    kv_local = key_matrix.shape[1] // HEAD_SIZE
    group_size = heads_local // kv_local
    score_scale = 1.0 / math.sqrt(HEAD_SIZE)
    token_positions = ctx_index * token_count + jnp.arange(token_count, dtype=jnp.int32)
    segment_here = lax.dynamic_slice_in_dim(segments, ctx_index * token_count, token_count)
    inputs_f32 = hidden_in.astype(f32)
    o_full = lax.all_gather(o_weight, "tensor", axis=1, tiled=True)
    normed_f32, scale_one = normalize(inputs_f32, attn_gain)
    normed_one = normed_f32.astype(bf16)
    query_rows = jnp.dot(normed_one, q_weight, preferred_element_type=f32).reshape(
        token_count, heads_local, HEAD_SIZE
    )
    keys_raw = jnp.dot(normed_one, key_matrix, preferred_element_type=f32).reshape(
        token_count, kv_local, HEAD_SIZE
    )
    values_raw = jnp.dot(normed_one, value_matrix, preferred_element_type=f32)
    query_grouped = (
        apply_rotary(query_rows, token_positions, 1.0)
        .astype(bf16)
        .reshape(token_count, kv_local, group_size, HEAD_SIZE)
    )
    key_flat = (
        apply_rotary(keys_raw, token_positions, 1.0)
        .astype(bf16)
        .reshape(token_count, kv_local * HEAD_SIZE)
    )
    value_flat = values_raw.astype(bf16)

    def piece_mask(piece_rows):
        key_pos = jnp.arange(piece_rows, dtype=jnp.int32)
        return (segment_here[:, None] == segments[None, :]) & (
            key_pos[None, :] <= token_positions[:, None]
        )

    ctx_count = segments.shape[0] // token_count
    attn_flat, lse_heads, kv_both = gather_attend(
        query_grouped.reshape(token_count, heads_local * HEAD_SIZE),
        jnp.concatenate([key_flat, value_flat], axis=1),
        jnp.tile(segment_here, group_size)[:, None],
        jnp.tile(token_positions, group_size)[:, None],
        segments[None, :],
        "ctx",
        ctx_count,
        group_size,
        1,
    )
    piece_rows = ctx_count * token_count
    kv_width = kv_local * HEAD_SIZE
    key_piece = kv_both[:, :, :kv_width].reshape(piece_rows, kv_local, HEAD_SIZE)
    value_piece = kv_both[:, :, kv_width:].reshape(piece_rows, kv_local, HEAD_SIZE)
    attn_grouped = jnp.transpose(
        attn_flat.reshape(token_count, kv_local, group_size, HEAD_SIZE), (1, 2, 0, 3)
    )
    log_sum = jnp.transpose(lse_heads.reshape(token_count, kv_local, group_size), (1, 2, 0))
    attn_bf = attn_flat.astype(bf16)
    tensor_count = o_weight.shape[0] // o_weight.shape[1]
    attn_all = gather_axis(attn_bf, "tensor", tensor_count, 2)
    attn_full = jnp.transpose(attn_all, (1, 0, 2)).reshape(token_count, tensor_count * attn_bf.shape[1])
    mixed_attn = contract_cols(attn_full, o_full)
    resid = inputs_f32 + mixed_attn
    normed_two_f32, scale_two = normalize(resid, moe_gain)
    normed_two = normed_two_f32.astype(bf16)
    logits = jnp.dot(normed_two, router_weight, preferred_element_type=f32)
    expert_range = jnp.arange(NEXP, dtype=jnp.int32)
    picked_onehot = expert_picks[:, :, None] == expert_range[None, None, :]
    picked = jnp.sum(jnp.where(picked_onehot, logits[:, None, :], 0.0), axis=2)
    gate_probs = jax.nn.softmax(picked, axis=-1)
    gates_dense = jnp.sum(jnp.where(picked_onehot, gate_probs[:, :, None], 0.0), axis=1)
    gates_by_expert = jnp.transpose(gates_dense)
    cot_bf = output_grad
    gcol = gates_dense
    grad_gate, grad_up, grad_down, hid_all, dga_all, dua_all = expert_grad_kernel(
        normed_two,
        jnp.transpose(normed_two),
        cot_bf,
        jnp.transpose(cot_bf),
        gcol,
        gates_by_expert[:, None, :],
        gate_weight,
        up_weight,
        down_weight,
        dpx_count,
    )
    gate_half = core_reduce(grad_gate, 8)
    gate_half, hid_all, dga_all, dua_all = lax.optimization_barrier(
        (gate_half, hid_all, dga_all, dua_all)
    )
    moe_acc, gate_parts, moe_grad_rows = expert_rows_kernel(
        hid_all, dga_all, dua_all, cot_bf, gcol, gate_weight, up_weight, down_weight
    )
    cot_f32 = output_grad.astype(f32)
    moe_total = sum_axis(moe_acc.astype(bf16), "tensor", 3)
    output = (resid + moe_total).astype(bf16)
    grad_rows_all = moe_grad_rows
    gate_parts = gate_parts[:, :, 0]
    grad_gate_out, grad_up_out, grad_down_out = [
        lax.psum_scatter(
            g.reshape(g.shape[0], -1, g.shape[3]), ("dpx", "ctx"), scatter_dimension=1, tiled=True
        ).astype(jnp.float32)
        for g in (gate_half, core_reduce(grad_up, 9), core_reduce(grad_down, 10))
    ]
    gate_pair = jnp.sum(
        jnp.where(picked_onehot, jnp.transpose(gate_parts)[:, None, :], 0.0), axis=2
    )
    moe_summed = sum_axis(grad_rows_all.astype(bf16), "tensor", 4)
    gate_summed = sum_axis(gate_pair.astype(bf16), "tensor", 5)
    grad_picked = gate_probs * (
        gate_summed - jnp.sum(gate_probs * gate_summed, axis=1, keepdims=True)
    )
    grad_logits = jnp.sum(jnp.where(picked_onehot, grad_picked[:, :, None], 0.0), axis=1).astype(
        bf16
    )
    grad_router = contract_rows(normed_two, grad_logits)
    grad_normed_two = moe_summed + contract_cols(grad_logits, router_weight)
    grad_two_rows, grad_moe_gain = norm_backward(resid, scale_two, moe_gain, grad_normed_two)
    grad_resid = cot_f32 + grad_two_rows
    grad_mix = grad_resid.astype(bf16)
    grad_o = contract_rows(grad_mix, attn_bf)
    grad_attn = jnp.dot(grad_mix, o_weight, preferred_element_type=f32).astype(bf16)
    grad_attn_grouped = jnp.transpose(
        grad_attn.reshape(token_count, kv_local, group_size, HEAD_SIZE), (1, 2, 0, 3)
    )
    row_delta = jnp.sum(grad_attn_grouped.astype(f32) * attn_grouped, axis=-1)
    allowed = piece_mask(piece_rows)
    scores = (
        jnp.einsum("tkgd,nkd->kgtn", query_grouped, key_piece, preferred_element_type=f32)
        * score_scale
    )
    probability = jnp.where(allowed, jnp.exp(scores - log_sum[..., None]), 0.0)
    grad_probs = jnp.einsum(
        "kgtd,nkd->kgtn", grad_attn_grouped, value_piece, preferred_element_type=f32
    )
    grad_scores = (probability * (grad_probs - row_delta[..., None])).astype(bf16)
    grad_query = score_scale * jnp.einsum(
        "kgtn,nkd->kgtd", grad_scores, key_piece, preferred_element_type=f32
    )
    key_part = score_scale * jnp.einsum(
        "kgtn,tkgd->nkd", grad_scores, query_grouped, preferred_element_type=f32
    )
    value_part = jnp.einsum(
        "kgtn,kgtd->nkd", probability.astype(bf16), grad_attn_grouped, preferred_element_type=f32
    )
    grad_keys_all = key_part.reshape(piece_rows, kv_local * HEAD_SIZE)
    grad_values_all = value_part.reshape(piece_rows, kv_local * HEAD_SIZE)
    back_state = (grad_query, grad_keys_all, grad_values_all)
    grad_query, grad_keys_all, grad_values_all = back_state
    grad_kv_here = chain_sum_down(
        jnp.concatenate([grad_keys_all, grad_values_all], axis=1)
        .astype(bf16)
        .reshape(ctx_count, token_count, 2 * kv_width),
        "ctx",
        ctx_count,
        6,
    )
    grad_keys_here = grad_kv_here[:, :kv_width]
    grad_values_here = grad_kv_here[:, kv_width:]
    grad_query_rows = jnp.transpose(grad_query, (2, 0, 1, 3)).reshape(
        token_count, heads_local, HEAD_SIZE
    )
    grad_query_bf = (
        apply_rotary(grad_query_rows, token_positions, -1.0)
        .reshape(token_count, heads_local * HEAD_SIZE)
        .astype(bf16)
    )
    grad_key_bf = (
        apply_rotary(
            grad_keys_here.reshape(token_count, kv_local, HEAD_SIZE), token_positions, -1.0
        )
        .reshape(token_count, kv_local * HEAD_SIZE)
        .astype(bf16)
    )
    grad_value_bf = grad_values_here.astype(bf16)
    grad_q = contract_rows(normed_one, grad_query_bf)
    grad_k = contract_rows(normed_one, grad_key_bf)
    grad_v = contract_rows(normed_one, grad_value_bf)
    partial_one = (
        contract_cols(grad_query_bf, q_weight)
        + contract_cols(grad_key_bf, key_matrix)
        + contract_cols(grad_value_bf, value_matrix)
    )
    grad_normed_one = sum_axis(partial_one.astype(bf16), "tensor", 7)
    grad_one_rows, grad_attn_gain = norm_backward(inputs_f32, scale_one, attn_gain, grad_normed_one)
    input_grad = grad_resid + grad_one_rows
    q_cols, o_cols, k_cols = grad_q.shape[1], grad_o.shape[1], grad_k.shape[1]
    small = jnp.concatenate(
        [
            grad_router,
            grad_attn_gain[:, None],
            grad_moe_gain[:, None],
            jnp.zeros((grad_router.shape[0], 128 - grad_router.shape[1] - 2), f32),
        ],
        axis=1,
    )
    dense_all = jnp.concatenate(
        [grad_q, grad_o, grad_k, grad_v, small], axis=1
    ).astype(bf16)
    width = dense_all.shape[0]
    dense_all = jnp.transpose(
        dense_all.reshape(dpx_count, 2, width // (2 * dpx_count), dense_all.shape[1]), (1, 0, 2, 3)
    )
    dense_half = core_reduce(dense_all, 11)
    dense_half, grad_gate_out, grad_up_out, grad_down_out = lax.optimization_barrier(
        (dense_half, grad_gate_out, grad_up_out, grad_down_out)
    )
    dense_here = lax.psum_scatter(
        dense_half.reshape(-1, dense_half.shape[-1]), ("dpx", "ctx"), scatter_dimension=0, tiled=True
    ).astype(f32)
    spans = [q_cols, o_cols, k_cols, k_cols, router_weight.shape[1], 1, 1]
    cuts = [sum(spans[:i]) for i in range(len(spans) + 1)]
    pieces_out = [dense_here[:, cuts[i] : cuts[i + 1]] for i in range(len(spans))]
    dense_out = (
        pieces_out[5][:, 0],
        pieces_out[0],
        pieces_out[2],
        pieces_out[3],
        pieces_out[1],
        pieces_out[6][:, 0],
        pieces_out[4],
    )
    return (
        output,
        input_grad,
        dense_out[0],
        dense_out[1],
        dense_out[2],
        dense_out[3],
        dense_out[4],
        dense_out[5],
        dense_out[6],
        grad_gate_out,
        grad_up_out,
        grad_down_out,
    )


def solution(mesh):
    dp_count, ctx_count, tensor_count = (mesh.shape[a] for a in ("dp", "ctx", "tensor"))
    split_mesh = jax.sharding.Mesh(
        mesh.devices.reshape(dp_count // 2, 2, ctx_count, tensor_count), ("dpx", "core", "ctx", "tensor")
    )
    return jax.shard_map(
        functools.partial(per_device, dp_count // 2),
        mesh=split_mesh,
        in_specs=(
            P(("dpx", "core", "ctx"), None),
            P(),
            P(None, "tensor"),
            P(None, "tensor"),
            P(None, "tensor"),
            P(None, "tensor"),
            P(),
            P(),
            P(None, None, "tensor"),
            P(None, None, "tensor"),
            P(None, None, "tensor"),
            P(("dpx", "core")),
            P(("dpx", "core", "ctx"), None),
            P(("dpx", "core", "ctx"), None),
        ),
        out_specs=(
            P(("dpx", "core", "ctx"), None),
            P(("dpx", "core", "ctx"), None),
            P(("dpx", "core", "ctx")),
            P(("dpx", "core", "ctx"), "tensor"),
            P(("dpx", "core", "ctx"), "tensor"),
            P(("dpx", "core", "ctx"), "tensor"),
            P(("dpx", "core", "ctx"), "tensor"),
            P(("dpx", "core", "ctx")),
            P(("dpx", "core", "ctx"), None),
            P(None, ("dpx", "core", "ctx"), "tensor"),
            P(None, ("dpx", "core", "ctx"), "tensor"),
            P(None, ("dpx", "core", "ctx"), "tensor"),
        ),
        check_vma=False,
    )
```

```python
import functools
import math

import jax
import jax.numpy as jnp
from jax import lax
from jax.experimental import pallas as pl
from jax.experimental.pallas import tpu as pltpu
from jax.sharding import PartitionSpec as P

HEAD_SIZE = 64
NEXP = 24
CAP = 341


EPSILON = 1e-06
ROPE_BASE = 10000.0
NEGATIVE = -1e30
HIGHEST = lax.Precision.HIGHEST


def normalize(rows, gain):
    scale_inv = lax.rsqrt(jnp.mean(rows * rows, axis=-1, keepdims=True) + EPSILON)
    return (rows * scale_inv * gain, scale_inv)


def norm_backward(rows, scale_inv, gain, grad_normed):
    weighted = gain * grad_normed
    grad_gain = jnp.sum(grad_normed * rows * scale_inv, axis=0)
    inner_mean = jnp.mean(weighted * rows, axis=-1, keepdims=True)
    grad_rows = scale_inv * weighted - rows * scale_inv * scale_inv * scale_inv * inner_mean
    return (grad_rows, grad_gain)


def apply_rotary(value_rows, token_positions, direction):
    half_dim = value_rows.shape[-1] // 2
    frequency = ROPE_BASE ** (-jnp.arange(half_dim, dtype=jnp.float32) / half_dim)
    angles = token_positions.astype(jnp.float32)[:, None] * frequency[None, :]
    cosine = jnp.cos(angles)[:, None, :]
    sine_part = direction * jnp.sin(angles)[:, None, :]
    first_half = value_rows[..., :half_dim]
    second = value_rows[..., half_dim:]
    return jnp.concatenate(
        [first_half * cosine - second * sine_part, second * cosine + first_half * sine_part],
        axis=-1,
    )


def contract_rows(left, right):
    return lax.dot_general(
        left, right, (((0,), (0,)), ((), ())), preferred_element_type=jnp.float32
    )


def contract_rows_exact(left, right):
    return lax.dot_general(
        left, right, (((0,), (0,)), ((), ())), precision=HIGHEST, preferred_element_type=jnp.float32
    )


def contract_cols(left, right):
    return lax.dot_general(
        left, right, (((1,), (1,)), ((), ())), preferred_element_type=jnp.float32
    )


def _store_split(out_ref, value):
    cores, _, groups, rows, _ = out_ref.shape
    for x in range(groups):
        for c in range(cores):
            start = (x * cores + c) * rows
            out_ref[c, 0, x] = value[start : start + rows].astype(out_ref.dtype)


def _gate_column(gates_ref):
    gates = gates_ref[...]
    lane = lax.broadcasted_iota(jnp.int32, gates.shape, 1)
    return jnp.sum(jnp.where(lane == pl.program_id(0), gates, 0.0), axis=1, keepdims=True)


def _grad_body(
    n2_ref, n2t_ref, dy_ref, gcol_ref, wg_ref, wu_ref, wd_ref,
    gg_ref, hid_ref, dga_ref, dua_ref,
):
    f32 = jnp.float32
    bf16 = jnp.bfloat16
    n2 = n2_ref[...]
    gate_act = jnp.dot(n2, wg_ref[0], preferred_element_type=f32)
    up_act = jnp.dot(n2, wu_ref[0], preferred_element_type=f32)
    sig = 1.0 / (1.0 + jnp.exp(-gate_act))
    silu = gate_act * sig
    hid_ref[0] = (silu * up_act).astype(bf16)
    deo = (_gate_column(gcol_ref) * dy_ref[...].astype(f32)).astype(bf16)
    grad_hidden = jnp.dot(deo, wd_ref[0], preferred_element_type=f32)
    grad_gate_act = (grad_hidden * up_act * sig * (1.0 + gate_act * (1.0 - sig))).astype(bf16)
    dga_ref[0] = grad_gate_act
    dua_ref[0] = (grad_hidden * silu).astype(bf16)
    _store_split(gg_ref, jnp.dot(n2t_ref[...], grad_gate_act, preferred_element_type=f32))


def _grad_rest_body(n2t_ref, dyt_ref, grow_ref, hid_ref, dua_ref, gu_ref, gd_ref):
    f32 = jnp.float32
    deo_t = (grow_ref[0] * dyt_ref[...].astype(f32)).astype(jnp.bfloat16)
    _store_split(gd_ref, jnp.dot(deo_t, hid_ref[0], preferred_element_type=f32))
    _store_split(gu_ref, jnp.dot(n2t_ref[...], dua_ref[0], preferred_element_type=f32))


def _rows_body(hid_ref, dga_ref, dua_ref, dy_ref, gcol_ref, wg_ref, wu_ref, wd_ref, acc_ref, dgate_ref, dn2_ref):
    f32 = jnp.float32
    nt = (((1,), (1,)), ((), ()))

    @pl.when(pl.program_id(0) == 0)
    def _():
        acc_ref[...] = jnp.zeros_like(acc_ref)
        dn2_ref[...] = jnp.zeros_like(dn2_ref)

    expert_out = lax.dot_general(hid_ref[0], wd_ref[0], nt, preferred_element_type=f32)
    acc_ref[...] += _gate_column(gcol_ref) * expert_out
    dgate_ref[0] = jnp.sum(expert_out * dy_ref[...].astype(f32), axis=1, keepdims=True)
    dn2_ref[...] += lax.dot_general(
        dga_ref[0], wg_ref[0], nt, preferred_element_type=f32
    ) + lax.dot_general(dua_ref[0], wu_ref[0], nt, preferred_element_type=f32)


def expert_grad_kernel(n2, n2t, dy, gcol, wg, wu, wd, groups):
    tokens, width = n2.shape
    experts, _, hidden = wg.shape
    bf16 = jnp.bfloat16
    whole = lambda shape: pl.BlockSpec(shape, lambda e: (0,) * len(shape))
    per_expert = lambda shape: pl.BlockSpec((1,) + shape, lambda e: (e,) + (0,) * len(shape))
    split_rows = width // (groups * 2)
    split = pl.BlockSpec((2, 1, groups, split_rows, hidden), lambda e: (0, e, 0, 0, 0))
    split_shape = jax.ShapeDtypeStruct((2, experts, groups, split_rows, hidden), bf16)
    act_shape = jax.ShapeDtypeStruct((experts, tokens, hidden), bf16)
    return pl.pallas_call(
        _grad_body,
        grid=(experts,),
        in_specs=[
            whole((tokens, width)),
            whole((width, tokens)),
            whole((tokens, width)),
            whole((tokens, experts)),
            per_expert((width, hidden)),
            per_expert((width, hidden)),
            per_expert((width, hidden)),
        ],
        out_specs=[split] + [per_expert((tokens, hidden))] * 3,
        out_shape=[split_shape] + [act_shape] * 3,
        compiler_params=pltpu.CompilerParams(
            dimension_semantics=("arbitrary",), vmem_limit_bytes=64 * 1024 * 1024
        ),
        cost_estimate=pl.CostEstimate(
            flops=experts * tokens * width * hidden * 2 * 4,
            transcendentals=experts * tokens * hidden,
            bytes_accessed=experts * width * hidden * 8 + tokens * width * 6 + experts * tokens * hidden * 6,
        ),
    )(n2, n2t, dy, gcol, wg, wu, wd)


def expert_grad_rest_kernel(n2t, dyt, grow, hid, dua, groups):
    width, tokens = n2t.shape
    experts, _, hidden = hid.shape
    bf16 = jnp.bfloat16
    whole = lambda shape: pl.BlockSpec(shape, lambda e: (0,) * len(shape))
    per_expert = lambda shape: pl.BlockSpec((1,) + shape, lambda e: (e,) + (0,) * len(shape))
    split_rows = width // (groups * 2)
    split = pl.BlockSpec((2, 1, groups, split_rows, hidden), lambda e: (0, e, 0, 0, 0))
    split_shape = jax.ShapeDtypeStruct((2, experts, groups, split_rows, hidden), bf16)
    return pl.pallas_call(
        _grad_rest_body,
        grid=(experts,),
        in_specs=[
            whole((width, tokens)),
            whole((width, tokens)),
            per_expert((1, tokens)),
            per_expert((tokens, hidden)),
            per_expert((tokens, hidden)),
        ],
        out_specs=[split, split],
        out_shape=[split_shape, split_shape],
        compiler_params=pltpu.CompilerParams(
            dimension_semantics=("arbitrary",), vmem_limit_bytes=64 * 1024 * 1024
        ),
        cost_estimate=pl.CostEstimate(
            flops=experts * tokens * width * hidden * 2 * 2,
            transcendentals=0,
            bytes_accessed=experts * width * hidden * 4 + tokens * width * 4 + experts * tokens * hidden * 4,
        ),
    )(n2t, dyt, grow, hid, dua)


def expert_rows_kernel(hid, dga, dua, dy, gcol, wg, wu, wd):
    experts, tokens, hidden = hid.shape
    width = dy.shape[1]
    f32 = jnp.float32
    whole = lambda shape: pl.BlockSpec(shape, lambda e: (0,) * len(shape))
    per_expert = lambda shape: pl.BlockSpec((1,) + shape, lambda e: (e,) + (0,) * len(shape))
    return pl.pallas_call(
        _rows_body,
        grid=(experts,),
        in_specs=[
            per_expert((tokens, hidden)),
            per_expert((tokens, hidden)),
            per_expert((tokens, hidden)),
            whole((tokens, width)),
            whole((tokens, experts)),
            per_expert((width, hidden)),
            per_expert((width, hidden)),
            per_expert((width, hidden)),
        ],
        out_specs=[whole((tokens, width)), per_expert((tokens, 1)), whole((tokens, width))],
        out_shape=[
            jax.ShapeDtypeStruct((tokens, width), f32),
            jax.ShapeDtypeStruct((experts, tokens, 1), f32),
            jax.ShapeDtypeStruct((tokens, width), f32),
        ],
        compiler_params=pltpu.CompilerParams(
            dimension_semantics=("arbitrary",), vmem_limit_bytes=64 * 1024 * 1024
        ),
        cost_estimate=pl.CostEstimate(
            flops=experts * tokens * width * hidden * 2 * 3,
            transcendentals=0,
            bytes_accessed=experts * width * hidden * 6 + tokens * width * 10 + experts * tokens * hidden * 6,
        ),
    )(hid, dga, dua, dy, gcol, wg, wu, wd)

MESH = pl.DeviceIdType.MESH


def _exchange_body(axis, n, per_peer, downward, src_ref, out_ref, send_sems, recv_sems):
    me = lax.axis_index(axis)
    barrier = pltpu.get_barrier_semaphore()
    for k in range(1, n):
        peer = lax.rem(me + k, n)
        pl.semaphore_signal(barrier, 1, device_id={axis: peer}, device_id_type=MESH)
    pl.semaphore_wait(barrier, n - 1)
    sends = []
    for k in range(1, n):
        peer = lax.rem(me + k, n)
        copy = pltpu.make_async_remote_copy(
            src_ref=src_ref.at[peer] if per_peer else src_ref,
            dst_ref=out_ref.at[me],
            send_sem=send_sems.at[k - 1],
            recv_sem=recv_sems.at[k - 1],
            device_id={axis: peer},
            device_id_type=MESH,
        )
        sends.append((peer, copy))
        if downward:
            pl.when(peer < me)(copy.start)
        else:
            copy.start()
    for k in range(1, n):
        source = lax.rem(me + n - k, n)
        incoming = pltpu.make_async_remote_copy(
            src_ref=src_ref.at[source] if per_peer else src_ref,
            dst_ref=out_ref.at[source],
            send_sem=send_sems.at[k - 1],
            recv_sem=recv_sems.at[k - 1],
            device_id={axis: source},
            device_id_type=MESH,
        )
        if downward:
            pl.when(source > me)(incoming.wait_recv)
        else:
            incoming.wait_recv()
    for peer, copy in sends:
        if downward:
            pl.when(peer < me)(copy.wait_send)
        else:
            copy.wait_send()


def exchange(x, axis, n, per_peer, collective_id, downward=False):
    block = x.shape[1:] if per_peer else x.shape
    nbytes = math.prod(block) * x.dtype.itemsize
    return pl.pallas_call(
        functools.partial(_exchange_body, axis, n, per_peer, downward),
        out_shape=jax.ShapeDtypeStruct((n,) + tuple(block), x.dtype),
        in_specs=[pl.BlockSpec(memory_space=pl.ANY)],
        out_specs=pl.BlockSpec(memory_space=pl.ANY),
        scratch_shapes=[pltpu.SemaphoreType.DMA((n - 1,)), pltpu.SemaphoreType.DMA((n - 1,))],
        compiler_params=pltpu.CompilerParams(collective_id=collective_id, has_side_effects=True),
        cost_estimate=pl.CostEstimate(flops=0, transcendentals=0, bytes_accessed=2 * (n - 1) * nbytes),
    )(x)


def gather_axis(x, axis, n, collective_id):
    got = exchange(x, axis, n, False, collective_id)
    return lax.dynamic_update_slice_in_dim(got, x[None], lax.axis_index(axis), 0)


def sum_axis(x, axis, collective_id):
    got = exchange(x, axis, 2, False, collective_id)
    me = lax.axis_index(axis)
    other = lax.dynamic_index_in_dim(got, 1 - me, 0, keepdims=False)
    return x.astype(jnp.float32) + other.astype(jnp.float32)


def _pair_add_body(me_ref, own_ref, other_ref, out_ref):
    out_ref[...] = (own_ref[...].astype(jnp.float32) + other_ref[...].astype(jnp.float32)).astype(out_ref.dtype)


def core_reduce(x, collective_id):
    got = exchange(x, "core", 2, True, collective_id)
    me = lax.axis_index("core")
    count = x.shape[1]
    rest = x.shape[2:]
    zeros = (0,) * len(rest)
    item_bytes = math.prod(rest) * x.dtype.itemsize
    step = max(d for d in range(1, count + 1) if count % d == 0 and d * item_bytes <= 4 * 1024 * 1024)
    grid_spec = pltpu.PrefetchScalarGridSpec(
        num_scalar_prefetch=1,
        grid=(count // step,),
        in_specs=[
            pl.BlockSpec((None, step) + rest, lambda i, c: (c[0], i) + zeros),
            pl.BlockSpec((None, step) + rest, lambda i, c: (1 - c[0], i) + zeros),
        ],
        out_specs=pl.BlockSpec((step,) + rest, lambda i, c: (i,) + zeros),
    )
    return pl.pallas_call(
        _pair_add_body,
        grid_spec=grid_spec,
        out_shape=jax.ShapeDtypeStruct(x.shape[1:], jnp.bfloat16),
        compiler_params=pltpu.CompilerParams(vmem_limit_bytes=56 * 1024 * 1024),
        cost_estimate=pl.CostEstimate(flops=x.size // 2, transcendentals=0, bytes_accessed=x.size * 3),
    )(jnp.reshape(me, (1,)).astype(jnp.int32), x, got)


def scatter_sum_downward(x, axis, n, collective_id):
    got = exchange(x, axis, n, True, collective_id, downward=True)
    me = lax.axis_index(axis)
    own = lax.dynamic_index_in_dim(x, me, 0, keepdims=False).astype(jnp.float32)
    above = (jnp.arange(n, dtype=jnp.int32) > me).reshape((n,) + (1,) * (x.ndim - 1))
    return own + jnp.sum(jnp.where(above, got.astype(jnp.float32), 0.0), axis=0)


def _flash_body(groups, ctx_ref, q_ref, k_ref, v_ref, qseg_ref, qpos_ref, kseg_ref, o_ref, lse_ref, qs_sc, m_sc, l_sc, acc_sc):
    f32 = jnp.float32
    block = pl.program_id(1)
    depth = HEAD_SIZE
    pair = k_ref.shape[2] // depth
    tokens = q_ref.shape[0]

    @pl.when(block == 0)
    def _():
        m_sc[...] = jnp.full_like(m_sc, NEGATIVE)
        l_sc[...] = jnp.zeros_like(l_sc)
        acc_sc[...] = jnp.zeros_like(acc_sc)
        scale = jnp.asarray(1.0 / math.sqrt(HEAD_SIZE), q_ref.dtype)
        for kk in range(pair):
            for gi in range(groups):
                i = kk * groups + gi
                qs_sc[kk, gi * tokens : (gi + 1) * tokens, :] = q_ref[:, i * depth : (i + 1) * depth] * scale

    @pl.when(block <= ctx_ref[0])
    def _():
        width = k_ref.shape[1]
        key_pos = block * width + lax.broadcasted_iota(jnp.int32, (1, width), 1)
        allowed = (qseg_ref[...] == kseg_ref[...]) & (key_pos <= qpos_ref[...])
        for kk in range(pair):
            keys = k_ref[0, :, kk * depth : (kk + 1) * depth]
            values = v_ref[0, :, kk * depth : (kk + 1) * depth]
            scores = lax.dot_general(
                qs_sc[kk], keys, (((1,), (1,)), ((), ())), preferred_element_type=f32
            )
            scores = jnp.where(allowed, scores, NEGATIVE)
            m_old = m_sc[kk]
            m_new = jnp.maximum(m_old, jnp.max(scores, axis=1, keepdims=True))
            alpha = jnp.exp(m_old - m_new)
            weights = jnp.where(allowed, jnp.exp(scores - m_new), 0.0)
            l_sc[kk] = alpha * l_sc[kk] + jnp.sum(weights, axis=1, keepdims=True)
            acc_sc[kk] = alpha * acc_sc[kk] + jnp.dot(
                weights.astype(jnp.bfloat16), values, preferred_element_type=f32
            )
            m_sc[kk] = m_new

    @pl.when(block == pl.num_programs(1) - 1)
    def _():
        for kk in range(pair):
            for gi in range(groups):
                i = kk * groups + gi
                rows = slice(gi * tokens, (gi + 1) * tokens)
                o_ref[:, i * depth : (i + 1) * depth] = acc_sc[kk, rows, :] / l_sc[kk, rows, :]
                lse_ref[0, :, i : i + 1] = m_sc[kk, rows, :] + jnp.log(l_sc[kk, rows, :])


def flash_forward(ctx_index, q, kv, qseg, qpos, kseg, groups):
    tokens, q_width = q.shape
    blocks, width, kv_width = kv.shape
    pair = 2
    pairs = kv_width // (2 * pair * HEAD_SIZE)
    heads_step = pair * groups
    f32 = jnp.float32
    capped = lambda p, b, c: (jnp.minimum(b, c[0]), 0, p)
    grid_spec = pltpu.PrefetchScalarGridSpec(
        num_scalar_prefetch=1,
        grid=(pairs, blocks),
        in_specs=[
            pl.BlockSpec((tokens, heads_step * HEAD_SIZE), lambda p, b, c: (0, p)),
            pl.BlockSpec((1, width, pair * HEAD_SIZE), capped),
            pl.BlockSpec((1, width, pair * HEAD_SIZE), lambda p, b, c: (jnp.minimum(b, c[0]), 0, pairs + p)),
            pl.BlockSpec((groups * tokens, 1), lambda p, b, c: (0, 0)),
            pl.BlockSpec((groups * tokens, 1), lambda p, b, c: (0, 0)),
            pl.BlockSpec((1, width), lambda p, b, c: (0, jnp.minimum(b, c[0]))),
        ],
        out_specs=[
            pl.BlockSpec((tokens, heads_step * HEAD_SIZE), lambda p, b, c: (0, p)),
            pl.BlockSpec((1, tokens, heads_step), lambda p, b, c: (p, 0, 0)),
        ],
        scratch_shapes=[
            pltpu.VMEM((pair, groups * tokens, HEAD_SIZE), q.dtype),
            pltpu.VMEM((pair, groups * tokens, 1), f32),
            pltpu.VMEM((pair, groups * tokens, 1), f32),
            pltpu.VMEM((pair, groups * tokens, HEAD_SIZE), f32),
        ],
    )
    return pl.pallas_call(
        functools.partial(_flash_body, groups),
        grid_spec=grid_spec,
        out_shape=[
            jax.ShapeDtypeStruct((tokens, q_width), f32),
            jax.ShapeDtypeStruct((pairs, tokens, heads_step), f32),
        ],
        compiler_params=pltpu.CompilerParams(
            dimension_semantics=("arbitrary", "arbitrary"), vmem_limit_bytes=48 * 1024 * 1024
        ),
        cost_estimate=pl.CostEstimate(
            flops=tokens * q_width * blocks * width * 4,
            transcendentals=tokens * (q_width // HEAD_SIZE) * blocks * width,
            bytes_accessed=(q.size + kv.size) * 2 + tokens * q_width * 4,
        ),
    )(jnp.reshape(ctx_index, (1,)).astype(jnp.int32), q, kv, kv, qseg, qpos, kseg)

def _chain_down_body(axis, n, x_ref, out_ref, recv, send, send_sems, recv_sems):
    f32 = jnp.float32
    me = lax.axis_index(axis)
    below = lax.rem(me + n - 1, n)
    above = lax.rem(me + 1, n)
    barrier = pltpu.get_barrier_semaphore()
    pl.semaphore_signal(barrier, 1, device_id={axis: below}, device_id_type=MESH)
    pl.semaphore_signal(barrier, 1, device_id={axis: above}, device_id_type=MESH)
    pl.semaphore_wait(barrier, 2)
    copies = []
    for j in range(n - 1):
        copy = pltpu.make_async_remote_copy(
            src_ref=send.at[j],
            dst_ref=recv.at[j],
            send_sem=send_sems.at[j],
            recv_sem=recv_sems.at[j],
            device_id={axis: below},
            device_id_type=MESH,
        )
        copies.append(copy)

        @pl.when((j < me) & (me < n - 1))
        def _():
            copy.wait_recv()
            send[j] = (x_ref[j].astype(f32) + recv[j].astype(f32)).astype(send.dtype)

        @pl.when((j < me) & (me == n - 1))
        def _():
            send[j] = x_ref[j]

        @pl.when(j < me)
        def _():
            copy.start()

        @pl.when(j == me)
        def _():
            copy.wait_recv()
            out_ref[...] = x_ref[j].astype(f32) + recv[j].astype(f32)

    @pl.when(me == n - 1)
    def _():
        out_ref[...] = x_ref[n - 1].astype(f32)

    for j in range(n - 1):
        pl.when(j < me)(copies[j].wait_send)


def chain_sum_down(x, axis, n, collective_id):
    _, rows, cols = x.shape
    return pl.pallas_call(
        functools.partial(_chain_down_body, axis, n),
        out_shape=jax.ShapeDtypeStruct((rows, cols), jnp.float32),
        in_specs=[pl.BlockSpec(memory_space=pltpu.VMEM)],
        out_specs=pl.BlockSpec(memory_space=pltpu.VMEM),
        scratch_shapes=[
            pltpu.VMEM((n - 1, rows, cols), x.dtype),
            pltpu.VMEM((n - 1, rows, cols), x.dtype),
            pltpu.SemaphoreType.DMA((n - 1,)),
            pltpu.SemaphoreType.DMA((n - 1,)),
        ],
        compiler_params=pltpu.CompilerParams(
            collective_id=collective_id, has_side_effects=True, vmem_limit_bytes=32 * 1024 * 1024
        ),
        cost_estimate=pl.CostEstimate(
            flops=(n - 1) * rows * cols, transcendentals=0, bytes_accessed=3 * n * rows * cols * 2
        ),
    )(x)


def _chain_up_body(axis, n, x_ref, out_ref, send_sems, recv_sems):
    me = lax.axis_index(axis)
    below = lax.rem(me + n - 1, n)
    above = lax.rem(me + 1, n)
    barrier = pltpu.get_barrier_semaphore()
    pl.semaphore_signal(barrier, 1, device_id={axis: below}, device_id_type=MESH)
    pl.semaphore_signal(barrier, 1, device_id={axis: above}, device_id_type=MESH)
    pl.semaphore_wait(barrier, 2)
    own = pltpu.make_async_remote_copy(
        src_ref=x_ref,
        dst_ref=out_ref.at[me],
        send_sem=send_sems.at[me],
        recv_sem=recv_sems.at[me],
        device_id={axis: above},
        device_id_type=MESH,
    )
    pl.when(me < n - 1)(own.start)
    forwards = []
    for k in range(1, n):
        block = jnp.maximum(me - k, 0)
        incoming = pltpu.make_async_remote_copy(
            src_ref=out_ref.at[block],
            dst_ref=out_ref.at[block],
            send_sem=send_sems.at[block],
            recv_sem=recv_sems.at[block],
            device_id={axis: below},
            device_id_type=MESH,
        )
        forward = pltpu.make_async_remote_copy(
            src_ref=out_ref.at[block],
            dst_ref=out_ref.at[block],
            send_sem=send_sems.at[block],
            recv_sem=recv_sems.at[block],
            device_id={axis: above},
            device_id_type=MESH,
        )
        forwards.append((k, forward))
        pl.when(k <= me)(incoming.wait_recv)
        pl.when((k <= me) & (me < n - 1))(forward.start)
    pl.when(me < n - 1)(own.wait_send)
    for k, forward in forwards:
        pl.when((k <= me) & (me < n - 1))(forward.wait_send)


def gather_up(x, axis, n, collective_id):
    got = pl.pallas_call(
        functools.partial(_chain_up_body, axis, n),
        out_shape=jax.ShapeDtypeStruct((n,) + x.shape, x.dtype),
        in_specs=[pl.BlockSpec(memory_space=pl.ANY)],
        out_specs=pl.BlockSpec(memory_space=pl.ANY),
        scratch_shapes=[pltpu.SemaphoreType.DMA((n,)), pltpu.SemaphoreType.DMA((n,))],
        compiler_params=pltpu.CompilerParams(collective_id=collective_id, has_side_effects=True),
        cost_estimate=pl.CostEstimate(
            flops=0, transcendentals=0, bytes_accessed=2 * (n - 1) * x.size * x.dtype.itemsize
        ),
    )(x)
    me = lax.axis_index(axis)
    below = (jnp.arange(n, dtype=jnp.int32) < me).reshape((n,) + (1,) * x.ndim)
    got = jnp.where(below, got, jnp.zeros_like(got))
    return lax.dynamic_update_slice_in_dim(got, x[None], me, 0)


def _attend_block(groups, kv_heads, q_sc, kv_buf, qseg_ref, qpos_ref, kseg_ref, m_sc, l_sc, acc_sc, block):
    f32 = jnp.float32
    depth = HEAD_SIZE
    width = kv_buf.shape[0]
    start = pl.multiple_of(block * width, width)
    key_pos = start + lax.broadcasted_iota(jnp.int32, (1, width), 1)
    allowed = (qseg_ref[...] == kseg_ref[:, pl.ds(start, width)]) & (key_pos <= qpos_ref[...])
    for kk in range(kv_heads):
        keys = kv_buf[:, kk * depth : (kk + 1) * depth]
        values = kv_buf[:, (kv_heads + kk) * depth : (kv_heads + kk + 1) * depth]
        scores = lax.dot_general(q_sc[kk], keys, (((1,), (1,)), ((), ())), preferred_element_type=f32)
        scores = jnp.where(allowed, scores, NEGATIVE)
        m_old = m_sc[kk]
        m_new = jnp.maximum(m_old, jnp.max(scores, axis=1, keepdims=True))
        alpha = jnp.exp(m_old - m_new)
        weights = jnp.where(allowed, jnp.exp(scores - m_new), 0.0)
        l_sc[kk] = alpha * l_sc[kk] + jnp.sum(weights, axis=1, keepdims=True)
        acc_sc[kk] = alpha * acc_sc[kk] + jnp.dot(
            weights.astype(jnp.bfloat16), values, preferred_element_type=f32
        )
        m_sc[kk] = m_new


def _gather_attend_body(
    axis, n, groups, q_ref, own_ref, qseg_ref, qpos_ref, kseg_ref,
    kv_ref, o_ref, lse_ref,
    q_sc, m_sc, l_sc, acc_sc, kv_buf, send_sems, recv_sems, copy_sem,
):
    depth = HEAD_SIZE
    tokens = q_ref.shape[0]
    kv_heads = own_ref.shape[1] // (2 * depth)
    me = lax.axis_index(axis)
    below = lax.rem(me + n - 1, n)
    above = lax.rem(me + 1, n)
    barrier = pltpu.get_barrier_semaphore()
    pl.semaphore_signal(barrier, 1, device_id={axis: below}, device_id_type=MESH)
    pl.semaphore_signal(barrier, 1, device_id={axis: above}, device_id_type=MESH)
    pl.semaphore_wait(barrier, 2)
    own = pltpu.make_async_remote_copy(
        src_ref=own_ref,
        dst_ref=kv_ref.at[me],
        send_sem=send_sems.at[me],
        recv_sem=recv_sems.at[me],
        device_id={axis: above},
        device_id_type=MESH,
    )
    pl.when(me < n - 1)(own.start)

    m_sc[...] = jnp.full_like(m_sc, NEGATIVE)
    l_sc[...] = jnp.zeros_like(l_sc)
    acc_sc[...] = jnp.zeros_like(acc_sc)
    scale = jnp.asarray(1.0 / math.sqrt(HEAD_SIZE), q_ref.dtype)
    for kk in range(kv_heads):
        for gi in range(groups):
            i = kk * groups + gi
            q_sc[kk, gi * tokens : (gi + 1) * tokens, :] = q_ref[:, i * depth : (i + 1) * depth] * scale

    local = pltpu.make_async_copy(own_ref, kv_buf, copy_sem)
    local.start()
    local.wait()
    _attend_block(groups, kv_heads, q_sc, kv_buf, qseg_ref, qpos_ref, kseg_ref, m_sc, l_sc, acc_sc, me)

    def step(k, carry):
        block = me - k
        incoming = pltpu.make_async_remote_copy(
            src_ref=kv_ref.at[block],
            dst_ref=kv_ref.at[block],
            send_sem=send_sems.at[block],
            recv_sem=recv_sems.at[block],
            device_id={axis: below},
            device_id_type=MESH,
        )
        incoming.wait_recv()
        forward = pltpu.make_async_remote_copy(
            src_ref=kv_ref.at[block],
            dst_ref=kv_ref.at[block],
            send_sem=send_sems.at[block],
            recv_sem=recv_sems.at[block],
            device_id={axis: above},
            device_id_type=MESH,
        )
        pl.when(me < n - 1)(forward.start)
        fetch = pltpu.make_async_copy(kv_ref.at[block], kv_buf, copy_sem)
        fetch.start()
        fetch.wait()
        _attend_block(groups, kv_heads, q_sc, kv_buf, qseg_ref, qpos_ref, kseg_ref, m_sc, l_sc, acc_sc, block)
        return carry

    lax.fori_loop(1, me + 1, step, 0)

    for kk in range(kv_heads):
        for gi in range(groups):
            i = kk * groups + gi
            rows = slice(gi * tokens, (gi + 1) * tokens)
            o_ref[:, i * depth : (i + 1) * depth] = acc_sc[kk, rows, :] / l_sc[kk, rows, :]
            lse_ref[:, i : i + 1] = m_sc[kk, rows, :] + jnp.log(l_sc[kk, rows, :])

    pl.when(me < n - 1)(own.wait_send)

    def drain(k, carry):
        block = me - k
        pltpu.make_async_remote_copy(
            src_ref=kv_ref.at[block],
            dst_ref=kv_ref.at[block],
            send_sem=send_sems.at[block],
            recv_sem=recv_sems.at[block],
            device_id={axis: above},
            device_id_type=MESH,
        ).wait_send()
        return carry

    lax.fori_loop(1, jnp.where(me < n - 1, me + 1, 1), drain, 0)


def gather_attend(q, own, qseg, qpos, kseg, axis, n, groups, collective_id):
    tokens, q_width = q.shape
    rows, kv_width = own.shape
    heads = q_width // HEAD_SIZE
    kv_heads = kv_width // (2 * HEAD_SIZE)
    f32 = jnp.float32
    vmem = pl.BlockSpec(memory_space=pltpu.VMEM)
    anywhere = pl.BlockSpec(memory_space=pl.ANY)
    kv_all, attn, lse = pl.pallas_call(
        functools.partial(_gather_attend_body, axis, n, groups),
        out_shape=[
            jax.ShapeDtypeStruct((n, rows, kv_width), own.dtype),
            jax.ShapeDtypeStruct((tokens, q_width), f32),
            jax.ShapeDtypeStruct((tokens, heads), f32),
        ],
        in_specs=[vmem, anywhere, vmem, vmem, vmem],
        out_specs=[anywhere, vmem, vmem],
        scratch_shapes=[
            pltpu.VMEM((kv_heads, groups * tokens, HEAD_SIZE), q.dtype),
            pltpu.VMEM((kv_heads, groups * tokens, 1), f32),
            pltpu.VMEM((kv_heads, groups * tokens, 1), f32),
            pltpu.VMEM((kv_heads, groups * tokens, HEAD_SIZE), f32),
            pltpu.VMEM((rows, kv_width), own.dtype),
            pltpu.SemaphoreType.DMA((n,)),
            pltpu.SemaphoreType.DMA((n,)),
            pltpu.SemaphoreType.DMA(()),
        ],
        compiler_params=pltpu.CompilerParams(
            collective_id=collective_id, has_side_effects=True, vmem_limit_bytes=48 * 1024 * 1024
        ),
        cost_estimate=pl.CostEstimate(
            flops=tokens * q_width * n * rows * 4,
            transcendentals=tokens * heads * n * rows,
            bytes_accessed=2 * n * own.size * own.dtype.itemsize + tokens * q_width * 6,
        ),
    )(q, own, qseg, qpos, kseg)
    me = lax.axis_index(axis)
    below = (jnp.arange(n, dtype=jnp.int32) < me).reshape((n, 1, 1))
    kv_all = jnp.where(below, kv_all, jnp.zeros_like(kv_all))
    return attn, lse, lax.dynamic_update_slice_in_dim(kv_all, own[None], me, 0)


def per_device(
    dpx_count,
    hidden_in,
    attn_gain,
    q_weight,
    key_matrix,
    value_matrix,
    o_weight,
    moe_gain,
    router_weight,
    gate_weight,
    up_weight,
    down_weight,
    segments,
    expert_picks,
    output_grad,
):
    bf16 = jnp.bfloat16
    f32 = jnp.float32
    token_count = hidden_in.shape[0]
    ctx_index = lax.axis_index("ctx")
    heads_local = q_weight.shape[1] // HEAD_SIZE
    kv_local = key_matrix.shape[1] // HEAD_SIZE
    group_size = heads_local // kv_local
    score_scale = 1.0 / math.sqrt(HEAD_SIZE)
    token_positions = ctx_index * token_count + jnp.arange(token_count, dtype=jnp.int32)
    segment_here = lax.dynamic_slice_in_dim(segments, ctx_index * token_count, token_count)
    inputs_f32 = hidden_in.astype(f32)
    o_full = lax.all_gather(o_weight, "tensor", axis=1, tiled=True)
    normed_f32, scale_one = normalize(inputs_f32, attn_gain)
    normed_one = normed_f32.astype(bf16)
    query_rows = jnp.dot(normed_one, q_weight, preferred_element_type=f32).reshape(
        token_count, heads_local, HEAD_SIZE
    )
    keys_raw = jnp.dot(normed_one, key_matrix, preferred_element_type=f32).reshape(
        token_count, kv_local, HEAD_SIZE
    )
    values_raw = jnp.dot(normed_one, value_matrix, preferred_element_type=f32)
    query_grouped = (
        apply_rotary(query_rows, token_positions, 1.0)
        .astype(bf16)
        .reshape(token_count, kv_local, group_size, HEAD_SIZE)
    )
    key_flat = (
        apply_rotary(keys_raw, token_positions, 1.0)
        .astype(bf16)
        .reshape(token_count, kv_local * HEAD_SIZE)
    )
    value_flat = values_raw.astype(bf16)

    def piece_mask(piece_rows):
        key_pos = jnp.arange(piece_rows, dtype=jnp.int32)
        return (segment_here[:, None] == segments[None, :]) & (
            key_pos[None, :] <= token_positions[:, None]
        )

    ctx_count = segments.shape[0] // token_count
    attn_flat, lse_heads, kv_both = gather_attend(
        query_grouped.reshape(token_count, heads_local * HEAD_SIZE),
        jnp.concatenate([key_flat, value_flat], axis=1),
        jnp.tile(segment_here, group_size)[:, None],
        jnp.tile(token_positions, group_size)[:, None],
        segments[None, :],
        "ctx",
        ctx_count,
        group_size,
        1,
    )
    piece_rows = ctx_count * token_count
    kv_width = kv_local * HEAD_SIZE
    key_piece = kv_both[:, :, :kv_width].reshape(piece_rows, kv_local, HEAD_SIZE)
    value_piece = kv_both[:, :, kv_width:].reshape(piece_rows, kv_local, HEAD_SIZE)
    attn_grouped = jnp.transpose(
        attn_flat.reshape(token_count, kv_local, group_size, HEAD_SIZE), (1, 2, 0, 3)
    )
    log_sum = jnp.transpose(lse_heads.reshape(token_count, kv_local, group_size), (1, 2, 0))
    attn_bf = attn_flat.astype(bf16)
    tensor_count = o_weight.shape[0] // o_weight.shape[1]
    attn_all = gather_axis(attn_bf, "tensor", tensor_count, 2)
    attn_full = jnp.transpose(attn_all, (1, 0, 2)).reshape(token_count, tensor_count * attn_bf.shape[1])
    mixed_attn = contract_cols(attn_full, o_full)
    resid = inputs_f32 + mixed_attn
    normed_two_f32, scale_two = normalize(resid, moe_gain)
    normed_two = normed_two_f32.astype(bf16)
    logits = jnp.dot(normed_two, router_weight, preferred_element_type=f32)
    expert_range = jnp.arange(NEXP, dtype=jnp.int32)
    picked_onehot = expert_picks[:, :, None] == expert_range[None, None, :]
    picked = jnp.sum(jnp.where(picked_onehot, logits[:, None, :], 0.0), axis=2)
    gate_probs = jax.nn.softmax(picked, axis=-1)
    gates_dense = jnp.sum(jnp.where(picked_onehot, gate_probs[:, :, None], 0.0), axis=1)
    gates_by_expert = jnp.transpose(gates_dense)
    cot_bf = output_grad
    gcol = gates_dense
    normed_two_t = jnp.transpose(normed_two)
    grad_gate, hid_all, dga_all, dua_all = expert_grad_kernel(
        normed_two,
        normed_two_t,
        cot_bf,
        gcol,
        gate_weight,
        up_weight,
        down_weight,
        dpx_count,
    )
    gate_half = core_reduce(grad_gate, 8)
    gate_half, hid_all, dga_all, dua_all = lax.optimization_barrier(
        (gate_half, hid_all, dga_all, dua_all)
    )
    grad_up, grad_down = expert_grad_rest_kernel(
        normed_two_t,
        jnp.transpose(cot_bf),
        gates_by_expert[:, None, :],
        hid_all,
        dua_all,
        dpx_count,
    )
    moe_acc, gate_parts, moe_grad_rows = expert_rows_kernel(
        hid_all, dga_all, dua_all, cot_bf, gcol, gate_weight, up_weight, down_weight
    )
    cot_f32 = output_grad.astype(f32)
    moe_total = sum_axis(moe_acc.astype(bf16), "tensor", 3)
    output = (resid + moe_total).astype(bf16)
    grad_rows_all = moe_grad_rows
    gate_parts = gate_parts[:, :, 0]
    grad_gate_out, grad_up_out, grad_down_out = [
        lax.psum_scatter(
            g.reshape(g.shape[0], -1, g.shape[3]), ("dpx", "ctx"), scatter_dimension=1, tiled=True
        ).astype(jnp.float32)
        for g in (gate_half, core_reduce(grad_up, 9), core_reduce(grad_down, 10))
    ]
    gate_pair = jnp.sum(
        jnp.where(picked_onehot, jnp.transpose(gate_parts)[:, None, :], 0.0), axis=2
    )
    moe_summed = sum_axis(grad_rows_all.astype(bf16), "tensor", 4)
    gate_summed = sum_axis(gate_pair.astype(bf16), "tensor", 5)
    grad_picked = gate_probs * (
        gate_summed - jnp.sum(gate_probs * gate_summed, axis=1, keepdims=True)
    )
    grad_logits = jnp.sum(jnp.where(picked_onehot, grad_picked[:, :, None], 0.0), axis=1).astype(
        bf16
    )
    grad_router = contract_rows(normed_two, grad_logits)
    grad_normed_two = moe_summed + contract_cols(grad_logits, router_weight)
    grad_two_rows, grad_moe_gain = norm_backward(resid, scale_two, moe_gain, grad_normed_two)
    grad_resid = cot_f32 + grad_two_rows
    grad_mix = grad_resid.astype(bf16)
    grad_o = contract_rows(grad_mix, attn_bf)
    grad_attn = jnp.dot(grad_mix, o_weight, preferred_element_type=f32).astype(bf16)
    grad_attn_grouped = jnp.transpose(
        grad_attn.reshape(token_count, kv_local, group_size, HEAD_SIZE), (1, 2, 0, 3)
    )
    row_delta = jnp.sum(grad_attn_grouped.astype(f32) * attn_grouped, axis=-1)
    allowed = piece_mask(piece_rows)
    scores = (
        jnp.einsum("tkgd,nkd->kgtn", query_grouped, key_piece, preferred_element_type=f32)
        * score_scale
    )
    probability = jnp.where(allowed, jnp.exp(scores - log_sum[..., None]), 0.0)
    grad_probs = jnp.einsum(
        "kgtd,nkd->kgtn", grad_attn_grouped, value_piece, preferred_element_type=f32
    )
    grad_scores = (probability * (grad_probs - row_delta[..., None])).astype(bf16)
    grad_query = score_scale * jnp.einsum(
        "kgtn,nkd->kgtd", grad_scores, key_piece, preferred_element_type=f32
    )
    key_part = score_scale * jnp.einsum(
        "kgtn,tkgd->nkd", grad_scores, query_grouped, preferred_element_type=f32
    )
    value_part = jnp.einsum(
        "kgtn,kgtd->nkd", probability.astype(bf16), grad_attn_grouped, preferred_element_type=f32
    )
    grad_keys_all = key_part.reshape(piece_rows, kv_local * HEAD_SIZE)
    grad_values_all = value_part.reshape(piece_rows, kv_local * HEAD_SIZE)
    back_state = (grad_query, grad_keys_all, grad_values_all)
    grad_query, grad_keys_all, grad_values_all = back_state
    grad_kv_here = chain_sum_down(
        jnp.concatenate([grad_keys_all, grad_values_all], axis=1)
        .astype(bf16)
        .reshape(ctx_count, token_count, 2 * kv_width),
        "ctx",
        ctx_count,
        6,
    )
    grad_keys_here = grad_kv_here[:, :kv_width]
    grad_values_here = grad_kv_here[:, kv_width:]
    grad_query_rows = jnp.transpose(grad_query, (2, 0, 1, 3)).reshape(
        token_count, heads_local, HEAD_SIZE
    )
    grad_query_bf = (
        apply_rotary(grad_query_rows, token_positions, -1.0)
        .reshape(token_count, heads_local * HEAD_SIZE)
        .astype(bf16)
    )
    grad_key_bf = (
        apply_rotary(
            grad_keys_here.reshape(token_count, kv_local, HEAD_SIZE), token_positions, -1.0
        )
        .reshape(token_count, kv_local * HEAD_SIZE)
        .astype(bf16)
    )
    grad_value_bf = grad_values_here.astype(bf16)
    grad_q = contract_rows(normed_one, grad_query_bf)
    grad_k = contract_rows(normed_one, grad_key_bf)
    grad_v = contract_rows(normed_one, grad_value_bf)
    partial_one = (
        contract_cols(grad_query_bf, q_weight)
        + contract_cols(grad_key_bf, key_matrix)
        + contract_cols(grad_value_bf, value_matrix)
    )
    grad_normed_one = sum_axis(partial_one.astype(bf16), "tensor", 7)
    grad_one_rows, grad_attn_gain = norm_backward(inputs_f32, scale_one, attn_gain, grad_normed_one)
    input_grad = grad_resid + grad_one_rows
    q_cols, o_cols, k_cols = grad_q.shape[1], grad_o.shape[1], grad_k.shape[1]
    small = jnp.concatenate(
        [
            grad_router,
            grad_attn_gain[:, None],
            grad_moe_gain[:, None],
            jnp.zeros((grad_router.shape[0], 128 - grad_router.shape[1] - 2), f32),
        ],
        axis=1,
    )
    dense_all = jnp.concatenate(
        [grad_q, grad_o, grad_k, grad_v, small], axis=1
    ).astype(bf16)
    width = dense_all.shape[0]
    dense_all = jnp.transpose(
        dense_all.reshape(dpx_count, 2, width // (2 * dpx_count), dense_all.shape[1]), (1, 0, 2, 3)
    )
    dense_half = core_reduce(dense_all, 11)
    dense_half, grad_gate_out, grad_up_out, grad_down_out = lax.optimization_barrier(
        (dense_half, grad_gate_out, grad_up_out, grad_down_out)
    )
    dense_here = lax.psum_scatter(
        dense_half.reshape(-1, dense_half.shape[-1]), ("dpx", "ctx"), scatter_dimension=0, tiled=True
    ).astype(f32)
    spans = [q_cols, o_cols, k_cols, k_cols, router_weight.shape[1], 1, 1]
    cuts = [sum(spans[:i]) for i in range(len(spans) + 1)]
    pieces_out = [dense_here[:, cuts[i] : cuts[i + 1]] for i in range(len(spans))]
    dense_out = (
        pieces_out[5][:, 0],
        pieces_out[0],
        pieces_out[2],
        pieces_out[3],
        pieces_out[1],
        pieces_out[6][:, 0],
        pieces_out[4],
    )
    return (
        output,
        input_grad,
        dense_out[0],
        dense_out[1],
        dense_out[2],
        dense_out[3],
        dense_out[4],
        dense_out[5],
        dense_out[6],
        grad_gate_out,
        grad_up_out,
        grad_down_out,
    )


def solution(mesh):
    dp_count, ctx_count, tensor_count = (mesh.shape[a] for a in ("dp", "ctx", "tensor"))
    split_mesh = jax.sharding.Mesh(
        mesh.devices.reshape(dp_count // 2, 2, ctx_count, tensor_count), ("dpx", "core", "ctx", "tensor")
    )
    return jax.shard_map(
        functools.partial(per_device, dp_count // 2),
        mesh=split_mesh,
        in_specs=(
            P(("dpx", "core", "ctx"), None),
            P(),
            P(None, "tensor"),
            P(None, "tensor"),
            P(None, "tensor"),
            P(None, "tensor"),
            P(),
            P(),
            P(None, None, "tensor"),
            P(None, None, "tensor"),
            P(None, None, "tensor"),
            P(("dpx", "core")),
            P(("dpx", "core", "ctx"), None),
            P(("dpx", "core", "ctx"), None),
        ),
        out_specs=(
            P(("dpx", "core", "ctx"), None),
            P(("dpx", "core", "ctx"), None),
            P(("dpx", "core", "ctx")),
            P(("dpx", "core", "ctx"), "tensor"),
            P(("dpx", "core", "ctx"), "tensor"),
            P(("dpx", "core", "ctx"), "tensor"),
            P(("dpx", "core", "ctx"), "tensor"),
            P(("dpx", "core", "ctx")),
            P(("dpx", "core", "ctx"), None),
            P(None, ("dpx", "core", "ctx"), "tensor"),
            P(None, ("dpx", "core", "ctx"), "tensor"),
            P(None, ("dpx", "core", "ctx"), "tensor"),
        ),
        check_vma=False,
    )
```

```python
import functools
import math

import jax
import jax.numpy as jnp
from jax import lax
from jax.experimental import pallas as pl
from jax.experimental.pallas import tpu as pltpu
from jax.sharding import PartitionSpec as P

HEAD_SIZE = 64
NEXP = 24
CAP = 341


EPSILON = 1e-06
ROPE_BASE = 10000.0
NEGATIVE = -1e30
HIGHEST = lax.Precision.HIGHEST


def normalize(rows, gain):
    scale_inv = lax.rsqrt(jnp.mean(rows * rows, axis=-1, keepdims=True) + EPSILON)
    return (rows * scale_inv * gain, scale_inv)


def norm_backward(rows, scale_inv, gain, grad_normed):
    weighted = gain * grad_normed
    grad_gain = jnp.sum(grad_normed * rows * scale_inv, axis=0)
    inner_mean = jnp.mean(weighted * rows, axis=-1, keepdims=True)
    grad_rows = scale_inv * weighted - rows * scale_inv * scale_inv * scale_inv * inner_mean
    return (grad_rows, grad_gain)


def apply_rotary(value_rows, token_positions, direction):
    half_dim = value_rows.shape[-1] // 2
    frequency = ROPE_BASE ** (-jnp.arange(half_dim, dtype=jnp.float32) / half_dim)
    angles = token_positions.astype(jnp.float32)[:, None] * frequency[None, :]
    cosine = jnp.cos(angles)[:, None, :]
    sine_part = direction * jnp.sin(angles)[:, None, :]
    first_half = value_rows[..., :half_dim]
    second = value_rows[..., half_dim:]
    return jnp.concatenate(
        [first_half * cosine - second * sine_part, second * cosine + first_half * sine_part],
        axis=-1,
    )


def contract_rows(left, right):
    return lax.dot_general(
        left, right, (((0,), (0,)), ((), ())), preferred_element_type=jnp.float32
    )


def contract_rows_exact(left, right):
    return lax.dot_general(
        left, right, (((0,), (0,)), ((), ())), precision=HIGHEST, preferred_element_type=jnp.float32
    )


def contract_cols(left, right):
    return lax.dot_general(
        left, right, (((1,), (1,)), ((), ())), preferred_element_type=jnp.float32
    )


def _store_split(out_ref, value):
    cores, _, groups, rows, _ = out_ref.shape
    for x in range(groups):
        for c in range(cores):
            start = (x * cores + c) * rows
            out_ref[c, 0, x] = value[start : start + rows].astype(out_ref.dtype)


def _gate_column(gates_ref):
    gates = gates_ref[...]
    lane = lax.broadcasted_iota(jnp.int32, gates.shape, 1)
    return jnp.sum(jnp.where(lane == pl.program_id(0), gates, 0.0), axis=1, keepdims=True)


def _grad_body(
    n2_ref, n2t_ref, dy_ref, dyt_ref, gcol_ref, wg_ref, wu_ref, wd_ref,
    gg_ref, gu_ref, gd_ref, hid_ref, dga_ref, dua_ref,
):
    f32 = jnp.float32
    bf16 = jnp.bfloat16
    n2 = n2_ref[...]
    wd = wd_ref[0]
    gate_act = jnp.dot(n2, wg_ref[0], preferred_element_type=f32)
    up_act = jnp.dot(n2, wu_ref[0], preferred_element_type=f32)
    sig = 1.0 / (1.0 + jnp.exp(-gate_act))
    silu = gate_act * sig
    hidden = (silu * up_act).astype(bf16)
    hid_ref[0] = hidden
    gate = _gate_column(gcol_ref)
    grad_hidden = gate * jnp.dot(dy_ref[...], wd, preferred_element_type=f32)
    gated_hidden = (gate * hidden.astype(f32)).astype(bf16)
    _store_split(gd_ref, jnp.dot(dyt_ref[...], gated_hidden, preferred_element_type=f32))
    grad_gate_act = (grad_hidden * up_act * sig * (1.0 + gate_act * (1.0 - sig))).astype(bf16)
    grad_up_act = (grad_hidden * silu).astype(bf16)
    dga_ref[0] = grad_gate_act
    dua_ref[0] = grad_up_act
    n2t = n2t_ref[...]
    _store_split(gg_ref, jnp.dot(n2t, grad_gate_act, preferred_element_type=f32))
    _store_split(gu_ref, jnp.dot(n2t, grad_up_act, preferred_element_type=f32))


def _rows_body(hid_ref, dga_ref, dua_ref, dy_ref, gcol_ref, wg_ref, wu_ref, wd_ref, acc_ref, dgate_ref, dn2_ref):
    f32 = jnp.float32
    nt = (((1,), (1,)), ((), ()))

    @pl.when(pl.program_id(0) == 0)
    def _():
        acc_ref[...] = jnp.zeros_like(acc_ref)
        dn2_ref[...] = jnp.zeros_like(dn2_ref)

    expert_out = lax.dot_general(hid_ref[0], wd_ref[0], nt, preferred_element_type=f32)
    acc_ref[...] += _gate_column(gcol_ref) * expert_out
    dgate_ref[0] = jnp.sum(expert_out * dy_ref[...].astype(f32), axis=1, keepdims=True)
    dn2_ref[...] += lax.dot_general(
        dga_ref[0], wg_ref[0], nt, preferred_element_type=f32
    ) + lax.dot_general(dua_ref[0], wu_ref[0], nt, preferred_element_type=f32)


def expert_grad_kernel(n2, n2t, dy, dyt, gcol, wg, wu, wd, groups):
    tokens, width = n2.shape
    experts, _, hidden = wg.shape
    bf16 = jnp.bfloat16
    whole = lambda shape: pl.BlockSpec(shape, lambda e: (0,) * len(shape))
    per_expert = lambda shape: pl.BlockSpec((1,) + shape, lambda e: (e,) + (0,) * len(shape))
    split_rows = width // (groups * 2)
    split = pl.BlockSpec((2, 1, groups, split_rows, hidden), lambda e: (0, e, 0, 0, 0))
    split_shape = jax.ShapeDtypeStruct((2, experts, groups, split_rows, hidden), bf16)
    act_shape = jax.ShapeDtypeStruct((experts, tokens, hidden), bf16)
    return pl.pallas_call(
        _grad_body,
        grid=(experts,),
        in_specs=[
            whole((tokens, width)),
            whole((width, tokens)),
            whole((tokens, width)),
            whole((width, tokens)),
            whole((tokens, experts)),
            per_expert((width, hidden)),
            per_expert((width, hidden)),
            per_expert((width, hidden)),
        ],
        out_specs=[split, split, split]
        + [per_expert((tokens, hidden))] * 3,
        out_shape=[split_shape] * 3 + [act_shape] * 3,
        compiler_params=pltpu.CompilerParams(
            dimension_semantics=("arbitrary",), vmem_limit_bytes=64 * 1024 * 1024
        ),
        cost_estimate=pl.CostEstimate(
            flops=experts * tokens * width * hidden * 2 * 6,
            transcendentals=experts * tokens * hidden,
            bytes_accessed=experts * width * hidden * 12 + tokens * width * 8 + experts * tokens * hidden * 6,
        ),
    )(n2, n2t, dy, dyt, gcol, wg, wu, wd)


def expert_rows_kernel(hid, dga, dua, dy, gcol, wg, wu, wd):
    experts, tokens, hidden = hid.shape
    width = dy.shape[1]
    f32 = jnp.float32
    whole = lambda shape: pl.BlockSpec(shape, lambda e: (0,) * len(shape))
    per_expert = lambda shape: pl.BlockSpec((1,) + shape, lambda e: (e,) + (0,) * len(shape))
    return pl.pallas_call(
        _rows_body,
        grid=(experts,),
        in_specs=[
            per_expert((tokens, hidden)),
            per_expert((tokens, hidden)),
            per_expert((tokens, hidden)),
            whole((tokens, width)),
            whole((tokens, experts)),
            per_expert((width, hidden)),
            per_expert((width, hidden)),
            per_expert((width, hidden)),
        ],
        out_specs=[whole((tokens, width)), per_expert((tokens, 1)), whole((tokens, width))],
        out_shape=[
            jax.ShapeDtypeStruct((tokens, width), f32),
            jax.ShapeDtypeStruct((experts, tokens, 1), f32),
            jax.ShapeDtypeStruct((tokens, width), f32),
        ],
        compiler_params=pltpu.CompilerParams(
            dimension_semantics=("arbitrary",), vmem_limit_bytes=64 * 1024 * 1024
        ),
        cost_estimate=pl.CostEstimate(
            flops=experts * tokens * width * hidden * 2 * 3,
            transcendentals=0,
            bytes_accessed=experts * width * hidden * 6 + tokens * width * 10 + experts * tokens * hidden * 6,
        ),
    )(hid, dga, dua, dy, gcol, wg, wu, wd)

MESH = pl.DeviceIdType.MESH


def _exchange_body(axis, n, per_peer, downward, src_ref, out_ref, send_sems, recv_sems):
    me = lax.axis_index(axis)
    barrier = pltpu.get_barrier_semaphore()
    for k in range(1, n):
        peer = lax.rem(me + k, n)
        pl.semaphore_signal(barrier, 1, device_id={axis: peer}, device_id_type=MESH)
    pl.semaphore_wait(barrier, n - 1)
    sends = []
    for k in range(1, n):
        peer = lax.rem(me + k, n)
        copy = pltpu.make_async_remote_copy(
            src_ref=src_ref.at[peer] if per_peer else src_ref,
            dst_ref=out_ref.at[me],
            send_sem=send_sems.at[k - 1],
            recv_sem=recv_sems.at[k - 1],
            device_id={axis: peer},
            device_id_type=MESH,
        )
        sends.append((peer, copy))
        if downward:
            pl.when(peer < me)(copy.start)
        else:
            copy.start()
    for k in range(1, n):
        source = lax.rem(me + n - k, n)
        incoming = pltpu.make_async_remote_copy(
            src_ref=src_ref.at[source] if per_peer else src_ref,
            dst_ref=out_ref.at[source],
            send_sem=send_sems.at[k - 1],
            recv_sem=recv_sems.at[k - 1],
            device_id={axis: source},
            device_id_type=MESH,
        )
        if downward:
            pl.when(source > me)(incoming.wait_recv)
        else:
            incoming.wait_recv()
    for peer, copy in sends:
        if downward:
            pl.when(peer < me)(copy.wait_send)
        else:
            copy.wait_send()


def exchange(x, axis, n, per_peer, collective_id, downward=False):
    block = x.shape[1:] if per_peer else x.shape
    nbytes = math.prod(block) * x.dtype.itemsize
    return pl.pallas_call(
        functools.partial(_exchange_body, axis, n, per_peer, downward),
        out_shape=jax.ShapeDtypeStruct((n,) + tuple(block), x.dtype),
        in_specs=[pl.BlockSpec(memory_space=pl.ANY)],
        out_specs=pl.BlockSpec(memory_space=pl.ANY),
        scratch_shapes=[pltpu.SemaphoreType.DMA((n - 1,)), pltpu.SemaphoreType.DMA((n - 1,))],
        compiler_params=pltpu.CompilerParams(collective_id=collective_id, has_side_effects=True),
        cost_estimate=pl.CostEstimate(flops=0, transcendentals=0, bytes_accessed=2 * (n - 1) * nbytes),
    )(x)


def gather_axis(x, axis, n, collective_id):
    got = exchange(x, axis, n, False, collective_id)
    return lax.dynamic_update_slice_in_dim(got, x[None], lax.axis_index(axis), 0)


def sum_axis(x, axis, collective_id):
    got = exchange(x, axis, 2, False, collective_id)
    me = lax.axis_index(axis)
    other = lax.dynamic_index_in_dim(got, 1 - me, 0, keepdims=False)
    return x.astype(jnp.float32) + other.astype(jnp.float32)


def _pair_add_body(me_ref, own_ref, other_ref, out_ref):
    out_ref[...] = (own_ref[...].astype(jnp.float32) + other_ref[...].astype(jnp.float32)).astype(out_ref.dtype)


def core_reduce(x, collective_id):
    got = exchange(x, "core", 2, True, collective_id)
    me = lax.axis_index("core")
    count = x.shape[1]
    rest = x.shape[2:]
    zeros = (0,) * len(rest)
    item_bytes = math.prod(rest) * x.dtype.itemsize
    step = max(d for d in range(1, count + 1) if count % d == 0 and d * item_bytes <= 4 * 1024 * 1024)
    grid_spec = pltpu.PrefetchScalarGridSpec(
        num_scalar_prefetch=1,
        grid=(count // step,),
        in_specs=[
            pl.BlockSpec((None, step) + rest, lambda i, c: (c[0], i) + zeros),
            pl.BlockSpec((None, step) + rest, lambda i, c: (1 - c[0], i) + zeros),
        ],
        out_specs=pl.BlockSpec((step,) + rest, lambda i, c: (i,) + zeros),
    )
    return pl.pallas_call(
        _pair_add_body,
        grid_spec=grid_spec,
        out_shape=jax.ShapeDtypeStruct(x.shape[1:], jnp.bfloat16),
        compiler_params=pltpu.CompilerParams(vmem_limit_bytes=56 * 1024 * 1024),
        cost_estimate=pl.CostEstimate(flops=x.size // 2, transcendentals=0, bytes_accessed=x.size * 3),
    )(jnp.reshape(me, (1,)).astype(jnp.int32), x, got)


def scatter_sum_downward(x, axis, n, collective_id):
    got = exchange(x, axis, n, True, collective_id, downward=True)
    me = lax.axis_index(axis)
    own = lax.dynamic_index_in_dim(x, me, 0, keepdims=False).astype(jnp.float32)
    above = (jnp.arange(n, dtype=jnp.int32) > me).reshape((n,) + (1,) * (x.ndim - 1))
    return own + jnp.sum(jnp.where(above, got.astype(jnp.float32), 0.0), axis=0)


def _flash_body(groups, ctx_ref, q_ref, k_ref, v_ref, qseg_ref, qpos_ref, kseg_ref, o_ref, lse_ref, qs_sc, m_sc, l_sc, acc_sc):
    f32 = jnp.float32
    block = pl.program_id(1)
    depth = HEAD_SIZE
    pair = k_ref.shape[2] // depth
    tokens = q_ref.shape[0]

    @pl.when(block == 0)
    def _():
        m_sc[...] = jnp.full_like(m_sc, NEGATIVE)
        l_sc[...] = jnp.zeros_like(l_sc)
        acc_sc[...] = jnp.zeros_like(acc_sc)
        scale = jnp.asarray(1.0 / math.sqrt(HEAD_SIZE), q_ref.dtype)
        for kk in range(pair):
            for gi in range(groups):
                i = kk * groups + gi
                qs_sc[kk, gi * tokens : (gi + 1) * tokens, :] = q_ref[:, i * depth : (i + 1) * depth] * scale

    @pl.when(block <= ctx_ref[0])
    def _():
        width = k_ref.shape[1]
        key_pos = block * width + lax.broadcasted_iota(jnp.int32, (1, width), 1)
        allowed = (qseg_ref[...] == kseg_ref[...]) & (key_pos <= qpos_ref[...])
        for kk in range(pair):
            keys = k_ref[0, :, kk * depth : (kk + 1) * depth]
            values = v_ref[0, :, kk * depth : (kk + 1) * depth]
            scores = lax.dot_general(
                qs_sc[kk], keys, (((1,), (1,)), ((), ())), preferred_element_type=f32
            )
            scores = jnp.where(allowed, scores, NEGATIVE)
            m_old = m_sc[kk]
            m_new = jnp.maximum(m_old, jnp.max(scores, axis=1, keepdims=True))
            alpha = jnp.exp(m_old - m_new)
            weights = jnp.where(allowed, jnp.exp(scores - m_new), 0.0)
            l_sc[kk] = alpha * l_sc[kk] + jnp.sum(weights, axis=1, keepdims=True)
            acc_sc[kk] = alpha * acc_sc[kk] + jnp.dot(
                weights.astype(jnp.bfloat16), values, preferred_element_type=f32
            )
            m_sc[kk] = m_new

    @pl.when(block == pl.num_programs(1) - 1)
    def _():
        for kk in range(pair):
            for gi in range(groups):
                i = kk * groups + gi
                rows = slice(gi * tokens, (gi + 1) * tokens)
                o_ref[:, i * depth : (i + 1) * depth] = acc_sc[kk, rows, :] / l_sc[kk, rows, :]
                lse_ref[0, :, i : i + 1] = m_sc[kk, rows, :] + jnp.log(l_sc[kk, rows, :])


def flash_forward(ctx_index, q, kv, qseg, qpos, kseg, groups):
    tokens, q_width = q.shape
    blocks, width, kv_width = kv.shape
    pair = 2
    pairs = kv_width // (2 * pair * HEAD_SIZE)
    heads_step = pair * groups
    f32 = jnp.float32
    capped = lambda p, b, c: (jnp.minimum(b, c[0]), 0, p)
    grid_spec = pltpu.PrefetchScalarGridSpec(
        num_scalar_prefetch=1,
        grid=(pairs, blocks),
        in_specs=[
            pl.BlockSpec((tokens, heads_step * HEAD_SIZE), lambda p, b, c: (0, p)),
            pl.BlockSpec((1, width, pair * HEAD_SIZE), capped),
            pl.BlockSpec((1, width, pair * HEAD_SIZE), lambda p, b, c: (jnp.minimum(b, c[0]), 0, pairs + p)),
            pl.BlockSpec((groups * tokens, 1), lambda p, b, c: (0, 0)),
            pl.BlockSpec((groups * tokens, 1), lambda p, b, c: (0, 0)),
            pl.BlockSpec((1, width), lambda p, b, c: (0, jnp.minimum(b, c[0]))),
        ],
        out_specs=[
            pl.BlockSpec((tokens, heads_step * HEAD_SIZE), lambda p, b, c: (0, p)),
            pl.BlockSpec((1, tokens, heads_step), lambda p, b, c: (p, 0, 0)),
        ],
        scratch_shapes=[
            pltpu.VMEM((pair, groups * tokens, HEAD_SIZE), q.dtype),
            pltpu.VMEM((pair, groups * tokens, 1), f32),
            pltpu.VMEM((pair, groups * tokens, 1), f32),
            pltpu.VMEM((pair, groups * tokens, HEAD_SIZE), f32),
        ],
    )
    return pl.pallas_call(
        functools.partial(_flash_body, groups),
        grid_spec=grid_spec,
        out_shape=[
            jax.ShapeDtypeStruct((tokens, q_width), f32),
            jax.ShapeDtypeStruct((pairs, tokens, heads_step), f32),
        ],
        compiler_params=pltpu.CompilerParams(
            dimension_semantics=("arbitrary", "arbitrary"), vmem_limit_bytes=48 * 1024 * 1024
        ),
        cost_estimate=pl.CostEstimate(
            flops=tokens * q_width * blocks * width * 4,
            transcendentals=tokens * (q_width // HEAD_SIZE) * blocks * width,
            bytes_accessed=(q.size + kv.size) * 2 + tokens * q_width * 4,
        ),
    )(jnp.reshape(ctx_index, (1,)).astype(jnp.int32), q, kv, kv, qseg, qpos, kseg)

def _chain_down_body(axis, n, x_ref, out_ref, recv, send, send_sems, recv_sems):
    f32 = jnp.float32
    me = lax.axis_index(axis)
    below = lax.rem(me + n - 1, n)
    above = lax.rem(me + 1, n)
    barrier = pltpu.get_barrier_semaphore()
    pl.semaphore_signal(barrier, 1, device_id={axis: below}, device_id_type=MESH)
    pl.semaphore_signal(barrier, 1, device_id={axis: above}, device_id_type=MESH)
    pl.semaphore_wait(barrier, 2)
    copies = []
    for j in range(n - 1):
        copy = pltpu.make_async_remote_copy(
            src_ref=send.at[j],
            dst_ref=recv.at[j],
            send_sem=send_sems.at[j],
            recv_sem=recv_sems.at[j],
            device_id={axis: below},
            device_id_type=MESH,
        )
        copies.append(copy)

        @pl.when((j < me) & (me < n - 1))
        def _():
            copy.wait_recv()
            send[j] = (x_ref[j].astype(f32) + recv[j].astype(f32)).astype(send.dtype)

        @pl.when((j < me) & (me == n - 1))
        def _():
            send[j] = x_ref[j]

        @pl.when(j < me)
        def _():
            copy.start()

        @pl.when(j == me)
        def _():
            copy.wait_recv()
            out_ref[...] = x_ref[j].astype(f32) + recv[j].astype(f32)

    @pl.when(me == n - 1)
    def _():
        out_ref[...] = x_ref[n - 1].astype(f32)

    for j in range(n - 1):
        pl.when(j < me)(copies[j].wait_send)


def chain_sum_down(x, axis, n, collective_id):
    _, rows, cols = x.shape
    return pl.pallas_call(
        functools.partial(_chain_down_body, axis, n),
        out_shape=jax.ShapeDtypeStruct((rows, cols), jnp.float32),
        in_specs=[pl.BlockSpec(memory_space=pltpu.VMEM)],
        out_specs=pl.BlockSpec(memory_space=pltpu.VMEM),
        scratch_shapes=[
            pltpu.VMEM((n - 1, rows, cols), x.dtype),
            pltpu.VMEM((n - 1, rows, cols), x.dtype),
            pltpu.SemaphoreType.DMA((n - 1,)),
            pltpu.SemaphoreType.DMA((n - 1,)),
        ],
        compiler_params=pltpu.CompilerParams(
            collective_id=collective_id, has_side_effects=True, vmem_limit_bytes=32 * 1024 * 1024
        ),
        cost_estimate=pl.CostEstimate(
            flops=(n - 1) * rows * cols, transcendentals=0, bytes_accessed=3 * n * rows * cols * 2
        ),
    )(x)


def _chain_up_body(axis, n, x_ref, out_ref, send_sems, recv_sems):
    me = lax.axis_index(axis)
    below = lax.rem(me + n - 1, n)
    above = lax.rem(me + 1, n)
    barrier = pltpu.get_barrier_semaphore()
    pl.semaphore_signal(barrier, 1, device_id={axis: below}, device_id_type=MESH)
    pl.semaphore_signal(barrier, 1, device_id={axis: above}, device_id_type=MESH)
    pl.semaphore_wait(barrier, 2)
    own = pltpu.make_async_remote_copy(
        src_ref=x_ref,
        dst_ref=out_ref.at[me],
        send_sem=send_sems.at[me],
        recv_sem=recv_sems.at[me],
        device_id={axis: above},
        device_id_type=MESH,
    )
    pl.when(me < n - 1)(own.start)
    forwards = []
    for k in range(1, n):
        block = jnp.maximum(me - k, 0)
        incoming = pltpu.make_async_remote_copy(
            src_ref=out_ref.at[block],
            dst_ref=out_ref.at[block],
            send_sem=send_sems.at[block],
            recv_sem=recv_sems.at[block],
            device_id={axis: below},
            device_id_type=MESH,
        )
        forward = pltpu.make_async_remote_copy(
            src_ref=out_ref.at[block],
            dst_ref=out_ref.at[block],
            send_sem=send_sems.at[block],
            recv_sem=recv_sems.at[block],
            device_id={axis: above},
            device_id_type=MESH,
        )
        forwards.append((k, forward))
        pl.when(k <= me)(incoming.wait_recv)
        pl.when((k <= me) & (me < n - 1))(forward.start)
    pl.when(me < n - 1)(own.wait_send)
    for k, forward in forwards:
        pl.when((k <= me) & (me < n - 1))(forward.wait_send)


def gather_up(x, axis, n, collective_id):
    got = pl.pallas_call(
        functools.partial(_chain_up_body, axis, n),
        out_shape=jax.ShapeDtypeStruct((n,) + x.shape, x.dtype),
        in_specs=[pl.BlockSpec(memory_space=pl.ANY)],
        out_specs=pl.BlockSpec(memory_space=pl.ANY),
        scratch_shapes=[pltpu.SemaphoreType.DMA((n,)), pltpu.SemaphoreType.DMA((n,))],
        compiler_params=pltpu.CompilerParams(collective_id=collective_id, has_side_effects=True),
        cost_estimate=pl.CostEstimate(
            flops=0, transcendentals=0, bytes_accessed=2 * (n - 1) * x.size * x.dtype.itemsize
        ),
    )(x)
    me = lax.axis_index(axis)
    below = (jnp.arange(n, dtype=jnp.int32) < me).reshape((n,) + (1,) * x.ndim)
    got = jnp.where(below, got, jnp.zeros_like(got))
    return lax.dynamic_update_slice_in_dim(got, x[None], me, 0)


def _attend_block(groups, kv_heads, q_sc, kv_buf, qseg_ref, qpos_ref, kseg_ref, m_sc, l_sc, acc_sc, block):
    f32 = jnp.float32
    depth = HEAD_SIZE
    width = kv_buf.shape[0]
    start = pl.multiple_of(block * width, width)
    key_pos = start + lax.broadcasted_iota(jnp.int32, (1, width), 1)
    allowed = (qseg_ref[...] == kseg_ref[:, pl.ds(start, width)]) & (key_pos <= qpos_ref[...])
    for kk in range(kv_heads):
        keys = kv_buf[:, kk * depth : (kk + 1) * depth]
        values = kv_buf[:, (kv_heads + kk) * depth : (kv_heads + kk + 1) * depth]
        scores = lax.dot_general(q_sc[kk], keys, (((1,), (1,)), ((), ())), preferred_element_type=f32)
        scores = jnp.where(allowed, scores, NEGATIVE)
        m_old = m_sc[kk]
        m_new = jnp.maximum(m_old, jnp.max(scores, axis=1, keepdims=True))
        alpha = jnp.exp(m_old - m_new)
        weights = jnp.where(allowed, jnp.exp(scores - m_new), 0.0)
        l_sc[kk] = alpha * l_sc[kk] + jnp.sum(weights, axis=1, keepdims=True)
        acc_sc[kk] = alpha * acc_sc[kk] + jnp.dot(
            weights.astype(jnp.bfloat16), values, preferred_element_type=f32
        )
        m_sc[kk] = m_new


def _gather_attend_body(
    axis, n, groups, q_ref, own_ref, qseg_ref, qpos_ref, kseg_ref,
    kv_ref, o_ref, lse_ref,
    q_sc, m_sc, l_sc, acc_sc, kv_buf, send_sems, recv_sems, copy_sem,
):
    depth = HEAD_SIZE
    tokens = q_ref.shape[0]
    kv_heads = own_ref.shape[1] // (2 * depth)
    me = lax.axis_index(axis)
    below = lax.rem(me + n - 1, n)
    above = lax.rem(me + 1, n)
    barrier = pltpu.get_barrier_semaphore()
    pl.semaphore_signal(barrier, 1, device_id={axis: below}, device_id_type=MESH)
    pl.semaphore_signal(barrier, 1, device_id={axis: above}, device_id_type=MESH)
    pl.semaphore_wait(barrier, 2)
    own = pltpu.make_async_remote_copy(
        src_ref=own_ref,
        dst_ref=kv_ref.at[me],
        send_sem=send_sems.at[me],
        recv_sem=recv_sems.at[me],
        device_id={axis: above},
        device_id_type=MESH,
    )
    pl.when(me < n - 1)(own.start)

    m_sc[...] = jnp.full_like(m_sc, NEGATIVE)
    l_sc[...] = jnp.zeros_like(l_sc)
    acc_sc[...] = jnp.zeros_like(acc_sc)
    scale = jnp.asarray(1.0 / math.sqrt(HEAD_SIZE), q_ref.dtype)
    for kk in range(kv_heads):
        for gi in range(groups):
            i = kk * groups + gi
            q_sc[kk, gi * tokens : (gi + 1) * tokens, :] = q_ref[:, i * depth : (i + 1) * depth] * scale

    local = pltpu.make_async_copy(own_ref, kv_buf, copy_sem)
    local.start()
    local.wait()
    _attend_block(groups, kv_heads, q_sc, kv_buf, qseg_ref, qpos_ref, kseg_ref, m_sc, l_sc, acc_sc, me)

    def step(k, carry):
        block = me - k
        incoming = pltpu.make_async_remote_copy(
            src_ref=kv_ref.at[block],
            dst_ref=kv_ref.at[block],
            send_sem=send_sems.at[block],
            recv_sem=recv_sems.at[block],
            device_id={axis: below},
            device_id_type=MESH,
        )
        incoming.wait_recv()
        forward = pltpu.make_async_remote_copy(
            src_ref=kv_ref.at[block],
            dst_ref=kv_ref.at[block],
            send_sem=send_sems.at[block],
            recv_sem=recv_sems.at[block],
            device_id={axis: above},
            device_id_type=MESH,
        )
        pl.when(me < n - 1)(forward.start)
        fetch = pltpu.make_async_copy(kv_ref.at[block], kv_buf, copy_sem)
        fetch.start()
        fetch.wait()
        _attend_block(groups, kv_heads, q_sc, kv_buf, qseg_ref, qpos_ref, kseg_ref, m_sc, l_sc, acc_sc, block)
        return carry

    lax.fori_loop(1, me + 1, step, 0)

    for kk in range(kv_heads):
        for gi in range(groups):
            i = kk * groups + gi
            rows = slice(gi * tokens, (gi + 1) * tokens)
            o_ref[:, i * depth : (i + 1) * depth] = acc_sc[kk, rows, :] / l_sc[kk, rows, :]
            lse_ref[:, i : i + 1] = m_sc[kk, rows, :] + jnp.log(l_sc[kk, rows, :])

    pl.when(me < n - 1)(own.wait_send)

    def drain(k, carry):
        block = me - k
        pltpu.make_async_remote_copy(
            src_ref=kv_ref.at[block],
            dst_ref=kv_ref.at[block],
            send_sem=send_sems.at[block],
            recv_sem=recv_sems.at[block],
            device_id={axis: above},
            device_id_type=MESH,
        ).wait_send()
        return carry

    lax.fori_loop(1, jnp.where(me < n - 1, me + 1, 1), drain, 0)


def gather_attend(q, own, qseg, qpos, kseg, axis, n, groups, collective_id):
    tokens, q_width = q.shape
    rows, kv_width = own.shape
    heads = q_width // HEAD_SIZE
    kv_heads = kv_width // (2 * HEAD_SIZE)
    f32 = jnp.float32
    vmem = pl.BlockSpec(memory_space=pltpu.VMEM)
    anywhere = pl.BlockSpec(memory_space=pl.ANY)
    kv_all, attn, lse = pl.pallas_call(
        functools.partial(_gather_attend_body, axis, n, groups),
        out_shape=[
            jax.ShapeDtypeStruct((n, rows, kv_width), own.dtype),
            jax.ShapeDtypeStruct((tokens, q_width), f32),
            jax.ShapeDtypeStruct((tokens, heads), f32),
        ],
        in_specs=[vmem, anywhere, vmem, vmem, vmem],
        out_specs=[anywhere, vmem, vmem],
        scratch_shapes=[
            pltpu.VMEM((kv_heads, groups * tokens, HEAD_SIZE), q.dtype),
            pltpu.VMEM((kv_heads, groups * tokens, 1), f32),
            pltpu.VMEM((kv_heads, groups * tokens, 1), f32),
            pltpu.VMEM((kv_heads, groups * tokens, HEAD_SIZE), f32),
            pltpu.VMEM((rows, kv_width), own.dtype),
            pltpu.SemaphoreType.DMA((n,)),
            pltpu.SemaphoreType.DMA((n,)),
            pltpu.SemaphoreType.DMA(()),
        ],
        compiler_params=pltpu.CompilerParams(
            collective_id=collective_id, has_side_effects=True, vmem_limit_bytes=48 * 1024 * 1024
        ),
        cost_estimate=pl.CostEstimate(
            flops=tokens * q_width * n * rows * 4,
            transcendentals=tokens * heads * n * rows,
            bytes_accessed=2 * n * own.size * own.dtype.itemsize + tokens * q_width * 6,
        ),
    )(q, own, qseg, qpos, kseg)
    me = lax.axis_index(axis)
    below = (jnp.arange(n, dtype=jnp.int32) < me).reshape((n, 1, 1))
    kv_all = jnp.where(below, kv_all, jnp.zeros_like(kv_all))
    return attn, lse, lax.dynamic_update_slice_in_dim(kv_all, own[None], me, 0)


def per_device(
    dpx_count,
    hidden_in,
    attn_gain,
    q_weight,
    key_matrix,
    value_matrix,
    o_weight,
    moe_gain,
    router_weight,
    gate_weight,
    up_weight,
    down_weight,
    segments,
    expert_picks,
    output_grad,
):
    bf16 = jnp.bfloat16
    f32 = jnp.float32
    token_count = hidden_in.shape[0]
    ctx_index = lax.axis_index("ctx")
    heads_local = q_weight.shape[1] // HEAD_SIZE
    kv_local = key_matrix.shape[1] // HEAD_SIZE
    group_size = heads_local // kv_local
    score_scale = 1.0 / math.sqrt(HEAD_SIZE)
    token_positions = ctx_index * token_count + jnp.arange(token_count, dtype=jnp.int32)
    segment_here = lax.dynamic_slice_in_dim(segments, ctx_index * token_count, token_count)
    inputs_f32 = hidden_in.astype(f32)
    o_full = lax.all_gather(o_weight, "tensor", axis=1, tiled=True)
    normed_f32, scale_one = normalize(inputs_f32, attn_gain)
    normed_one = normed_f32.astype(bf16)
    query_rows = jnp.dot(normed_one, q_weight, preferred_element_type=f32).reshape(
        token_count, heads_local, HEAD_SIZE
    )
    keys_raw = jnp.dot(normed_one, key_matrix, preferred_element_type=f32).reshape(
        token_count, kv_local, HEAD_SIZE
    )
    values_raw = jnp.dot(normed_one, value_matrix, preferred_element_type=f32)
    query_grouped = (
        apply_rotary(query_rows, token_positions, 1.0)
        .astype(bf16)
        .reshape(token_count, kv_local, group_size, HEAD_SIZE)
    )
    key_flat = (
        apply_rotary(keys_raw, token_positions, 1.0)
        .astype(bf16)
        .reshape(token_count, kv_local * HEAD_SIZE)
    )
    value_flat = values_raw.astype(bf16)

    def piece_mask(piece_rows):
        key_pos = jnp.arange(piece_rows, dtype=jnp.int32)
        return (segment_here[:, None] == segments[None, :]) & (
            key_pos[None, :] <= token_positions[:, None]
        )

    ctx_count = segments.shape[0] // token_count
    attn_flat, lse_heads, kv_both = gather_attend(
        query_grouped.reshape(token_count, heads_local * HEAD_SIZE),
        jnp.concatenate([key_flat, value_flat], axis=1),
        jnp.tile(segment_here, group_size)[:, None],
        jnp.tile(token_positions, group_size)[:, None],
        segments[None, :],
        "ctx",
        ctx_count,
        group_size,
        1,
    )
    piece_rows = ctx_count * token_count
    kv_width = kv_local * HEAD_SIZE
    key_piece = kv_both[:, :, :kv_width].reshape(piece_rows, kv_local, HEAD_SIZE)
    value_piece = kv_both[:, :, kv_width:].reshape(piece_rows, kv_local, HEAD_SIZE)
    attn_grouped = jnp.transpose(
        attn_flat.reshape(token_count, kv_local, group_size, HEAD_SIZE), (1, 2, 0, 3)
    )
    log_sum = jnp.transpose(lse_heads.reshape(token_count, kv_local, group_size), (1, 2, 0))
    attn_bf = attn_flat.astype(bf16)
    tensor_count = o_weight.shape[0] // o_weight.shape[1]
    attn_all = gather_axis(attn_bf, "tensor", tensor_count, 2)
    attn_full = jnp.transpose(attn_all, (1, 0, 2)).reshape(token_count, tensor_count * attn_bf.shape[1])
    mixed_attn = contract_cols(attn_full, o_full)
    resid = inputs_f32 + mixed_attn
    normed_two_f32, scale_two = normalize(resid, moe_gain)
    normed_two = normed_two_f32.astype(bf16)
    logits = jnp.dot(normed_two, router_weight, preferred_element_type=f32)
    expert_range = jnp.arange(NEXP, dtype=jnp.int32)
    picked_onehot = expert_picks[:, :, None] == expert_range[None, None, :]
    picked = jnp.sum(jnp.where(picked_onehot, logits[:, None, :], 0.0), axis=2)
    gate_probs = jax.nn.softmax(picked, axis=-1)
    gates_dense = jnp.sum(jnp.where(picked_onehot, gate_probs[:, :, None], 0.0), axis=1)
    gates_by_expert = jnp.transpose(gates_dense)
    cot_bf = output_grad
    gcol = gates_dense
    grad_gate, grad_up, grad_down, hid_all, dga_all, dua_all = expert_grad_kernel(
        normed_two,
        jnp.transpose(normed_two),
        cot_bf,
        jnp.transpose(cot_bf),
        gcol,
        gate_weight,
        up_weight,
        down_weight,
        dpx_count,
    )
    gate_half = core_reduce(grad_gate, 8)
    gate_half, hid_all, dga_all, dua_all = lax.optimization_barrier(
        (gate_half, hid_all, dga_all, dua_all)
    )
    moe_acc, gate_parts, moe_grad_rows = expert_rows_kernel(
        hid_all, dga_all, dua_all, cot_bf, gcol, gate_weight, up_weight, down_weight
    )
    cot_f32 = output_grad.astype(f32)
    moe_total = sum_axis(moe_acc.astype(bf16), "tensor", 3)
    output = (resid + moe_total).astype(bf16)
    grad_rows_all = moe_grad_rows
    gate_parts = gate_parts[:, :, 0]
    grad_gate_out, grad_up_out, grad_down_out = [
        lax.psum_scatter(
            g.reshape(g.shape[0], -1, g.shape[3]), ("dpx", "ctx"), scatter_dimension=1, tiled=True
        )
        for g in (gate_half, core_reduce(grad_up, 9), core_reduce(grad_down, 10))
    ]
    gate_pair = jnp.sum(
        jnp.where(picked_onehot, jnp.transpose(gate_parts)[:, None, :], 0.0), axis=2
    )
    moe_summed = sum_axis(grad_rows_all.astype(bf16), "tensor", 4)
    gate_summed = sum_axis(gate_pair.astype(bf16), "tensor", 5)
    grad_picked = gate_probs * (
        gate_summed - jnp.sum(gate_probs * gate_summed, axis=1, keepdims=True)
    )
    grad_logits = jnp.sum(jnp.where(picked_onehot, grad_picked[:, :, None], 0.0), axis=1).astype(
        bf16
    )
    grad_router = contract_rows(normed_two, grad_logits)
    grad_normed_two = moe_summed + contract_cols(grad_logits, router_weight)
    grad_two_rows, grad_moe_gain = norm_backward(resid, scale_two, moe_gain, grad_normed_two)
    grad_resid = cot_f32 + grad_two_rows
    grad_mix = grad_resid.astype(bf16)
    grad_o = contract_rows(grad_mix, attn_bf)
    grad_attn = jnp.dot(grad_mix, o_weight, preferred_element_type=f32).astype(bf16)
    grad_attn_grouped = jnp.transpose(
        grad_attn.reshape(token_count, kv_local, group_size, HEAD_SIZE), (1, 2, 0, 3)
    )
    row_delta = jnp.sum(grad_attn_grouped.astype(f32) * attn_grouped, axis=-1)
    allowed = piece_mask(piece_rows)
    scores = (
        jnp.einsum("tkgd,nkd->kgtn", query_grouped, key_piece, preferred_element_type=f32)
        * score_scale
    )
    probability = jnp.where(allowed, jnp.exp(scores - log_sum[..., None]), 0.0)
    grad_probs = jnp.einsum(
        "kgtd,nkd->kgtn", grad_attn_grouped, value_piece, preferred_element_type=f32
    )
    grad_scores = (probability * (grad_probs - row_delta[..., None])).astype(bf16)
    grad_query = score_scale * jnp.einsum(
        "kgtn,nkd->kgtd", grad_scores, key_piece, preferred_element_type=f32
    )
    key_part = score_scale * jnp.einsum(
        "kgtn,tkgd->nkd", grad_scores, query_grouped, preferred_element_type=f32
    )
    value_part = jnp.einsum(
        "kgtn,kgtd->nkd", probability.astype(bf16), grad_attn_grouped, preferred_element_type=f32
    )
    grad_keys_all = key_part.reshape(piece_rows, kv_local * HEAD_SIZE)
    grad_values_all = value_part.reshape(piece_rows, kv_local * HEAD_SIZE)
    back_state = (grad_query, grad_keys_all, grad_values_all)
    grad_query, grad_keys_all, grad_values_all = back_state
    grad_kv_here = chain_sum_down(
        jnp.concatenate([grad_keys_all, grad_values_all], axis=1)
        .astype(bf16)
        .reshape(ctx_count, token_count, 2 * kv_width),
        "ctx",
        ctx_count,
        6,
    )
    grad_keys_here = grad_kv_here[:, :kv_width]
    grad_values_here = grad_kv_here[:, kv_width:]
    grad_query_rows = jnp.transpose(grad_query, (2, 0, 1, 3)).reshape(
        token_count, heads_local, HEAD_SIZE
    )
    grad_query_bf = (
        apply_rotary(grad_query_rows, token_positions, -1.0)
        .reshape(token_count, heads_local * HEAD_SIZE)
        .astype(bf16)
    )
    grad_key_bf = (
        apply_rotary(
            grad_keys_here.reshape(token_count, kv_local, HEAD_SIZE), token_positions, -1.0
        )
        .reshape(token_count, kv_local * HEAD_SIZE)
        .astype(bf16)
    )
    grad_value_bf = grad_values_here.astype(bf16)
    grad_q = contract_rows(normed_one, grad_query_bf)
    grad_k = contract_rows(normed_one, grad_key_bf)
    grad_v = contract_rows(normed_one, grad_value_bf)
    partial_one = (
        contract_cols(grad_query_bf, q_weight)
        + contract_cols(grad_key_bf, key_matrix)
        + contract_cols(grad_value_bf, value_matrix)
    )
    grad_normed_one = sum_axis(partial_one.astype(bf16), "tensor", 7)
    grad_one_rows, grad_attn_gain = norm_backward(inputs_f32, scale_one, attn_gain, grad_normed_one)
    input_grad = grad_resid + grad_one_rows
    q_cols, o_cols, k_cols = grad_q.shape[1], grad_o.shape[1], grad_k.shape[1]
    small = jnp.concatenate(
        [
            grad_router,
            grad_attn_gain[:, None],
            grad_moe_gain[:, None],
            jnp.zeros((grad_router.shape[0], 128 - grad_router.shape[1] - 2), f32),
        ],
        axis=1,
    )
    dense_all = jnp.concatenate(
        [grad_q, grad_o, grad_k, grad_v, small], axis=1
    ).astype(bf16)
    width = dense_all.shape[0]
    dense_all = jnp.transpose(
        dense_all.reshape(dpx_count, 2, width // (2 * dpx_count), dense_all.shape[1]), (1, 0, 2, 3)
    )
    dense_half = core_reduce(dense_all, 11)
    dense_half, grad_gate_out, grad_up_out, grad_down_out = lax.optimization_barrier(
        (dense_half, grad_gate_out, grad_up_out, grad_down_out)
    )
    grad_gate_out, grad_up_out, grad_down_out = (
        grad_gate_out.astype(f32),
        grad_up_out.astype(f32),
        grad_down_out.astype(f32),
    )
    dense_here = lax.psum_scatter(
        dense_half.reshape(-1, dense_half.shape[-1]), ("dpx", "ctx"), scatter_dimension=0, tiled=True
    ).astype(f32)
    spans = [q_cols, o_cols, k_cols, k_cols, router_weight.shape[1], 1, 1]
    cuts = [sum(spans[:i]) for i in range(len(spans) + 1)]
    pieces_out = [dense_here[:, cuts[i] : cuts[i + 1]] for i in range(len(spans))]
    dense_out = (
        pieces_out[5][:, 0],
        pieces_out[0],
        pieces_out[2],
        pieces_out[3],
        pieces_out[1],
        pieces_out[6][:, 0],
        pieces_out[4],
    )
    return (
        output,
        input_grad,
        dense_out[0],
        dense_out[1],
        dense_out[2],
        dense_out[3],
        dense_out[4],
        dense_out[5],
        dense_out[6],
        grad_gate_out,
        grad_up_out,
        grad_down_out,
    )


def solution(mesh):
    dp_count, ctx_count, tensor_count = (mesh.shape[a] for a in ("dp", "ctx", "tensor"))
    split_mesh = jax.sharding.Mesh(
        mesh.devices.reshape(dp_count // 2, 2, ctx_count, tensor_count), ("dpx", "core", "ctx", "tensor")
    )
    return jax.shard_map(
        functools.partial(per_device, dp_count // 2),
        mesh=split_mesh,
        in_specs=(
            P(("dpx", "core", "ctx"), None),
            P(),
            P(None, "tensor"),
            P(None, "tensor"),
            P(None, "tensor"),
            P(None, "tensor"),
            P(),
            P(),
            P(None, None, "tensor"),
            P(None, None, "tensor"),
            P(None, None, "tensor"),
            P(("dpx", "core")),
            P(("dpx", "core", "ctx"), None),
            P(("dpx", "core", "ctx"), None),
        ),
        out_specs=(
            P(("dpx", "core", "ctx"), None),
            P(("dpx", "core", "ctx"), None),
            P(("dpx", "core", "ctx")),
            P(("dpx", "core", "ctx"), "tensor"),
            P(("dpx", "core", "ctx"), "tensor"),
            P(("dpx", "core", "ctx"), "tensor"),
            P(("dpx", "core", "ctx"), "tensor"),
            P(("dpx", "core", "ctx")),
            P(("dpx", "core", "ctx"), None),
            P(None, ("dpx", "core", "ctx"), "tensor"),
            P(None, ("dpx", "core", "ctx"), "tensor"),
            P(None, ("dpx", "core", "ctx"), "tensor"),
        ),
        check_vma=False,
    )
```

```python
import functools
import math

import jax
import jax.numpy as jnp
from jax import lax
from jax.experimental import pallas as pl
from jax.experimental.pallas import tpu as pltpu
from jax.sharding import PartitionSpec as P

HEAD_SIZE = 64
NEXP = 24
CAP = 341


EPSILON = 1e-06
ROPE_BASE = 10000.0
NEGATIVE = -1e30
HIGHEST = lax.Precision.HIGHEST


def normalize(rows, gain):
    scale_inv = lax.rsqrt(jnp.mean(rows * rows, axis=-1, keepdims=True) + EPSILON)
    return (rows * scale_inv * gain, scale_inv)


def norm_backward(rows, scale_inv, gain, grad_normed):
    weighted = gain * grad_normed
    grad_gain = jnp.sum(grad_normed * rows * scale_inv, axis=0)
    inner_mean = jnp.mean(weighted * rows, axis=-1, keepdims=True)
    grad_rows = scale_inv * weighted - rows * scale_inv * scale_inv * scale_inv * inner_mean
    return (grad_rows, grad_gain)


def apply_rotary(value_rows, token_positions, direction):
    half_dim = value_rows.shape[-1] // 2
    frequency = ROPE_BASE ** (-jnp.arange(half_dim, dtype=jnp.float32) / half_dim)
    angles = token_positions.astype(jnp.float32)[:, None] * frequency[None, :]
    cosine = jnp.cos(angles)[:, None, :]
    sine_part = direction * jnp.sin(angles)[:, None, :]
    first_half = value_rows[..., :half_dim]
    second = value_rows[..., half_dim:]
    return jnp.concatenate(
        [first_half * cosine - second * sine_part, second * cosine + first_half * sine_part],
        axis=-1,
    )


def contract_rows(left, right):
    return lax.dot_general(
        left, right, (((0,), (0,)), ((), ())), preferred_element_type=jnp.float32
    )


def contract_rows_exact(left, right):
    return lax.dot_general(
        left, right, (((0,), (0,)), ((), ())), precision=HIGHEST, preferred_element_type=jnp.float32
    )


def contract_cols(left, right):
    return lax.dot_general(
        left, right, (((1,), (1,)), ((), ())), preferred_element_type=jnp.float32
    )


def _store_split(out_ref, value):
    cores, _, groups, rows, _ = out_ref.shape
    for x in range(groups):
        for c in range(cores):
            start = (x * cores + c) * rows
            out_ref[c, 0, x] = value[start : start + rows].astype(out_ref.dtype)


def _gate_column(gates_ref):
    gates = gates_ref[...]
    lane = lax.broadcasted_iota(jnp.int32, gates.shape, 1)
    return jnp.sum(jnp.where(lane == pl.program_id(0), gates, 0.0), axis=1, keepdims=True)


def _grad_body(
    n2_ref, dy_ref, gcol_ref, wg_ref, wu_ref, wd_ref,
    gg_ref, gu_ref, gd_ref, hid_ref, dga_ref, dua_ref,
):
    f32 = jnp.float32
    bf16 = jnp.bfloat16
    n2 = n2_ref[...]
    wd = wd_ref[0]
    gate_act = jnp.dot(n2, wg_ref[0], preferred_element_type=f32)
    up_act = jnp.dot(n2, wu_ref[0], preferred_element_type=f32)
    sig = 1.0 / (1.0 + jnp.exp(-gate_act))
    silu = gate_act * sig
    hidden = (silu * up_act).astype(bf16)
    hid_ref[0] = hidden
    gate = _gate_column(gcol_ref)
    grad_hidden = gate * jnp.dot(dy_ref[...], wd, preferred_element_type=f32)
    gated_hidden = (gate * hidden.astype(f32)).astype(bf16)
    tn = (((0,), (0,)), ((), ()))
    _store_split(gd_ref, lax.dot_general(dy_ref[...], gated_hidden, tn, preferred_element_type=f32))
    grad_gate_act = (grad_hidden * up_act * sig * (1.0 + gate_act * (1.0 - sig))).astype(bf16)
    grad_up_act = (grad_hidden * silu).astype(bf16)
    dga_ref[0] = grad_gate_act
    dua_ref[0] = grad_up_act
    _store_split(gg_ref, lax.dot_general(n2, grad_gate_act, tn, preferred_element_type=f32))
    _store_split(gu_ref, lax.dot_general(n2, grad_up_act, tn, preferred_element_type=f32))


def _rows_body(hid_ref, dga_ref, dua_ref, dy_ref, gcol_ref, wg_ref, wu_ref, wd_ref, acc_ref, dgate_ref, dn2_ref):
    f32 = jnp.float32
    nt = (((1,), (1,)), ((), ()))

    @pl.when(pl.program_id(0) == 0)
    def _():
        acc_ref[...] = jnp.zeros_like(acc_ref)
        dn2_ref[...] = jnp.zeros_like(dn2_ref)

    expert_out = lax.dot_general(hid_ref[0], wd_ref[0], nt, preferred_element_type=f32)
    acc_ref[...] += _gate_column(gcol_ref) * expert_out
    dgate_ref[0] = jnp.sum(expert_out * dy_ref[...].astype(f32), axis=1, keepdims=True)
    dn2_ref[...] += lax.dot_general(
        dga_ref[0], wg_ref[0], nt, preferred_element_type=f32
    ) + lax.dot_general(dua_ref[0], wu_ref[0], nt, preferred_element_type=f32)


def expert_grad_kernel(n2, dy, gcol, wg, wu, wd, groups):
    tokens, width = n2.shape
    experts, _, hidden = wg.shape
    bf16 = jnp.bfloat16
    whole = lambda shape: pl.BlockSpec(shape, lambda e: (0,) * len(shape))
    per_expert = lambda shape: pl.BlockSpec((1,) + shape, lambda e: (e,) + (0,) * len(shape))
    split_rows = width // (groups * 2)
    split = pl.BlockSpec((2, 1, groups, split_rows, hidden), lambda e: (0, e, 0, 0, 0))
    split_shape = jax.ShapeDtypeStruct((2, experts, groups, split_rows, hidden), bf16)
    act_shape = jax.ShapeDtypeStruct((experts, tokens, hidden), bf16)
    return pl.pallas_call(
        _grad_body,
        grid=(experts,),
        in_specs=[
            whole((tokens, width)),
            whole((tokens, width)),
            whole((tokens, experts)),
            per_expert((width, hidden)),
            per_expert((width, hidden)),
            per_expert((width, hidden)),
        ],
        out_specs=[split, split, split]
        + [per_expert((tokens, hidden))] * 3,
        out_shape=[split_shape] * 3 + [act_shape] * 3,
        compiler_params=pltpu.CompilerParams(
            dimension_semantics=("arbitrary",), vmem_limit_bytes=64 * 1024 * 1024
        ),
        cost_estimate=pl.CostEstimate(
            flops=experts * tokens * width * hidden * 2 * 6,
            transcendentals=experts * tokens * hidden,
            bytes_accessed=experts * width * hidden * 12 + tokens * width * 8 + experts * tokens * hidden * 6,
        ),
    )(n2, dy, gcol, wg, wu, wd)


def expert_rows_kernel(hid, dga, dua, dy, gcol, wg, wu, wd):
    experts, tokens, hidden = hid.shape
    width = dy.shape[1]
    f32 = jnp.float32
    whole = lambda shape: pl.BlockSpec(shape, lambda e: (0,) * len(shape))
    per_expert = lambda shape: pl.BlockSpec((1,) + shape, lambda e: (e,) + (0,) * len(shape))
    return pl.pallas_call(
        _rows_body,
        grid=(experts,),
        in_specs=[
            per_expert((tokens, hidden)),
            per_expert((tokens, hidden)),
            per_expert((tokens, hidden)),
            whole((tokens, width)),
            whole((tokens, experts)),
            per_expert((width, hidden)),
            per_expert((width, hidden)),
            per_expert((width, hidden)),
        ],
        out_specs=[whole((tokens, width)), per_expert((tokens, 1)), whole((tokens, width))],
        out_shape=[
            jax.ShapeDtypeStruct((tokens, width), f32),
            jax.ShapeDtypeStruct((experts, tokens, 1), f32),
            jax.ShapeDtypeStruct((tokens, width), f32),
        ],
        compiler_params=pltpu.CompilerParams(
            dimension_semantics=("arbitrary",), vmem_limit_bytes=64 * 1024 * 1024
        ),
        cost_estimate=pl.CostEstimate(
            flops=experts * tokens * width * hidden * 2 * 3,
            transcendentals=0,
            bytes_accessed=experts * width * hidden * 6 + tokens * width * 10 + experts * tokens * hidden * 6,
        ),
    )(hid, dga, dua, dy, gcol, wg, wu, wd)

MESH = pl.DeviceIdType.MESH


def _exchange_body(axis, n, per_peer, downward, src_ref, out_ref, send_sems, recv_sems):
    me = lax.axis_index(axis)
    barrier = pltpu.get_barrier_semaphore()
    for k in range(1, n):
        peer = lax.rem(me + k, n)
        pl.semaphore_signal(barrier, 1, device_id={axis: peer}, device_id_type=MESH)
    pl.semaphore_wait(barrier, n - 1)
    sends = []
    for k in range(1, n):
        peer = lax.rem(me + k, n)
        copy = pltpu.make_async_remote_copy(
            src_ref=src_ref.at[peer] if per_peer else src_ref,
            dst_ref=out_ref.at[me],
            send_sem=send_sems.at[k - 1],
            recv_sem=recv_sems.at[k - 1],
            device_id={axis: peer},
            device_id_type=MESH,
        )
        sends.append((peer, copy))
        if downward:
            pl.when(peer < me)(copy.start)
        else:
            copy.start()
    for k in range(1, n):
        source = lax.rem(me + n - k, n)
        incoming = pltpu.make_async_remote_copy(
            src_ref=src_ref.at[source] if per_peer else src_ref,
            dst_ref=out_ref.at[source],
            send_sem=send_sems.at[k - 1],
            recv_sem=recv_sems.at[k - 1],
            device_id={axis: source},
            device_id_type=MESH,
        )
        if downward:
            pl.when(source > me)(incoming.wait_recv)
        else:
            incoming.wait_recv()
    for peer, copy in sends:
        if downward:
            pl.when(peer < me)(copy.wait_send)
        else:
            copy.wait_send()


def exchange(x, axis, n, per_peer, collective_id, downward=False):
    block = x.shape[1:] if per_peer else x.shape
    nbytes = math.prod(block) * x.dtype.itemsize
    return pl.pallas_call(
        functools.partial(_exchange_body, axis, n, per_peer, downward),
        out_shape=jax.ShapeDtypeStruct((n,) + tuple(block), x.dtype),
        in_specs=[pl.BlockSpec(memory_space=pl.ANY)],
        out_specs=pl.BlockSpec(memory_space=pl.ANY),
        scratch_shapes=[pltpu.SemaphoreType.DMA((n - 1,)), pltpu.SemaphoreType.DMA((n - 1,))],
        compiler_params=pltpu.CompilerParams(collective_id=collective_id, has_side_effects=True),
        cost_estimate=pl.CostEstimate(flops=0, transcendentals=0, bytes_accessed=2 * (n - 1) * nbytes),
    )(x)


def gather_axis(x, axis, n, collective_id):
    got = exchange(x, axis, n, False, collective_id)
    return lax.dynamic_update_slice_in_dim(got, x[None], lax.axis_index(axis), 0)


def sum_axis(x, axis, collective_id):
    got = exchange(x, axis, 2, False, collective_id)
    me = lax.axis_index(axis)
    other = lax.dynamic_index_in_dim(got, 1 - me, 0, keepdims=False)
    return x.astype(jnp.float32) + other.astype(jnp.float32)


def _pair_add_body(me_ref, own_ref, other_ref, out_ref):
    out_ref[...] = (own_ref[...].astype(jnp.float32) + other_ref[...].astype(jnp.float32)).astype(out_ref.dtype)


def core_reduce(x, collective_id):
    got = exchange(x, "core", 2, True, collective_id)
    me = lax.axis_index("core")
    count = x.shape[1]
    rest = x.shape[2:]
    zeros = (0,) * len(rest)
    item_bytes = math.prod(rest) * x.dtype.itemsize
    step = max(d for d in range(1, count + 1) if count % d == 0 and d * item_bytes <= 4 * 1024 * 1024)
    grid_spec = pltpu.PrefetchScalarGridSpec(
        num_scalar_prefetch=1,
        grid=(count // step,),
        in_specs=[
            pl.BlockSpec((None, step) + rest, lambda i, c: (c[0], i) + zeros),
            pl.BlockSpec((None, step) + rest, lambda i, c: (1 - c[0], i) + zeros),
        ],
        out_specs=pl.BlockSpec((step,) + rest, lambda i, c: (i,) + zeros),
    )
    return pl.pallas_call(
        _pair_add_body,
        grid_spec=grid_spec,
        out_shape=jax.ShapeDtypeStruct(x.shape[1:], jnp.bfloat16),
        compiler_params=pltpu.CompilerParams(vmem_limit_bytes=56 * 1024 * 1024),
        cost_estimate=pl.CostEstimate(flops=x.size // 2, transcendentals=0, bytes_accessed=x.size * 3),
    )(jnp.reshape(me, (1,)).astype(jnp.int32), x, got)


def scatter_sum_downward(x, axis, n, collective_id):
    got = exchange(x, axis, n, True, collective_id, downward=True)
    me = lax.axis_index(axis)
    own = lax.dynamic_index_in_dim(x, me, 0, keepdims=False).astype(jnp.float32)
    above = (jnp.arange(n, dtype=jnp.int32) > me).reshape((n,) + (1,) * (x.ndim - 1))
    return own + jnp.sum(jnp.where(above, got.astype(jnp.float32), 0.0), axis=0)


def _flash_body(groups, ctx_ref, q_ref, k_ref, v_ref, qseg_ref, qpos_ref, kseg_ref, o_ref, lse_ref, qs_sc, m_sc, l_sc, acc_sc):
    f32 = jnp.float32
    block = pl.program_id(1)
    depth = HEAD_SIZE
    pair = k_ref.shape[2] // depth
    tokens = q_ref.shape[0]

    @pl.when(block == 0)
    def _():
        m_sc[...] = jnp.full_like(m_sc, NEGATIVE)
        l_sc[...] = jnp.zeros_like(l_sc)
        acc_sc[...] = jnp.zeros_like(acc_sc)
        scale = jnp.asarray(1.0 / math.sqrt(HEAD_SIZE), q_ref.dtype)
        for kk in range(pair):
            for gi in range(groups):
                i = kk * groups + gi
                qs_sc[kk, gi * tokens : (gi + 1) * tokens, :] = q_ref[:, i * depth : (i + 1) * depth] * scale

    @pl.when(block <= ctx_ref[0])
    def _():
        width = k_ref.shape[1]
        key_pos = block * width + lax.broadcasted_iota(jnp.int32, (1, width), 1)
        allowed = (qseg_ref[...] == kseg_ref[...]) & (key_pos <= qpos_ref[...])
        for kk in range(pair):
            keys = k_ref[0, :, kk * depth : (kk + 1) * depth]
            values = v_ref[0, :, kk * depth : (kk + 1) * depth]
            scores = lax.dot_general(
                qs_sc[kk], keys, (((1,), (1,)), ((), ())), preferred_element_type=f32
            )
            scores = jnp.where(allowed, scores, NEGATIVE)
            m_old = m_sc[kk]
            m_new = jnp.maximum(m_old, jnp.max(scores, axis=1, keepdims=True))
            alpha = jnp.exp(m_old - m_new)
            weights = jnp.where(allowed, jnp.exp(scores - m_new), 0.0)
            l_sc[kk] = alpha * l_sc[kk] + jnp.sum(weights, axis=1, keepdims=True)
            acc_sc[kk] = alpha * acc_sc[kk] + jnp.dot(
                weights.astype(jnp.bfloat16), values, preferred_element_type=f32
            )
            m_sc[kk] = m_new

    @pl.when(block == pl.num_programs(1) - 1)
    def _():
        for kk in range(pair):
            for gi in range(groups):
                i = kk * groups + gi
                rows = slice(gi * tokens, (gi + 1) * tokens)
                o_ref[:, i * depth : (i + 1) * depth] = acc_sc[kk, rows, :] / l_sc[kk, rows, :]
                lse_ref[0, :, i : i + 1] = m_sc[kk, rows, :] + jnp.log(l_sc[kk, rows, :])


def flash_forward(ctx_index, q, kv, qseg, qpos, kseg, groups):
    tokens, q_width = q.shape
    blocks, width, kv_width = kv.shape
    pair = 2
    pairs = kv_width // (2 * pair * HEAD_SIZE)
    heads_step = pair * groups
    f32 = jnp.float32
    capped = lambda p, b, c: (jnp.minimum(b, c[0]), 0, p)
    grid_spec = pltpu.PrefetchScalarGridSpec(
        num_scalar_prefetch=1,
        grid=(pairs, blocks),
        in_specs=[
            pl.BlockSpec((tokens, heads_step * HEAD_SIZE), lambda p, b, c: (0, p)),
            pl.BlockSpec((1, width, pair * HEAD_SIZE), capped),
            pl.BlockSpec((1, width, pair * HEAD_SIZE), lambda p, b, c: (jnp.minimum(b, c[0]), 0, pairs + p)),
            pl.BlockSpec((groups * tokens, 1), lambda p, b, c: (0, 0)),
            pl.BlockSpec((groups * tokens, 1), lambda p, b, c: (0, 0)),
            pl.BlockSpec((1, width), lambda p, b, c: (0, jnp.minimum(b, c[0]))),
        ],
        out_specs=[
            pl.BlockSpec((tokens, heads_step * HEAD_SIZE), lambda p, b, c: (0, p)),
            pl.BlockSpec((1, tokens, heads_step), lambda p, b, c: (p, 0, 0)),
        ],
        scratch_shapes=[
            pltpu.VMEM((pair, groups * tokens, HEAD_SIZE), q.dtype),
            pltpu.VMEM((pair, groups * tokens, 1), f32),
            pltpu.VMEM((pair, groups * tokens, 1), f32),
            pltpu.VMEM((pair, groups * tokens, HEAD_SIZE), f32),
        ],
    )
    return pl.pallas_call(
        functools.partial(_flash_body, groups),
        grid_spec=grid_spec,
        out_shape=[
            jax.ShapeDtypeStruct((tokens, q_width), f32),
            jax.ShapeDtypeStruct((pairs, tokens, heads_step), f32),
        ],
        compiler_params=pltpu.CompilerParams(
            dimension_semantics=("arbitrary", "arbitrary"), vmem_limit_bytes=48 * 1024 * 1024
        ),
        cost_estimate=pl.CostEstimate(
            flops=tokens * q_width * blocks * width * 4,
            transcendentals=tokens * (q_width // HEAD_SIZE) * blocks * width,
            bytes_accessed=(q.size + kv.size) * 2 + tokens * q_width * 4,
        ),
    )(jnp.reshape(ctx_index, (1,)).astype(jnp.int32), q, kv, kv, qseg, qpos, kseg)

def _chain_down_body(axis, n, x_ref, out_ref, recv, send, send_sems, recv_sems):
    f32 = jnp.float32
    me = lax.axis_index(axis)
    below = lax.rem(me + n - 1, n)
    above = lax.rem(me + 1, n)
    barrier = pltpu.get_barrier_semaphore()
    pl.semaphore_signal(barrier, 1, device_id={axis: below}, device_id_type=MESH)
    pl.semaphore_signal(barrier, 1, device_id={axis: above}, device_id_type=MESH)
    pl.semaphore_wait(barrier, 2)
    copies = []
    for j in range(n - 1):
        copy = pltpu.make_async_remote_copy(
            src_ref=send.at[j],
            dst_ref=recv.at[j],
            send_sem=send_sems.at[j],
            recv_sem=recv_sems.at[j],
            device_id={axis: below},
            device_id_type=MESH,
        )
        copies.append(copy)

        @pl.when((j < me) & (me < n - 1))
        def _():
            copy.wait_recv()
            send[j] = (x_ref[j].astype(f32) + recv[j].astype(f32)).astype(send.dtype)

        @pl.when((j < me) & (me == n - 1))
        def _():
            send[j] = x_ref[j]

        @pl.when(j < me)
        def _():
            copy.start()

        @pl.when(j == me)
        def _():
            copy.wait_recv()
            out_ref[...] = x_ref[j].astype(f32) + recv[j].astype(f32)

    @pl.when(me == n - 1)
    def _():
        out_ref[...] = x_ref[n - 1].astype(f32)

    for j in range(n - 1):
        pl.when(j < me)(copies[j].wait_send)


def chain_sum_down(x, axis, n, collective_id):
    _, rows, cols = x.shape
    return pl.pallas_call(
        functools.partial(_chain_down_body, axis, n),
        out_shape=jax.ShapeDtypeStruct((rows, cols), jnp.float32),
        in_specs=[pl.BlockSpec(memory_space=pltpu.VMEM)],
        out_specs=pl.BlockSpec(memory_space=pltpu.VMEM),
        scratch_shapes=[
            pltpu.VMEM((n - 1, rows, cols), x.dtype),
            pltpu.VMEM((n - 1, rows, cols), x.dtype),
            pltpu.SemaphoreType.DMA((n - 1,)),
            pltpu.SemaphoreType.DMA((n - 1,)),
        ],
        compiler_params=pltpu.CompilerParams(
            collective_id=collective_id, has_side_effects=True, vmem_limit_bytes=32 * 1024 * 1024
        ),
        cost_estimate=pl.CostEstimate(
            flops=(n - 1) * rows * cols, transcendentals=0, bytes_accessed=3 * n * rows * cols * 2
        ),
    )(x)


def _chain_up_body(axis, n, x_ref, out_ref, send_sems, recv_sems):
    me = lax.axis_index(axis)
    below = lax.rem(me + n - 1, n)
    above = lax.rem(me + 1, n)
    barrier = pltpu.get_barrier_semaphore()
    pl.semaphore_signal(barrier, 1, device_id={axis: below}, device_id_type=MESH)
    pl.semaphore_signal(barrier, 1, device_id={axis: above}, device_id_type=MESH)
    pl.semaphore_wait(barrier, 2)
    own = pltpu.make_async_remote_copy(
        src_ref=x_ref,
        dst_ref=out_ref.at[me],
        send_sem=send_sems.at[me],
        recv_sem=recv_sems.at[me],
        device_id={axis: above},
        device_id_type=MESH,
    )
    pl.when(me < n - 1)(own.start)
    forwards = []
    for k in range(1, n):
        block = jnp.maximum(me - k, 0)
        incoming = pltpu.make_async_remote_copy(
            src_ref=out_ref.at[block],
            dst_ref=out_ref.at[block],
            send_sem=send_sems.at[block],
            recv_sem=recv_sems.at[block],
            device_id={axis: below},
            device_id_type=MESH,
        )
        forward = pltpu.make_async_remote_copy(
            src_ref=out_ref.at[block],
            dst_ref=out_ref.at[block],
            send_sem=send_sems.at[block],
            recv_sem=recv_sems.at[block],
            device_id={axis: above},
            device_id_type=MESH,
        )
        forwards.append((k, forward))
        pl.when(k <= me)(incoming.wait_recv)
        pl.when((k <= me) & (me < n - 1))(forward.start)
    pl.when(me < n - 1)(own.wait_send)
    for k, forward in forwards:
        pl.when((k <= me) & (me < n - 1))(forward.wait_send)


def gather_up(x, axis, n, collective_id):
    got = pl.pallas_call(
        functools.partial(_chain_up_body, axis, n),
        out_shape=jax.ShapeDtypeStruct((n,) + x.shape, x.dtype),
        in_specs=[pl.BlockSpec(memory_space=pl.ANY)],
        out_specs=pl.BlockSpec(memory_space=pl.ANY),
        scratch_shapes=[pltpu.SemaphoreType.DMA((n,)), pltpu.SemaphoreType.DMA((n,))],
        compiler_params=pltpu.CompilerParams(collective_id=collective_id, has_side_effects=True),
        cost_estimate=pl.CostEstimate(
            flops=0, transcendentals=0, bytes_accessed=2 * (n - 1) * x.size * x.dtype.itemsize
        ),
    )(x)
    me = lax.axis_index(axis)
    below = (jnp.arange(n, dtype=jnp.int32) < me).reshape((n,) + (1,) * x.ndim)
    got = jnp.where(below, got, jnp.zeros_like(got))
    return lax.dynamic_update_slice_in_dim(got, x[None], me, 0)


def _attend_block(groups, kv_heads, q_sc, kv_buf, qseg_ref, qpos_ref, kseg_ref, m_sc, l_sc, acc_sc, block):
    f32 = jnp.float32
    depth = HEAD_SIZE
    width = kv_buf.shape[0]
    start = pl.multiple_of(block * width, width)
    key_pos = start + lax.broadcasted_iota(jnp.int32, (1, width), 1)
    allowed = (qseg_ref[...] == kseg_ref[:, pl.ds(start, width)]) & (key_pos <= qpos_ref[...])
    for kk in range(kv_heads):
        keys = kv_buf[:, kk * depth : (kk + 1) * depth]
        values = kv_buf[:, (kv_heads + kk) * depth : (kv_heads + kk + 1) * depth]
        scores = lax.dot_general(q_sc[kk], keys, (((1,), (1,)), ((), ())), preferred_element_type=f32)
        scores = jnp.where(allowed, scores, NEGATIVE)
        m_old = m_sc[kk]
        m_new = jnp.maximum(m_old, jnp.max(scores, axis=1, keepdims=True))
        alpha = jnp.exp(m_old - m_new)
        weights = jnp.where(allowed, jnp.exp(scores - m_new), 0.0)
        l_sc[kk] = alpha * l_sc[kk] + jnp.sum(weights, axis=1, keepdims=True)
        acc_sc[kk] = alpha * acc_sc[kk] + jnp.dot(
            weights.astype(jnp.bfloat16), values, preferred_element_type=f32
        )
        m_sc[kk] = m_new


def _gather_attend_body(
    axis, n, groups, q_ref, own_ref, qseg_ref, qpos_ref, kseg_ref,
    kv_ref, o_ref, lse_ref,
    q_sc, m_sc, l_sc, acc_sc, kv_buf, send_sems, recv_sems, copy_sem,
):
    depth = HEAD_SIZE
    tokens = q_ref.shape[0]
    kv_heads = own_ref.shape[1] // (2 * depth)
    me = lax.axis_index(axis)
    below = lax.rem(me + n - 1, n)
    above = lax.rem(me + 1, n)
    barrier = pltpu.get_barrier_semaphore()
    pl.semaphore_signal(barrier, 1, device_id={axis: below}, device_id_type=MESH)
    pl.semaphore_signal(barrier, 1, device_id={axis: above}, device_id_type=MESH)
    pl.semaphore_wait(barrier, 2)
    own = pltpu.make_async_remote_copy(
        src_ref=own_ref,
        dst_ref=kv_ref.at[me],
        send_sem=send_sems.at[me],
        recv_sem=recv_sems.at[me],
        device_id={axis: above},
        device_id_type=MESH,
    )
    pl.when(me < n - 1)(own.start)

    m_sc[...] = jnp.full_like(m_sc, NEGATIVE)
    l_sc[...] = jnp.zeros_like(l_sc)
    acc_sc[...] = jnp.zeros_like(acc_sc)
    scale = jnp.asarray(1.0 / math.sqrt(HEAD_SIZE), q_ref.dtype)
    for kk in range(kv_heads):
        for gi in range(groups):
            i = kk * groups + gi
            q_sc[kk, gi * tokens : (gi + 1) * tokens, :] = q_ref[:, i * depth : (i + 1) * depth] * scale

    local = pltpu.make_async_copy(own_ref, kv_buf, copy_sem)
    local.start()
    local.wait()
    _attend_block(groups, kv_heads, q_sc, kv_buf, qseg_ref, qpos_ref, kseg_ref, m_sc, l_sc, acc_sc, me)

    def step(k, carry):
        block = me - k
        incoming = pltpu.make_async_remote_copy(
            src_ref=kv_ref.at[block],
            dst_ref=kv_ref.at[block],
            send_sem=send_sems.at[block],
            recv_sem=recv_sems.at[block],
            device_id={axis: below},
            device_id_type=MESH,
        )
        incoming.wait_recv()
        forward = pltpu.make_async_remote_copy(
            src_ref=kv_ref.at[block],
            dst_ref=kv_ref.at[block],
            send_sem=send_sems.at[block],
            recv_sem=recv_sems.at[block],
            device_id={axis: above},
            device_id_type=MESH,
        )
        pl.when(me < n - 1)(forward.start)
        fetch = pltpu.make_async_copy(kv_ref.at[block], kv_buf, copy_sem)
        fetch.start()
        fetch.wait()
        _attend_block(groups, kv_heads, q_sc, kv_buf, qseg_ref, qpos_ref, kseg_ref, m_sc, l_sc, acc_sc, block)
        return carry

    lax.fori_loop(1, me + 1, step, 0)

    for kk in range(kv_heads):
        for gi in range(groups):
            i = kk * groups + gi
            rows = slice(gi * tokens, (gi + 1) * tokens)
            o_ref[:, i * depth : (i + 1) * depth] = acc_sc[kk, rows, :] / l_sc[kk, rows, :]
            lse_ref[:, i : i + 1] = m_sc[kk, rows, :] + jnp.log(l_sc[kk, rows, :])

    pl.when(me < n - 1)(own.wait_send)

    def drain(k, carry):
        block = me - k
        pltpu.make_async_remote_copy(
            src_ref=kv_ref.at[block],
            dst_ref=kv_ref.at[block],
            send_sem=send_sems.at[block],
            recv_sem=recv_sems.at[block],
            device_id={axis: above},
            device_id_type=MESH,
        ).wait_send()
        return carry

    lax.fori_loop(1, jnp.where(me < n - 1, me + 1, 1), drain, 0)


def gather_attend(q, own, qseg, qpos, kseg, axis, n, groups, collective_id):
    tokens, q_width = q.shape
    rows, kv_width = own.shape
    heads = q_width // HEAD_SIZE
    kv_heads = kv_width // (2 * HEAD_SIZE)
    f32 = jnp.float32
    vmem = pl.BlockSpec(memory_space=pltpu.VMEM)
    anywhere = pl.BlockSpec(memory_space=pl.ANY)
    kv_all, attn, lse = pl.pallas_call(
        functools.partial(_gather_attend_body, axis, n, groups),
        out_shape=[
            jax.ShapeDtypeStruct((n, rows, kv_width), own.dtype),
            jax.ShapeDtypeStruct((tokens, q_width), f32),
            jax.ShapeDtypeStruct((tokens, heads), f32),
        ],
        in_specs=[vmem, anywhere, vmem, vmem, vmem],
        out_specs=[anywhere, vmem, vmem],
        scratch_shapes=[
            pltpu.VMEM((kv_heads, groups * tokens, HEAD_SIZE), q.dtype),
            pltpu.VMEM((kv_heads, groups * tokens, 1), f32),
            pltpu.VMEM((kv_heads, groups * tokens, 1), f32),
            pltpu.VMEM((kv_heads, groups * tokens, HEAD_SIZE), f32),
            pltpu.VMEM((rows, kv_width), own.dtype),
            pltpu.SemaphoreType.DMA((n,)),
            pltpu.SemaphoreType.DMA((n,)),
            pltpu.SemaphoreType.DMA(()),
        ],
        compiler_params=pltpu.CompilerParams(
            collective_id=collective_id, has_side_effects=True, vmem_limit_bytes=48 * 1024 * 1024
        ),
        cost_estimate=pl.CostEstimate(
            flops=tokens * q_width * n * rows * 4,
            transcendentals=tokens * heads * n * rows,
            bytes_accessed=2 * n * own.size * own.dtype.itemsize + tokens * q_width * 6,
        ),
    )(q, own, qseg, qpos, kseg)
    me = lax.axis_index(axis)
    below = (jnp.arange(n, dtype=jnp.int32) < me).reshape((n, 1, 1))
    kv_all = jnp.where(below, kv_all, jnp.zeros_like(kv_all))
    return attn, lse, lax.dynamic_update_slice_in_dim(kv_all, own[None], me, 0)


def per_device(
    dpx_count,
    hidden_in,
    attn_gain,
    q_weight,
    key_matrix,
    value_matrix,
    o_weight,
    moe_gain,
    router_weight,
    gate_weight,
    up_weight,
    down_weight,
    segments,
    expert_picks,
    output_grad,
):
    bf16 = jnp.bfloat16
    f32 = jnp.float32
    token_count = hidden_in.shape[0]
    ctx_index = lax.axis_index("ctx")
    heads_local = q_weight.shape[1] // HEAD_SIZE
    kv_local = key_matrix.shape[1] // HEAD_SIZE
    group_size = heads_local // kv_local
    score_scale = 1.0 / math.sqrt(HEAD_SIZE)
    token_positions = ctx_index * token_count + jnp.arange(token_count, dtype=jnp.int32)
    segment_here = lax.dynamic_slice_in_dim(segments, ctx_index * token_count, token_count)
    inputs_f32 = hidden_in.astype(f32)
    o_full = lax.all_gather(o_weight, "tensor", axis=0, tiled=False)
    normed_f32, scale_one = normalize(inputs_f32, attn_gain)
    normed_one = normed_f32.astype(bf16)
    query_rows = jnp.dot(normed_one, q_weight, preferred_element_type=f32).reshape(
        token_count, heads_local, HEAD_SIZE
    )
    keys_raw = jnp.dot(normed_one, key_matrix, preferred_element_type=f32).reshape(
        token_count, kv_local, HEAD_SIZE
    )
    values_raw = jnp.dot(normed_one, value_matrix, preferred_element_type=f32)
    query_grouped = (
        apply_rotary(query_rows, token_positions, 1.0)
        .astype(bf16)
        .reshape(token_count, kv_local, group_size, HEAD_SIZE)
    )
    key_flat = (
        apply_rotary(keys_raw, token_positions, 1.0)
        .astype(bf16)
        .reshape(token_count, kv_local * HEAD_SIZE)
    )
    value_flat = values_raw.astype(bf16)

    def piece_mask(piece_rows):
        key_pos = jnp.arange(piece_rows, dtype=jnp.int32)
        return (segment_here[:, None] == segments[None, :]) & (
            key_pos[None, :] <= token_positions[:, None]
        )

    ctx_count = segments.shape[0] // token_count
    attn_flat, lse_heads, kv_both = gather_attend(
        query_grouped.reshape(token_count, heads_local * HEAD_SIZE),
        jnp.concatenate([key_flat, value_flat], axis=1),
        jnp.tile(segment_here, group_size)[:, None],
        jnp.tile(token_positions, group_size)[:, None],
        segments[None, :],
        "ctx",
        ctx_count,
        group_size,
        1,
    )
    piece_rows = ctx_count * token_count
    kv_width = kv_local * HEAD_SIZE
    key_piece = kv_both[:, :, :kv_width].reshape(piece_rows, kv_local, HEAD_SIZE)
    value_piece = kv_both[:, :, kv_width:].reshape(piece_rows, kv_local, HEAD_SIZE)
    attn_grouped = jnp.transpose(
        attn_flat.reshape(token_count, kv_local, group_size, HEAD_SIZE), (1, 2, 0, 3)
    )
    log_sum = jnp.transpose(lse_heads.reshape(token_count, kv_local, group_size), (1, 2, 0))
    attn_bf = attn_flat.astype(bf16)
    tensor_count = o_weight.shape[0] // o_weight.shape[1]
    attn_all = gather_axis(attn_bf, "tensor", tensor_count, 2)
    mixed_attn = lax.dot_general(
        attn_all, o_full, (((0, 2), (0, 2)), ((), ())), preferred_element_type=f32
    )
    resid = inputs_f32 + mixed_attn
    normed_two_f32, scale_two = normalize(resid, moe_gain)
    normed_two = normed_two_f32.astype(bf16)
    logits = jnp.dot(normed_two, router_weight, preferred_element_type=f32)
    expert_range = jnp.arange(NEXP, dtype=jnp.int32)
    picked_onehot = expert_picks[:, :, None] == expert_range[None, None, :]
    picked = jnp.sum(jnp.where(picked_onehot, logits[:, None, :], 0.0), axis=2)
    gate_probs = jax.nn.softmax(picked, axis=-1)
    gates_dense = jnp.sum(jnp.where(picked_onehot, gate_probs[:, :, None], 0.0), axis=1)
    gates_by_expert = jnp.transpose(gates_dense)
    cot_bf = output_grad
    gcol = gates_dense
    grad_gate, grad_up, grad_down, hid_all, dga_all, dua_all = expert_grad_kernel(
        normed_two,
        cot_bf,
        gcol,
        gate_weight,
        up_weight,
        down_weight,
        dpx_count,
    )
    gate_half = core_reduce(grad_gate, 8)
    gate_half, hid_all, dga_all, dua_all = lax.optimization_barrier(
        (gate_half, hid_all, dga_all, dua_all)
    )
    moe_acc, gate_parts, moe_grad_rows = expert_rows_kernel(
        hid_all, dga_all, dua_all, cot_bf, gcol, gate_weight, up_weight, down_weight
    )
    cot_f32 = output_grad.astype(f32)
    moe_total = sum_axis(moe_acc.astype(bf16), "tensor", 3)
    output = (resid + moe_total).astype(bf16)
    grad_rows_all = moe_grad_rows
    gate_parts = gate_parts[:, :, 0]
    grad_gate_out, grad_up_out, grad_down_out = [
        lax.psum_scatter(
            g.reshape(g.shape[0], -1, g.shape[3]), ("dpx", "ctx"), scatter_dimension=1, tiled=True
        )
        for g in (gate_half, core_reduce(grad_up, 9), core_reduce(grad_down, 10))
    ]
    gate_pair = jnp.sum(
        jnp.where(picked_onehot, jnp.transpose(gate_parts)[:, None, :], 0.0), axis=2
    )
    moe_summed = sum_axis(grad_rows_all.astype(bf16), "tensor", 4)
    gate_summed = sum_axis(gate_pair.astype(bf16), "tensor", 5)
    grad_picked = gate_probs * (
        gate_summed - jnp.sum(gate_probs * gate_summed, axis=1, keepdims=True)
    )
    grad_logits = jnp.sum(jnp.where(picked_onehot, grad_picked[:, :, None], 0.0), axis=1).astype(
        bf16
    )
    grad_router = contract_rows(normed_two, grad_logits)
    grad_normed_two = moe_summed + contract_cols(grad_logits, router_weight)
    grad_two_rows, grad_moe_gain = norm_backward(resid, scale_two, moe_gain, grad_normed_two)
    grad_resid = cot_f32 + grad_two_rows
    grad_mix = grad_resid.astype(bf16)
    grad_o = contract_rows(grad_mix, attn_bf)
    grad_attn = jnp.dot(grad_mix, o_weight, preferred_element_type=f32).astype(bf16)
    grad_attn_grouped = jnp.transpose(
        grad_attn.reshape(token_count, kv_local, group_size, HEAD_SIZE), (1, 2, 0, 3)
    )
    row_delta = jnp.sum(grad_attn_grouped.astype(f32) * attn_grouped, axis=-1)
    allowed = piece_mask(piece_rows)
    scores = (
        jnp.einsum("tkgd,nkd->kgtn", query_grouped, key_piece, preferred_element_type=f32)
        * score_scale
    )
    probability = jnp.where(allowed, jnp.exp(scores - log_sum[..., None]), 0.0)
    grad_probs = jnp.einsum(
        "kgtd,nkd->kgtn", grad_attn_grouped, value_piece, preferred_element_type=f32
    )
    grad_scores = (probability * (grad_probs - row_delta[..., None])).astype(bf16)
    grad_query = score_scale * jnp.einsum(
        "kgtn,nkd->kgtd", grad_scores, key_piece, preferred_element_type=f32
    )
    key_part = score_scale * jnp.einsum(
        "kgtn,tkgd->nkd", grad_scores, query_grouped, preferred_element_type=f32
    )
    value_part = jnp.einsum(
        "kgtn,kgtd->nkd", probability.astype(bf16), grad_attn_grouped, preferred_element_type=f32
    )
    grad_keys_all = key_part.reshape(piece_rows, kv_local * HEAD_SIZE)
    grad_values_all = value_part.reshape(piece_rows, kv_local * HEAD_SIZE)
    back_state = (grad_query, grad_keys_all, grad_values_all)
    grad_query, grad_keys_all, grad_values_all = back_state
    grad_kv_here = chain_sum_down(
        jnp.concatenate([grad_keys_all, grad_values_all], axis=1)
        .astype(bf16)
        .reshape(ctx_count, token_count, 2 * kv_width),
        "ctx",
        ctx_count,
        6,
    )
    grad_keys_here = grad_kv_here[:, :kv_width]
    grad_values_here = grad_kv_here[:, kv_width:]
    grad_query_rows = jnp.transpose(grad_query, (2, 0, 1, 3)).reshape(
        token_count, heads_local, HEAD_SIZE
    )
    grad_query_bf = (
        apply_rotary(grad_query_rows, token_positions, -1.0)
        .reshape(token_count, heads_local * HEAD_SIZE)
        .astype(bf16)
    )
    grad_key_bf = (
        apply_rotary(
            grad_keys_here.reshape(token_count, kv_local, HEAD_SIZE), token_positions, -1.0
        )
        .reshape(token_count, kv_local * HEAD_SIZE)
        .astype(bf16)
    )
    grad_value_bf = grad_values_here.astype(bf16)
    grad_q = contract_rows(normed_one, grad_query_bf)
    grad_k = contract_rows(normed_one, grad_key_bf)
    grad_v = contract_rows(normed_one, grad_value_bf)
    partial_one = (
        contract_cols(grad_query_bf, q_weight)
        + contract_cols(grad_key_bf, key_matrix)
        + contract_cols(grad_value_bf, value_matrix)
    )
    grad_normed_one = sum_axis(partial_one.astype(bf16), "tensor", 7)
    grad_one_rows, grad_attn_gain = norm_backward(inputs_f32, scale_one, attn_gain, grad_normed_one)
    input_grad = grad_resid + grad_one_rows
    q_cols, o_cols, k_cols = grad_q.shape[1], grad_o.shape[1], grad_k.shape[1]
    small = jnp.concatenate(
        [
            grad_router,
            grad_attn_gain[:, None],
            grad_moe_gain[:, None],
            jnp.zeros((grad_router.shape[0], 128 - grad_router.shape[1] - 2), f32),
        ],
        axis=1,
    )
    dense_all = jnp.concatenate(
        [grad_q, grad_o, grad_k, grad_v, small], axis=1
    ).astype(bf16)
    width = dense_all.shape[0]
    dense_all = jnp.transpose(
        dense_all.reshape(dpx_count, 2, width // (2 * dpx_count), dense_all.shape[1]), (1, 0, 2, 3)
    )
    dense_half = core_reduce(dense_all, 11)
    dense_half, grad_gate_out, grad_up_out, grad_down_out = lax.optimization_barrier(
        (dense_half, grad_gate_out, grad_up_out, grad_down_out)
    )
    grad_gate_out, grad_up_out, grad_down_out = (
        grad_gate_out.astype(f32),
        grad_up_out.astype(f32),
        grad_down_out.astype(f32),
    )
    dense_here = lax.psum_scatter(
        dense_half.reshape(-1, dense_half.shape[-1]), ("dpx", "ctx"), scatter_dimension=0, tiled=True
    ).astype(f32)
    spans = [q_cols, o_cols, k_cols, k_cols, router_weight.shape[1], 1, 1]
    cuts = [sum(spans[:i]) for i in range(len(spans) + 1)]
    pieces_out = [dense_here[:, cuts[i] : cuts[i + 1]] for i in range(len(spans))]
    dense_out = (
        pieces_out[5][:, 0],
        pieces_out[0],
        pieces_out[2],
        pieces_out[3],
        pieces_out[1],
        pieces_out[6][:, 0],
        pieces_out[4],
    )
    return (
        output,
        input_grad,
        dense_out[0],
        dense_out[1],
        dense_out[2],
        dense_out[3],
        dense_out[4],
        dense_out[5],
        dense_out[6],
        grad_gate_out,
        grad_up_out,
        grad_down_out,
    )


def solution(mesh):
    dp_count, ctx_count, tensor_count = (mesh.shape[a] for a in ("dp", "ctx", "tensor"))
    split_mesh = jax.sharding.Mesh(
        mesh.devices.reshape(dp_count // 2, 2, ctx_count, tensor_count), ("dpx", "core", "ctx", "tensor")
    )
    return jax.shard_map(
        functools.partial(per_device, dp_count // 2),
        mesh=split_mesh,
        in_specs=(
            P(("dpx", "core", "ctx"), None),
            P(),
            P(None, "tensor"),
            P(None, "tensor"),
            P(None, "tensor"),
            P(None, "tensor"),
            P(),
            P(),
            P(None, None, "tensor"),
            P(None, None, "tensor"),
            P(None, None, "tensor"),
            P(("dpx", "core")),
            P(("dpx", "core", "ctx"), None),
            P(("dpx", "core", "ctx"), None),
        ),
        out_specs=(
            P(("dpx", "core", "ctx"), None),
            P(("dpx", "core", "ctx"), None),
            P(("dpx", "core", "ctx")),
            P(("dpx", "core", "ctx"), "tensor"),
            P(("dpx", "core", "ctx"), "tensor"),
            P(("dpx", "core", "ctx"), "tensor"),
            P(("dpx", "core", "ctx"), "tensor"),
            P(("dpx", "core", "ctx")),
            P(("dpx", "core", "ctx"), None),
            P(None, ("dpx", "core", "ctx"), "tensor"),
            P(None, ("dpx", "core", "ctx"), "tensor"),
            P(None, ("dpx", "core", "ctx"), "tensor"),
        ),
        check_vma=False,
    )
```

```python
import functools
import math

import jax
import jax.numpy as jnp
from jax import lax
from jax.experimental import pallas as pl
from jax.experimental.pallas import tpu as pltpu
from jax.sharding import PartitionSpec as P

HEAD_SIZE = 64
NEXP = 24
CAP = 341


EPSILON = 1e-06
ROPE_BASE = 10000.0
NEGATIVE = -1e30
HIGHEST = lax.Precision.HIGHEST


def normalize(rows, gain):
    scale_inv = lax.rsqrt(jnp.mean(rows * rows, axis=-1, keepdims=True) + EPSILON)
    return (rows * scale_inv * gain, scale_inv)


def norm_backward(rows, scale_inv, gain, grad_normed):
    weighted = gain * grad_normed
    grad_gain = jnp.sum(grad_normed * rows * scale_inv, axis=0)
    inner_mean = jnp.mean(weighted * rows, axis=-1, keepdims=True)
    grad_rows = scale_inv * weighted - rows * scale_inv * scale_inv * scale_inv * inner_mean
    return (grad_rows, grad_gain)


def apply_rotary(value_rows, token_positions, direction):
    half_dim = value_rows.shape[-1] // 2
    frequency = ROPE_BASE ** (-jnp.arange(half_dim, dtype=jnp.float32) / half_dim)
    angles = token_positions.astype(jnp.float32)[:, None] * frequency[None, :]
    cosine = jnp.cos(angles)[:, None, :]
    sine_part = direction * jnp.sin(angles)[:, None, :]
    first_half = value_rows[..., :half_dim]
    second = value_rows[..., half_dim:]
    return jnp.concatenate(
        [first_half * cosine - second * sine_part, second * cosine + first_half * sine_part],
        axis=-1,
    )


def contract_rows(left, right):
    return lax.dot_general(
        left, right, (((0,), (0,)), ((), ())), preferred_element_type=jnp.float32
    )


def contract_rows_exact(left, right):
    return lax.dot_general(
        left, right, (((0,), (0,)), ((), ())), precision=HIGHEST, preferred_element_type=jnp.float32
    )


def contract_cols(left, right):
    return lax.dot_general(
        left, right, (((1,), (1,)), ((), ())), preferred_element_type=jnp.float32
    )


def _store_split(out_ref, value):
    cores, _, groups, rows, _ = out_ref.shape
    for x in range(groups):
        for c in range(cores):
            start = (x * cores + c) * rows
            out_ref[c, 0, x] = value[start : start + rows].astype(out_ref.dtype)


def _gate_column(gates_ref):
    gates = gates_ref[...]
    lane = lax.broadcasted_iota(jnp.int32, gates.shape, 1)
    return jnp.sum(jnp.where(lane == pl.program_id(0), gates, 0.0), axis=1, keepdims=True)


def _grad_body(
    n2_ref, dy_ref, gcol_ref, wg_ref, wu_ref, wd_ref,
    gg_ref, gu_ref, gd_ref, hid_ref, dga_ref, dua_ref,
):
    f32 = jnp.float32
    bf16 = jnp.bfloat16
    n2 = n2_ref[...]
    wd = wd_ref[0]
    gate_act = jnp.dot(n2, wg_ref[0], preferred_element_type=f32)
    up_act = jnp.dot(n2, wu_ref[0], preferred_element_type=f32)
    sig = 1.0 / (1.0 + jnp.exp(-gate_act))
    silu = gate_act * sig
    hidden = (silu * up_act).astype(bf16)
    hid_ref[0] = hidden
    gate = _gate_column(gcol_ref)
    grad_hidden = gate * jnp.dot(dy_ref[...], wd, preferred_element_type=f32)
    gated_hidden = (gate * hidden.astype(f32)).astype(bf16)
    tn = (((0,), (0,)), ((), ()))
    _store_split(gd_ref, lax.dot_general(dy_ref[...], gated_hidden, tn, preferred_element_type=f32))
    grad_gate_act = (grad_hidden * up_act * sig * (1.0 + gate_act * (1.0 - sig))).astype(bf16)
    grad_up_act = (grad_hidden * silu).astype(bf16)
    dga_ref[0] = grad_gate_act
    dua_ref[0] = grad_up_act
    _store_split(gg_ref, lax.dot_general(n2, grad_gate_act, tn, preferred_element_type=f32))
    _store_split(gu_ref, lax.dot_general(n2, grad_up_act, tn, preferred_element_type=f32))


def _rows_body(hid_ref, dga_ref, dua_ref, dy_ref, gcol_ref, wg_ref, wu_ref, wd_ref, acc_ref, dgate_ref, dn2_ref):
    f32 = jnp.float32
    nt = (((1,), (1,)), ((), ()))

    @pl.when(pl.program_id(0) == 0)
    def _():
        acc_ref[...] = jnp.zeros_like(acc_ref)
        dn2_ref[...] = jnp.zeros_like(dn2_ref)

    expert_out = lax.dot_general(hid_ref[0], wd_ref[0], nt, preferred_element_type=f32)
    acc_ref[...] += _gate_column(gcol_ref) * expert_out
    dgate_ref[0] = jnp.sum(expert_out * dy_ref[...].astype(f32), axis=1, keepdims=True)
    dn2_ref[...] += lax.dot_general(
        dga_ref[0], wg_ref[0], nt, preferred_element_type=f32
    ) + lax.dot_general(dua_ref[0], wu_ref[0], nt, preferred_element_type=f32)


def expert_grad_kernel(n2, dy, gcol, wg, wu, wd, groups):
    tokens, width = n2.shape
    experts, _, hidden = wg.shape
    bf16 = jnp.bfloat16
    whole = lambda shape: pl.BlockSpec(shape, lambda e: (0,) * len(shape))
    per_expert = lambda shape: pl.BlockSpec((1,) + shape, lambda e: (e,) + (0,) * len(shape))
    split_rows = width // (groups * 2)
    split = pl.BlockSpec((2, 1, groups, split_rows, hidden), lambda e: (0, e, 0, 0, 0))
    split_shape = jax.ShapeDtypeStruct((2, experts, groups, split_rows, hidden), bf16)
    act_shape = jax.ShapeDtypeStruct((experts, tokens, hidden), bf16)
    return pl.pallas_call(
        _grad_body,
        grid=(experts,),
        in_specs=[
            whole((tokens, width)),
            whole((tokens, width)),
            whole((tokens, experts)),
            per_expert((width, hidden)),
            per_expert((width, hidden)),
            per_expert((width, hidden)),
        ],
        out_specs=[split, split, split]
        + [per_expert((tokens, hidden))] * 3,
        out_shape=[split_shape] * 3 + [act_shape] * 3,
        compiler_params=pltpu.CompilerParams(
            dimension_semantics=("arbitrary",), vmem_limit_bytes=64 * 1024 * 1024
        ),
        cost_estimate=pl.CostEstimate(
            flops=experts * tokens * width * hidden * 2 * 6,
            transcendentals=experts * tokens * hidden,
            bytes_accessed=experts * width * hidden * 12 + tokens * width * 8 + experts * tokens * hidden * 6,
        ),
    )(n2, dy, gcol, wg, wu, wd)


def expert_rows_kernel(hid, dga, dua, dy, gcol, wg, wu, wd):
    experts, tokens, hidden = hid.shape
    width = dy.shape[1]
    f32 = jnp.float32
    whole = lambda shape: pl.BlockSpec(shape, lambda e: (0,) * len(shape))
    per_expert = lambda shape: pl.BlockSpec((1,) + shape, lambda e: (e,) + (0,) * len(shape))
    return pl.pallas_call(
        _rows_body,
        grid=(experts,),
        in_specs=[
            per_expert((tokens, hidden)),
            per_expert((tokens, hidden)),
            per_expert((tokens, hidden)),
            whole((tokens, width)),
            whole((tokens, experts)),
            per_expert((width, hidden)),
            per_expert((width, hidden)),
            per_expert((width, hidden)),
        ],
        out_specs=[whole((tokens, width)), per_expert((tokens, 1)), whole((tokens, width))],
        out_shape=[
            jax.ShapeDtypeStruct((tokens, width), f32),
            jax.ShapeDtypeStruct((experts, tokens, 1), f32),
            jax.ShapeDtypeStruct((tokens, width), f32),
        ],
        compiler_params=pltpu.CompilerParams(
            dimension_semantics=("arbitrary",), vmem_limit_bytes=64 * 1024 * 1024
        ),
        cost_estimate=pl.CostEstimate(
            flops=experts * tokens * width * hidden * 2 * 3,
            transcendentals=0,
            bytes_accessed=experts * width * hidden * 6 + tokens * width * 10 + experts * tokens * hidden * 6,
        ),
    )(hid, dga, dua, dy, gcol, wg, wu, wd)

MESH = pl.DeviceIdType.MESH


def _exchange_body(axis, n, per_peer, downward, src_ref, out_ref, send_sems, recv_sems):
    me = lax.axis_index(axis)
    barrier = pltpu.get_barrier_semaphore()
    for k in range(1, n):
        peer = lax.rem(me + k, n)
        pl.semaphore_signal(barrier, 1, device_id={axis: peer}, device_id_type=MESH)
    pl.semaphore_wait(barrier, n - 1)
    sends = []
    for k in range(1, n):
        peer = lax.rem(me + k, n)
        copy = pltpu.make_async_remote_copy(
            src_ref=src_ref.at[peer] if per_peer else src_ref,
            dst_ref=out_ref.at[me],
            send_sem=send_sems.at[k - 1],
            recv_sem=recv_sems.at[k - 1],
            device_id={axis: peer},
            device_id_type=MESH,
        )
        sends.append((peer, copy))
        if downward:
            pl.when(peer < me)(copy.start)
        else:
            copy.start()
    for k in range(1, n):
        source = lax.rem(me + n - k, n)
        incoming = pltpu.make_async_remote_copy(
            src_ref=src_ref.at[source] if per_peer else src_ref,
            dst_ref=out_ref.at[source],
            send_sem=send_sems.at[k - 1],
            recv_sem=recv_sems.at[k - 1],
            device_id={axis: source},
            device_id_type=MESH,
        )
        if downward:
            pl.when(source > me)(incoming.wait_recv)
        else:
            incoming.wait_recv()
    for peer, copy in sends:
        if downward:
            pl.when(peer < me)(copy.wait_send)
        else:
            copy.wait_send()


def exchange(x, axis, n, per_peer, collective_id, downward=False):
    block = x.shape[1:] if per_peer else x.shape
    nbytes = math.prod(block) * x.dtype.itemsize
    return pl.pallas_call(
        functools.partial(_exchange_body, axis, n, per_peer, downward),
        out_shape=jax.ShapeDtypeStruct((n,) + tuple(block), x.dtype),
        in_specs=[pl.BlockSpec(memory_space=pl.ANY)],
        out_specs=pl.BlockSpec(memory_space=pl.ANY),
        scratch_shapes=[pltpu.SemaphoreType.DMA((n - 1,)), pltpu.SemaphoreType.DMA((n - 1,))],
        compiler_params=pltpu.CompilerParams(collective_id=collective_id, has_side_effects=True),
        cost_estimate=pl.CostEstimate(flops=0, transcendentals=0, bytes_accessed=2 * (n - 1) * nbytes),
    )(x)


def gather_axis(x, axis, n, collective_id):
    got = exchange(x, axis, n, False, collective_id)
    return lax.dynamic_update_slice_in_dim(got, x[None], lax.axis_index(axis), 0)


def sum_axis(x, axis, collective_id):
    got = exchange(x, axis, 2, False, collective_id)
    me = lax.axis_index(axis)
    other = lax.dynamic_index_in_dim(got, 1 - me, 0, keepdims=False)
    return x.astype(jnp.float32) + other.astype(jnp.float32)


def _pair_add_body(me_ref, own_ref, other_ref, out_ref):
    out_ref[...] = (own_ref[...].astype(jnp.float32) + other_ref[...].astype(jnp.float32)).astype(out_ref.dtype)


def core_reduce(x, collective_id):
    got = exchange(x, "core", 2, True, collective_id)
    me = lax.axis_index("core")
    count = x.shape[1]
    rest = x.shape[2:]
    zeros = (0,) * len(rest)
    item_bytes = math.prod(rest) * x.dtype.itemsize
    step = max(
        [1] + [d for d in range(1, count + 1) if count % d == 0 and d * item_bytes <= 3 * 1024 * 1024 // 2]
    )
    grid_spec = pltpu.PrefetchScalarGridSpec(
        num_scalar_prefetch=1,
        grid=(count // step,),
        in_specs=[
            pl.BlockSpec((None, step) + rest, lambda i, c: (c[0], i) + zeros),
            pl.BlockSpec((None, step) + rest, lambda i, c: (1 - c[0], i) + zeros),
        ],
        out_specs=pl.BlockSpec((step,) + rest, lambda i, c: (i,) + zeros),
    )
    return pl.pallas_call(
        _pair_add_body,
        grid_spec=grid_spec,
        out_shape=jax.ShapeDtypeStruct(x.shape[1:], jnp.bfloat16),
        compiler_params=pltpu.CompilerParams(vmem_limit_bytes=56 * 1024 * 1024),
        cost_estimate=pl.CostEstimate(flops=x.size // 2, transcendentals=0, bytes_accessed=x.size * 3),
    )(jnp.reshape(me, (1,)).astype(jnp.int32), x, got)


def scatter_sum_downward(x, axis, n, collective_id):
    got = exchange(x, axis, n, True, collective_id, downward=True)
    me = lax.axis_index(axis)
    own = lax.dynamic_index_in_dim(x, me, 0, keepdims=False).astype(jnp.float32)
    above = (jnp.arange(n, dtype=jnp.int32) > me).reshape((n,) + (1,) * (x.ndim - 1))
    return own + jnp.sum(jnp.where(above, got.astype(jnp.float32), 0.0), axis=0)


def _flash_body(groups, ctx_ref, q_ref, k_ref, v_ref, qseg_ref, qpos_ref, kseg_ref, o_ref, lse_ref, qs_sc, m_sc, l_sc, acc_sc):
    f32 = jnp.float32
    block = pl.program_id(1)
    depth = HEAD_SIZE
    pair = k_ref.shape[2] // depth
    tokens = q_ref.shape[0]

    @pl.when(block == 0)
    def _():
        m_sc[...] = jnp.full_like(m_sc, NEGATIVE)
        l_sc[...] = jnp.zeros_like(l_sc)
        acc_sc[...] = jnp.zeros_like(acc_sc)
        scale = jnp.asarray(1.0 / math.sqrt(HEAD_SIZE), q_ref.dtype)
        for kk in range(pair):
            for gi in range(groups):
                i = kk * groups + gi
                qs_sc[kk, gi * tokens : (gi + 1) * tokens, :] = q_ref[:, i * depth : (i + 1) * depth] * scale

    @pl.when(block <= ctx_ref[0])
    def _():
        width = k_ref.shape[1]
        key_pos = block * width + lax.broadcasted_iota(jnp.int32, (1, width), 1)
        allowed = (qseg_ref[...] == kseg_ref[...]) & (key_pos <= qpos_ref[...])
        for kk in range(pair):
            keys = k_ref[0, :, kk * depth : (kk + 1) * depth]
            values = v_ref[0, :, kk * depth : (kk + 1) * depth]
            scores = lax.dot_general(
                qs_sc[kk], keys, (((1,), (1,)), ((), ())), preferred_element_type=f32
            )
            scores = jnp.where(allowed, scores, NEGATIVE)
            m_old = m_sc[kk]
            m_new = jnp.maximum(m_old, jnp.max(scores, axis=1, keepdims=True))
            alpha = jnp.exp(m_old - m_new)
            weights = jnp.where(allowed, jnp.exp(scores - m_new), 0.0)
            l_sc[kk] = alpha * l_sc[kk] + jnp.sum(weights, axis=1, keepdims=True)
            acc_sc[kk] = alpha * acc_sc[kk] + jnp.dot(
                weights.astype(jnp.bfloat16), values, preferred_element_type=f32
            )
            m_sc[kk] = m_new

    @pl.when(block == pl.num_programs(1) - 1)
    def _():
        for kk in range(pair):
            for gi in range(groups):
                i = kk * groups + gi
                rows = slice(gi * tokens, (gi + 1) * tokens)
                o_ref[:, i * depth : (i + 1) * depth] = acc_sc[kk, rows, :] / l_sc[kk, rows, :]
                lse_ref[0, :, i : i + 1] = m_sc[kk, rows, :] + jnp.log(l_sc[kk, rows, :])


def flash_forward(ctx_index, q, kv, qseg, qpos, kseg, groups):
    tokens, q_width = q.shape
    blocks, width, kv_width = kv.shape
    pair = 2
    pairs = kv_width // (2 * pair * HEAD_SIZE)
    heads_step = pair * groups
    f32 = jnp.float32
    capped = lambda p, b, c: (jnp.minimum(b, c[0]), 0, p)
    grid_spec = pltpu.PrefetchScalarGridSpec(
        num_scalar_prefetch=1,
        grid=(pairs, blocks),
        in_specs=[
            pl.BlockSpec((tokens, heads_step * HEAD_SIZE), lambda p, b, c: (0, p)),
            pl.BlockSpec((1, width, pair * HEAD_SIZE), capped),
            pl.BlockSpec((1, width, pair * HEAD_SIZE), lambda p, b, c: (jnp.minimum(b, c[0]), 0, pairs + p)),
            pl.BlockSpec((groups * tokens, 1), lambda p, b, c: (0, 0)),
            pl.BlockSpec((groups * tokens, 1), lambda p, b, c: (0, 0)),
            pl.BlockSpec((1, width), lambda p, b, c: (0, jnp.minimum(b, c[0]))),
        ],
        out_specs=[
            pl.BlockSpec((tokens, heads_step * HEAD_SIZE), lambda p, b, c: (0, p)),
            pl.BlockSpec((1, tokens, heads_step), lambda p, b, c: (p, 0, 0)),
        ],
        scratch_shapes=[
            pltpu.VMEM((pair, groups * tokens, HEAD_SIZE), q.dtype),
            pltpu.VMEM((pair, groups * tokens, 1), f32),
            pltpu.VMEM((pair, groups * tokens, 1), f32),
            pltpu.VMEM((pair, groups * tokens, HEAD_SIZE), f32),
        ],
    )
    return pl.pallas_call(
        functools.partial(_flash_body, groups),
        grid_spec=grid_spec,
        out_shape=[
            jax.ShapeDtypeStruct((tokens, q_width), f32),
            jax.ShapeDtypeStruct((pairs, tokens, heads_step), f32),
        ],
        compiler_params=pltpu.CompilerParams(
            dimension_semantics=("arbitrary", "arbitrary"), vmem_limit_bytes=48 * 1024 * 1024
        ),
        cost_estimate=pl.CostEstimate(
            flops=tokens * q_width * blocks * width * 4,
            transcendentals=tokens * (q_width // HEAD_SIZE) * blocks * width,
            bytes_accessed=(q.size + kv.size) * 2 + tokens * q_width * 4,
        ),
    )(jnp.reshape(ctx_index, (1,)).astype(jnp.int32), q, kv, kv, qseg, qpos, kseg)

def _chain_down_body(axis, n, x_ref, out_ref, recv, send, send_sems, recv_sems):
    f32 = jnp.float32
    me = lax.axis_index(axis)
    below = lax.rem(me + n - 1, n)
    above = lax.rem(me + 1, n)
    barrier = pltpu.get_barrier_semaphore()
    pl.semaphore_signal(barrier, 1, device_id={axis: below}, device_id_type=MESH)
    pl.semaphore_signal(barrier, 1, device_id={axis: above}, device_id_type=MESH)
    pl.semaphore_wait(barrier, 2)
    copies = []
    for j in range(n - 1):
        copy = pltpu.make_async_remote_copy(
            src_ref=send.at[j],
            dst_ref=recv.at[j],
            send_sem=send_sems.at[j],
            recv_sem=recv_sems.at[j],
            device_id={axis: below},
            device_id_type=MESH,
        )
        copies.append(copy)

        @pl.when((j < me) & (me < n - 1))
        def _():
            copy.wait_recv()
            send[j] = (x_ref[j].astype(f32) + recv[j].astype(f32)).astype(send.dtype)

        @pl.when((j < me) & (me == n - 1))
        def _():
            send[j] = x_ref[j]

        @pl.when(j < me)
        def _():
            copy.start()

        @pl.when(j == me)
        def _():
            copy.wait_recv()
            out_ref[...] = x_ref[j].astype(f32) + recv[j].astype(f32)

    @pl.when(me == n - 1)
    def _():
        out_ref[...] = x_ref[n - 1].astype(f32)

    for j in range(n - 1):
        pl.when(j < me)(copies[j].wait_send)


def chain_sum_down(x, axis, n, collective_id):
    _, rows, cols = x.shape
    return pl.pallas_call(
        functools.partial(_chain_down_body, axis, n),
        out_shape=jax.ShapeDtypeStruct((rows, cols), jnp.float32),
        in_specs=[pl.BlockSpec(memory_space=pltpu.VMEM)],
        out_specs=pl.BlockSpec(memory_space=pltpu.VMEM),
        scratch_shapes=[
            pltpu.VMEM((n - 1, rows, cols), x.dtype),
            pltpu.VMEM((n - 1, rows, cols), x.dtype),
            pltpu.SemaphoreType.DMA((n - 1,)),
            pltpu.SemaphoreType.DMA((n - 1,)),
        ],
        compiler_params=pltpu.CompilerParams(
            collective_id=collective_id, has_side_effects=True, vmem_limit_bytes=32 * 1024 * 1024
        ),
        cost_estimate=pl.CostEstimate(
            flops=(n - 1) * rows * cols, transcendentals=0, bytes_accessed=3 * n * rows * cols * 2
        ),
    )(x)


def _chain_up_body(axis, n, x_ref, out_ref, send_sems, recv_sems):
    me = lax.axis_index(axis)
    below = lax.rem(me + n - 1, n)
    above = lax.rem(me + 1, n)
    barrier = pltpu.get_barrier_semaphore()
    pl.semaphore_signal(barrier, 1, device_id={axis: below}, device_id_type=MESH)
    pl.semaphore_signal(barrier, 1, device_id={axis: above}, device_id_type=MESH)
    pl.semaphore_wait(barrier, 2)
    own = pltpu.make_async_remote_copy(
        src_ref=x_ref,
        dst_ref=out_ref.at[me],
        send_sem=send_sems.at[me],
        recv_sem=recv_sems.at[me],
        device_id={axis: above},
        device_id_type=MESH,
    )
    pl.when(me < n - 1)(own.start)
    forwards = []
    for k in range(1, n):
        block = jnp.maximum(me - k, 0)
        incoming = pltpu.make_async_remote_copy(
            src_ref=out_ref.at[block],
            dst_ref=out_ref.at[block],
            send_sem=send_sems.at[block],
            recv_sem=recv_sems.at[block],
            device_id={axis: below},
            device_id_type=MESH,
        )
        forward = pltpu.make_async_remote_copy(
            src_ref=out_ref.at[block],
            dst_ref=out_ref.at[block],
            send_sem=send_sems.at[block],
            recv_sem=recv_sems.at[block],
            device_id={axis: above},
            device_id_type=MESH,
        )
        forwards.append((k, forward))
        pl.when(k <= me)(incoming.wait_recv)
        pl.when((k <= me) & (me < n - 1))(forward.start)
    pl.when(me < n - 1)(own.wait_send)
    for k, forward in forwards:
        pl.when((k <= me) & (me < n - 1))(forward.wait_send)


def gather_up(x, axis, n, collective_id):
    got = pl.pallas_call(
        functools.partial(_chain_up_body, axis, n),
        out_shape=jax.ShapeDtypeStruct((n,) + x.shape, x.dtype),
        in_specs=[pl.BlockSpec(memory_space=pl.ANY)],
        out_specs=pl.BlockSpec(memory_space=pl.ANY),
        scratch_shapes=[pltpu.SemaphoreType.DMA((n,)), pltpu.SemaphoreType.DMA((n,))],
        compiler_params=pltpu.CompilerParams(collective_id=collective_id, has_side_effects=True),
        cost_estimate=pl.CostEstimate(
            flops=0, transcendentals=0, bytes_accessed=2 * (n - 1) * x.size * x.dtype.itemsize
        ),
    )(x)
    me = lax.axis_index(axis)
    below = (jnp.arange(n, dtype=jnp.int32) < me).reshape((n,) + (1,) * x.ndim)
    got = jnp.where(below, got, jnp.zeros_like(got))
    return lax.dynamic_update_slice_in_dim(got, x[None], me, 0)


def _attend_block(groups, kv_heads, q_sc, kv_buf, qseg_ref, qpos_ref, kseg_ref, m_sc, l_sc, acc_sc, block):
    f32 = jnp.float32
    depth = HEAD_SIZE
    width = kv_buf.shape[0]
    start = pl.multiple_of(block * width, width)
    key_pos = start + lax.broadcasted_iota(jnp.int32, (1, width), 1)
    allowed = (qseg_ref[...] == kseg_ref[:, pl.ds(start, width)]) & (key_pos <= qpos_ref[...])
    for kk in range(kv_heads):
        keys = kv_buf[:, kk * depth : (kk + 1) * depth]
        values = kv_buf[:, (kv_heads + kk) * depth : (kv_heads + kk + 1) * depth]
        scores = lax.dot_general(q_sc[kk], keys, (((1,), (1,)), ((), ())), preferred_element_type=f32)
        scores = jnp.where(allowed, scores, NEGATIVE)
        m_old = m_sc[kk]
        m_new = jnp.maximum(m_old, jnp.max(scores, axis=1, keepdims=True))
        alpha = jnp.exp(m_old - m_new)
        weights = jnp.where(allowed, jnp.exp(scores - m_new), 0.0)
        l_sc[kk] = alpha * l_sc[kk] + jnp.sum(weights, axis=1, keepdims=True)
        acc_sc[kk] = alpha * acc_sc[kk] + jnp.dot(
            weights.astype(jnp.bfloat16), values, preferred_element_type=f32
        )
        m_sc[kk] = m_new


def _gather_attend_body(
    axis, n, groups, q_ref, own_ref, qseg_ref, qpos_ref, kseg_ref,
    kv_ref, o_ref, lse_ref,
    q_sc, m_sc, l_sc, acc_sc, kv_buf, send_sems, recv_sems, copy_sem,
):
    depth = HEAD_SIZE
    tokens = q_ref.shape[0]
    kv_heads = own_ref.shape[1] // (2 * depth)
    me = lax.axis_index(axis)
    below = lax.rem(me + n - 1, n)
    above = lax.rem(me + 1, n)
    barrier = pltpu.get_barrier_semaphore()
    pl.semaphore_signal(barrier, 1, device_id={axis: below}, device_id_type=MESH)
    pl.semaphore_signal(barrier, 1, device_id={axis: above}, device_id_type=MESH)
    pl.semaphore_wait(barrier, 2)
    own = pltpu.make_async_remote_copy(
        src_ref=own_ref,
        dst_ref=kv_ref.at[me],
        send_sem=send_sems.at[me],
        recv_sem=recv_sems.at[me],
        device_id={axis: above},
        device_id_type=MESH,
    )
    pl.when(me < n - 1)(own.start)

    m_sc[...] = jnp.full_like(m_sc, NEGATIVE)
    l_sc[...] = jnp.zeros_like(l_sc)
    acc_sc[...] = jnp.zeros_like(acc_sc)
    scale = jnp.asarray(1.0 / math.sqrt(HEAD_SIZE), q_ref.dtype)
    for kk in range(kv_heads):
        for gi in range(groups):
            i = kk * groups + gi
            q_sc[kk, gi * tokens : (gi + 1) * tokens, :] = q_ref[:, i * depth : (i + 1) * depth] * scale

    local = pltpu.make_async_copy(own_ref, kv_buf, copy_sem)
    local.start()
    local.wait()
    _attend_block(groups, kv_heads, q_sc, kv_buf, qseg_ref, qpos_ref, kseg_ref, m_sc, l_sc, acc_sc, me)

    def step(k, carry):
        block = me - k
        incoming = pltpu.make_async_remote_copy(
            src_ref=kv_ref.at[block],
            dst_ref=kv_ref.at[block],
            send_sem=send_sems.at[block],
            recv_sem=recv_sems.at[block],
            device_id={axis: below},
            device_id_type=MESH,
        )
        incoming.wait_recv()
        forward = pltpu.make_async_remote_copy(
            src_ref=kv_ref.at[block],
            dst_ref=kv_ref.at[block],
            send_sem=send_sems.at[block],
            recv_sem=recv_sems.at[block],
            device_id={axis: above},
            device_id_type=MESH,
        )
        pl.when(me < n - 1)(forward.start)
        fetch = pltpu.make_async_copy(kv_ref.at[block], kv_buf, copy_sem)
        fetch.start()
        fetch.wait()
        _attend_block(groups, kv_heads, q_sc, kv_buf, qseg_ref, qpos_ref, kseg_ref, m_sc, l_sc, acc_sc, block)
        return carry

    lax.fori_loop(1, me + 1, step, 0)

    for kk in range(kv_heads):
        for gi in range(groups):
            i = kk * groups + gi
            rows = slice(gi * tokens, (gi + 1) * tokens)
            o_ref[:, i * depth : (i + 1) * depth] = acc_sc[kk, rows, :] / l_sc[kk, rows, :]
            lse_ref[:, i : i + 1] = m_sc[kk, rows, :] + jnp.log(l_sc[kk, rows, :])

    pl.when(me < n - 1)(own.wait_send)

    def drain(k, carry):
        block = me - k
        pltpu.make_async_remote_copy(
            src_ref=kv_ref.at[block],
            dst_ref=kv_ref.at[block],
            send_sem=send_sems.at[block],
            recv_sem=recv_sems.at[block],
            device_id={axis: above},
            device_id_type=MESH,
        ).wait_send()
        return carry

    lax.fori_loop(1, jnp.where(me < n - 1, me + 1, 1), drain, 0)


def gather_attend(q, own, qseg, qpos, kseg, axis, n, groups, collective_id):
    tokens, q_width = q.shape
    rows, kv_width = own.shape
    heads = q_width // HEAD_SIZE
    kv_heads = kv_width // (2 * HEAD_SIZE)
    f32 = jnp.float32
    vmem = pl.BlockSpec(memory_space=pltpu.VMEM)
    anywhere = pl.BlockSpec(memory_space=pl.ANY)
    kv_all, attn, lse = pl.pallas_call(
        functools.partial(_gather_attend_body, axis, n, groups),
        out_shape=[
            jax.ShapeDtypeStruct((n, rows, kv_width), own.dtype),
            jax.ShapeDtypeStruct((tokens, q_width), f32),
            jax.ShapeDtypeStruct((tokens, heads), f32),
        ],
        in_specs=[vmem, anywhere, vmem, vmem, vmem],
        out_specs=[anywhere, vmem, vmem],
        scratch_shapes=[
            pltpu.VMEM((kv_heads, groups * tokens, HEAD_SIZE), q.dtype),
            pltpu.VMEM((kv_heads, groups * tokens, 1), f32),
            pltpu.VMEM((kv_heads, groups * tokens, 1), f32),
            pltpu.VMEM((kv_heads, groups * tokens, HEAD_SIZE), f32),
            pltpu.VMEM((rows, kv_width), own.dtype),
            pltpu.SemaphoreType.DMA((n,)),
            pltpu.SemaphoreType.DMA((n,)),
            pltpu.SemaphoreType.DMA(()),
        ],
        compiler_params=pltpu.CompilerParams(
            collective_id=collective_id, has_side_effects=True, vmem_limit_bytes=48 * 1024 * 1024
        ),
        cost_estimate=pl.CostEstimate(
            flops=tokens * q_width * n * rows * 4,
            transcendentals=tokens * heads * n * rows,
            bytes_accessed=2 * n * own.size * own.dtype.itemsize + tokens * q_width * 6,
        ),
    )(q, own, qseg, qpos, kseg)
    me = lax.axis_index(axis)
    below = (jnp.arange(n, dtype=jnp.int32) < me).reshape((n, 1, 1))
    kv_all = jnp.where(below, kv_all, jnp.zeros_like(kv_all))
    return attn, lse, lax.dynamic_update_slice_in_dim(kv_all, own[None], me, 0)


def per_device(
    dpx_count,
    hidden_in,
    attn_gain,
    q_weight,
    key_matrix,
    value_matrix,
    o_weight,
    moe_gain,
    router_weight,
    gate_weight,
    up_weight,
    down_weight,
    segments,
    expert_picks,
    output_grad,
):
    bf16 = jnp.bfloat16
    f32 = jnp.float32
    token_count = hidden_in.shape[0]
    ctx_index = lax.axis_index("ctx")
    heads_local = q_weight.shape[1] // HEAD_SIZE
    kv_local = key_matrix.shape[1] // HEAD_SIZE
    group_size = heads_local // kv_local
    score_scale = 1.0 / math.sqrt(HEAD_SIZE)
    token_positions = ctx_index * token_count + jnp.arange(token_count, dtype=jnp.int32)
    segment_here = lax.dynamic_slice_in_dim(segments, ctx_index * token_count, token_count)
    inputs_f32 = hidden_in.astype(f32)
    o_full = lax.all_gather(o_weight, "tensor", axis=0, tiled=False)
    normed_f32, scale_one = normalize(inputs_f32, attn_gain)
    normed_one = normed_f32.astype(bf16)
    query_rows = jnp.dot(normed_one, q_weight, preferred_element_type=f32).reshape(
        token_count, heads_local, HEAD_SIZE
    )
    keys_raw = jnp.dot(normed_one, key_matrix, preferred_element_type=f32).reshape(
        token_count, kv_local, HEAD_SIZE
    )
    values_raw = jnp.dot(normed_one, value_matrix, preferred_element_type=f32)
    query_grouped = (
        apply_rotary(query_rows, token_positions, 1.0)
        .astype(bf16)
        .reshape(token_count, kv_local, group_size, HEAD_SIZE)
    )
    key_flat = (
        apply_rotary(keys_raw, token_positions, 1.0)
        .astype(bf16)
        .reshape(token_count, kv_local * HEAD_SIZE)
    )
    value_flat = values_raw.astype(bf16)

    def piece_mask(piece_rows):
        key_pos = jnp.arange(piece_rows, dtype=jnp.int32)
        return (segment_here[:, None] == segments[None, :]) & (
            key_pos[None, :] <= token_positions[:, None]
        )

    ctx_count = segments.shape[0] // token_count
    attn_flat, lse_heads, kv_both = gather_attend(
        query_grouped.reshape(token_count, heads_local * HEAD_SIZE),
        jnp.concatenate([key_flat, value_flat], axis=1),
        jnp.tile(segment_here, group_size)[:, None],
        jnp.tile(token_positions, group_size)[:, None],
        segments[None, :],
        "ctx",
        ctx_count,
        group_size,
        1,
    )
    piece_rows = ctx_count * token_count
    kv_width = kv_local * HEAD_SIZE
    key_piece = kv_both[:, :, :kv_width].reshape(piece_rows, kv_local, HEAD_SIZE)
    value_piece = kv_both[:, :, kv_width:].reshape(piece_rows, kv_local, HEAD_SIZE)
    attn_grouped = jnp.transpose(
        attn_flat.reshape(token_count, kv_local, group_size, HEAD_SIZE), (1, 2, 0, 3)
    )
    log_sum = jnp.transpose(lse_heads.reshape(token_count, kv_local, group_size), (1, 2, 0))
    attn_bf = attn_flat.astype(bf16)
    tensor_count = o_weight.shape[0] // o_weight.shape[1]
    attn_all = gather_axis(attn_bf, "tensor", tensor_count, 2)
    mixed_attn = lax.dot_general(
        attn_all, o_full, (((0, 2), (0, 2)), ((), ())), preferred_element_type=f32
    )
    resid = inputs_f32 + mixed_attn
    normed_two_f32, scale_two = normalize(resid, moe_gain)
    normed_two = normed_two_f32.astype(bf16)
    logits = jnp.dot(normed_two, router_weight, preferred_element_type=f32)
    expert_range = jnp.arange(NEXP, dtype=jnp.int32)
    picked_onehot = expert_picks[:, :, None] == expert_range[None, None, :]
    picked = jnp.sum(jnp.where(picked_onehot, logits[:, None, :], 0.0), axis=2)
    gate_probs = jax.nn.softmax(picked, axis=-1)
    gates_dense = jnp.sum(jnp.where(picked_onehot, gate_probs[:, :, None], 0.0), axis=1)
    gates_by_expert = jnp.transpose(gates_dense)
    cot_bf = output_grad
    gcol = gates_dense
    grad_gate, grad_up, grad_down, hid_all, dga_all, dua_all = expert_grad_kernel(
        normed_two,
        cot_bf,
        gcol,
        gate_weight,
        up_weight,
        down_weight,
        dpx_count,
    )
    gate_half = core_reduce(grad_gate, 8)
    gate_half, hid_all, dga_all, dua_all = lax.optimization_barrier(
        (gate_half, hid_all, dga_all, dua_all)
    )
    moe_acc, gate_parts, moe_grad_rows = expert_rows_kernel(
        hid_all, dga_all, dua_all, cot_bf, gcol, gate_weight, up_weight, down_weight
    )
    cot_f32 = output_grad.astype(f32)
    moe_total = sum_axis(moe_acc.astype(bf16), "tensor", 3)
    output = (resid + moe_total).astype(bf16)
    grad_rows_all = moe_grad_rows
    gate_parts = gate_parts[:, :, 0]
    grad_gate_out, grad_up_out, grad_down_out = [
        lax.psum_scatter(
            g.reshape(g.shape[0], -1, g.shape[3]), ("dpx", "ctx"), scatter_dimension=1, tiled=True
        )
        for g in (gate_half, core_reduce(grad_up, 9), core_reduce(grad_down, 10))
    ]
    gate_pair = jnp.sum(
        jnp.where(picked_onehot, jnp.transpose(gate_parts)[:, None, :], 0.0), axis=2
    )
    moe_summed = sum_axis(grad_rows_all.astype(bf16), "tensor", 4)
    gate_summed = sum_axis(gate_pair.astype(bf16), "tensor", 5)
    grad_picked = gate_probs * (
        gate_summed - jnp.sum(gate_probs * gate_summed, axis=1, keepdims=True)
    )
    grad_logits = jnp.sum(jnp.where(picked_onehot, grad_picked[:, :, None], 0.0), axis=1).astype(
        bf16
    )
    grad_router = contract_rows(normed_two, grad_logits)
    grad_normed_two = moe_summed + contract_cols(grad_logits, router_weight)
    grad_two_rows, grad_moe_gain = norm_backward(resid, scale_two, moe_gain, grad_normed_two)
    grad_resid = cot_f32 + grad_two_rows
    grad_mix = grad_resid.astype(bf16)
    grad_o = contract_rows(grad_mix, attn_bf)
    grad_attn = jnp.dot(grad_mix, o_weight, preferred_element_type=f32).astype(bf16)
    grad_attn_grouped = jnp.transpose(
        grad_attn.reshape(token_count, kv_local, group_size, HEAD_SIZE), (1, 2, 0, 3)
    )
    row_delta = jnp.sum(grad_attn_grouped.astype(f32) * attn_grouped, axis=-1)
    allowed = piece_mask(piece_rows)
    scores = (
        jnp.einsum("tkgd,nkd->kgtn", query_grouped, key_piece, preferred_element_type=f32)
        * score_scale
    )
    probability = jnp.where(allowed, jnp.exp(scores - log_sum[..., None]), 0.0)
    grad_probs = jnp.einsum(
        "kgtd,nkd->kgtn", grad_attn_grouped, value_piece, preferred_element_type=f32
    )
    grad_scores = (probability * (grad_probs - row_delta[..., None])).astype(bf16)
    grad_query = score_scale * jnp.einsum(
        "kgtn,nkd->kgtd", grad_scores, key_piece, preferred_element_type=f32
    )
    key_part = score_scale * jnp.einsum(
        "kgtn,tkgd->nkd", grad_scores, query_grouped, preferred_element_type=f32
    )
    value_part = jnp.einsum(
        "kgtn,kgtd->nkd", probability.astype(bf16), grad_attn_grouped, preferred_element_type=f32
    )
    grad_keys_all = key_part.reshape(piece_rows, kv_local * HEAD_SIZE)
    grad_values_all = value_part.reshape(piece_rows, kv_local * HEAD_SIZE)
    back_state = (grad_query, grad_keys_all, grad_values_all)
    grad_query, grad_keys_all, grad_values_all = back_state
    grad_kv_here = chain_sum_down(
        jnp.concatenate([grad_keys_all, grad_values_all], axis=1)
        .astype(bf16)
        .reshape(ctx_count, token_count, 2 * kv_width),
        "ctx",
        ctx_count,
        6,
    )
    grad_keys_here = grad_kv_here[:, :kv_width]
    grad_values_here = grad_kv_here[:, kv_width:]
    grad_query_rows = jnp.transpose(grad_query, (2, 0, 1, 3)).reshape(
        token_count, heads_local, HEAD_SIZE
    )
    grad_query_bf = (
        apply_rotary(grad_query_rows, token_positions, -1.0)
        .reshape(token_count, heads_local * HEAD_SIZE)
        .astype(bf16)
    )
    grad_key_bf = (
        apply_rotary(
            grad_keys_here.reshape(token_count, kv_local, HEAD_SIZE), token_positions, -1.0
        )
        .reshape(token_count, kv_local * HEAD_SIZE)
        .astype(bf16)
    )
    grad_value_bf = grad_values_here.astype(bf16)
    grad_q = contract_rows(normed_one, grad_query_bf)
    grad_k = contract_rows(normed_one, grad_key_bf)
    grad_v = contract_rows(normed_one, grad_value_bf)
    partial_one = (
        contract_cols(grad_query_bf, q_weight)
        + contract_cols(grad_key_bf, key_matrix)
        + contract_cols(grad_value_bf, value_matrix)
    )
    grad_normed_one = sum_axis(partial_one.astype(bf16), "tensor", 7)
    grad_one_rows, grad_attn_gain = norm_backward(inputs_f32, scale_one, attn_gain, grad_normed_one)
    input_grad = grad_resid + grad_one_rows
    q_cols, o_cols, k_cols = grad_q.shape[1], grad_o.shape[1], grad_k.shape[1]
    small = jnp.concatenate(
        [
            grad_router,
            grad_attn_gain[:, None],
            grad_moe_gain[:, None],
            jnp.zeros((grad_router.shape[0], 128 - grad_router.shape[1] - 2), f32),
        ],
        axis=1,
    )
    dense_all = jnp.concatenate(
        [grad_q, grad_o, grad_k, grad_v, small], axis=1
    ).astype(bf16)
    width = dense_all.shape[0]
    dense_all = jnp.transpose(
        dense_all.reshape(dpx_count, 2, width // (2 * dpx_count), dense_all.shape[1]), (1, 0, 2, 3)
    )
    dense_half = core_reduce(dense_all, 11)
    dense_half, grad_gate_out, grad_up_out, grad_down_out = lax.optimization_barrier(
        (dense_half, grad_gate_out, grad_up_out, grad_down_out)
    )
    grad_gate_out, grad_up_out, grad_down_out = (
        grad_gate_out.astype(f32),
        grad_up_out.astype(f32),
        grad_down_out.astype(f32),
    )
    dense_here = lax.psum_scatter(
        dense_half.reshape(-1, dense_half.shape[-1]), ("dpx", "ctx"), scatter_dimension=0, tiled=True
    ).astype(f32)
    spans = [q_cols, o_cols, k_cols, k_cols, router_weight.shape[1], 1, 1]
    cuts = [sum(spans[:i]) for i in range(len(spans) + 1)]
    pieces_out = [dense_here[:, cuts[i] : cuts[i + 1]] for i in range(len(spans))]
    dense_out = (
        pieces_out[5][:, 0],
        pieces_out[0],
        pieces_out[2],
        pieces_out[3],
        pieces_out[1],
        pieces_out[6][:, 0],
        pieces_out[4],
    )
    return (
        output,
        input_grad,
        dense_out[0],
        dense_out[1],
        dense_out[2],
        dense_out[3],
        dense_out[4],
        dense_out[5],
        dense_out[6],
        grad_gate_out,
        grad_up_out,
        grad_down_out,
    )


def solution(mesh):
    dp_count, ctx_count, tensor_count = (mesh.shape[a] for a in ("dp", "ctx", "tensor"))
    split_mesh = jax.sharding.Mesh(
        mesh.devices.reshape(dp_count // 2, 2, ctx_count, tensor_count), ("dpx", "core", "ctx", "tensor")
    )
    return jax.shard_map(
        functools.partial(per_device, dp_count // 2),
        mesh=split_mesh,
        in_specs=(
            P(("dpx", "core", "ctx"), None),
            P(),
            P(None, "tensor"),
            P(None, "tensor"),
            P(None, "tensor"),
            P(None, "tensor"),
            P(),
            P(),
            P(None, None, "tensor"),
            P(None, None, "tensor"),
            P(None, None, "tensor"),
            P(("dpx", "core")),
            P(("dpx", "core", "ctx"), None),
            P(("dpx", "core", "ctx"), None),
        ),
        out_specs=(
            P(("dpx", "core", "ctx"), None),
            P(("dpx", "core", "ctx"), None),
            P(("dpx", "core", "ctx")),
            P(("dpx", "core", "ctx"), "tensor"),
            P(("dpx", "core", "ctx"), "tensor"),
            P(("dpx", "core", "ctx"), "tensor"),
            P(("dpx", "core", "ctx"), "tensor"),
            P(("dpx", "core", "ctx")),
            P(("dpx", "core", "ctx"), None),
            P(None, ("dpx", "core", "ctx"), "tensor"),
            P(None, ("dpx", "core", "ctx"), "tensor"),
            P(None, ("dpx", "core", "ctx"), "tensor"),
        ),
        check_vma=False,
    )
```

```python
import functools
import math

import jax
import jax.numpy as jnp
from jax import lax
from jax.experimental import pallas as pl
from jax.experimental.pallas import tpu as pltpu
from jax.sharding import PartitionSpec as P

HEAD_SIZE = 64
NEXP = 24
CAP = 341


EPSILON = 1e-06
ROPE_BASE = 10000.0
NEGATIVE = -1e30
HIGHEST = lax.Precision.HIGHEST


def normalize(rows, gain):
    scale_inv = lax.rsqrt(jnp.mean(rows * rows, axis=-1, keepdims=True) + EPSILON)
    return (rows * scale_inv * gain, scale_inv)


def norm_backward(rows, scale_inv, gain, grad_normed):
    weighted = gain * grad_normed
    grad_gain = jnp.sum(grad_normed * rows * scale_inv, axis=0)
    inner_mean = jnp.mean(weighted * rows, axis=-1, keepdims=True)
    grad_rows = scale_inv * weighted - rows * scale_inv * scale_inv * scale_inv * inner_mean
    return (grad_rows, grad_gain)


def apply_rotary(value_rows, token_positions, direction):
    half_dim = value_rows.shape[-1] // 2
    frequency = ROPE_BASE ** (-jnp.arange(half_dim, dtype=jnp.float32) / half_dim)
    angles = token_positions.astype(jnp.float32)[:, None] * frequency[None, :]
    cosine = jnp.cos(angles)[:, None, :]
    sine_part = direction * jnp.sin(angles)[:, None, :]
    first_half = value_rows[..., :half_dim]
    second = value_rows[..., half_dim:]
    return jnp.concatenate(
        [first_half * cosine - second * sine_part, second * cosine + first_half * sine_part],
        axis=-1,
    )


def contract_rows(left, right):
    return lax.dot_general(
        left, right, (((0,), (0,)), ((), ())), preferred_element_type=jnp.float32
    )


def contract_rows_exact(left, right):
    return lax.dot_general(
        left, right, (((0,), (0,)), ((), ())), precision=HIGHEST, preferred_element_type=jnp.float32
    )


def contract_cols(left, right):
    return lax.dot_general(
        left, right, (((1,), (1,)), ((), ())), preferred_element_type=jnp.float32
    )


def _store_split(out_ref, value, slot=0):
    cores, _, groups, rows, _ = out_ref.shape
    for x in range(groups):
        for c in range(cores):
            start = (x * cores + c) * rows
            out_ref[c, slot, x] = value[start : start + rows].astype(out_ref.dtype)


def _gate_column(gates_ref, expert=None):
    gates = gates_ref[...]
    lane = lax.broadcasted_iota(jnp.int32, gates.shape, 1)
    expert = pl.program_id(0) if expert is None else expert
    return jnp.sum(jnp.where(lane == expert, gates, 0.0), axis=1, keepdims=True)


def _grad_body(
    n2_ref, dy_ref, gcol_ref, wg_ref, wu_ref, wd_ref,
    gg_ref, gu_ref, gd_ref, hid_ref, dga_ref, dua_ref,
):
    f32 = jnp.float32
    bf16 = jnp.bfloat16
    tn = (((0,), (0,)), ((), ()))
    n2 = n2_ref[...]
    per_step = wg_ref.shape[0]
    for i in range(per_step):
        wd = wd_ref[i]
        gate_act = jnp.dot(n2, wg_ref[i], preferred_element_type=f32)
        up_act = jnp.dot(n2, wu_ref[i], preferred_element_type=f32)
        sig = 1.0 / (1.0 + jnp.exp(-gate_act))
        silu = gate_act * sig
        hidden = (silu * up_act).astype(bf16)
        hid_ref[i] = hidden
        gate = _gate_column(gcol_ref, pl.program_id(0) * per_step + i)
        grad_hidden = gate * jnp.dot(dy_ref[...], wd, preferred_element_type=f32)
        gated_hidden = (gate * hidden.astype(f32)).astype(bf16)
        _store_split(gd_ref, lax.dot_general(dy_ref[...], gated_hidden, tn, preferred_element_type=f32), i)
        grad_gate_act = (grad_hidden * up_act * sig * (1.0 + gate_act * (1.0 - sig))).astype(bf16)
        grad_up_act = (grad_hidden * silu).astype(bf16)
        dga_ref[i] = grad_gate_act
        dua_ref[i] = grad_up_act
        _store_split(gg_ref, lax.dot_general(n2, grad_gate_act, tn, preferred_element_type=f32), i)
        _store_split(gu_ref, lax.dot_general(n2, grad_up_act, tn, preferred_element_type=f32), i)


def _rows_body(hid_ref, dga_ref, dua_ref, dy_ref, gcol_ref, wg_ref, wu_ref, wd_ref, acc_ref, dgate_ref, dn2_ref):
    f32 = jnp.float32
    nt = (((1,), (1,)), ((), ()))

    @pl.when(pl.program_id(0) == 0)
    def _():
        acc_ref[...] = jnp.zeros_like(acc_ref)
        dn2_ref[...] = jnp.zeros_like(dn2_ref)

    expert_out = lax.dot_general(hid_ref[0], wd_ref[0], nt, preferred_element_type=f32)
    acc_ref[...] += _gate_column(gcol_ref) * expert_out
    dgate_ref[0] = jnp.sum(expert_out * dy_ref[...].astype(f32), axis=1, keepdims=True)
    dn2_ref[...] += lax.dot_general(
        dga_ref[0], wg_ref[0], nt, preferred_element_type=f32
    ) + lax.dot_general(dua_ref[0], wu_ref[0], nt, preferred_element_type=f32)


def expert_grad_kernel(n2, dy, gcol, wg, wu, wd, groups):
    tokens, width = n2.shape
    experts, _, hidden = wg.shape
    bf16 = jnp.bfloat16
    whole = lambda shape: pl.BlockSpec(shape, lambda e: (0,) * len(shape))
    step = 2 if experts % 2 == 0 else 1
    per_expert = lambda shape: pl.BlockSpec((step,) + shape, lambda e: (e,) + (0,) * len(shape))
    split_rows = width // (groups * 2)
    split = pl.BlockSpec((2, step, groups, split_rows, hidden), lambda e: (0, e, 0, 0, 0))
    split_shape = jax.ShapeDtypeStruct((2, experts, groups, split_rows, hidden), bf16)
    act_shape = jax.ShapeDtypeStruct((experts, tokens, hidden), bf16)
    return pl.pallas_call(
        _grad_body,
        grid=(experts // step,),
        in_specs=[
            whole((tokens, width)),
            whole((tokens, width)),
            whole((tokens, experts)),
            per_expert((width, hidden)),
            per_expert((width, hidden)),
            per_expert((width, hidden)),
        ],
        out_specs=[split, split, split]
        + [per_expert((tokens, hidden))] * 3,
        out_shape=[split_shape] * 3 + [act_shape] * 3,
        compiler_params=pltpu.CompilerParams(
            dimension_semantics=("arbitrary",), vmem_limit_bytes=64 * 1024 * 1024
        ),
        cost_estimate=pl.CostEstimate(
            flops=experts * tokens * width * hidden * 2 * 6,
            transcendentals=experts * tokens * hidden,
            bytes_accessed=experts * width * hidden * 12 + tokens * width * 8 + experts * tokens * hidden * 6,
        ),
    )(n2, dy, gcol, wg, wu, wd)


def expert_rows_kernel(hid, dga, dua, dy, gcol, wg, wu, wd):
    experts, tokens, hidden = hid.shape
    width = dy.shape[1]
    f32 = jnp.float32
    whole = lambda shape: pl.BlockSpec(shape, lambda e: (0,) * len(shape))
    per_expert = lambda shape: pl.BlockSpec((1,) + shape, lambda e: (e,) + (0,) * len(shape))
    return pl.pallas_call(
        _rows_body,
        grid=(experts,),
        in_specs=[
            per_expert((tokens, hidden)),
            per_expert((tokens, hidden)),
            per_expert((tokens, hidden)),
            whole((tokens, width)),
            whole((tokens, experts)),
            per_expert((width, hidden)),
            per_expert((width, hidden)),
            per_expert((width, hidden)),
        ],
        out_specs=[whole((tokens, width)), per_expert((tokens, 1)), whole((tokens, width))],
        out_shape=[
            jax.ShapeDtypeStruct((tokens, width), f32),
            jax.ShapeDtypeStruct((experts, tokens, 1), f32),
            jax.ShapeDtypeStruct((tokens, width), f32),
        ],
        compiler_params=pltpu.CompilerParams(
            dimension_semantics=("arbitrary",), vmem_limit_bytes=64 * 1024 * 1024
        ),
        cost_estimate=pl.CostEstimate(
            flops=experts * tokens * width * hidden * 2 * 3,
            transcendentals=0,
            bytes_accessed=experts * width * hidden * 6 + tokens * width * 10 + experts * tokens * hidden * 6,
        ),
    )(hid, dga, dua, dy, gcol, wg, wu, wd)

MESH = pl.DeviceIdType.MESH


def _exchange_body(axis, n, per_peer, downward, src_ref, out_ref, send_sems, recv_sems):
    me = lax.axis_index(axis)
    barrier = pltpu.get_barrier_semaphore()
    for k in range(1, n):
        peer = lax.rem(me + k, n)
        pl.semaphore_signal(barrier, 1, device_id={axis: peer}, device_id_type=MESH)
    pl.semaphore_wait(barrier, n - 1)
    sends = []
    for k in range(1, n):
        peer = lax.rem(me + k, n)
        copy = pltpu.make_async_remote_copy(
            src_ref=src_ref.at[peer] if per_peer else src_ref,
            dst_ref=out_ref.at[me],
            send_sem=send_sems.at[k - 1],
            recv_sem=recv_sems.at[k - 1],
            device_id={axis: peer},
            device_id_type=MESH,
        )
        sends.append((peer, copy))
        if downward:
            pl.when(peer < me)(copy.start)
        else:
            copy.start()
    for k in range(1, n):
        source = lax.rem(me + n - k, n)
        incoming = pltpu.make_async_remote_copy(
            src_ref=src_ref.at[source] if per_peer else src_ref,
            dst_ref=out_ref.at[source],
            send_sem=send_sems.at[k - 1],
            recv_sem=recv_sems.at[k - 1],
            device_id={axis: source},
            device_id_type=MESH,
        )
        if downward:
            pl.when(source > me)(incoming.wait_recv)
        else:
            incoming.wait_recv()
    for peer, copy in sends:
        if downward:
            pl.when(peer < me)(copy.wait_send)
        else:
            copy.wait_send()


def exchange(x, axis, n, per_peer, collective_id, downward=False):
    block = x.shape[1:] if per_peer else x.shape
    nbytes = math.prod(block) * x.dtype.itemsize
    return pl.pallas_call(
        functools.partial(_exchange_body, axis, n, per_peer, downward),
        out_shape=jax.ShapeDtypeStruct((n,) + tuple(block), x.dtype),
        in_specs=[pl.BlockSpec(memory_space=pl.ANY)],
        out_specs=pl.BlockSpec(memory_space=pl.ANY),
        scratch_shapes=[pltpu.SemaphoreType.DMA((n - 1,)), pltpu.SemaphoreType.DMA((n - 1,))],
        compiler_params=pltpu.CompilerParams(collective_id=collective_id, has_side_effects=True),
        cost_estimate=pl.CostEstimate(flops=0, transcendentals=0, bytes_accessed=2 * (n - 1) * nbytes),
    )(x)


def gather_axis(x, axis, n, collective_id):
    got = exchange(x, axis, n, False, collective_id)
    return lax.dynamic_update_slice_in_dim(got, x[None], lax.axis_index(axis), 0)


def sum_axis(x, axis, collective_id):
    got = exchange(x, axis, 2, False, collective_id)
    me = lax.axis_index(axis)
    other = lax.dynamic_index_in_dim(got, 1 - me, 0, keepdims=False)
    return x.astype(jnp.float32) + other.astype(jnp.float32)


def _pair_add_body(me_ref, own_ref, other_ref, out_ref):
    out_ref[...] = (own_ref[...].astype(jnp.float32) + other_ref[...].astype(jnp.float32)).astype(out_ref.dtype)


def core_reduce(x, collective_id):
    got = exchange(x, "core", 2, True, collective_id)
    me = lax.axis_index("core")
    count = x.shape[1]
    rest = x.shape[2:]
    zeros = (0,) * len(rest)
    item_bytes = math.prod(rest) * x.dtype.itemsize
    step = max(
        [1] + [d for d in range(1, count + 1) if count % d == 0 and d * item_bytes <= 3 * 1024 * 1024 // 2]
    )
    grid_spec = pltpu.PrefetchScalarGridSpec(
        num_scalar_prefetch=1,
        grid=(count // step,),
        in_specs=[
            pl.BlockSpec((None, step) + rest, lambda i, c: (c[0], i) + zeros),
            pl.BlockSpec((None, step) + rest, lambda i, c: (1 - c[0], i) + zeros),
        ],
        out_specs=pl.BlockSpec((step,) + rest, lambda i, c: (i,) + zeros),
    )
    return pl.pallas_call(
        _pair_add_body,
        grid_spec=grid_spec,
        out_shape=jax.ShapeDtypeStruct(x.shape[1:], jnp.bfloat16),
        compiler_params=pltpu.CompilerParams(vmem_limit_bytes=56 * 1024 * 1024),
        cost_estimate=pl.CostEstimate(flops=x.size // 2, transcendentals=0, bytes_accessed=x.size * 3),
    )(jnp.reshape(me, (1,)).astype(jnp.int32), x, got)


def scatter_sum_downward(x, axis, n, collective_id):
    got = exchange(x, axis, n, True, collective_id, downward=True)
    me = lax.axis_index(axis)
    own = lax.dynamic_index_in_dim(x, me, 0, keepdims=False).astype(jnp.float32)
    above = (jnp.arange(n, dtype=jnp.int32) > me).reshape((n,) + (1,) * (x.ndim - 1))
    return own + jnp.sum(jnp.where(above, got.astype(jnp.float32), 0.0), axis=0)


def _flash_body(groups, ctx_ref, q_ref, k_ref, v_ref, qseg_ref, qpos_ref, kseg_ref, o_ref, lse_ref, qs_sc, m_sc, l_sc, acc_sc):
    f32 = jnp.float32
    block = pl.program_id(1)
    depth = HEAD_SIZE
    pair = k_ref.shape[2] // depth
    tokens = q_ref.shape[0]

    @pl.when(block == 0)
    def _():
        m_sc[...] = jnp.full_like(m_sc, NEGATIVE)
        l_sc[...] = jnp.zeros_like(l_sc)
        acc_sc[...] = jnp.zeros_like(acc_sc)
        scale = jnp.asarray(1.0 / math.sqrt(HEAD_SIZE), q_ref.dtype)
        for kk in range(pair):
            for gi in range(groups):
                i = kk * groups + gi
                qs_sc[kk, gi * tokens : (gi + 1) * tokens, :] = q_ref[:, i * depth : (i + 1) * depth] * scale

    @pl.when(block <= ctx_ref[0])
    def _():
        width = k_ref.shape[1]
        key_pos = block * width + lax.broadcasted_iota(jnp.int32, (1, width), 1)
        allowed = (qseg_ref[...] == kseg_ref[...]) & (key_pos <= qpos_ref[...])
        for kk in range(pair):
            keys = k_ref[0, :, kk * depth : (kk + 1) * depth]
            values = v_ref[0, :, kk * depth : (kk + 1) * depth]
            scores = lax.dot_general(
                qs_sc[kk], keys, (((1,), (1,)), ((), ())), preferred_element_type=f32
            )
            scores = jnp.where(allowed, scores, NEGATIVE)
            m_old = m_sc[kk]
            m_new = jnp.maximum(m_old, jnp.max(scores, axis=1, keepdims=True))
            alpha = jnp.exp(m_old - m_new)
            weights = jnp.where(allowed, jnp.exp(scores - m_new), 0.0)
            l_sc[kk] = alpha * l_sc[kk] + jnp.sum(weights, axis=1, keepdims=True)
            acc_sc[kk] = alpha * acc_sc[kk] + jnp.dot(
                weights.astype(jnp.bfloat16), values, preferred_element_type=f32
            )
            m_sc[kk] = m_new

    @pl.when(block == pl.num_programs(1) - 1)
    def _():
        for kk in range(pair):
            for gi in range(groups):
                i = kk * groups + gi
                rows = slice(gi * tokens, (gi + 1) * tokens)
                o_ref[:, i * depth : (i + 1) * depth] = acc_sc[kk, rows, :] / l_sc[kk, rows, :]
                lse_ref[0, :, i : i + 1] = m_sc[kk, rows, :] + jnp.log(l_sc[kk, rows, :])


def flash_forward(ctx_index, q, kv, qseg, qpos, kseg, groups):
    tokens, q_width = q.shape
    blocks, width, kv_width = kv.shape
    pair = 2
    pairs = kv_width // (2 * pair * HEAD_SIZE)
    heads_step = pair * groups
    f32 = jnp.float32
    capped = lambda p, b, c: (jnp.minimum(b, c[0]), 0, p)
    grid_spec = pltpu.PrefetchScalarGridSpec(
        num_scalar_prefetch=1,
        grid=(pairs, blocks),
        in_specs=[
            pl.BlockSpec((tokens, heads_step * HEAD_SIZE), lambda p, b, c: (0, p)),
            pl.BlockSpec((1, width, pair * HEAD_SIZE), capped),
            pl.BlockSpec((1, width, pair * HEAD_SIZE), lambda p, b, c: (jnp.minimum(b, c[0]), 0, pairs + p)),
            pl.BlockSpec((groups * tokens, 1), lambda p, b, c: (0, 0)),
            pl.BlockSpec((groups * tokens, 1), lambda p, b, c: (0, 0)),
            pl.BlockSpec((1, width), lambda p, b, c: (0, jnp.minimum(b, c[0]))),
        ],
        out_specs=[
            pl.BlockSpec((tokens, heads_step * HEAD_SIZE), lambda p, b, c: (0, p)),
            pl.BlockSpec((1, tokens, heads_step), lambda p, b, c: (p, 0, 0)),
        ],
        scratch_shapes=[
            pltpu.VMEM((pair, groups * tokens, HEAD_SIZE), q.dtype),
            pltpu.VMEM((pair, groups * tokens, 1), f32),
            pltpu.VMEM((pair, groups * tokens, 1), f32),
            pltpu.VMEM((pair, groups * tokens, HEAD_SIZE), f32),
        ],
    )
    return pl.pallas_call(
        functools.partial(_flash_body, groups),
        grid_spec=grid_spec,
        out_shape=[
            jax.ShapeDtypeStruct((tokens, q_width), f32),
            jax.ShapeDtypeStruct((pairs, tokens, heads_step), f32),
        ],
        compiler_params=pltpu.CompilerParams(
            dimension_semantics=("arbitrary", "arbitrary"), vmem_limit_bytes=48 * 1024 * 1024
        ),
        cost_estimate=pl.CostEstimate(
            flops=tokens * q_width * blocks * width * 4,
            transcendentals=tokens * (q_width // HEAD_SIZE) * blocks * width,
            bytes_accessed=(q.size + kv.size) * 2 + tokens * q_width * 4,
        ),
    )(jnp.reshape(ctx_index, (1,)).astype(jnp.int32), q, kv, kv, qseg, qpos, kseg)

def _chain_down_body(axis, n, x_ref, out_ref, recv, send, send_sems, recv_sems):
    f32 = jnp.float32
    me = lax.axis_index(axis)
    below = lax.rem(me + n - 1, n)
    above = lax.rem(me + 1, n)
    barrier = pltpu.get_barrier_semaphore()
    pl.semaphore_signal(barrier, 1, device_id={axis: below}, device_id_type=MESH)
    pl.semaphore_signal(barrier, 1, device_id={axis: above}, device_id_type=MESH)
    pl.semaphore_wait(barrier, 2)
    copies = []
    for j in range(n - 1):
        copy = pltpu.make_async_remote_copy(
            src_ref=send.at[j],
            dst_ref=recv.at[j],
            send_sem=send_sems.at[j],
            recv_sem=recv_sems.at[j],
            device_id={axis: below},
            device_id_type=MESH,
        )
        copies.append(copy)

        @pl.when((j < me) & (me < n - 1))
        def _():
            copy.wait_recv()
            send[j] = (x_ref[j].astype(f32) + recv[j].astype(f32)).astype(send.dtype)

        @pl.when((j < me) & (me == n - 1))
        def _():
            send[j] = x_ref[j]

        @pl.when(j < me)
        def _():
            copy.start()

        @pl.when(j == me)
        def _():
            copy.wait_recv()
            out_ref[...] = x_ref[j].astype(f32) + recv[j].astype(f32)

    @pl.when(me == n - 1)
    def _():
        out_ref[...] = x_ref[n - 1].astype(f32)

    for j in range(n - 1):
        pl.when(j < me)(copies[j].wait_send)


def chain_sum_down(x, axis, n, collective_id):
    _, rows, cols = x.shape
    return pl.pallas_call(
        functools.partial(_chain_down_body, axis, n),
        out_shape=jax.ShapeDtypeStruct((rows, cols), jnp.float32),
        in_specs=[pl.BlockSpec(memory_space=pltpu.VMEM)],
        out_specs=pl.BlockSpec(memory_space=pltpu.VMEM),
        scratch_shapes=[
            pltpu.VMEM((n - 1, rows, cols), x.dtype),
            pltpu.VMEM((n - 1, rows, cols), x.dtype),
            pltpu.SemaphoreType.DMA((n - 1,)),
            pltpu.SemaphoreType.DMA((n - 1,)),
        ],
        compiler_params=pltpu.CompilerParams(
            collective_id=collective_id, has_side_effects=True, vmem_limit_bytes=32 * 1024 * 1024
        ),
        cost_estimate=pl.CostEstimate(
            flops=(n - 1) * rows * cols, transcendentals=0, bytes_accessed=3 * n * rows * cols * 2
        ),
    )(x)


def _chain_up_body(axis, n, x_ref, out_ref, send_sems, recv_sems):
    me = lax.axis_index(axis)
    below = lax.rem(me + n - 1, n)
    above = lax.rem(me + 1, n)
    barrier = pltpu.get_barrier_semaphore()
    pl.semaphore_signal(barrier, 1, device_id={axis: below}, device_id_type=MESH)
    pl.semaphore_signal(barrier, 1, device_id={axis: above}, device_id_type=MESH)
    pl.semaphore_wait(barrier, 2)
    own = pltpu.make_async_remote_copy(
        src_ref=x_ref,
        dst_ref=out_ref.at[me],
        send_sem=send_sems.at[me],
        recv_sem=recv_sems.at[me],
        device_id={axis: above},
        device_id_type=MESH,
    )
    pl.when(me < n - 1)(own.start)
    forwards = []
    for k in range(1, n):
        block = jnp.maximum(me - k, 0)
        incoming = pltpu.make_async_remote_copy(
            src_ref=out_ref.at[block],
            dst_ref=out_ref.at[block],
            send_sem=send_sems.at[block],
            recv_sem=recv_sems.at[block],
            device_id={axis: below},
            device_id_type=MESH,
        )
        forward = pltpu.make_async_remote_copy(
            src_ref=out_ref.at[block],
            dst_ref=out_ref.at[block],
            send_sem=send_sems.at[block],
            recv_sem=recv_sems.at[block],
            device_id={axis: above},
            device_id_type=MESH,
        )
        forwards.append((k, forward))
        pl.when(k <= me)(incoming.wait_recv)
        pl.when((k <= me) & (me < n - 1))(forward.start)
    pl.when(me < n - 1)(own.wait_send)
    for k, forward in forwards:
        pl.when((k <= me) & (me < n - 1))(forward.wait_send)


def gather_up(x, axis, n, collective_id):
    got = pl.pallas_call(
        functools.partial(_chain_up_body, axis, n),
        out_shape=jax.ShapeDtypeStruct((n,) + x.shape, x.dtype),
        in_specs=[pl.BlockSpec(memory_space=pl.ANY)],
        out_specs=pl.BlockSpec(memory_space=pl.ANY),
        scratch_shapes=[pltpu.SemaphoreType.DMA((n,)), pltpu.SemaphoreType.DMA((n,))],
        compiler_params=pltpu.CompilerParams(collective_id=collective_id, has_side_effects=True),
        cost_estimate=pl.CostEstimate(
            flops=0, transcendentals=0, bytes_accessed=2 * (n - 1) * x.size * x.dtype.itemsize
        ),
    )(x)
    me = lax.axis_index(axis)
    below = (jnp.arange(n, dtype=jnp.int32) < me).reshape((n,) + (1,) * x.ndim)
    got = jnp.where(below, got, jnp.zeros_like(got))
    return lax.dynamic_update_slice_in_dim(got, x[None], me, 0)


def _attend_block(groups, kv_heads, q_sc, kv_buf, qseg_ref, qpos_ref, kseg_ref, m_sc, l_sc, acc_sc, block):
    f32 = jnp.float32
    depth = HEAD_SIZE
    width = kv_buf.shape[0]
    start = pl.multiple_of(block * width, width)
    key_pos = start + lax.broadcasted_iota(jnp.int32, (1, width), 1)
    allowed = (qseg_ref[...] == kseg_ref[:, pl.ds(start, width)]) & (key_pos <= qpos_ref[...])
    for kk in range(kv_heads):
        keys = kv_buf[:, kk * depth : (kk + 1) * depth]
        values = kv_buf[:, (kv_heads + kk) * depth : (kv_heads + kk + 1) * depth]
        scores = lax.dot_general(q_sc[kk], keys, (((1,), (1,)), ((), ())), preferred_element_type=f32)
        scores = jnp.where(allowed, scores, NEGATIVE)
        m_old = m_sc[kk]
        m_new = jnp.maximum(m_old, jnp.max(scores, axis=1, keepdims=True))
        alpha = jnp.exp(m_old - m_new)
        weights = jnp.where(allowed, jnp.exp(scores - m_new), 0.0)
        l_sc[kk] = alpha * l_sc[kk] + jnp.sum(weights, axis=1, keepdims=True)
        acc_sc[kk] = alpha * acc_sc[kk] + jnp.dot(
            weights.astype(jnp.bfloat16), values, preferred_element_type=f32
        )
        m_sc[kk] = m_new


def _gather_attend_body(
    axis, n, groups, q_ref, own_ref, qseg_ref, qpos_ref, kseg_ref,
    kv_ref, o_ref, lse_ref,
    q_sc, m_sc, l_sc, acc_sc, kv_buf, send_sems, recv_sems, copy_sem,
):
    depth = HEAD_SIZE
    tokens = q_ref.shape[0]
    kv_heads = own_ref.shape[1] // (2 * depth)
    me = lax.axis_index(axis)
    below = lax.rem(me + n - 1, n)
    above = lax.rem(me + 1, n)
    barrier = pltpu.get_barrier_semaphore()
    pl.semaphore_signal(barrier, 1, device_id={axis: below}, device_id_type=MESH)
    pl.semaphore_signal(barrier, 1, device_id={axis: above}, device_id_type=MESH)
    pl.semaphore_wait(barrier, 2)
    own = pltpu.make_async_remote_copy(
        src_ref=own_ref,
        dst_ref=kv_ref.at[me],
        send_sem=send_sems.at[me],
        recv_sem=recv_sems.at[me],
        device_id={axis: above},
        device_id_type=MESH,
    )
    pl.when(me < n - 1)(own.start)

    m_sc[...] = jnp.full_like(m_sc, NEGATIVE)
    l_sc[...] = jnp.zeros_like(l_sc)
    acc_sc[...] = jnp.zeros_like(acc_sc)
    scale = jnp.asarray(1.0 / math.sqrt(HEAD_SIZE), q_ref.dtype)
    for kk in range(kv_heads):
        for gi in range(groups):
            i = kk * groups + gi
            q_sc[kk, gi * tokens : (gi + 1) * tokens, :] = q_ref[:, i * depth : (i + 1) * depth] * scale

    local = pltpu.make_async_copy(own_ref, kv_buf, copy_sem)
    local.start()
    local.wait()
    _attend_block(groups, kv_heads, q_sc, kv_buf, qseg_ref, qpos_ref, kseg_ref, m_sc, l_sc, acc_sc, me)

    def step(k, carry):
        block = me - k
        incoming = pltpu.make_async_remote_copy(
            src_ref=kv_ref.at[block],
            dst_ref=kv_ref.at[block],
            send_sem=send_sems.at[block],
            recv_sem=recv_sems.at[block],
            device_id={axis: below},
            device_id_type=MESH,
        )
        incoming.wait_recv()
        forward = pltpu.make_async_remote_copy(
            src_ref=kv_ref.at[block],
            dst_ref=kv_ref.at[block],
            send_sem=send_sems.at[block],
            recv_sem=recv_sems.at[block],
            device_id={axis: above},
            device_id_type=MESH,
        )
        pl.when(me < n - 1)(forward.start)
        fetch = pltpu.make_async_copy(kv_ref.at[block], kv_buf, copy_sem)
        fetch.start()
        fetch.wait()
        _attend_block(groups, kv_heads, q_sc, kv_buf, qseg_ref, qpos_ref, kseg_ref, m_sc, l_sc, acc_sc, block)
        return carry

    lax.fori_loop(1, me + 1, step, 0)

    for kk in range(kv_heads):
        for gi in range(groups):
            i = kk * groups + gi
            rows = slice(gi * tokens, (gi + 1) * tokens)
            o_ref[:, i * depth : (i + 1) * depth] = acc_sc[kk, rows, :] / l_sc[kk, rows, :]
            lse_ref[:, i : i + 1] = m_sc[kk, rows, :] + jnp.log(l_sc[kk, rows, :])

    pl.when(me < n - 1)(own.wait_send)

    def drain(k, carry):
        block = me - k
        pltpu.make_async_remote_copy(
            src_ref=kv_ref.at[block],
            dst_ref=kv_ref.at[block],
            send_sem=send_sems.at[block],
            recv_sem=recv_sems.at[block],
            device_id={axis: above},
            device_id_type=MESH,
        ).wait_send()
        return carry

    lax.fori_loop(1, jnp.where(me < n - 1, me + 1, 1), drain, 0)


def gather_attend(q, own, qseg, qpos, kseg, axis, n, groups, collective_id):
    tokens, q_width = q.shape
    rows, kv_width = own.shape
    heads = q_width // HEAD_SIZE
    kv_heads = kv_width // (2 * HEAD_SIZE)
    f32 = jnp.float32
    vmem = pl.BlockSpec(memory_space=pltpu.VMEM)
    anywhere = pl.BlockSpec(memory_space=pl.ANY)
    kv_all, attn, lse = pl.pallas_call(
        functools.partial(_gather_attend_body, axis, n, groups),
        out_shape=[
            jax.ShapeDtypeStruct((n, rows, kv_width), own.dtype),
            jax.ShapeDtypeStruct((tokens, q_width), f32),
            jax.ShapeDtypeStruct((tokens, heads), f32),
        ],
        in_specs=[vmem, anywhere, vmem, vmem, vmem],
        out_specs=[anywhere, vmem, vmem],
        scratch_shapes=[
            pltpu.VMEM((kv_heads, groups * tokens, HEAD_SIZE), q.dtype),
            pltpu.VMEM((kv_heads, groups * tokens, 1), f32),
            pltpu.VMEM((kv_heads, groups * tokens, 1), f32),
            pltpu.VMEM((kv_heads, groups * tokens, HEAD_SIZE), f32),
            pltpu.VMEM((rows, kv_width), own.dtype),
            pltpu.SemaphoreType.DMA((n,)),
            pltpu.SemaphoreType.DMA((n,)),
            pltpu.SemaphoreType.DMA(()),
        ],
        compiler_params=pltpu.CompilerParams(
            collective_id=collective_id, has_side_effects=True, vmem_limit_bytes=48 * 1024 * 1024
        ),
        cost_estimate=pl.CostEstimate(
            flops=tokens * q_width * n * rows * 4,
            transcendentals=tokens * heads * n * rows,
            bytes_accessed=2 * n * own.size * own.dtype.itemsize + tokens * q_width * 6,
        ),
    )(q, own, qseg, qpos, kseg)
    me = lax.axis_index(axis)
    below = (jnp.arange(n, dtype=jnp.int32) < me).reshape((n, 1, 1))
    kv_all = jnp.where(below, kv_all, jnp.zeros_like(kv_all))
    return attn, lse, lax.dynamic_update_slice_in_dim(kv_all, own[None], me, 0)


def per_device(
    dpx_count,
    hidden_in,
    attn_gain,
    q_weight,
    key_matrix,
    value_matrix,
    o_weight,
    moe_gain,
    router_weight,
    gate_weight,
    up_weight,
    down_weight,
    segments,
    expert_picks,
    output_grad,
):
    bf16 = jnp.bfloat16
    f32 = jnp.float32
    token_count = hidden_in.shape[0]
    ctx_index = lax.axis_index("ctx")
    heads_local = q_weight.shape[1] // HEAD_SIZE
    kv_local = key_matrix.shape[1] // HEAD_SIZE
    group_size = heads_local // kv_local
    score_scale = 1.0 / math.sqrt(HEAD_SIZE)
    token_positions = ctx_index * token_count + jnp.arange(token_count, dtype=jnp.int32)
    segment_here = lax.dynamic_slice_in_dim(segments, ctx_index * token_count, token_count)
    inputs_f32 = hidden_in.astype(f32)
    o_full = lax.all_gather(o_weight, "tensor", axis=0, tiled=False)
    normed_f32, scale_one = normalize(inputs_f32, attn_gain)
    normed_one = normed_f32.astype(bf16)
    query_rows = jnp.dot(normed_one, q_weight, preferred_element_type=f32).reshape(
        token_count, heads_local, HEAD_SIZE
    )
    keys_raw = jnp.dot(normed_one, key_matrix, preferred_element_type=f32).reshape(
        token_count, kv_local, HEAD_SIZE
    )
    values_raw = jnp.dot(normed_one, value_matrix, preferred_element_type=f32)
    query_grouped = (
        apply_rotary(query_rows, token_positions, 1.0)
        .astype(bf16)
        .reshape(token_count, kv_local, group_size, HEAD_SIZE)
    )
    key_flat = (
        apply_rotary(keys_raw, token_positions, 1.0)
        .astype(bf16)
        .reshape(token_count, kv_local * HEAD_SIZE)
    )
    value_flat = values_raw.astype(bf16)

    def piece_mask(piece_rows):
        key_pos = jnp.arange(piece_rows, dtype=jnp.int32)
        return (segment_here[:, None] == segments[None, :]) & (
            key_pos[None, :] <= token_positions[:, None]
        )

    ctx_count = segments.shape[0] // token_count
    attn_flat, lse_heads, kv_both = gather_attend(
        query_grouped.reshape(token_count, heads_local * HEAD_SIZE),
        jnp.concatenate([key_flat, value_flat], axis=1),
        jnp.tile(segment_here, group_size)[:, None],
        jnp.tile(token_positions, group_size)[:, None],
        segments[None, :],
        "ctx",
        ctx_count,
        group_size,
        1,
    )
    piece_rows = ctx_count * token_count
    kv_width = kv_local * HEAD_SIZE
    key_piece = kv_both[:, :, :kv_width].reshape(piece_rows, kv_local, HEAD_SIZE)
    value_piece = kv_both[:, :, kv_width:].reshape(piece_rows, kv_local, HEAD_SIZE)
    attn_grouped = jnp.transpose(
        attn_flat.reshape(token_count, kv_local, group_size, HEAD_SIZE), (1, 2, 0, 3)
    )
    log_sum = jnp.transpose(lse_heads.reshape(token_count, kv_local, group_size), (1, 2, 0))
    attn_bf = attn_flat.astype(bf16)
    tensor_count = o_weight.shape[0] // o_weight.shape[1]
    attn_all = gather_axis(attn_bf, "tensor", tensor_count, 2)
    mixed_attn = lax.dot_general(
        attn_all, o_full, (((0, 2), (0, 2)), ((), ())), preferred_element_type=f32
    )
    resid = inputs_f32 + mixed_attn
    normed_two_f32, scale_two = normalize(resid, moe_gain)
    normed_two = normed_two_f32.astype(bf16)
    logits = jnp.dot(normed_two, router_weight, preferred_element_type=f32)
    expert_range = jnp.arange(NEXP, dtype=jnp.int32)
    picked_onehot = expert_picks[:, :, None] == expert_range[None, None, :]
    picked = jnp.sum(jnp.where(picked_onehot, logits[:, None, :], 0.0), axis=2)
    gate_probs = jax.nn.softmax(picked, axis=-1)
    gates_dense = jnp.sum(jnp.where(picked_onehot, gate_probs[:, :, None], 0.0), axis=1)
    gates_by_expert = jnp.transpose(gates_dense)
    cot_bf = output_grad
    gcol = gates_dense
    grad_gate, grad_up, grad_down, hid_all, dga_all, dua_all = expert_grad_kernel(
        normed_two,
        cot_bf,
        gcol,
        gate_weight,
        up_weight,
        down_weight,
        dpx_count,
    )
    gate_half = core_reduce(grad_gate, 8)
    gate_half, hid_all, dga_all, dua_all = lax.optimization_barrier(
        (gate_half, hid_all, dga_all, dua_all)
    )
    moe_acc, gate_parts, moe_grad_rows = expert_rows_kernel(
        hid_all, dga_all, dua_all, cot_bf, gcol, gate_weight, up_weight, down_weight
    )
    cot_f32 = output_grad.astype(f32)
    moe_total = sum_axis(moe_acc.astype(bf16), "tensor", 3)
    output = (resid + moe_total).astype(bf16)
    grad_rows_all = moe_grad_rows
    gate_parts = gate_parts[:, :, 0]
    grad_gate_out, grad_up_out, grad_down_out = [
        lax.psum_scatter(
            g.reshape(g.shape[0], -1, g.shape[3]), ("dpx", "ctx"), scatter_dimension=1, tiled=True
        )
        for g in (gate_half, core_reduce(grad_up, 9), core_reduce(grad_down, 10))
    ]
    gate_pair = jnp.sum(
        jnp.where(picked_onehot, jnp.transpose(gate_parts)[:, None, :], 0.0), axis=2
    )
    moe_summed = sum_axis(grad_rows_all.astype(bf16), "tensor", 4)
    gate_summed = sum_axis(gate_pair.astype(bf16), "tensor", 5)
    grad_picked = gate_probs * (
        gate_summed - jnp.sum(gate_probs * gate_summed, axis=1, keepdims=True)
    )
    grad_logits = jnp.sum(jnp.where(picked_onehot, grad_picked[:, :, None], 0.0), axis=1).astype(
        bf16
    )
    grad_router = contract_rows(normed_two, grad_logits)
    grad_normed_two = moe_summed + contract_cols(grad_logits, router_weight)
    grad_two_rows, grad_moe_gain = norm_backward(resid, scale_two, moe_gain, grad_normed_two)
    grad_resid = cot_f32 + grad_two_rows
    grad_mix = grad_resid.astype(bf16)
    grad_o = contract_rows(grad_mix, attn_bf)
    grad_attn = jnp.dot(grad_mix, o_weight, preferred_element_type=f32).astype(bf16)
    grad_attn_grouped = jnp.transpose(
        grad_attn.reshape(token_count, kv_local, group_size, HEAD_SIZE), (1, 2, 0, 3)
    )
    row_delta = jnp.sum(grad_attn_grouped.astype(f32) * attn_grouped, axis=-1)
    allowed = piece_mask(piece_rows)
    scores = (
        jnp.einsum("tkgd,nkd->kgtn", query_grouped, key_piece, preferred_element_type=f32)
        * score_scale
    )
    probability = jnp.where(allowed, jnp.exp(scores - log_sum[..., None]), 0.0)
    grad_probs = jnp.einsum(
        "kgtd,nkd->kgtn", grad_attn_grouped, value_piece, preferred_element_type=f32
    )
    grad_scores = (probability * (grad_probs - row_delta[..., None])).astype(bf16)
    grad_query = score_scale * jnp.einsum(
        "kgtn,nkd->kgtd", grad_scores, key_piece, preferred_element_type=f32
    )
    key_part = score_scale * jnp.einsum(
        "kgtn,tkgd->nkd", grad_scores, query_grouped, preferred_element_type=f32
    )
    value_part = jnp.einsum(
        "kgtn,kgtd->nkd", probability.astype(bf16), grad_attn_grouped, preferred_element_type=f32
    )
    grad_keys_all = key_part.reshape(piece_rows, kv_local * HEAD_SIZE)
    grad_values_all = value_part.reshape(piece_rows, kv_local * HEAD_SIZE)
    back_state = (grad_query, grad_keys_all, grad_values_all)
    grad_query, grad_keys_all, grad_values_all = back_state
    grad_kv_here = chain_sum_down(
        jnp.concatenate([grad_keys_all, grad_values_all], axis=1)
        .astype(bf16)
        .reshape(ctx_count, token_count, 2 * kv_width),
        "ctx",
        ctx_count,
        6,
    )
    grad_keys_here = grad_kv_here[:, :kv_width]
    grad_values_here = grad_kv_here[:, kv_width:]
    grad_query_rows = jnp.transpose(grad_query, (2, 0, 1, 3)).reshape(
        token_count, heads_local, HEAD_SIZE
    )
    grad_query_bf = (
        apply_rotary(grad_query_rows, token_positions, -1.0)
        .reshape(token_count, heads_local * HEAD_SIZE)
        .astype(bf16)
    )
    grad_key_bf = (
        apply_rotary(
            grad_keys_here.reshape(token_count, kv_local, HEAD_SIZE), token_positions, -1.0
        )
        .reshape(token_count, kv_local * HEAD_SIZE)
        .astype(bf16)
    )
    grad_value_bf = grad_values_here.astype(bf16)
    grad_q = contract_rows(normed_one, grad_query_bf)
    grad_k = contract_rows(normed_one, grad_key_bf)
    grad_v = contract_rows(normed_one, grad_value_bf)
    partial_one = (
        contract_cols(grad_query_bf, q_weight)
        + contract_cols(grad_key_bf, key_matrix)
        + contract_cols(grad_value_bf, value_matrix)
    )
    grad_normed_one = sum_axis(partial_one.astype(bf16), "tensor", 7)
    grad_one_rows, grad_attn_gain = norm_backward(inputs_f32, scale_one, attn_gain, grad_normed_one)
    input_grad = grad_resid + grad_one_rows
    q_cols, o_cols, k_cols = grad_q.shape[1], grad_o.shape[1], grad_k.shape[1]
    small = jnp.concatenate(
        [
            grad_router,
            grad_attn_gain[:, None],
            grad_moe_gain[:, None],
            jnp.zeros((grad_router.shape[0], 128 - grad_router.shape[1] - 2), f32),
        ],
        axis=1,
    )
    dense_all = jnp.concatenate(
        [grad_q, grad_o, grad_k, grad_v, small], axis=1
    ).astype(bf16)
    width = dense_all.shape[0]
    dense_all = jnp.transpose(
        dense_all.reshape(dpx_count, 2, width // (2 * dpx_count), dense_all.shape[1]), (1, 0, 2, 3)
    )
    dense_half = core_reduce(dense_all, 11)
    dense_half, grad_gate_out, grad_up_out, grad_down_out = lax.optimization_barrier(
        (dense_half, grad_gate_out, grad_up_out, grad_down_out)
    )
    grad_gate_out, grad_up_out, grad_down_out = (
        grad_gate_out.astype(f32),
        grad_up_out.astype(f32),
        grad_down_out.astype(f32),
    )
    dense_here = lax.psum_scatter(
        dense_half.reshape(-1, dense_half.shape[-1]), ("dpx", "ctx"), scatter_dimension=0, tiled=True
    ).astype(f32)
    spans = [q_cols, o_cols, k_cols, k_cols, router_weight.shape[1], 1, 1]
    cuts = [sum(spans[:i]) for i in range(len(spans) + 1)]
    pieces_out = [dense_here[:, cuts[i] : cuts[i + 1]] for i in range(len(spans))]
    dense_out = (
        pieces_out[5][:, 0],
        pieces_out[0],
        pieces_out[2],
        pieces_out[3],
        pieces_out[1],
        pieces_out[6][:, 0],
        pieces_out[4],
    )
    return (
        output,
        input_grad,
        dense_out[0],
        dense_out[1],
        dense_out[2],
        dense_out[3],
        dense_out[4],
        dense_out[5],
        dense_out[6],
        grad_gate_out,
        grad_up_out,
        grad_down_out,
    )


def solution(mesh):
    dp_count, ctx_count, tensor_count = (mesh.shape[a] for a in ("dp", "ctx", "tensor"))
    split_mesh = jax.sharding.Mesh(
        mesh.devices.reshape(dp_count // 2, 2, ctx_count, tensor_count), ("dpx", "core", "ctx", "tensor")
    )
    return jax.shard_map(
        functools.partial(per_device, dp_count // 2),
        mesh=split_mesh,
        in_specs=(
            P(("dpx", "core", "ctx"), None),
            P(),
            P(None, "tensor"),
            P(None, "tensor"),
            P(None, "tensor"),
            P(None, "tensor"),
            P(),
            P(),
            P(None, None, "tensor"),
            P(None, None, "tensor"),
            P(None, None, "tensor"),
            P(("dpx", "core")),
            P(("dpx", "core", "ctx"), None),
            P(("dpx", "core", "ctx"), None),
        ),
        out_specs=(
            P(("dpx", "core", "ctx"), None),
            P(("dpx", "core", "ctx"), None),
            P(("dpx", "core", "ctx")),
            P(("dpx", "core", "ctx"), "tensor"),
            P(("dpx", "core", "ctx"), "tensor"),
            P(("dpx", "core", "ctx"), "tensor"),
            P(("dpx", "core", "ctx"), "tensor"),
            P(("dpx", "core", "ctx")),
            P(("dpx", "core", "ctx"), None),
            P(None, ("dpx", "core", "ctx"), "tensor"),
            P(None, ("dpx", "core", "ctx"), "tensor"),
            P(None, ("dpx", "core", "ctx"), "tensor"),
        ),
        check_vma=False,
    )
```
